32 devices in a mesh: ctx: 8 (over z, x), fsdp: 4 (over y, core).
Axes of the slice: x: 2, y: 2, z: 4, core: 2. Of those that a mesh axis runs over, the one named last changes fastest.
Arguments:
- inputs: bfloat16 [4, 4096, 768], P('fsdp', 'ctx'), may hold values from -6 to 6
- doc_starts: int32 [4, 8], P('fsdp'), may hold values from 0 to 4095, as said below
- qkv_weight: bfloat16 [768, 2304], P('fsdp'), may hold values from -0.21875 to 0.21875
- query_bias: bfloat16 [768], P('fsdp'), may hold values from -3 to 3
- value_bias: bfloat16 [768], P('fsdp'), may hold values from -3 to 3
- out_weight: bfloat16 [768, 768], P('fsdp'), may hold values from -2 to 2
- out_bias: bfloat16 [768], P('fsdp'), may hold values from -2 to 2
- norm1_gain: bfloat16 [768], P('fsdp'), may hold values from 0.25 to 1.75
- norm1_bias: bfloat16 [768], P('fsdp'), may hold values from -2 to 2
- in_weight: bfloat16 [768, 3072], P('fsdp'), may hold values from -0.21875 to 0.21875
- in_bias: bfloat16 [3072], P('fsdp'), may hold values from -3 to 3
- back_weight: bfloat16 [3072, 768], P('fsdp'), may hold values from -0.109375 to 0.109375
- back_bias: bfloat16 [768], P('fsdp'), may hold values from -2 to 2
- norm2_gain: bfloat16 [768], P('fsdp'), may hold values from 0.25 to 1.75
- norm2_bias: bfloat16 [768], P('fsdp'), may hold values from -2 to 2
- cotangent: bfloat16 [4, 4096, 768], P('fsdp', 'ctx'), may hold values from -6 to 6
Outputs:
- output: bfloat16 [4, 4096, 768], P('fsdp', 'ctx')
- input_grad: float32 [4, 4096, 768], P('fsdp', 'ctx')
- qkv_weight_grad: float32 [768, 2304], P('fsdp')
- query_bias_grad: float32 [768], P('fsdp')
- value_bias_grad: float32 [768], P('fsdp')
- out_weight_grad: float32 [768, 768], P('fsdp')
- out_bias_grad: float32 [768], P('fsdp')
- norm1_gain_grad: float32 [768], P('fsdp')
- norm1_bias_grad: float32 [768], P('fsdp')
- in_weight_grad: float32 [768, 3072], P('fsdp')
- in_bias_grad: float32 [3072], P('fsdp')
- back_weight_grad: float32 [3072, 768], P('fsdp')
- back_bias_grad: float32 [768], P('fsdp')
- norm2_gain_grad: float32 [768], P('fsdp')
- norm2_bias_grad: float32 [768], P('fsdp')
The draws below stay inside these ranges and needn't reach their ends.
Inputs may be any that keep to these rules, and one draw needn't show every extreme that they name: `doc_starts`: row s lists the first positions of the 8 documents of stream s in increasing order, all different; the first is 0 and the last is 4095, a one-token document at the stream's end. A document runs from its start to the next start.
All inputs are finite; a program needn't handle non-finite values.
Results may differ from the reference program's by a relative error of at most 0.022.
Values may be sent and summed in bfloat16 or wider, within the bound.
No kernel may reach another device: no remote copies, remote signals or barrier semaphores. Data moves between devices by JAX's collectives and lax.ppermute only.
A program may use at most 192 MiB of HBM per device.

```python
import math
import jax
import jax.numpy as jnp
from jax import lax

D = 768
H = 12
HD = 64
FF = 3072
DOCS = 8
STREAM = 4096
NSTREAM = 4


def draw_doc_starts(key, part):

    def one_stream(stream_key):
        picks = jax.random.permutation(stream_key, STREAM - 2)[:DOCS - 2] + 1
        ordered = jnp.sort(picks.astype(jnp.int32))
        return jnp.concatenate([jnp.zeros((1,), jnp.int32), ordered, jnp.full((1,), STREAM - 1, jnp.int32)])
    return jax.vmap(one_stream)(jax.random.split(key, NSTREAM))


def levels(key, extent, cuts, low, high):
    factor_of, own = 1.0, jax.random.fold_in(key, 6)
    for dim, shards_of in cuts:
        draws = jnp.exp(jax.random.uniform(jax.random.fold_in(own, dim), (shards_of,), jnp.float32, low / len(cuts), high / len(cuts)))
        factor_of = factor_of * jnp.repeat(draws, extent[dim] // shards_of).reshape([-1 if axis == dim else 1 for axis in range(len(extent))])
    return factor_of


def normal_values(own_key, extent, scale, limit, cuts=(), kind=jnp.bfloat16):
    values = scale * jax.random.normal(own_key, extent, jnp.float32)
    if cuts:
        values = values * levels(own_key, extent, cuts, -0.22, 0.18)
    return jnp.clip(values, -limit, limit).astype(kind)


def setup_inputs(seed: int = 0) -> dict:
    seeds = jax.random.split(jax.random.key(seed), 17)
    inputs = normal_values(seeds[0], (NSTREAM, STREAM, D), 1.0, 6.0, ((0, 4), (1, 8)))
    doc_starts = draw_doc_starts(jax.random.fold_in(seeds[16], 71), 0)
    qkv_weight = normal_values(seeds[2], (D, 3 * D), D ** -0.5, 0.21875, ((0, 4),))
    query_bias = normal_values(seeds[3], (D,), 0.5, 3.0, ((0, 4),))
    value_bias = normal_values(seeds[4], (D,), 0.5, 3.0, ((0, 4),))
    out_weight = normal_values(seeds[5], (D, D), 8 ** -0.5, 2.0, ((0, 4),))
    out_bias = normal_values(seeds[6], (D,), 0.3, 2.0, ((0, 4),))
    norm1_gain = jnp.clip(1.0 + 0.15 * jax.random.normal(seeds[7], (D,), jnp.float32), 0.25, 1.75).astype(jnp.bfloat16)
    norm1_bias = normal_values(seeds[8], (D,), 0.3, 2.0, ((0, 4),))
    in_weight = normal_values(seeds[9], (D, FF), D ** -0.5, 0.21875, ((0, 4),))
    in_bias = normal_values(seeds[10], (FF,), 0.5, 3.0, ((0, 4),))
    back_weight = normal_values(seeds[11], (FF, D), FF ** -0.5, 0.109375, ((0, 4),))
    back_bias = normal_values(seeds[12], (D,), 0.3, 2.0, ((0, 4),))
    norm2_gain = jnp.clip(1.0 + 0.15 * jax.random.normal(seeds[13], (D,), jnp.float32), 0.25, 1.75).astype(jnp.bfloat16)
    norm2_bias = normal_values(seeds[14], (D,), 0.3, 2.0, ((0, 4),))
    cotangent = normal_values(seeds[15], (NSTREAM, STREAM, D), 1.0, 6.0, ((0, 4), (1, 8)))
    return dict(inputs=inputs, doc_starts=doc_starts, qkv_weight=qkv_weight, query_bias=query_bias, value_bias=value_bias, out_weight=out_weight, out_bias=out_bias, norm1_gain=norm1_gain, norm1_bias=norm1_bias, in_weight=in_weight, in_bias=in_bias, back_weight=back_weight, back_bias=back_bias, norm2_gain=norm2_gain, norm2_bias=norm2_bias, cotangent=cotangent)


EPSILON = 1e-05
NEGATIVE = -1e+30
HIGHEST = lax.Precision.HIGHEST

@jax.custom_vjp
def low(v):
    return lax.optimization_barrier(v.astype(jnp.bfloat16)).astype(jnp.float32)

@jax.custom_vjp
def low_back(v):
    return v

def low_keep(v):
    return (low(v), None)

def low_pass(kept, grad):
    return (grad,)

def back_keep(v):
    return (v, None)

def back_low(kept, grad):
    return (low(grad),)
low.defvjp(low_keep, low_pass)
low_back.defvjp(back_keep, back_low)

def layer_norm(resid, gain, shift):
    centre = lax.optimization_barrier(jnp.mean(resid, axis=-1, keepdims=True))
    centred = resid - centre
    spread = lax.optimization_barrier(jnp.mean(centred * centred, axis=-1, keepdims=True))
    return centred * lax.rsqrt(spread + EPSILON) * gain + shift

def doc_index(start_row, length):
    positions = jnp.arange(length, dtype=jnp.int32)
    return lax.optimization_barrier(jnp.sum((start_row[None, :] <= positions[:, None]).astype(jnp.int32), axis=1)) - 1

def attend_stream(query_rows, key_rows, value_rows, doc_ids):
    length = query_rows.shape[0]
    size = math.gcd(length, 512)
    count = length // size
    query_blocks = query_rows.reshape(count, size, H, HD)
    doc_blocks = doc_ids.reshape(count, size)
    key_heads = key_rows.reshape(length, H, HD)
    value_heads = value_rows.reshape(length, H, HD)

    def one_block(element):
        query_block, doc_block = element
        raw_scores = low_back(jnp.einsum('qhd,khd->hqk', query_block, key_heads, precision=HIGHEST))
        allowed = (doc_block[:, None] == doc_ids[None, :])[None]
        scores = jnp.where(allowed, raw_scores * HD ** (-0.5), NEGATIVE)
        row_max = lax.optimization_barrier(jnp.max(scores, axis=-1, keepdims=True))
        weights = jnp.where(allowed, jnp.exp(scores - row_max), 0.0)
        probs = weights / lax.optimization_barrier(jnp.sum(weights, axis=-1, keepdims=True))
        return jnp.einsum('hqk,khd->qhd', low(probs), value_heads, precision=HIGHEST)
    attended = lax.map(jax.checkpoint(one_block), (query_blocks, doc_blocks))
    return attended.reshape(length, H * HD)

def forward(inputs, qkv_weight, query_bias, value_bias, out_weight, out_bias, norm1_gain, norm1_bias, in_weight, in_bias, back_weight, back_bias, norm2_gain, norm2_bias, doc_ids):
    projected = jnp.einsum('std,de->ste', inputs, qkv_weight, precision=HIGHEST)
    query_rows = low(low_back(projected[..., :D] + query_bias))
    key_rows = low(low_back(projected[..., D:2 * D]))
    value_rows = low(low_back(projected[..., 2 * D:] + value_bias))
    attended = lax.map(lambda element: attend_stream(*element), (query_rows, key_rows, value_rows, doc_ids))
    attended_low = low(low_back(attended))
    branch = low_back(jnp.einsum('stc,cd->std', attended_low, out_weight, precision=HIGHEST) + out_bias)
    hidden = layer_norm(inputs + branch, norm1_gain, norm1_bias)
    pre_act = low_back(jnp.einsum('std,df->stf', low(hidden), in_weight, precision=HIGHEST) + in_bias)
    act_low = low(jax.nn.gelu(pre_act, approximate=False))
    ffn_out = low_back(jnp.einsum('stf,fd->std', act_low, back_weight, precision=HIGHEST) + back_bias)
    return layer_norm(hidden + ffn_out, norm2_gain, norm2_bias)

def reference(inputs, doc_starts, qkv_weight, query_bias, value_bias, out_weight, out_bias, norm1_gain, norm1_bias, in_weight, in_bias, back_weight, back_bias, norm2_gain, norm2_bias, cotangent):
    length = inputs.shape[1]
    doc_ids = jax.vmap(lambda start_row: doc_index(start_row, length))(doc_starts)
    floats = tuple((array.astype(jnp.float32) for array in (inputs, qkv_weight, query_bias, value_bias, out_weight, out_bias, norm1_gain, norm1_bias, in_weight, in_bias, back_weight, back_bias, norm2_gain, norm2_bias)))
    result, backward = jax.vjp(lambda *params: forward(*params, doc_ids), *floats)
    grads = backward(cotangent.astype(jnp.float32))
    return (result.astype(jnp.bfloat16), grads[0], grads[1], grads[2], grads[3], grads[4], grads[5], grads[6], grads[7], grads[8], grads[9], grads[10], grads[11], grads[12], grads[13])
```

```python
from functools import partial
import math

import jax
import jax.numpy as jnp
from jax import lax
from jax.experimental import pallas as pl
from jax.experimental.pallas import tpu as pltpu
from jax.sharding import PartitionSpec as P

H = 12
HD = 64
EPSILON = 1e-05
BIG = 2.0**100
LOG2E = 1.4426950408889634
TQ = 256
TK = 256
PAD = 16


def layer_norm(resid, gain, shift):
    centre = jnp.mean(resid, axis=-1, keepdims=True)
    centred = resid - centre
    spread = jnp.mean(centred * centred, axis=-1, keepdims=True)
    return centred * lax.rsqrt(spread + EPSILON) * gain + shift


def ctx_shift(array, groups, parts, dg, ds):
    pairs = []
    for g in range(groups):
        for s in range(parts):
            pairs.append((g * parts + s, ((g + dg) % groups) * parts + (s + ds) % parts))
    return lax.ppermute(array, "ctx", pairs)


def swap(array, axis, bit):
    size = lax.axis_size(axis)
    return lax.ppermute(array, axis, [(i, i ^ (1 << bit)) for i in range(size)])


def gather_rows(shard, axis):
    size = lax.axis_size(axis)
    bits = size.bit_length() - 1
    index = lax.axis_index(axis)
    held = shard[None]
    for bit in reversed(range(bits)):
        other = swap(held, axis, bit)
        mine = (index >> bit) & 1
        pair = jnp.where(
            mine == 0, jnp.stack([held, other], axis=1), jnp.stack([other, held], axis=1)
        )
        held = pair.reshape((-1,) + shard.shape)
    return held.reshape((size * shard.shape[0],) + shard.shape[1:])


def pick(array, which, dim):
    return lax.dynamic_index_in_dim(array, which, dim, keepdims=False)


def scatter_sum(blocks, axis):
    size = lax.axis_size(axis)
    bits = size.bit_length() - 1
    index = lax.axis_index(axis)
    held = blocks
    for bit in range(bits):
        mine = (index >> bit) & 1
        pairs = held.reshape((held.shape[0] // 2, 2) + held.shape[1:])
        keep = pick(pairs, mine, 1)
        send = pick(pairs, 1 - mine, 1)
        got = swap(send.astype(jnp.bfloat16), axis, bit)
        held = keep.astype(jnp.float32) + got.astype(jnp.float32)
    return held[0]


def total_sum(array, axis, dim):
    size = lax.axis_size(axis)
    bits = size.bit_length() - 1
    index = lax.axis_index(axis)
    held = array
    for bit in range(bits):
        mine = (index >> bit) & 1
        half = held.shape[dim] // 2
        keep = lax.dynamic_slice_in_dim(held, mine * half, half, dim)
        send = lax.dynamic_slice_in_dim(held, (1 - mine) * half, half, dim)
        got = swap(send.astype(jnp.bfloat16), axis, bit)
        held = keep.astype(jnp.float32) + got.astype(jnp.float32)
    held = held.astype(jnp.bfloat16)
    for bit in reversed(range(bits)):
        mine = (index >> bit) & 1
        other = swap(held, axis, bit)
        held = jnp.where(
            mine == 0,
            jnp.concatenate([held, other], axis=dim),
            jnp.concatenate([other, held], axis=dim),
        )
    return held


def doc_row(meta, base, length, docs):
    pos = base + lax.broadcasted_iota(jnp.int32, (1, length), 1)
    doc = jnp.full((1, length), -1, jnp.int32)
    for j in range(docs):
        doc = doc + (pos >= meta[2 + j]).astype(jnp.int32)
    return doc


def dot(a, b):
    return jnp.dot(a, b, preferred_element_type=jnp.float32)


def dot_t(a, b):
    return lax.dot_general(a, b, (((1,), (1,)), ((), ())), preferred_element_type=jnp.float32)


def fill_keys(meta, own, others, groups, parts, docs, rows, store):
    g, s = meta[0], meta[1]
    for j in range(groups):
        for e in range(parts):
            block = lax.rem(g - j + groups, groups) * parts + lax.rem(s - e + parts, parts)
            if e == 0:
                key_t, value_t = own[j][1, 0], own[j][2, 0]
            else:
                ref = others[(e - 1) * groups + j]
                key_t, value_t = ref[0, 0], ref[1, 0]
            doc = doc_row(meta, block * rows, rows, docs)
            hot = (lax.broadcasted_iota(jnp.int32, (HD, rows), 0) == doc).astype(jnp.float32)
            keys = jnp.concatenate([key_t, hot.astype(jnp.bfloat16)], axis=0)
            store(block * (rows // TK), keys, key_t, value_t)


def query_tile(meta, own, groups, parts, docs, rows, j, part):
    g, s = meta[0], meta[1]
    block = lax.rem(g - j + groups, groups) * parts + s
    query_t = own[j][0, 0, :, part * TQ : (part + 1) * TQ]
    doc = doc_row(meta, block * rows + part * TQ, TQ, docs)
    shut = jnp.where(lax.broadcasted_iota(jnp.int32, (HD, TQ), 0) == doc, 0.0, -BIG)
    slot = 2 + docs + 2 * (j * (rows // TQ) + part)
    full = jnp.concatenate([query_t, shut.astype(jnp.bfloat16)], axis=0)
    return query_t, full, meta[slot], meta[slot + 1]


def attend_kernel(groups, parts, docs, rows, meta, *refs):
    own = refs[:groups]
    others = refs[groups : groups * parts]
    low_ref, wide_ref, log_ref, keys_ref, values_ref = refs[groups * parts :]
    coeff = LOG2E * HD**-0.5

    def store(first, keys, key_t, value_t):
        flat = keys.T
        for part in range(rows // TK):
            keys_ref[first + part] = flat[part * TK : (part + 1) * TK]
            values_ref[first + part] = value_t[:, part * TK : (part + 1) * TK]

    fill_keys(meta, own, others, groups, parts, docs, rows, store)
    for j in range(groups):
        for part in range(rows // TQ):
            unused, full, lo, hi = query_tile(meta, own, groups, parts, docs, rows, j, part)

            def step(t, state):
                best, total, accum = state
                scores = dot(keys_ref[t], full)
                new_best = jnp.maximum(best, jnp.max(scores, axis=0, keepdims=True))
                weights = jnp.exp2((scores - new_best) * coeff)
                shrink = jnp.exp2((best - new_best) * coeff)
                total = total * shrink + jnp.sum(weights, axis=0, keepdims=True)
                accum = accum * shrink + dot(values_ref[t], weights.astype(jnp.bfloat16))
                return new_best, total, accum

            best, total, accum = lax.fori_loop(
                lo,
                hi,
                step,
                (
                    jnp.full((1, TQ), -BIG, jnp.float32),
                    jnp.zeros((1, TQ), jnp.float32),
                    jnp.zeros((HD, TQ), jnp.float32),
                ),
            )
            attended = accum / total
            at = slice(j * rows + part * TQ, j * rows + (part + 1) * TQ)
            wide_ref[0, :, at] = attended
            low_ref[0, :, at] = attended.astype(jnp.bfloat16)
            log_ref[0, :, at] = best * coeff + jnp.log2(total)


def attend_back_kernel(groups, parts, docs, rows, meta, *refs):
    own = refs[:groups]
    others = refs[groups : groups * parts]
    grads = refs[groups * parts : groups * parts + groups]
    rest = refs[groups * parts + groups :]
    wide_ref, log_ref = rest[:2]
    dq_ref, mine_ref = rest[2:4]
    theirs = rest[4] if parts > 1 else None
    keys_ref, keys_t_ref, values_ref, accum_ref = rest[-4:]
    coeff = LOG2E * HD**-0.5
    per = rows // TK

    def store(first, keys, key_t, value_t):
        flat = keys.T
        flat_values = value_t.T
        for part in range(per):
            keys_ref[first + part] = flat[part * TK : (part + 1) * TK]
            keys_t_ref[first + part] = key_t[:, part * TK : (part + 1) * TK]
            values_ref[first + part] = flat_values[part * TK : (part + 1) * TK]

    fill_keys(meta, own, others, groups, parts, docs, rows, store)
    accum_ref[...] = jnp.zeros_like(accum_ref)
    for j in range(groups):
        for part in range(rows // TQ):
            query_t, full, lo, hi = query_tile(meta, own, groups, parts, docs, rows, j, part)
            at = slice(j * rows + part * TQ, j * rows + (part + 1) * TQ)
            grad_t = grads[j][0, :, part * TQ : (part + 1) * TQ]
            delta = jnp.sum(grad_t.astype(jnp.float32) * wide_ref[0, :, at], axis=0, keepdims=True)
            log_total = log_ref[0, :, at]
            blank = jnp.zeros((HD, TQ), jnp.bfloat16)
            both = jnp.concatenate(
                [
                    jnp.concatenate([query_t, blank], axis=1),
                    jnp.concatenate([blank, grad_t], axis=1),
                ],
                axis=0,
            )

            def step(t, grad_query):
                scores = dot(keys_ref[t], full)
                probs = jnp.exp2(scores * coeff - log_total)
                d_probs = dot(values_ref[t], grad_t)
                d_scores = (probs * (d_probs - delta)).astype(jnp.bfloat16)
                joined = jnp.concatenate([d_scores, probs.astype(jnp.bfloat16)], axis=1)
                accum_ref[t] += dot_t(joined, both)
                return grad_query + dot(keys_t_ref[t], d_scores)

            grad_query = lax.fori_loop(lo, hi, step, jnp.zeros((HD, TQ), jnp.float32))
            dq_ref[0, :, at] = (grad_query * HD**-0.5).astype(jnp.bfloat16)
    g, s = meta[0], meta[1]
    for j in range(groups):
        for e in range(parts):
            block = lax.rem(g - j + groups, groups) * parts + lax.rem(s - e + parts, parts)
            for part in range(per):
                terms = accum_ref[block * per + part].T
                at = slice(j * rows + part * TK, j * rows + (part + 1) * TK)
                d_key = terms[:HD] * HD**-0.5
                d_value = terms[HD:]
                if e == 0:
                    mine_ref[0, 0, :, at] = d_key
                    mine_ref[1, 0, :, at] = d_value
                else:
                    theirs[e - 1, 0, 0, :, at] = d_key.astype(jnp.bfloat16)
                    theirs[e - 1, 1, 0, :, at] = d_value.astype(jnp.bfloat16)


def whole_block(*shape):
    dims = tuple(1 if n is None else n for n in shape)
    where = shape.index(None)
    return pl.BlockSpec(dims, lambda h, meta: tuple(h if i == where else 0 for i in range(len(dims))))


def attend(meta, own, others, groups, parts, docs, rows, heads):
    tiles = groups * parts * rows // TK
    tokens = groups * rows
    grid_spec = pltpu.PrefetchScalarGridSpec(
        num_scalar_prefetch=1,
        grid=(heads,),
        in_specs=[whole_block(3, None, HD, rows)] * groups
        + [whole_block(2, None, HD, rows)] * (groups * (parts - 1)),
        out_specs=[
            whole_block(None, HD, tokens),
            whole_block(None, HD, tokens),
            whole_block(None, 1, tokens),
        ],
        scratch_shapes=[
            pltpu.VMEM((tiles, TK, 2 * HD), jnp.bfloat16),
            pltpu.VMEM((tiles, HD, TK), jnp.bfloat16),
        ],
    )
    return pl.pallas_call(
        partial(attend_kernel, groups, parts, docs, rows),
        grid_spec=grid_spec,
        out_shape=[
            jax.ShapeDtypeStruct((heads, HD, tokens), jnp.bfloat16),
            jax.ShapeDtypeStruct((heads, HD, tokens), jnp.float32),
            jax.ShapeDtypeStruct((heads, 1, tokens), jnp.float32),
        ],
        name="attend",
    )(meta, *own, *others)


def attend_back(meta, own, others, grads, wide, log_total, groups, parts, docs, rows, heads):
    tiles = groups * parts * rows // TK
    tokens = groups * rows
    out_specs = [whole_block(None, HD, tokens), whole_block(2, None, HD, tokens)]
    out_shape = [
        jax.ShapeDtypeStruct((heads, HD, tokens), jnp.bfloat16),
        jax.ShapeDtypeStruct((2, heads, HD, tokens), jnp.float32),
    ]
    if parts > 1:
        out_specs.append(whole_block(parts - 1, 2, None, HD, tokens))
        out_shape.append(
            jax.ShapeDtypeStruct((parts - 1, 2, heads, HD, tokens), jnp.bfloat16)
        )
    grid_spec = pltpu.PrefetchScalarGridSpec(
        num_scalar_prefetch=1,
        grid=(heads,),
        in_specs=[whole_block(3, None, HD, rows)] * groups
        + [whole_block(2, None, HD, rows)] * (groups * (parts - 1))
        + [whole_block(None, HD, rows)] * groups
        + [whole_block(None, HD, tokens), whole_block(None, 1, tokens)],
        out_specs=out_specs,
        scratch_shapes=[
            pltpu.VMEM((tiles, TK, 2 * HD), jnp.bfloat16),
            pltpu.VMEM((tiles, HD, TK), jnp.bfloat16),
            pltpu.VMEM((tiles, TK, HD), jnp.bfloat16),
            pltpu.VMEM((tiles, TK, 2 * HD), jnp.float32),
        ],
    )
    return pl.pallas_call(
        partial(attend_back_kernel, groups, parts, docs, rows),
        grid_spec=grid_spec,
        out_shape=out_shape,
        name="attend_back",
    )(meta, *own, *others, *grads, wide, log_total)


def body(
    inputs,
    doc_starts,
    qkv_weight,
    query_bias,
    value_bias,
    out_weight,
    out_bias,
    norm1_gain,
    norm1_bias,
    in_weight,
    in_bias,
    back_weight,
    back_bias,
    norm2_gain,
    norm2_bias,
    cotangent,
):
    bf16, f32 = jnp.bfloat16, jnp.float32
    tokens = inputs[0]
    rows, model = tokens.shape
    starts = doc_starts[0]
    docs = starts.shape[0]
    ctx = lax.axis_size("ctx")
    fsdp = lax.axis_size("fsdp")
    groups = math.gcd(H, ctx)
    parts = ctx // groups
    heads = H // groups
    span = heads * HD
    width = 3 * span
    index = lax.axis_index("ctx")
    g, s = index // parts, index % parts
    f = lax.axis_index("fsdp")
    shard = model // fsdp

    slots = [tokens] + [ctx_shift(tokens, groups, parts, d, 0) for d in range(1, groups)]

    local = qkv_weight.reshape(shard, 3, groups, span)
    own_cols = pick(local, g, 2).reshape(shard, width)
    small = jnp.concatenate(
        [
            query_bias, value_bias, out_bias, norm1_gain, norm1_bias,
            back_bias, norm2_gain, norm2_bias, in_bias,
        ]
    )
    count = small.shape[0]
    small_rows = -(-count // width)
    extra = -(-small_rows // PAD) * PAD
    small_block = jnp.pad(small, (0, extra * width - count)).reshape(extra, width)
    first = gather_rows(jnp.concatenate([own_cols, small_block], axis=0), "fsdp")
    first = first.reshape(fsdp, shard + extra, width)
    own_weight = first[:, :shard].reshape(model, width)
    flat = first[:, shard:].reshape(fsdp, extra * width)[:, :count].astype(f32)
    vector = lambda i: flat[:, i * shard : (i + 1) * shard].reshape(model)
    query_shift, value_shift, out_shift, gain_one, shift_one, back_shift, gain_two, shift_two = (
        vector(i) for i in range(8)
    )
    in_shift = flat[:, 8 * shard :].reshape(-1)
    out_full = gather_rows(out_weight, "fsdp")
    in_full = gather_rows(in_weight, "fsdp")
    back_full = gather_rows(back_weight, "fsdp")
    qkv_full = gather_rows(qkv_weight, "fsdp")

    zero = jnp.zeros((span,), f32)
    own_shift = jnp.concatenate(
        [
            lax.dynamic_slice(query_shift, (g * span,), (span,)),
            zero,
            lax.dynamic_slice(value_shift, (g * span,), (span,)),
        ]
    )
    own, others = [], []
    for slot in slots:
        projected = lax.dot_general(
            own_weight, slot, (((0,), (1,)), ((), ())), preferred_element_type=f32
        )
        low = (projected + own_shift[:, None]).astype(bf16).reshape(3, heads, HD, rows)
        own.append(low)
    for e in range(1, parts):
        for low in own:
            others.append(ctx_shift(low[1:], groups, parts, 0, e))

    bounds = jnp.concatenate([starts, jnp.full((1,), ctx * rows, jnp.int32)])
    base = ((g - jnp.arange(groups, dtype=jnp.int32) + groups) % groups) * parts + s
    heads_at = (base[:, None] * rows + TQ * jnp.arange(rows // TQ, dtype=jnp.int32)).reshape(-1)
    tails_at = heads_at + TQ - 1
    low_edge = jnp.max(jnp.where(starts[None] <= heads_at[:, None], starts[None], 0), axis=1)
    high_edge = jnp.min(
        jnp.where(bounds[None] > tails_at[:, None], bounds[None], ctx * rows), axis=1
    )
    ranges = jnp.stack([low_edge // TK, (high_edge + TK - 1) // TK], axis=1).reshape(-1)
    meta = jnp.concatenate([jnp.stack([g, s]).astype(jnp.int32), starts, ranges.astype(jnp.int32)])

    low, wide, log_total = attend(meta, own, others, groups, parts, docs, rows, heads)
    pieces = [low[:, :, :rows]] + [
        ctx_shift(low[:, :, j * rows : (j + 1) * rows], groups, parts, -j, 0)
        for j in range(1, groups)
    ]
    turned = jnp.stack(pieces + pieces[:-1]).reshape((2 * groups - 1) * span, rows)
    attended_t = lax.dynamic_slice(
        turned, (((groups - g) % groups) * span, 0), (groups * span, rows)
    )

    branch = (
        lax.dot_general(attended_t, out_full, (((0,), (0,)), ((), ())), preferred_element_type=f32)
        + out_shift
    )
    hidden, norm1_back = jax.vjp(layer_norm, tokens.astype(f32) + branch, gain_one, shift_one)
    hidden_low = hidden.astype(bf16)
    pre_act = jnp.dot(hidden_low, in_full, preferred_element_type=f32) + in_shift
    activated, gelu_back = jax.vjp(partial(jax.nn.gelu, approximate=False), pre_act)
    act_low = activated.astype(bf16)
    ffn_out = jnp.dot(act_low, back_full, preferred_element_type=f32) + back_shift
    result, norm2_back = jax.vjp(layer_norm, hidden + ffn_out, gain_two, shift_two)
    d_resid2, grad_gain_two, grad_shift_two = norm2_back(cotangent[0].astype(f32))
    d_ffn_low = d_resid2.astype(bf16)
    d_act = jnp.einsum("td,fd->tf", d_ffn_low, back_full, preferred_element_type=f32)
    d_pre_low = gelu_back(d_act)[0].astype(bf16)
    d_hidden = d_resid2 + jnp.einsum("tf,df->td", d_pre_low, in_full, preferred_element_type=f32)
    d_resid1, grad_gain_one, grad_shift_one = norm1_back(d_hidden)
    d_branch_low = d_resid1.astype(bf16)
    d_attended_t = lax.dot_general(
        out_full, d_branch_low, (((1,), (1,)), ((), ())), preferred_element_type=f32
    ).astype(bf16)
    grads = []
    for j in range(groups):
        part = lax.dynamic_slice(d_attended_t, (((g + j) % groups) * span, 0), (span, rows))
        part = part.reshape(heads, HD, rows)
        grads.append(ctx_shift(part, groups, parts, j, 0) if j else part)

    grad_back = jnp.einsum("tf,td->fd", act_low, d_ffn_low, preferred_element_type=f32)
    grad_in = jnp.einsum("td,tf->df", hidden_low, d_pre_low, preferred_element_type=f32)
    grad_out = jnp.dot(attended_t, d_branch_low, preferred_element_type=f32)
    grad_back_shift = jnp.sum(d_ffn_low, axis=0, dtype=f32)
    grad_in_shift = jnp.sum(d_pre_low, axis=0, dtype=f32)
    grad_out_shift = jnp.sum(d_branch_low, axis=0, dtype=f32)
    vectors = [
        grad_out_shift, grad_gain_one, grad_shift_one, grad_back_shift, grad_gain_two, grad_shift_two,
    ]
    line = jnp.concatenate(
        [v.reshape(fsdp, -1) for v in vectors] + [grad_in_shift.reshape(fsdp, -1)], axis=1
    )
    inner = grad_in.shape[1]
    line = jnp.pad(line, ((0, 0), (0, inner - line.shape[1])))
    line = jnp.pad(line[:, None], ((0, 0), (0, PAD - 1), (0, 0)))
    in_block = jnp.concatenate([grad_in.reshape(fsdp, shard, inner), line], axis=1).astype(bf16)
    back_sum = scatter_sum(grad_back.astype(bf16).reshape(fsdp, -1, model), "fsdp")
    in_sum = scatter_sum(in_block, "fsdp")
    out_sum = scatter_sum(grad_out.astype(bf16).reshape(fsdp, shard, model), "fsdp")
    back_rows = back_sum.shape[0]
    lower = total_sum(jnp.concatenate([back_sum, out_sum], axis=0), "ctx", 0).astype(f32)
    upper = total_sum(in_sum, "ctx", 1).astype(f32)

    back = attend_back(
        meta, own, others, grads, wide, log_total, groups, parts, docs, rows, heads
    )
    dq, dkv = back[0], back[1]
    for e in range(1, parts):
        dkv = dkv + ctx_shift(back[2][e - 1], groups, parts, 0, -e).astype(f32)
    d_qkv_t = jnp.concatenate([dq[None], dkv.astype(bf16)], axis=0).reshape(width, groups * rows)
    gathered = jnp.concatenate(slots, axis=0)
    grad_qkv = lax.dot_general(
        gathered, d_qkv_t, (((0,), (1,)), ((), ())), preferred_element_type=f32
    )
    sums = jnp.sum(d_qkv_t, axis=1, dtype=f32)
    sums = jnp.pad(jnp.broadcast_to(sums, (fsdp, 1, width)), ((0, 0), (0, PAD - 1), (0, 0)))
    qkv_block = jnp.concatenate([grad_qkv.reshape(fsdp, shard, width), sums], axis=1).astype(bf16)
    qkv_sum = scatter_sum(qkv_block, "fsdp")
    qkv_low = qkv_sum.astype(bf16)
    for e in range(1, parts):
        qkv_sum = qkv_sum + ctx_shift(qkv_low, groups, parts, 0, e).astype(f32)
    qkv_low = qkv_sum.astype(bf16)
    turns = [qkv_low] + [ctx_shift(qkv_low, groups, parts, -j, 0) for j in range(1, groups)]
    turned = jnp.stack(turns + turns[:-1])
    by_group = lax.dynamic_slice(
        turned, ((groups - g) % groups, 0, 0), (groups,) + qkv_low.shape
    ).astype(f32)
    natural = by_group.reshape(groups, shard + PAD, 3, span).transpose(1, 2, 0, 3)
    natural = natural.reshape(shard + PAD, 3 * model)
    grad_qkv_shard = natural[:shard]
    bias_line = natural[shard]
    grad_query_shift = lax.dynamic_slice(bias_line, (f * shard,), (shard,))
    grad_value_shift = lax.dynamic_slice(bias_line, (2 * model + f * shard,), (shard,))

    qkv_cols = qkv_full.reshape(model, 3, groups, span)
    input_grad = d_resid1
    for j in range(groups):
        part = d_qkv_t[:, j * rows : (j + 1) * rows]
        if j:
            part = ctx_shift(part, groups, parts, -j, 0)
        cols = pick(qkv_cols, (g + j) % groups, 2).reshape(model, width)
        input_grad = input_grad + lax.dot_general(
            part, cols, (((0,), (1,)), ((), ())), preferred_element_type=f32
        )

    line = upper[shard]
    offsets = lambda i: line[i * shard : (i + 1) * shard]
    inner_shard = in_bias.shape[0]
    return (
        result.astype(bf16)[None],
        input_grad[None],
        grad_qkv_shard,
        grad_query_shift,
        grad_value_shift,
        lower[back_rows:],
        offsets(0),
        offsets(1),
        offsets(2),
        upper[:shard],
        line[6 * shard : 6 * shard + inner_shard],
        lower[:back_rows],
        offsets(3),
        offsets(4),
        offsets(5),
    )


def solution(mesh):
    rows, one = P("fsdp", None), P("fsdp")
    whole = P("fsdp", "ctx", None)
    return jax.shard_map(
        body,
        mesh=mesh,
        in_specs=(
            whole, rows, rows, one, one, rows, one, one, one, rows, one, rows, one, one, one, whole,
        ),
        out_specs=(
            whole, whole, rows, one, one, rows, one, one, one, rows, one, rows, one, one, one,
        ),
        check_vma=False,
    )
```

```python
from functools import partial
import math

import jax
import jax.numpy as jnp
from jax import lax
from jax.experimental import pallas as pl
from jax.experimental.pallas import tpu as pltpu
from jax.sharding import PartitionSpec as P

H = 12
HD = 64
EPSILON = 1e-05
BIG = 2.0**100
LOG2E = 1.4426950408889634
PAD = 16
KERNEL_FLOPS = 3_000_000_000
KERNEL_BYTES = 20_000_000


def layer_norm(resid, gain, shift):
    centre = jnp.mean(resid, axis=-1, keepdims=True)
    centred = resid - centre
    spread = jnp.mean(centred * centred, axis=-1, keepdims=True)
    return centred * lax.rsqrt(spread + EPSILON) * gain + shift


def ctx_shift(array, groups, parts, dg, ds):
    pairs = []
    for g in range(groups):
        for s in range(parts):
            pairs.append((g * parts + s, ((g + dg) % groups) * parts + (s + ds) % parts))
    return lax.ppermute(array, "ctx", pairs)


def swap(array, axis, bit):
    size = lax.axis_size(axis)
    return lax.ppermute(array, axis, [(i, i ^ (1 << bit)) for i in range(size)])


def bits_of(axis):
    return lax.axis_size(axis).bit_length() - 1


def bit_at(axis, bit):
    return (lax.axis_index(axis) >> bit) & 1


def pick(array, which, dim):
    return lax.dynamic_index_in_dim(array, which, dim, keepdims=False)


def together(*values):
    return lax.optimization_barrier(values)


def join(mine, own, other, dim):
    return jnp.where(
        mine == 0,
        jnp.concatenate([own, other], axis=dim),
        jnp.concatenate([other, own], axis=dim),
    )


def gather_top(shard):
    return swap(shard, "fsdp", bits_of("fsdp") - 1)


def gather_rest(shard, other):
    top = bits_of("fsdp") - 1
    held = join(bit_at("fsdp", top), shard[None], other[None], 0)
    for bit in reversed(range(top)):
        got = swap(held, "fsdp", bit)
        pair = join(bit_at("fsdp", bit), held[:, None], got[:, None], 1)
        held = pair.reshape((-1,) + shard.shape)
    return held


def halve(held, axis, bit, dim):
    mine = bit_at(axis, bit)
    if axis == "fsdp":
        pairs = held.reshape((held.shape[0] // 2, 2) + held.shape[1:])
        keep, send = pick(pairs, mine, 1), pick(pairs, 1 - mine, 1)
    else:
        half = held.shape[dim] // 2
        keep = lax.dynamic_slice_in_dim(held, mine * half, half, dim)
        send = lax.dynamic_slice_in_dim(held, (1 - mine) * half, half, dim)
    got = swap(send, axis, bit)
    return (keep.astype(jnp.float32) + got.astype(jnp.float32)).astype(jnp.bfloat16)


def double(held, axis, bit, dim):
    return join(bit_at(axis, bit), held, swap(held, axis, bit), dim)


def doc_row(meta, base, length, docs):
    pos = base + lax.broadcasted_iota(jnp.int32, (1, length), 1)
    doc = jnp.full((1, length), -1, jnp.int32)
    for j in range(docs):
        doc = doc + (pos >= meta[2 + j]).astype(jnp.int32)
    return doc


def dot(a, b):
    return jnp.dot(a, b, preferred_element_type=jnp.float32)


def dot_t(a, b):
    return lax.dot_general(a, b, (((1,), (1,)), ((), ())), preferred_element_type=jnp.float32)


def fill_keys(meta, own, others, groups, parts, docs, rows, store):
    g, s = meta[0], meta[1]
    for j in range(groups):
        for e in range(parts):
            block = lax.rem(g - j + groups, groups) * parts + lax.rem(s - e + parts, parts)
            if e == 0:
                key_t, value_t = own[j][1, 0], own[j][2, 0]
            else:
                ref = others[(e - 1) * groups + j]
                key_t, value_t = ref[0, 0], ref[1, 0]
            doc = doc_row(meta, block * rows, rows, docs)
            hot = (lax.broadcasted_iota(jnp.int32, (HD, rows), 0) == doc).astype(jnp.float32)
            keys = jnp.concatenate([key_t, hot.astype(jnp.bfloat16)], axis=0)
            store(block, keys, key_t, value_t)


def query_full(meta, query_t, j, groups, parts, docs, rows):
    g, s = meta[0], meta[1]
    block = lax.rem(g - j + groups, groups) * parts + s
    doc = doc_row(meta, block * rows, rows, docs)
    shut = jnp.where(lax.broadcasted_iota(jnp.int32, (HD, rows), 0) == doc, 0.0, -BIG)
    return jnp.concatenate([query_t, shut.astype(jnp.bfloat16)], axis=0)


def attend_kernel(groups, parts, docs, rows, meta, *refs):
    own = refs[:groups]
    others = refs[groups : groups * parts]
    low_ref, wide_ref, log_ref, queries_ref, keys_ref, values_ref = refs[groups * parts :]
    coeff = LOG2E * HD**-0.5

    def store(block, keys, key_t, value_t):
        keys_ref[block] = keys.T
        values_ref[block] = value_t

    fill_keys(meta, own, others, groups, parts, docs, rows, store)
    for j in range(groups):
        queries_ref[j] = query_full(meta, own[j][0, 0], j, groups, parts, docs, rows)

    def one_slot(j, carry):
        full = queries_ref[j]

        def step(t, state):
            best, total, accum = state
            scores = dot(keys_ref[t], full)
            new_best = jnp.maximum(best, jnp.max(scores, axis=0, keepdims=True))
            weights = jnp.exp2((scores - new_best) * coeff)
            shrink = jnp.exp2((best - new_best) * coeff)
            total = total * shrink + jnp.sum(weights, axis=0, keepdims=True)
            accum = accum * shrink + dot(values_ref[t], weights.astype(jnp.bfloat16))
            return new_best, total, accum

        best, total, accum = lax.fori_loop(
            meta[2 + docs + 2 * j],
            meta[3 + docs + 2 * j],
            step,
            (
                jnp.full((1, rows), -BIG, jnp.float32),
                jnp.zeros((1, rows), jnp.float32),
                jnp.zeros((HD, rows), jnp.float32),
            ),
        )
        attended = accum / total
        at = pl.ds(pl.multiple_of(j * rows, rows), rows)
        wide_ref[0, :, at] = attended
        low_ref[0, :, at] = attended.astype(jnp.bfloat16)
        log_ref[0, :, at] = best * coeff + jnp.log2(total)
        return carry

    lax.fori_loop(0, groups, one_slot, 0)


def attend_back_kernel(groups, parts, docs, rows, meta, *refs):
    own = refs[:groups]
    others = refs[groups : groups * parts]
    grads = refs[groups * parts : groups * parts + groups]
    rest = refs[groups * parts + groups :]
    wide_ref, log_ref = rest[:2]
    dq_ref, mine_ref = rest[2:4]
    theirs = rest[4] if parts > 1 else None
    queries_ref, grads_ref, keys_ref, keys_t_ref, values_ref, accum_ref = rest[-6:]
    coeff = LOG2E * HD**-0.5

    def store(block, keys, key_t, value_t):
        keys_ref[block] = keys.T
        keys_t_ref[block] = key_t
        values_ref[block] = value_t.T

    fill_keys(meta, own, others, groups, parts, docs, rows, store)
    accum_ref[...] = jnp.zeros_like(accum_ref)
    for j in range(groups):
        queries_ref[j] = query_full(meta, own[j][0, 0], j, groups, parts, docs, rows)
        grads_ref[j] = grads[j][0]

    def one_slot(j, carry):
        at = pl.ds(pl.multiple_of(j * rows, rows), rows)
        full = queries_ref[j]
        grad_t = grads_ref[j]
        delta = jnp.sum(grad_t.astype(jnp.float32) * wide_ref[0, :, at], axis=0, keepdims=True)
        log_total = log_ref[0, :, at]
        blank = jnp.zeros((HD, rows), jnp.bfloat16)
        both = jnp.concatenate(
            [
                jnp.concatenate([full[:HD], blank], axis=1),
                jnp.concatenate([blank, grad_t], axis=1),
            ],
            axis=0,
        )

        def step(t, grad_query):
            scores = dot(keys_ref[t], full)
            probs = jnp.exp2(scores * coeff - log_total)
            d_probs = dot(values_ref[t], grad_t)
            d_scores = (probs * (d_probs - delta)).astype(jnp.bfloat16)
            joined = jnp.concatenate([d_scores, probs.astype(jnp.bfloat16)], axis=1)
            accum_ref[t] += dot_t(joined, both)
            return grad_query + dot(keys_t_ref[t], d_scores)

        grad_query = lax.fori_loop(
            meta[2 + docs + 2 * j],
            meta[3 + docs + 2 * j],
            step,
            jnp.zeros((HD, rows), jnp.float32),
        )
        dq_ref[:, at] = (grad_query * HD**-0.5).astype(jnp.bfloat16)
        return carry

    lax.fori_loop(0, groups, one_slot, 0)
    g, s = meta[0], meta[1]
    for j in range(groups):
        for e in range(parts):
            block = lax.rem(g - j + groups, groups) * parts + lax.rem(s - e + parts, parts)
            terms = accum_ref[block].T
            at = slice(j * rows, (j + 1) * rows)
            d_key = terms[:HD] * HD**-0.5
            d_value = terms[HD:]
            if e == 0:
                mine_ref[0, :, at] = d_key
                mine_ref[1, :, at] = d_value
            else:
                theirs[e - 1, 0, :, at] = d_key.astype(jnp.bfloat16)
                theirs[e - 1, 1, :, at] = d_value.astype(jnp.bfloat16)


def head_block(head, *shape):
    dims = tuple(1 if n is None else n for n in shape)
    where = shape.index(None)

    def at(h, meta):
        chosen = h if head is None else head
        return tuple(chosen if i == where else 0 for i in range(len(dims)))

    return pl.BlockSpec(dims, at)


def attend(meta, own, others, groups, parts, docs, rows, heads):
    tiles = groups * parts
    tokens = groups * rows
    block = partial(head_block, None)
    grid_spec = pltpu.PrefetchScalarGridSpec(
        num_scalar_prefetch=1,
        grid=(heads,),
        in_specs=[block(3, None, HD, rows)] * groups
        + [block(2, None, HD, rows)] * (groups * (parts - 1)),
        out_specs=[block(None, HD, tokens), block(None, HD, tokens), block(None, 1, tokens)],
        scratch_shapes=[
            pltpu.VMEM((groups, 2 * HD, rows), jnp.bfloat16),
            pltpu.VMEM((tiles, rows, 2 * HD), jnp.bfloat16),
            pltpu.VMEM((tiles, HD, rows), jnp.bfloat16),
        ],
    )
    return pl.pallas_call(
        partial(attend_kernel, groups, parts, docs, rows),
        grid_spec=grid_spec,
        out_shape=[
            jax.ShapeDtypeStruct((heads, HD, tokens), jnp.bfloat16),
            jax.ShapeDtypeStruct((heads, HD, tokens), jnp.float32),
            jax.ShapeDtypeStruct((heads, 1, tokens), jnp.float32),
        ],
        cost_estimate=pl.CostEstimate(
            flops=KERNEL_FLOPS * 2 * heads,
            transcendentals=0,
            bytes_accessed=KERNEL_BYTES * heads,
        ),
        name="attend",
    )(meta, *own, *others)


def attend_back(head, meta, own, others, grads, wide, log_total, groups, parts, docs, rows):
    tiles = groups * parts
    tokens = groups * rows
    block = partial(head_block, head)
    plain = lambda *dims: pl.BlockSpec(dims, lambda h, meta: (0,) * len(dims))
    out_specs = [plain(HD, tokens), plain(2, HD, tokens)]
    out_shape = [
        jax.ShapeDtypeStruct((HD, tokens), jnp.bfloat16),
        jax.ShapeDtypeStruct((2, HD, tokens), jnp.float32),
    ]
    if parts > 1:
        out_specs.append(plain(parts - 1, 2, HD, tokens))
        out_shape.append(jax.ShapeDtypeStruct((parts - 1, 2, HD, tokens), jnp.bfloat16))
    grid_spec = pltpu.PrefetchScalarGridSpec(
        num_scalar_prefetch=1,
        grid=(1,),
        in_specs=[block(3, None, HD, rows)] * groups
        + [block(2, None, HD, rows)] * (groups * (parts - 1))
        + [block(None, HD, rows)] * groups
        + [block(None, HD, tokens), block(None, 1, tokens)],
        out_specs=out_specs,
        scratch_shapes=[
            pltpu.VMEM((groups, 2 * HD, rows), jnp.bfloat16),
            pltpu.VMEM((groups, HD, rows), jnp.bfloat16),
            pltpu.VMEM((tiles, rows, 2 * HD), jnp.bfloat16),
            pltpu.VMEM((tiles, HD, rows), jnp.bfloat16),
            pltpu.VMEM((tiles, rows, HD), jnp.bfloat16),
            pltpu.VMEM((tiles, rows, 2 * HD), jnp.float32),
        ],
    )
    return pl.pallas_call(
        partial(attend_back_kernel, groups, parts, docs, rows),
        grid_spec=grid_spec,
        out_shape=out_shape,
        cost_estimate=pl.CostEstimate(
            flops=KERNEL_FLOPS * 5, transcendentals=0, bytes_accessed=KERNEL_BYTES
        ),
        name="attend_back",
    )(meta, *own, *others, *grads, wide, log_total)


def body(
    inputs,
    doc_starts,
    qkv_weight,
    query_bias,
    value_bias,
    out_weight,
    out_bias,
    norm1_gain,
    norm1_bias,
    in_weight,
    in_bias,
    back_weight,
    back_bias,
    norm2_gain,
    norm2_bias,
    cotangent,
):
    bf16, f32 = jnp.bfloat16, jnp.float32
    tokens = inputs[0]
    rows, model = tokens.shape
    starts = doc_starts[0]
    docs = starts.shape[0]
    ctx = lax.axis_size("ctx")
    fsdp = lax.axis_size("fsdp")
    groups = math.gcd(H, ctx)
    parts = ctx // groups
    heads = H // groups
    span = heads * HD
    width = 3 * span
    index = lax.axis_index("ctx")
    g, s = index // parts, index % parts
    f = lax.axis_index("fsdp")
    shard = model // fsdp

    slots = [tokens] + [ctx_shift(tokens, groups, parts, d, 0) for d in range(1, groups)]

    local = qkv_weight.reshape(shard, 3, groups, span).transpose(2, 0, 1, 3)
    local = local.reshape(groups, shard, width)
    small = jnp.concatenate(
        [
            query_bias, value_bias, out_bias, norm1_gain, norm1_bias,
            back_bias, norm2_gain, norm2_bias, in_bias,
        ]
    )
    count = small.shape[0]
    extra = -(-count // (width * PAD)) * PAD
    small_block = jnp.pad(small, (0, extra * width - count)).reshape(extra, width)
    first = jnp.concatenate([pick(local, g, 0), small_block], axis=0)
    first_top = gather_top(first)
    first_top, out_held, in_held, back_held = together(
        first_top, out_weight, in_weight, back_weight
    )
    out_top, in_top, back_top = gather_top(out_held), gather_top(in_held), gather_top(back_held)
    first = gather_rest(first, first_top)
    own_weight = first[:, :shard].reshape(model, width)
    flat = first[:, shard:].reshape(fsdp, extra * width)[:, :count].astype(f32)
    vector = lambda i: flat[:, i * shard : (i + 1) * shard].reshape(model)
    query_shift, value_shift, out_shift, gain_one, shift_one, back_shift, gain_two, shift_two = (
        vector(i) for i in range(8)
    )
    in_shift = flat[:, 8 * shard :].reshape(-1)

    zero = jnp.zeros((span,), f32)
    own_shift = jnp.concatenate(
        [
            lax.dynamic_slice(query_shift, (g * span,), (span,)),
            zero,
            lax.dynamic_slice(value_shift, (g * span,), (span,)),
        ]
    )
    own, others = [], []
    for slot in slots:
        projected = lax.dot_general(
            own_weight, slot, (((0,), (1,)), ((), ())), preferred_element_type=f32
        )
        low = (projected + own_shift[:, None]).astype(bf16).reshape(3, heads, HD, rows)
        own.append(low)
    for e in range(1, parts):
        for low in own:
            others.append(ctx_shift(low[1:], groups, parts, 0, e))

    bounds = jnp.concatenate([starts, jnp.full((1,), ctx * rows, jnp.int32)])
    base = ((g - jnp.arange(groups, dtype=jnp.int32) + groups) % groups) * parts + s
    heads_at = base * rows
    tails_at = heads_at + rows - 1
    low_edge = jnp.max(jnp.where(starts[None] <= heads_at[:, None], starts[None], 0), axis=1)
    high_edge = jnp.min(
        jnp.where(bounds[None] > tails_at[:, None], bounds[None], ctx * rows), axis=1
    )
    ranges = jnp.stack([low_edge // rows, (high_edge + rows - 1) // rows], axis=1).reshape(-1)
    meta = jnp.concatenate([jnp.stack([g, s]).astype(jnp.int32), starts, ranges.astype(jnp.int32)])

    out_full = gather_rest(out_weight, out_top).reshape(model, model)
    in_full = gather_rest(in_weight, in_top).reshape(model, -1)
    meta, out_full, in_full = together(meta, out_full, in_full)
    low, wide, log_total = attend(meta, own, others, groups, parts, docs, rows, heads)
    low, qkv_held = together(low, local)
    attended_t = jnp.zeros((groups * span, rows), bf16)
    turned = []
    for j in range(groups):
        piece = low[:, :, j * rows : (j + 1) * rows]
        turned.append(ctx_shift(piece, groups, parts, -j, 0) if j else piece)
    for j, piece in enumerate(together(*turned)):
        attended_t = lax.dynamic_update_slice(
            attended_t, piece.reshape(span, rows), (((g + j) % groups) * span, 0)
        )
    back_full = gather_rest(back_weight, back_top).reshape(-1, model)

    branch = (
        lax.dot_general(attended_t, out_full, (((0,), (0,)), ((), ())), preferred_element_type=f32)
        + out_shift
    )
    hidden, norm1_back = jax.vjp(layer_norm, tokens.astype(f32) + branch, gain_one, shift_one)
    hidden_low = hidden.astype(bf16)
    pre_act = jnp.dot(hidden_low, in_full, preferred_element_type=f32) + in_shift
    activated, gelu_back = jax.vjp(partial(jax.nn.gelu, approximate=False), pre_act)
    act_low = activated.astype(bf16)
    ffn_out = jnp.dot(act_low, back_full, preferred_element_type=f32) + back_shift
    result, norm2_back = jax.vjp(layer_norm, hidden + ffn_out, gain_two, shift_two)
    d_resid2, grad_gain_two, grad_shift_two = norm2_back(cotangent[0].astype(f32))
    d_ffn_low = d_resid2.astype(bf16)
    d_act = jnp.einsum("td,fd->tf", d_ffn_low, back_full, preferred_element_type=f32)
    d_pre_low = gelu_back(d_act)[0].astype(bf16)
    d_hidden = d_resid2 + jnp.einsum("tf,df->td", d_pre_low, in_full, preferred_element_type=f32)
    d_resid1, grad_gain_one, grad_shift_one = norm1_back(d_hidden)
    d_branch_low = d_resid1.astype(bf16)
    d_attended_t = lax.dot_general(
        out_full, d_branch_low, (((1,), (1,)), ((), ())), preferred_element_type=f32
    ).astype(bf16)
    grads = []
    for j in range(groups):
        part = lax.dynamic_slice(d_attended_t, (((g + j) % groups) * span, 0), (span, rows))
        part = part.reshape(heads, HD, rows)
        grads.append(ctx_shift(part, groups, parts, j, 0) if j else part)

    grad_back = jnp.einsum("tf,td->fd", act_low, d_ffn_low, preferred_element_type=f32)
    grad_in = jnp.einsum("td,tf->df", hidden_low, d_pre_low, preferred_element_type=f32)
    grad_out = jnp.dot(attended_t, d_branch_low, preferred_element_type=f32)
    grad_back_shift = jnp.sum(d_ffn_low, axis=0, dtype=f32)
    grad_in_shift = jnp.sum(d_pre_low, axis=0, dtype=f32)
    grad_out_shift = jnp.sum(d_branch_low, axis=0, dtype=f32)
    vectors = [
        grad_out_shift, grad_gain_one, grad_shift_one, grad_back_shift, grad_gain_two, grad_shift_two,
    ]
    line = jnp.concatenate(
        [v.reshape(fsdp, -1) for v in vectors] + [grad_in_shift.reshape(fsdp, -1)], axis=1
    )
    inner = grad_in.shape[1]
    line = jnp.pad(line, ((0, 0), (0, inner - line.shape[1])))
    line = jnp.pad(line[:, None], ((0, 0), (0, PAD - 1), (0, 0))).astype(bf16)
    upper = jnp.concatenate([grad_in.astype(bf16).reshape(fsdp, shard, inner), line], axis=1)
    lower = jnp.concatenate(
        [grad_back.astype(bf16).reshape(fsdp, -1, model), grad_out.astype(bf16).reshape(fsdp, shard, model)],
        axis=1,
    )
    back_rows = lower.shape[1] - shard
    fsdp_bits, ctx_bits = range(bits_of("fsdp")), range(bits_of("ctx"))
    lower_steps = [("fsdp", b) for b in fsdp_bits] + [("ctx", b) for b in ctx_bits]
    upper_steps = [("fsdp", 0), ("ctx", 0)]
    upper_steps += [("fsdp", b) for b in fsdp_bits[1:]] + [("ctx", b) for b in ctx_bits[1:]]

    pieces, received = [], [[] for unused in range(groups)]
    mine, theirs, step = None, None, 0

    def send(piece):
        pieces.append(piece)
        for j in range(groups):
            part = piece[:, :, j * rows : (j + 1) * rows]
            received[j].append(ctx_shift(part, groups, parts, -j, 0) if j else part)

    def settle(dq, dkv, theirs):
        for other in theirs:
            dkv = dkv + other.astype(f32)
        send(jnp.concatenate([dq[None], dkv.astype(bf16)], axis=0))

    for head in range(heads):
        lower = halve(lower, *lower_steps[step], 1)
        upper = halve(upper, *upper_steps[step], 2)
        step += 1
        meta, lower, upper = together(meta, lower, upper)
        dq, dkv, *rest = attend_back(
            head, meta, own, others, grads, wide, log_total, groups, parts, docs, rows
        )
        if head:
            dq, *theirs = together(dq, *theirs)
            settle(*mine, theirs)
        mine = (dq, dkv)
        theirs = [ctx_shift(rest[0][e - 1], groups, parts, 0, -e) for e in range(1, parts)]
    settle(*mine, theirs)
    qkv_top = gather_top(qkv_held)
    qkv_full = gather_rest(qkv_held, qkv_top)
    while step < len(lower_steps):
        lower = halve(lower, *lower_steps[step], 1)
        upper = halve(upper, *upper_steps[step], 2)
        step += 1
    lower, upper = lower[0], upper[0]
    for bit in reversed(ctx_bits):
        lower = double(lower, "ctx", bit, 0)
        upper = double(upper, "ctx", bit, 1)
    lower, upper = lower.astype(f32), upper.astype(f32)

    d_qkv_t = jnp.stack(pieces, axis=1).reshape(width, groups * rows)
    gathered = jnp.concatenate(slots, axis=0)
    grad_qkv = lax.dot_general(
        gathered, d_qkv_t, (((0,), (1,)), ((), ())), preferred_element_type=f32
    )
    sums = jnp.sum(d_qkv_t, axis=1, dtype=f32)
    sums = jnp.pad(jnp.broadcast_to(sums, (fsdp, 1, width)), ((0, 0), (0, PAD - 1), (0, 0)))
    qkv_sum = jnp.concatenate([grad_qkv.reshape(fsdp, shard, width), sums], axis=1).astype(bf16)
    for bit in fsdp_bits:
        qkv_sum = halve(qkv_sum, "fsdp", bit, 1)
    qkv_sum = qkv_sum[0]
    wide_sum = qkv_sum.astype(f32)
    for e in range(1, parts):
        wide_sum = wide_sum + ctx_shift(qkv_sum, groups, parts, 0, e).astype(f32)
    qkv_low = wide_sum.astype(bf16)
    by_group = jnp.zeros((groups,) + qkv_low.shape, bf16)
    for j in range(groups):
        piece = ctx_shift(qkv_low, groups, parts, -j, 0) if j else qkv_low
        by_group = lax.dynamic_update_slice(by_group, piece[None], ((g + j) % groups, 0, 0))
    natural = by_group.reshape(groups, shard + PAD, 3, span).transpose(1, 2, 0, 3)
    natural = natural.reshape(shard + PAD, 3 * model).astype(f32)
    grad_qkv_shard = natural[:shard]
    bias_line = natural[shard]
    grad_query_shift = lax.dynamic_slice(bias_line, (f * shard,), (shard,))
    grad_value_shift = lax.dynamic_slice(bias_line, (2 * model + f * shard,), (shard,))

    input_grad = d_resid1
    for j in range(groups):
        part = jnp.stack(received[j], axis=1).reshape(width, rows)
        cols = pick(qkv_full, (g + j) % groups, 1).reshape(model, width)
        input_grad = input_grad + lax.dot_general(
            part, cols, (((0,), (1,)), ((), ())), preferred_element_type=f32
        )

    line = upper[shard]
    offsets = lambda i: line[i * shard : (i + 1) * shard]
    inner_shard = in_bias.shape[0]
    return (
        result.astype(bf16)[None],
        input_grad[None],
        grad_qkv_shard,
        grad_query_shift,
        grad_value_shift,
        lower[back_rows:],
        offsets(0),
        offsets(1),
        offsets(2),
        upper[:shard],
        line[6 * shard : 6 * shard + inner_shard],
        lower[:back_rows],
        offsets(3),
        offsets(4),
        offsets(5),
    )


def solution(mesh):
    rows, one = P("fsdp", None), P("fsdp")
    whole = P("fsdp", "ctx", None)
    return jax.shard_map(
        body,
        mesh=mesh,
        in_specs=(
            whole, rows, rows, one, one, rows, one, one, one, rows, one, rows, one, one, one, whole,
        ),
        out_specs=(
            whole, whole, rows, one, one, rows, one, one, one, rows, one, rows, one, one, one,
        ),
        check_vma=False,
    )
```

```python
from functools import partial
import math

import jax
import jax.numpy as jnp
from jax import lax
from jax.experimental import pallas as pl
from jax.experimental.pallas import tpu as pltpu
from jax.sharding import PartitionSpec as P

H = 12
HD = 64
EPSILON = 1e-05
BIG = 2.0**100
LOG2E = 1.4426950408889634
PAD = 16
KERNEL_FLOPS = 3_000_000_000
KERNEL_BYTES = 20_000_000


def ctx_shift(array, groups, parts, dg, ds):
    pairs = []
    for g in range(groups):
        for s in range(parts):
            pairs.append((g * parts + s, ((g + dg) % groups) * parts + (s + ds) % parts))
    return lax.ppermute(array, "ctx", pairs)


def swap(array, axis, bit):
    size = lax.axis_size(axis)
    return lax.ppermute(array, axis, [(i, i ^ (1 << bit)) for i in range(size)])


def bits_of(axis):
    return lax.axis_size(axis).bit_length() - 1


def bit_at(axis, bit):
    return (lax.axis_index(axis) >> bit) & 1


def pick(array, which, dim):
    return lax.dynamic_index_in_dim(array, which, dim, keepdims=False)


def together(*values):
    return lax.optimization_barrier(values)


def join(mine, own, other, dim):
    return jnp.where(
        mine == 0,
        jnp.concatenate([own, other], axis=dim),
        jnp.concatenate([other, own], axis=dim),
    )


def gather_top(shard):
    return swap(shard, "fsdp", bits_of("fsdp") - 1)


def gather_rest(shard, other):
    top = bits_of("fsdp") - 1
    held = join(bit_at("fsdp", top), shard[None], other[None], 0)
    for bit in reversed(range(top)):
        got = swap(held, "fsdp", bit)
        pair = join(bit_at("fsdp", bit), held[:, None], got[:, None], 1)
        held = pair.reshape((-1,) + shard.shape)
    return held


def halve(held, axis, bit, dim):
    mine = bit_at(axis, bit)
    if axis == "fsdp":
        pairs = held.reshape((held.shape[0] // 2, 2) + held.shape[1:])
        keep, send = pick(pairs, mine, 1), pick(pairs, 1 - mine, 1)
    else:
        half = held.shape[dim] // 2
        keep = lax.dynamic_slice_in_dim(held, mine * half, half, dim)
        send = lax.dynamic_slice_in_dim(held, (1 - mine) * half, half, dim)
    got = swap(send, axis, bit)
    return (keep.astype(jnp.float32) + got.astype(jnp.float32)).astype(jnp.bfloat16)


def split_blocks(array, dim, size):
    mine = bit_at("fsdp", 0)
    count = lax.axis_size("fsdp")
    shape = array.shape
    pairs = array.reshape(shape[:dim] + (count // 2, 2, size) + shape[dim + 1 :])
    flat = shape[:dim] + (count // 2 * size,) + shape[dim + 1 :]
    return pick(pairs, mine, dim + 1).reshape(flat), pick(pairs, 1 - mine, dim + 1).reshape(flat)


def exchange(held, axis, bit):
    got = swap(held, axis, bit)
    return (held.astype(jnp.float32) + got.astype(jnp.float32)).astype(jnp.bfloat16)


def double(held, axis, bit, dim):
    return join(bit_at(axis, bit), held, swap(held, axis, bit), dim)


def doc_row(meta, base, length, docs):
    pos = base + lax.broadcasted_iota(jnp.int32, (1, length), 1)
    doc = jnp.full((1, length), -1, jnp.int32)
    for j in range(docs):
        doc = doc + (pos >= meta[2 + j]).astype(jnp.int32)
    return doc


def dot(a, b):
    return jnp.dot(a, b, preferred_element_type=jnp.float32)


def dot_t(a, b):
    return lax.dot_general(a, b, (((1,), (1,)), ((), ())), preferred_element_type=jnp.float32)


def fill_keys(meta, own, others, groups, parts, docs, rows, store):
    g, s = meta[0], meta[1]
    for j in range(groups):
        for e in range(parts):
            block = lax.rem(g - j + groups, groups) * parts + lax.rem(s - e + parts, parts)
            if e == 0:
                key_t, value_t = own[j][1, 0], own[j][2, 0]
            else:
                ref = others[(e - 1) * groups + j]
                key_t, value_t = ref[0, 0], ref[1, 0]
            doc = doc_row(meta, block * rows, rows, docs)
            hot = (lax.broadcasted_iota(jnp.int32, (HD, rows), 0) == doc).astype(jnp.float32)
            keys = jnp.concatenate([key_t, hot.astype(jnp.bfloat16)], axis=0)
            store(block, keys, key_t, value_t)


def query_full(meta, query_t, j, groups, parts, docs, rows):
    g, s = meta[0], meta[1]
    block = lax.rem(g - j + groups, groups) * parts + s
    doc = doc_row(meta, block * rows, rows, docs)
    shut = jnp.where(lax.broadcasted_iota(jnp.int32, (HD, rows), 0) == doc, 0.0, -BIG)
    return jnp.concatenate([query_t, shut.astype(jnp.bfloat16)], axis=0)


def attend_kernel(groups, parts, docs, rows, meta, *refs):
    own = refs[:groups]
    others = refs[groups : groups * parts]
    low_ref, wide_ref, log_ref, queries_ref, keys_ref, values_ref = refs[groups * parts :]
    coeff = LOG2E * HD**-0.5

    def store(block, keys, key_t, value_t):
        keys_ref[block] = keys.T
        values_ref[block] = value_t

    fill_keys(meta, own, others, groups, parts, docs, rows, store)
    for j in range(groups):
        queries_ref[j] = query_full(meta, own[j][0, 0], j, groups, parts, docs, rows)

    def one_slot(j, carry):
        full = queries_ref[j]

        def step(t, state):
            best, total, accum = state
            scores = dot(keys_ref[t], full)
            new_best = jnp.maximum(best, jnp.max(scores, axis=0, keepdims=True))
            weights = jnp.exp2((scores - new_best) * coeff)
            shrink = jnp.exp2((best - new_best) * coeff)
            total = total * shrink + jnp.sum(weights, axis=0, keepdims=True)
            accum = accum * shrink + dot(values_ref[t], weights.astype(jnp.bfloat16))
            return new_best, total, accum

        best, total, accum = lax.fori_loop(
            meta[2 + docs + 2 * j],
            meta[3 + docs + 2 * j],
            step,
            (
                jnp.full((1, rows), -BIG, jnp.float32),
                jnp.zeros((1, rows), jnp.float32),
                jnp.zeros((HD, rows), jnp.float32),
            ),
        )
        attended = accum / total
        at = pl.ds(pl.multiple_of(j * rows, rows), rows)
        wide_ref[0, :, at] = attended
        low_ref[0, :, at] = attended.astype(jnp.bfloat16)
        log_ref[0, :, at] = best * coeff + jnp.log2(total)
        return carry

    lax.fori_loop(0, groups, one_slot, 0)


def attend_back_kernel(groups, parts, docs, rows, meta, *refs):
    own = refs[:groups]
    others = refs[groups : groups * parts]
    grads = refs[groups * parts : groups * parts + groups]
    rest = refs[groups * parts + groups :]
    wide_ref, log_ref = rest[:2]
    dq_ref, mine_ref = rest[2:4]
    theirs = rest[4] if parts > 1 else None
    queries_ref, grads_ref, keys_ref, keys_t_ref, values_ref, accum_ref = rest[-6:]
    coeff = LOG2E * HD**-0.5

    def store(block, keys, key_t, value_t):
        keys_ref[block] = keys.T
        keys_t_ref[block] = key_t
        values_ref[block] = value_t.T

    fill_keys(meta, own, others, groups, parts, docs, rows, store)
    accum_ref[...] = jnp.zeros_like(accum_ref)
    for j in range(groups):
        queries_ref[j] = query_full(meta, own[j][0, 0], j, groups, parts, docs, rows)
        grads_ref[j] = grads[j][0]

    def one_slot(j, carry):
        at = pl.ds(pl.multiple_of(j * rows, rows), rows)
        full = queries_ref[j]
        grad_t = grads_ref[j]
        delta = jnp.sum(grad_t.astype(jnp.float32) * wide_ref[0, :, at], axis=0, keepdims=True)
        log_total = log_ref[0, :, at]
        blank = jnp.zeros((HD, rows), jnp.bfloat16)
        both = jnp.concatenate(
            [
                jnp.concatenate([full[:HD], blank], axis=1),
                jnp.concatenate([blank, grad_t], axis=1),
            ],
            axis=0,
        )

        def step(t, grad_query):
            scores = dot(keys_ref[t], full)
            probs = jnp.exp2(scores * coeff - log_total)
            d_probs = dot(values_ref[t], grad_t)
            d_scores = (probs * (d_probs - delta)).astype(jnp.bfloat16)
            joined = jnp.concatenate([d_scores, probs.astype(jnp.bfloat16)], axis=1)
            accum_ref[t] += dot_t(joined, both)
            return grad_query + dot(keys_t_ref[t], d_scores)

        grad_query = lax.fori_loop(
            meta[2 + docs + 2 * j],
            meta[3 + docs + 2 * j],
            step,
            jnp.zeros((HD, rows), jnp.float32),
        )
        dq_ref[:, at] = (grad_query * HD**-0.5).astype(jnp.bfloat16)
        return carry

    lax.fori_loop(0, groups, one_slot, 0)
    g, s = meta[0], meta[1]
    for j in range(groups):
        for e in range(parts):
            block = lax.rem(g - j + groups, groups) * parts + lax.rem(s - e + parts, parts)
            terms = accum_ref[block].T
            at = slice(j * rows, (j + 1) * rows)
            d_key = terms[:HD] * HD**-0.5
            d_value = terms[HD:]
            if e == 0:
                mine_ref[0, :, at] = d_key
                mine_ref[1, :, at] = d_value
            else:
                theirs[e - 1, 0, :, at] = d_key.astype(jnp.bfloat16)
                theirs[e - 1, 1, :, at] = d_value.astype(jnp.bfloat16)


def head_block(head, *shape):
    dims = tuple(1 if n is None else n for n in shape)
    where = shape.index(None)

    def at(h, meta):
        chosen = h if head is None else head
        return tuple(chosen if i == where else 0 for i in range(len(dims)))

    return pl.BlockSpec(dims, at)


def attend(meta, own, others, groups, parts, docs, rows, heads):
    tiles = groups * parts
    tokens = groups * rows
    block = partial(head_block, None)
    grid_spec = pltpu.PrefetchScalarGridSpec(
        num_scalar_prefetch=1,
        grid=(heads,),
        in_specs=[block(3, None, HD, rows)] * groups
        + [block(2, None, HD, rows)] * (groups * (parts - 1)),
        out_specs=[block(None, HD, tokens), block(None, HD, tokens), block(None, 1, tokens)],
        scratch_shapes=[
            pltpu.VMEM((groups, 2 * HD, rows), jnp.bfloat16),
            pltpu.VMEM((tiles, rows, 2 * HD), jnp.bfloat16),
            pltpu.VMEM((tiles, HD, rows), jnp.bfloat16),
        ],
    )
    return pl.pallas_call(
        partial(attend_kernel, groups, parts, docs, rows),
        grid_spec=grid_spec,
        out_shape=[
            jax.ShapeDtypeStruct((heads, HD, tokens), jnp.bfloat16),
            jax.ShapeDtypeStruct((heads, HD, tokens), jnp.float32),
            jax.ShapeDtypeStruct((heads, 1, tokens), jnp.float32),
        ],
        cost_estimate=pl.CostEstimate(
            flops=KERNEL_FLOPS * 2 * heads,
            transcendentals=0,
            bytes_accessed=KERNEL_BYTES * heads,
        ),
        name="attend",
    )(meta, *own, *others)


def attend_back(head, meta, own, others, grads, wide, log_total, groups, parts, docs, rows):
    tiles = groups * parts
    tokens = groups * rows
    block = partial(head_block, head)
    plain = lambda *dims: pl.BlockSpec(dims, lambda h, meta: (0,) * len(dims))
    out_specs = [plain(HD, tokens), plain(2, HD, tokens)]
    out_shape = [
        jax.ShapeDtypeStruct((HD, tokens), jnp.bfloat16),
        jax.ShapeDtypeStruct((2, HD, tokens), jnp.float32),
    ]
    if parts > 1:
        out_specs.append(plain(parts - 1, 2, HD, tokens))
        out_shape.append(jax.ShapeDtypeStruct((parts - 1, 2, HD, tokens), jnp.bfloat16))
    grid_spec = pltpu.PrefetchScalarGridSpec(
        num_scalar_prefetch=1,
        grid=(1,),
        in_specs=[block(3, None, HD, rows)] * groups
        + [block(2, None, HD, rows)] * (groups * (parts - 1))
        + [block(None, HD, rows)] * groups
        + [block(None, HD, tokens), block(None, 1, tokens)],
        out_specs=out_specs,
        scratch_shapes=[
            pltpu.VMEM((groups, 2 * HD, rows), jnp.bfloat16),
            pltpu.VMEM((groups, HD, rows), jnp.bfloat16),
            pltpu.VMEM((tiles, rows, 2 * HD), jnp.bfloat16),
            pltpu.VMEM((tiles, HD, rows), jnp.bfloat16),
            pltpu.VMEM((tiles, rows, HD), jnp.bfloat16),
            pltpu.VMEM((tiles, rows, 2 * HD), jnp.float32),
        ],
    )
    return pl.pallas_call(
        partial(attend_back_kernel, groups, parts, docs, rows),
        grid_spec=grid_spec,
        out_shape=out_shape,
        cost_estimate=pl.CostEstimate(
            flops=KERNEL_FLOPS * 5, transcendentals=0, bytes_accessed=KERNEL_BYTES
        ),
        name="attend_back",
    )(meta, *own, *others, *grads, wide, log_total)


ERFC = (
    -1.26551223, 1.00002368, 0.37409196, 0.09678418, -0.18628806,
    0.27886807, -1.13520398, 1.48851587, -0.82215223, 0.17087277,
)


def normal_terms(v):
    z = jnp.abs(v) * (0.5**0.5)
    t = 1.0 / (1.0 + 0.5 * z)
    poly = jnp.full_like(t, ERFC[-1])
    for term in reversed(ERFC[:-1]):
        poly = poly * t + term
    square = z * z
    tail = 0.5 * t * jnp.exp(poly - square)
    below = jnp.where(v < 0, tail, 1.0 - tail)
    return below, jnp.exp(-square) * (2.0 * math.pi) ** -0.5


def normed(resid):
    centred = resid - jnp.mean(resid, axis=-1, keepdims=True)
    spread = jnp.mean(centred * centred, axis=-1, keepdims=True)
    scale = lax.rsqrt(spread + EPSILON)
    return centred * scale, scale


def norm_back(grad, gain, unit, scale):
    e = grad * gain
    inner = jnp.mean(e * unit, axis=-1, keepdims=True)
    return (e - jnp.mean(e, axis=-1, keepdims=True) - unit * inner) * scale


def feed_kernel(
    chunk,
    tokens_ref,
    attended_ref,
    cot_ref,
    out_ref,
    in_ref,
    back_ref,
    vec_ref,
    in_bias_ref,
    result_ref,
    d_resid1_ref,
    d_attended_ref,
    hidden_ref,
    act_ref,
    d_ffn_ref,
    d_pre_ref,
    d_branch_ref,
    sums_ref,
    in_sums_ref,
    slope_ref,
):
    f32, bf16 = jnp.float32, jnp.bfloat16
    rows = tokens_ref.shape[0]
    inner = in_ref.shape[1]
    out_shift, gain_one, shift_one = vec_ref[0:1], vec_ref[1:2], vec_ref[2:3]
    back_shift, gain_two, shift_two = vec_ref[3:4], vec_ref[4:5], vec_ref[5:6]

    @pl.when(pl.program_id(0) == 0)
    def _():
        sums_ref[...] = jnp.zeros_like(sums_ref)
        in_sums_ref[...] = jnp.zeros_like(in_sums_ref)

    total = lambda a: jnp.sum(a, axis=0, keepdims=True)
    branch = dot(attended_ref[...].T, out_ref[...]) + out_shift
    unit1, scale1 = normed(tokens_ref[...].astype(f32) + branch)
    hidden = unit1 * gain_one + shift_one
    hidden_low = hidden.astype(bf16)
    hidden_ref[...] = hidden_low
    resid2 = hidden + back_shift
    for at in range(0, inner, chunk):
        cols = slice(at, at + chunk)
        pre = dot(hidden_low, in_ref[:, cols]) + in_bias_ref[:, cols]
        below, density = normal_terms(pre)
        act = (pre * below).astype(bf16)
        act_ref[:, cols] = act
        slope_ref[:, cols] = below + pre * density
        resid2 = resid2 + dot(act, back_ref[cols, :])
    unit2, scale2 = normed(resid2)
    result_ref[...] = (unit2 * gain_two + shift_two).astype(bf16)
    cot = cot_ref[...].astype(f32)
    d_resid2 = norm_back(cot, gain_two, unit2, scale2)
    d_ffn = d_resid2.astype(bf16)
    d_ffn_ref[...] = d_ffn
    d_hidden = d_resid2
    for at in range(0, inner, chunk):
        cols = slice(at, at + chunk)
        d_act = dot_t(d_ffn, back_ref[cols, :])
        d_pre = (d_act * slope_ref[:, cols]).astype(bf16)
        d_pre_ref[:, cols] = d_pre
        in_sums_ref[:, cols] += total(d_pre.astype(f32))
        d_hidden = d_hidden + dot_t(d_pre, in_ref[:, cols])
    d_resid1 = norm_back(d_hidden, gain_one, unit1, scale1)
    d_resid1_ref[...] = d_resid1
    d_branch = d_resid1.astype(bf16)
    d_branch_ref[...] = d_branch
    d_attended_ref[...] = dot_t(out_ref[...], d_branch).astype(bf16)
    sums_ref[...] += jnp.concatenate(
        [
            total(d_branch.astype(f32)),
            total(d_hidden * unit1),
            total(d_hidden),
            total(d_ffn.astype(f32)),
            total(cot * unit2),
            total(cot),
            jnp.zeros((2, cot.shape[1]), f32),
        ],
        axis=0,
    )


def feed_forward(tokens, attended_t, cotangent, out_full, in_full, back_full, vectors, in_shift):
    f32, bf16 = jnp.float32, jnp.bfloat16
    rows, model = tokens.shape
    inner = in_full.shape[1]
    tile = math.gcd(rows, 256)
    chunk = math.gcd(inner, 512)
    by_rows = lambda n: pl.BlockSpec((tile, n), lambda i: (i, 0))
    by_cols = lambda n: pl.BlockSpec((n, tile), lambda i: (0, i))
    fixed = lambda m, n: pl.BlockSpec((m, n), lambda i: (0, 0))
    shape = jax.ShapeDtypeStruct
    return pl.pallas_call(
        partial(feed_kernel, chunk),
        grid=(rows // tile,),
        in_specs=[
            by_rows(model), by_cols(model), by_rows(model), fixed(model, model),
            fixed(model, inner), fixed(inner, model), fixed(8, model), fixed(1, inner),
        ],
        out_specs=[
            by_rows(model), by_rows(model), by_cols(model), by_rows(model), by_rows(inner),
            by_rows(model), by_rows(inner), by_rows(model), fixed(8, model), fixed(1, inner),
        ],
        out_shape=[
            shape((rows, model), bf16), shape((rows, model), f32), shape((model, rows), bf16),
            shape((rows, model), bf16), shape((rows, inner), bf16), shape((rows, model), bf16),
            shape((rows, inner), bf16), shape((rows, model), bf16), shape((8, model), f32),
            shape((1, inner), f32),
        ],
        scratch_shapes=[pltpu.VMEM((tile, inner), f32)],
        cost_estimate=pl.CostEstimate(
            flops=rows * model * (8 * inner + 4 * model), transcendentals=0, bytes_accessed=30_000_000
        ),
        name="feed_forward",
    )(tokens, attended_t, cotangent, out_full, in_full, back_full, vectors, in_shift)


def body(
    inputs,
    doc_starts,
    qkv_weight,
    query_bias,
    value_bias,
    out_weight,
    out_bias,
    norm1_gain,
    norm1_bias,
    in_weight,
    in_bias,
    back_weight,
    back_bias,
    norm2_gain,
    norm2_bias,
    cotangent,
):
    bf16, f32 = jnp.bfloat16, jnp.float32
    tokens = inputs[0]
    rows, model = tokens.shape
    starts = doc_starts[0]
    docs = starts.shape[0]
    ctx = lax.axis_size("ctx")
    fsdp = lax.axis_size("fsdp")
    groups = math.gcd(H, ctx)
    parts = ctx // groups
    heads = H // groups
    span = heads * HD
    width = 3 * span
    index = lax.axis_index("ctx")
    g, s = index // parts, index % parts
    f = lax.axis_index("fsdp")
    shard = model // fsdp

    slots = [tokens] + [ctx_shift(tokens, groups, parts, d, 0) for d in range(1, groups)]

    own_cols = pick(qkv_weight.reshape(shard, 3, groups, span), g, 2).reshape(shard, width)
    small = jnp.concatenate(
        [
            query_bias, value_bias, out_bias, norm1_gain, norm1_bias,
            back_bias, norm2_gain, norm2_bias, in_bias,
        ]
    )
    count = small.shape[0]
    extra = -(-count // (width * PAD)) * PAD
    small_block = jnp.pad(small, (0, extra * width - count)).reshape(extra, width)
    first = jnp.concatenate([own_cols, small_block], axis=0)
    first_top = gather_top(first)
    first_top, out_held, in_held, back_held = together(
        first_top, out_weight, in_weight, back_weight
    )
    out_top, in_top, back_top = gather_top(out_held), gather_top(in_held), gather_top(back_held)
    first = gather_rest(first, first_top)
    own_weight = first[:, :shard].reshape(model, width)
    flat = first[:, shard:].reshape(fsdp, extra * width)[:, :count].astype(f32)
    vector = lambda i: flat[:, i * shard : (i + 1) * shard].reshape(model)
    query_shift, value_shift = vector(0), vector(1)
    vectors = jnp.pad(jnp.stack([vector(i) for i in range(2, 8)]), ((0, 2), (0, 0)))
    in_shift = flat[:, 8 * shard :].reshape(1, -1)

    zero = jnp.zeros((span,), f32)
    own_shift = jnp.concatenate(
        [
            lax.dynamic_slice(query_shift, (g * span,), (span,)),
            zero,
            lax.dynamic_slice(value_shift, (g * span,), (span,)),
        ]
    )
    own, others = [], []
    for slot in slots:
        projected = lax.dot_general(
            own_weight, slot, (((0,), (1,)), ((), ())), preferred_element_type=f32
        )
        low = (projected + own_shift[:, None]).astype(bf16).reshape(3, heads, HD, rows)
        own.append(low)
    for e in range(1, parts):
        for low in own:
            others.append(ctx_shift(low[1:], groups, parts, 0, e))
    if parts > 1:
        in_top, others[0], others[1] = together(in_top, others[0], others[1])

    bounds = jnp.concatenate([starts, jnp.full((1,), ctx * rows, jnp.int32)])
    base = ((g - jnp.arange(groups, dtype=jnp.int32) + groups) % groups) * parts + s
    heads_at = base * rows
    tails_at = heads_at + rows - 1
    low_edge = jnp.max(jnp.where(starts[None] <= heads_at[:, None], starts[None], 0), axis=1)
    high_edge = jnp.min(
        jnp.where(bounds[None] > tails_at[:, None], bounds[None], ctx * rows), axis=1
    )
    ranges = jnp.stack([low_edge // rows, (high_edge + rows - 1) // rows], axis=1).reshape(-1)
    meta = jnp.concatenate([jnp.stack([g, s]).astype(jnp.int32), starts, ranges.astype(jnp.int32)])

    out_full = gather_rest(out_weight, out_top).reshape(model, model)
    in_full = gather_rest(in_weight, in_top).reshape(model, -1)
    meta, out_full, in_full = together(meta, out_full, in_full)
    low, wide, log_total = attend(meta, own, others, groups, parts, docs, rows, heads)
    low, qkv_held = together(low, qkv_weight)
    attended_t = jnp.zeros((groups * span, rows), bf16)
    turned = []
    for j in range(groups):
        piece = low[:, :, j * rows : (j + 1) * rows]
        turned.append(ctx_shift(piece, groups, parts, -j, 0) if j else piece)
    for j, piece in enumerate(together(*turned)):
        attended_t = lax.dynamic_update_slice(
            attended_t, piece.reshape(span, rows), (((g + j) % groups) * span, 0)
        )
    back_full = gather_rest(back_weight, back_top).reshape(-1, model)

    (
        result, d_resid1, d_attended_t, hidden_low, act_low, d_ffn_low, d_pre_low, d_branch_low,
        sums, in_sums,
    ) = feed_forward(
        tokens, attended_t, cotangent[0], out_full, in_full, back_full, vectors, in_shift
    )
    grads = []
    for j in range(groups):
        part = lax.dynamic_slice(d_attended_t, (((g + j) % groups) * span, 0), (span, rows))
        part = part.reshape(heads, HD, rows)
        grads.append(ctx_shift(part, groups, parts, j, 0) if j else part)

    inner = in_full.shape[1]
    inner_shard = in_bias.shape[0]
    lead = (fsdp // 2,)
    first_dim = (((0,), (0,)), ((), ()))

    def product(a, b, dims, *shape):
        return lax.dot_general(a, b, dims, preferred_element_type=f32).reshape(lead + shape)

    def reduce_first(keep, send):
        got = swap(send.astype(bf16), "fsdp", 0)
        return (keep + got.astype(f32)).astype(bf16)

    line = jnp.concatenate(
        [sums[:6].reshape(6, fsdp, shard).transpose(1, 0, 2).reshape(fsdp, -1), in_sums.reshape(fsdp, -1)],
        axis=1,
    )
    line_rows = -(inner_shard + shard) % 64 or 64
    line = jnp.pad(line, ((0, 0), (0, line_rows * model - line.shape[1])))
    line = line.reshape(fsdp * line_rows, model)
    act_keep, act_send = split_blocks(act_low, 1, inner_shard)
    hidden_keep, hidden_send = split_blocks(hidden_low, 1, shard)
    out_keep, out_send = split_blocks(attended_t, 0, shard)
    line_keep, line_send = split_blocks(line, 0, line_rows)
    plain = (((1,), (0,)), ((), ()))
    lower = reduce_first(
        product(act_keep, d_ffn_low, first_dim, inner_shard, model),
        product(act_send, d_ffn_low, first_dim, inner_shard, model),
    )
    upper = reduce_first(
        product(hidden_keep, d_pre_low, first_dim, shard, inner),
        product(hidden_send, d_pre_low, first_dim, shard, inner),
    )
    rest = reduce_first(
        jnp.concatenate(
            [product(out_keep, d_branch_low, plain, shard, model), line_keep.reshape(lead + (line_rows, model))],
            axis=1,
        ),
        jnp.concatenate(
            [product(out_send, d_branch_low, plain, shard, model), line_send.reshape(lead + (line_rows, model))],
            axis=1,
        ),
    )
    lower = jnp.concatenate([lower, rest], axis=1)
    fsdp_bits, ctx_bits = range(bits_of("fsdp")), range(bits_of("ctx"))
    chunks = inner // (2 * model)

    def pair_step(i, state):
        lower, upper = state
        lower_steps = [("fsdp", b) for b in fsdp_bits[1:]] + [("ctx", 0)]
        upper_steps = [("ctx", 0)] + [("fsdp", b) for b in fsdp_bits[1:]]
        return halve(lower, *lower_steps[i], 1), halve(upper, *upper_steps[i], 2)

    def merge(state):
        lower, upper = state
        return (
            jnp.concatenate(
                [lower[0]] + [upper[0, :, c * model : (c + 1) * model] for c in range(chunks)], axis=0
            ),
        )

    steps = [partial(pair_step, i) for i in range(len(fsdp_bits))]
    last = steps.pop()
    steps.append(lambda state: merge(last(state)))
    for bit in ctx_bits[1:-1]:
        steps.append(lambda state, bit=bit: (halve(state[0], "ctx", bit, 0),))
    state = (lower, upper)

    pieces, received = [], [[] for unused in range(groups)]
    mine, theirs = None, None

    def send(piece):
        pieces.append(piece)
        for j in range(groups):
            part = piece[:, :, j * rows : (j + 1) * rows]
            received[j].append(ctx_shift(part, groups, parts, -j, 0) if j else part)

    def settle(dq, dkv, theirs):
        for other in theirs:
            dkv = dkv + other.astype(f32)
        send(jnp.concatenate([dq[None], dkv.astype(bf16)], axis=0))

    for head in range(heads):
        if head and steps:
            state = steps.pop(0)(state)
        meta, *state = together(meta, *state)
        dq, dkv, *rest = attend_back(
            head, meta, own, others, grads, wide, log_total, groups, parts, docs, rows
        )
        if head:
            dq, *theirs = together(dq, *theirs)
            settle(*mine, theirs)
        mine = (dq, dkv)
        theirs = [ctx_shift(rest[0][e - 1], groups, parts, 0, -e) for e in range(1, parts)]
    settle(*mine, theirs)
    qkv_top = gather_top(qkv_held)
    qkv_full = gather_rest(qkv_held, qkv_top).reshape(model, 3 * model)
    for advance in steps:
        state = advance(state)
    merged = exchange(state[0], "ctx", ctx_bits[-1])
    for bit in reversed(ctx_bits[1:-1]):
        merged = double(merged, "ctx", bit, 0)
    other = swap(merged, "ctx", 0)
    lower_rows = (inner_shard + shard + line_rows) // 2
    lower = join(bit_at("ctx", 0), merged[:lower_rows], other[:lower_rows], 0)
    wide_half = lambda m: jnp.concatenate(
        [m[lower_rows + c * shard : lower_rows + (c + 1) * shard] for c in range(chunks)], axis=1
    )
    upper = join(bit_at("ctx", 0), wide_half(merged), wide_half(other), 1)

    d_qkv_t = jnp.stack(pieces, axis=1).reshape(width, groups * rows)
    gathered = jnp.concatenate(slots, axis=0)
    grad_qkv = lax.dot_general(
        gathered, d_qkv_t, (((0,), (1,)), ((), ())), preferred_element_type=f32
    )
    sums = jnp.sum(d_qkv_t, axis=1, dtype=f32)
    sums = jnp.pad(jnp.broadcast_to(sums, (fsdp, 1, width)), ((0, 0), (0, PAD - 1), (0, 0)))
    qkv_sum = jnp.concatenate([grad_qkv.reshape(fsdp, shard, width), sums], axis=1).astype(bf16)
    for bit in fsdp_bits:
        qkv_sum = halve(qkv_sum, "fsdp", bit, 1)
    qkv_sum = qkv_sum[0]
    wide_sum = qkv_sum.astype(f32)
    for e in range(1, parts):
        wide_sum = wide_sum + ctx_shift(qkv_sum, groups, parts, 0, e).astype(f32)
    qkv_low = wide_sum.astype(bf16)
    by_group = jnp.zeros((groups,) + qkv_low.shape, bf16)
    for j in range(groups):
        piece = ctx_shift(qkv_low, groups, parts, -j, 0) if j else qkv_low
        by_group = lax.dynamic_update_slice(by_group, piece[None], ((g + j) % groups, 0, 0))
    natural = by_group.reshape(groups, shard + PAD, 3, span).transpose(1, 2, 0, 3)
    natural = natural.reshape(shard + PAD, 3 * model).astype(f32)
    grad_qkv_shard = natural[:shard]
    bias_line = natural[shard]
    grad_query_shift = lax.dynamic_slice(bias_line, (f * shard,), (shard,))
    grad_value_shift = lax.dynamic_slice(bias_line, (2 * model + f * shard,), (shard,))

    natural = jnp.zeros((3, groups, heads, HD, rows), bf16)
    for j in range(groups):
        part = jnp.stack(received[j], axis=1)[:, None]
        natural = lax.dynamic_update_slice(natural, part, (0, (g + j) % groups, 0, 0, 0))
    input_grad = d_resid1 + lax.dot_general(
        natural.reshape(3 * model, rows),
        qkv_full,
        (((0,), (1,)), ((), ())),
        preferred_element_type=f32,
    )

    ends = inner_shard + shard
    flat = lower[ends:].reshape(-1).astype(f32)
    offsets = lambda i: flat[i * shard : (i + 1) * shard]
    return (
        result[None],
        input_grad[None],
        grad_qkv_shard,
        grad_query_shift,
        grad_value_shift,
        lower[inner_shard:ends].astype(f32),
        offsets(0),
        offsets(1),
        offsets(2),
        upper.astype(f32),
        flat[6 * shard : 6 * shard + inner_shard],
        lower[:inner_shard].astype(f32),
        offsets(3),
        offsets(4),
        offsets(5),
    )


def solution(mesh):
    rows, one = P("fsdp", None), P("fsdp")
    whole = P("fsdp", "ctx", None)
    return jax.shard_map(
        body,
        mesh=mesh,
        in_specs=(
            whole, rows, rows, one, one, rows, one, one, one, rows, one, rows, one, one, one, whole,
        ),
        out_specs=(
            whole, whole, rows, one, one, rows, one, one, one, rows, one, rows, one, one, one,
        ),
        check_vma=False,
    )
```

```python
from functools import partial
import math

import jax
import jax.numpy as jnp
from jax import lax
from jax.experimental import pallas as pl
from jax.experimental.pallas import tpu as pltpu
from jax.sharding import PartitionSpec as P

H = 12
HD = 64
EPSILON = 1e-05
BIG = 2.0**100
LOG2E = 1.4426950408889634
PAD = 16
KERNEL_FLOPS = 3_000_000_000
KERNEL_BYTES = 20_000_000


def ctx_shift(array, groups, parts, dg, ds):
    pairs = []
    for g in range(groups):
        for s in range(parts):
            pairs.append((g * parts + s, ((g + dg) % groups) * parts + (s + ds) % parts))
    return lax.ppermute(array, "ctx", pairs)


def swap(array, axis, bit):
    size = lax.axis_size(axis)
    return lax.ppermute(array, axis, [(i, i ^ (1 << bit)) for i in range(size)])


def bits_of(axis):
    return lax.axis_size(axis).bit_length() - 1


def bit_at(axis, bit):
    return (lax.axis_index(axis) >> bit) & 1


def pick(array, which, dim):
    return lax.dynamic_index_in_dim(array, which, dim, keepdims=False)


def together(*values):
    return lax.optimization_barrier(values)


def join(mine, own, other, dim):
    return jnp.where(
        mine == 0,
        jnp.concatenate([own, other], axis=dim),
        jnp.concatenate([other, own], axis=dim),
    )


def gather_top(shard):
    return swap(shard, "fsdp", bits_of("fsdp") - 1)


def gather_rest(shard, other):
    top = bits_of("fsdp") - 1
    held = join(bit_at("fsdp", top), shard[None], other[None], 0)
    for bit in reversed(range(top)):
        got = swap(held, "fsdp", bit)
        pair = join(bit_at("fsdp", bit), held[:, None], got[:, None], 1)
        held = pair.reshape((-1,) + shard.shape)
    return held


def halve(held, axis, bit, dim):
    mine = bit_at(axis, bit)
    if axis == "fsdp":
        pairs = held.reshape((held.shape[0] // 2, 2) + held.shape[1:])
        keep, send = pick(pairs, mine, 1), pick(pairs, 1 - mine, 1)
    else:
        half = held.shape[dim] // 2
        keep = lax.dynamic_slice_in_dim(held, mine * half, half, dim)
        send = lax.dynamic_slice_in_dim(held, (1 - mine) * half, half, dim)
    return add_low(keep, swap(send, axis, bit))


def add_low(a, b):
    return (a.astype(jnp.float32) + b.astype(jnp.float32)).astype(jnp.bfloat16)


def exchange(held, axis, bit):
    return add_low(held, swap(held, axis, bit))


def double(held, axis, bit, dim):
    return join(bit_at(axis, bit), held, swap(held, axis, bit), dim)


def doc_row(meta, base, length, docs):
    pos = base + lax.broadcasted_iota(jnp.int32, (1, length), 1)
    doc = jnp.full((1, length), -1, jnp.int32)
    for j in range(docs):
        doc = doc + (pos >= meta[2 + j]).astype(jnp.int32)
    return doc


def dot(a, b):
    return jnp.dot(a, b, preferred_element_type=jnp.float32)


def dot_t(a, b):
    return lax.dot_general(a, b, (((1,), (1,)), ((), ())), preferred_element_type=jnp.float32)


def fill_keys(meta, own, others, groups, parts, docs, rows, store):
    g, s = meta[0], meta[1]
    for j in range(groups):
        for e in range(parts):
            block = lax.rem(g - j + groups, groups) * parts + lax.rem(s - e + parts, parts)
            if e == 0:
                key_t, value_t = own[j][1, 0], own[j][2, 0]
            else:
                ref = others[(e - 1) * groups + j]
                key_t, value_t = ref[0, 0], ref[1, 0]
            doc = doc_row(meta, block * rows, rows, docs)
            hot = (lax.broadcasted_iota(jnp.int32, (HD, rows), 0) == doc).astype(jnp.float32)
            keys = jnp.concatenate([key_t, hot.astype(jnp.bfloat16)], axis=0)
            store(block, keys, key_t, value_t)


def query_full(meta, query_t, j, groups, parts, docs, rows):
    g, s = meta[0], meta[1]
    block = lax.rem(g - j + groups, groups) * parts + s
    doc = doc_row(meta, block * rows, rows, docs)
    shut = jnp.where(lax.broadcasted_iota(jnp.int32, (HD, rows), 0) == doc, 0.0, -BIG)
    return jnp.concatenate([query_t, shut.astype(jnp.bfloat16)], axis=0)


def attend_kernel(groups, parts, docs, rows, meta, *refs):
    own = refs[:groups]
    others = refs[groups : groups * parts]
    low_ref, wide_ref, log_ref, queries_ref, keys_ref, values_ref = refs[groups * parts :]
    coeff = LOG2E * HD**-0.5

    def store(block, keys, key_t, value_t):
        keys_ref[block] = keys.T
        values_ref[block] = value_t

    fill_keys(meta, own, others, groups, parts, docs, rows, store)
    for j in range(groups):
        queries_ref[j] = query_full(meta, own[j][0, 0], j, groups, parts, docs, rows)

    def one_slot(j, carry):
        full = queries_ref[j]

        def step(t, state):
            best, total, accum = state
            scores = dot(keys_ref[t], full)
            new_best = jnp.maximum(best, jnp.max(scores, axis=0, keepdims=True))
            weights = jnp.exp2((scores - new_best) * coeff)
            shrink = jnp.exp2((best - new_best) * coeff)
            total = total * shrink + jnp.sum(weights, axis=0, keepdims=True)
            accum = accum * shrink + dot(values_ref[t], weights.astype(jnp.bfloat16))
            return new_best, total, accum

        best, total, accum = lax.fori_loop(
            meta[2 + docs + 2 * j],
            meta[3 + docs + 2 * j],
            step,
            (
                jnp.full((1, rows), -BIG, jnp.float32),
                jnp.zeros((1, rows), jnp.float32),
                jnp.zeros((HD, rows), jnp.float32),
            ),
        )
        attended = accum / total
        at = pl.ds(pl.multiple_of(j * rows, rows), rows)
        wide_ref[0, :, at] = attended
        low_ref[0, :, at] = attended.astype(jnp.bfloat16)
        log_ref[0, :, at] = best * coeff + jnp.log2(total)
        return carry

    lax.fori_loop(0, groups, one_slot, 0)


def attend_back_kernel(groups, parts, docs, rows, meta, *refs):
    own = refs[:groups]
    others = refs[groups : groups * parts]
    grads = refs[groups * parts : groups * parts + groups]
    rest = refs[groups * parts + groups :]
    wide_ref, log_ref = rest[:2]
    dq_ref, mine_ref = rest[2:4]
    theirs = rest[4] if parts > 1 else None
    queries_ref, grads_ref, keys_ref, keys_t_ref, values_ref, accum_ref = rest[-6:]
    coeff = LOG2E * HD**-0.5

    def store(block, keys, key_t, value_t):
        keys_ref[block] = keys.T
        keys_t_ref[block] = key_t
        values_ref[block] = value_t.T

    fill_keys(meta, own, others, groups, parts, docs, rows, store)
    accum_ref[...] = jnp.zeros_like(accum_ref)
    for j in range(groups):
        queries_ref[j] = query_full(meta, own[j][0, 0], j, groups, parts, docs, rows)
        grads_ref[j] = grads[j][0]

    def one_slot(j, carry):
        at = pl.ds(pl.multiple_of(j * rows, rows), rows)
        full = queries_ref[j]
        grad_t = grads_ref[j]
        delta = jnp.sum(grad_t.astype(jnp.float32) * wide_ref[0, :, at], axis=0, keepdims=True)
        log_total = log_ref[0, :, at]
        blank = jnp.zeros((HD, rows), jnp.bfloat16)
        both = jnp.concatenate(
            [
                jnp.concatenate([full[:HD], blank], axis=1),
                jnp.concatenate([blank, grad_t], axis=1),
            ],
            axis=0,
        )

        def step(t, grad_query):
            scores = dot(keys_ref[t], full)
            probs = jnp.exp2(scores * coeff - log_total)
            d_probs = dot(values_ref[t], grad_t)
            d_scores = (probs * (d_probs - delta)).astype(jnp.bfloat16)
            joined = jnp.concatenate([d_scores, probs.astype(jnp.bfloat16)], axis=1)
            accum_ref[t] += dot_t(joined, both)
            return grad_query + dot(keys_t_ref[t], d_scores)

        grad_query = lax.fori_loop(
            meta[2 + docs + 2 * j],
            meta[3 + docs + 2 * j],
            step,
            jnp.zeros((HD, rows), jnp.float32),
        )
        dq_ref[:, at] = (grad_query * HD**-0.5).astype(jnp.bfloat16)
        return carry

    lax.fori_loop(0, groups, one_slot, 0)
    g, s = meta[0], meta[1]
    for j in range(groups):
        for e in range(parts):
            block = lax.rem(g - j + groups, groups) * parts + lax.rem(s - e + parts, parts)
            terms = accum_ref[block].T
            at = slice(j * rows, (j + 1) * rows)
            d_key = terms[:HD] * HD**-0.5
            d_value = terms[HD:]
            if e == 0:
                mine_ref[0, :, at] = d_key
                mine_ref[1, :, at] = d_value
            else:
                theirs[e - 1, 0, :, at] = d_key.astype(jnp.bfloat16)
                theirs[e - 1, 1, :, at] = d_value.astype(jnp.bfloat16)


def head_block(head, *shape):
    dims = tuple(1 if n is None else n for n in shape)
    where = shape.index(None)

    def at(h, meta):
        chosen = h if head is None else head
        return tuple(chosen if i == where else 0 for i in range(len(dims)))

    return pl.BlockSpec(dims, at)


def attend(meta, own, others, groups, parts, docs, rows, heads):
    tiles = groups * parts
    tokens = groups * rows
    block = partial(head_block, None)
    grid_spec = pltpu.PrefetchScalarGridSpec(
        num_scalar_prefetch=1,
        grid=(heads,),
        in_specs=[block(3, None, HD, rows)] * groups
        + [block(2, None, HD, rows)] * (groups * (parts - 1)),
        out_specs=[block(None, HD, tokens), block(None, HD, tokens), block(None, 1, tokens)],
        scratch_shapes=[
            pltpu.VMEM((groups, 2 * HD, rows), jnp.bfloat16),
            pltpu.VMEM((tiles, rows, 2 * HD), jnp.bfloat16),
            pltpu.VMEM((tiles, HD, rows), jnp.bfloat16),
        ],
    )
    return pl.pallas_call(
        partial(attend_kernel, groups, parts, docs, rows),
        grid_spec=grid_spec,
        out_shape=[
            jax.ShapeDtypeStruct((heads, HD, tokens), jnp.bfloat16),
            jax.ShapeDtypeStruct((heads, HD, tokens), jnp.float32),
            jax.ShapeDtypeStruct((heads, 1, tokens), jnp.float32),
        ],
        cost_estimate=pl.CostEstimate(
            flops=KERNEL_FLOPS * 2 * heads,
            transcendentals=0,
            bytes_accessed=KERNEL_BYTES * heads,
        ),
        name="attend",
    )(meta, *own, *others)


def attend_back(head, meta, own, others, grads, wide, log_total, groups, parts, docs, rows):
    tiles = groups * parts
    tokens = groups * rows
    block = partial(head_block, head)
    plain = lambda *dims: pl.BlockSpec(dims, lambda h, meta: (0,) * len(dims))
    out_specs = [plain(HD, tokens), plain(2, HD, tokens)]
    out_shape = [
        jax.ShapeDtypeStruct((HD, tokens), jnp.bfloat16),
        jax.ShapeDtypeStruct((2, HD, tokens), jnp.float32),
    ]
    if parts > 1:
        out_specs.append(plain(parts - 1, 2, HD, tokens))
        out_shape.append(jax.ShapeDtypeStruct((parts - 1, 2, HD, tokens), jnp.bfloat16))
    grid_spec = pltpu.PrefetchScalarGridSpec(
        num_scalar_prefetch=1,
        grid=(1,),
        in_specs=[block(3, None, HD, rows)] * groups
        + [block(2, None, HD, rows)] * (groups * (parts - 1))
        + [block(None, HD, rows)] * groups
        + [block(None, HD, tokens), block(None, 1, tokens)],
        out_specs=out_specs,
        scratch_shapes=[
            pltpu.VMEM((groups, 2 * HD, rows), jnp.bfloat16),
            pltpu.VMEM((groups, HD, rows), jnp.bfloat16),
            pltpu.VMEM((tiles, rows, 2 * HD), jnp.bfloat16),
            pltpu.VMEM((tiles, HD, rows), jnp.bfloat16),
            pltpu.VMEM((tiles, rows, HD), jnp.bfloat16),
            pltpu.VMEM((tiles, rows, 2 * HD), jnp.float32),
        ],
    )
    return pl.pallas_call(
        partial(attend_back_kernel, groups, parts, docs, rows),
        grid_spec=grid_spec,
        out_shape=out_shape,
        cost_estimate=pl.CostEstimate(
            flops=KERNEL_FLOPS * 5, transcendentals=0, bytes_accessed=KERNEL_BYTES
        ),
        name="attend_back",
    )(meta, *own, *others, *grads, wide, log_total)


ERFC = (
    -1.26551223, 1.00002368, 0.37409196, 0.09678418, -0.18628806,
    0.27886807, -1.13520398, 1.48851587, -0.82215223, 0.17087277,
)


def normal_terms(v):
    z = jnp.abs(v) * (0.5**0.5)
    t = 1.0 / (1.0 + 0.5 * z)
    poly = jnp.full_like(t, ERFC[-1])
    for term in reversed(ERFC[:-1]):
        poly = poly * t + term
    square = z * z
    tail = 0.5 * t * jnp.exp(poly - square)
    below = jnp.where(v < 0, tail, 1.0 - tail)
    return below, jnp.exp(-square) * (2.0 * math.pi) ** -0.5


def normed(resid):
    centred = resid - jnp.mean(resid, axis=-1, keepdims=True)
    spread = jnp.mean(centred * centred, axis=-1, keepdims=True)
    scale = lax.rsqrt(spread + EPSILON)
    return centred * scale, scale


def norm_back(grad, gain, unit, scale):
    e = grad * gain
    inner = jnp.mean(e * unit, axis=-1, keepdims=True)
    return (e - jnp.mean(e, axis=-1, keepdims=True) - unit * inner) * scale


def over_blocks(count, aligned, step, value):
    if aligned:
        return lax.fori_loop(0, count, step, value)
    for i in range(count):
        value = step(i, value)
    return value


def feed_kernel(
    tokens_ref,
    attended_ref,
    cot_ref,
    out_ref,
    in_ref,
    back_ref,
    vec_ref,
    in_bias_ref,
    result_ref,
    d_resid1_ref,
    d_attended_ref,
    hidden_ref,
    act_ref,
    d_ffn_ref,
    d_pre_ref,
    d_branch_ref,
    sums_ref,
    in_sums_ref,
    slope_ref,
):
    f32, bf16 = jnp.float32, jnp.bfloat16
    out_shift, gain_one, shift_one = vec_ref[0:1], vec_ref[1:2], vec_ref[2:3]
    back_shift, gain_two, shift_two = vec_ref[3:4], vec_ref[4:5], vec_ref[5:6]

    @pl.when(pl.program_id(0) == 0)
    def _():
        sums_ref[...] = jnp.zeros_like(sums_ref)
        in_sums_ref[...] = jnp.zeros_like(in_sums_ref)

    total = lambda a: jnp.sum(a, axis=0, keepdims=True)
    branch = dot(attended_ref[...].T, out_ref[...]) + out_shift
    unit1, scale1 = normed(tokens_ref[...].astype(f32) + branch)
    hidden = unit1 * gain_one + shift_one
    hidden_low = hidden.astype(bf16)
    count, unused, shard = hidden_ref.shape
    for i in range(count):
        hidden_ref[i] = hidden_low[:, i * shard : (i + 1) * shard]
    resid2 = hidden + back_shift
    blocks, unused, size = act_ref.shape
    aligned = size % 128 == 0
    columns = lambda i: pl.ds(pl.multiple_of(i * size, size) if aligned else i * size, size)

    def forward(i, resid2):
        cols = columns(i)
        pre = dot(hidden_low, in_ref[:, cols]) + in_bias_ref[:, cols]
        below, density = normal_terms(pre)
        act = (pre * below).astype(bf16)
        act_ref[i] = act
        slope_ref[i] = below + pre * density
        return resid2 + dot(act, back_ref[cols, :])

    resid2 = over_blocks(blocks, aligned, forward, hidden + back_shift)
    unit2, scale2 = normed(resid2)
    result_ref[...] = (unit2 * gain_two + shift_two).astype(bf16)
    cot = cot_ref[...].astype(f32)
    d_resid2 = norm_back(cot, gain_two, unit2, scale2)
    d_ffn = d_resid2.astype(bf16)
    d_ffn_ref[...] = d_ffn

    def backward(i, d_hidden):
        cols = columns(i)
        d_act = dot_t(d_ffn, back_ref[cols, :])
        d_pre = (d_act * slope_ref[i]).astype(bf16)
        d_pre_ref[:, cols] = d_pre
        in_sums_ref[:, cols] += total(d_pre.astype(f32))
        return d_hidden + dot_t(d_pre, in_ref[:, cols])

    d_hidden = over_blocks(blocks, aligned, backward, d_resid2)
    d_resid1 = norm_back(d_hidden, gain_one, unit1, scale1)
    d_resid1_ref[...] = d_resid1
    d_branch = d_resid1.astype(bf16)
    d_branch_ref[...] = d_branch
    d_attended_ref[...] = dot_t(out_ref[...], d_branch).astype(bf16)
    sums_ref[...] += jnp.concatenate(
        [
            total(d_branch.astype(f32)),
            total(d_hidden * unit1),
            total(d_hidden),
            total(d_ffn.astype(f32)),
            total(cot * unit2),
            total(cot),
            jnp.zeros((2, cot.shape[1]), f32),
        ],
        axis=0,
    )


def feed_forward(fsdp, tokens, attended_t, cotangent, out_full, in_full, back_full, vectors, in_shift):
    f32, bf16 = jnp.float32, jnp.bfloat16
    rows, model = tokens.shape
    inner = in_full.shape[1]
    tile = math.gcd(rows, 256)
    by_rows = lambda n: pl.BlockSpec((tile, n), lambda i: (i, 0))
    by_cols = lambda n: pl.BlockSpec((n, tile), lambda i: (0, i))
    blocks = lambda n: pl.BlockSpec((fsdp, tile, n // fsdp), lambda i: (0, i, 0))
    fixed = lambda m, n: pl.BlockSpec((m, n), lambda i: (0, 0))
    shape = jax.ShapeDtypeStruct
    return pl.pallas_call(
        feed_kernel,
        grid=(rows // tile,),
        in_specs=[
            by_rows(model), by_cols(model), by_rows(model), fixed(model, model),
            fixed(model, inner), fixed(inner, model), fixed(8, model), fixed(1, inner),
        ],
        out_specs=[
            by_rows(model), by_rows(model), by_cols(model), blocks(model), blocks(inner),
            by_rows(model), by_rows(inner), by_rows(model), fixed(8, model), fixed(1, inner),
        ],
        out_shape=[
            shape((rows, model), bf16), shape((rows, model), f32), shape((model, rows), bf16),
            shape((fsdp, rows, model // fsdp), bf16), shape((fsdp, rows, inner // fsdp), bf16),
            shape((rows, model), bf16),
            shape((rows, inner), bf16), shape((rows, model), bf16), shape((8, model), f32),
            shape((1, inner), f32),
        ],
        scratch_shapes=[pltpu.VMEM((fsdp, tile, inner // fsdp), f32)],
        cost_estimate=pl.CostEstimate(
            flops=rows * model * (8 * inner + 4 * model), transcendentals=0, bytes_accessed=30_000_000
        ),
        name="feed_forward",
    )(tokens, attended_t, cotangent, out_full, in_full, back_full, vectors, in_shift)


def weight_grad_kernel(which, *refs):
    ins, (d_ffn, d_pre, d_branch), outs = refs[:8], refs[8:11], refs[11:]
    bf16 = jnp.bfloat16
    for side in range(2):
        act, hidden, attended_t, line = ins[4 * side : 4 * side + 4]
        lower, upper = outs[2 * side : 2 * side + 2]
        first, second = act.shape[2], attended_t.shape[0]
        lower[0, :first] = dot(act[0].T, d_ffn[...]).astype(bf16)
        lower[0, first : first + second] = dot(attended_t[...], d_branch[...]).astype(bf16)
        lower[0, first + second :] = line[0].astype(bf16)
        upper[0] = dot(hidden[0].T, d_pre[...]).astype(bf16)


def weight_grads(which, act, hidden, attended_t, line, d_ffn, d_pre, d_branch):
    fsdp, rows, inner_shard = act.shape
    shard = hidden.shape[2]
    model, inner = d_ffn.shape[1], d_pre.shape[1]
    line_rows = line.shape[1]
    tall = inner_shard + shard + line_rows
    half = fsdp // 2
    in_specs = []
    for side in range(2):
        block = lambda i, w, side=side: 2 * i + w[side]
        in_specs += [
            pl.BlockSpec((1, rows, inner_shard), lambda i, w, b=block: (b(i, w), 0, 0)),
            pl.BlockSpec((1, rows, shard), lambda i, w, b=block: (b(i, w), 0, 0)),
            pl.BlockSpec((shard, rows), lambda i, w, b=block: (b(i, w), 0)),
            pl.BlockSpec((1, line_rows, model), lambda i, w, b=block: (b(i, w), 0, 0)),
        ]
    in_specs += [pl.BlockSpec((rows, n), lambda i, w: (0, 0)) for n in (model, inner, model)]
    out = [(tall, model), (shard, inner)] * 2
    return pl.pallas_call(
        weight_grad_kernel,
        grid_spec=pltpu.PrefetchScalarGridSpec(
            num_scalar_prefetch=1,
            grid=(half,),
            in_specs=in_specs,
            out_specs=[pl.BlockSpec((1,) + o, lambda i, w: (i, 0, 0)) for o in out],
        ),
        out_shape=[jax.ShapeDtypeStruct((half,) + o, jnp.bfloat16) for o in out],
        cost_estimate=pl.CostEstimate(
            flops=2 * rows * model * (2 * inner + model), transcendentals=0, bytes_accessed=25_000_000
        ),
        name="weight_grads",
    )(which, act, hidden, attended_t, line, act, hidden, attended_t, line, d_ffn, d_pre, d_branch)


def qkv_grad_kernel(fsdp, which, *refs):
    slots, (d_qkv, send, keep, total) = refs[:-4], refs[-4:]
    rows = slots[0].shape[0]
    shard = send.shape[1] - PAD
    value = None
    for j, slot in enumerate(slots):
        term = dot_t(slot[...].T, d_qkv[:, j * rows : (j + 1) * rows])
        value = term if value is None else value + term
    total[...] = value
    ones = jnp.ones((PAD, d_qkv.shape[1]), jnp.bfloat16)
    sums = dot_t(ones, d_qkv[...]).astype(jnp.bfloat16)
    for side, ref in enumerate((send, keep)):
        for i in range(fsdp // 2):
            at = pl.multiple_of((2 * i + which[side]) * shard, math.gcd(shard, 64))
            ref[i, :shard] = total[pl.ds(at, shard), :].astype(jnp.bfloat16)
            ref[i, shard:] = sums


def qkv_grads(which, slots, d_qkv_t, fsdp):
    rows, model = slots[0].shape
    width = d_qkv_t.shape[0]
    out = (fsdp // 2, model // fsdp + PAD, width)
    fixed = lambda dims: pl.BlockSpec(dims, lambda i, w: (0,) * len(dims))
    return pl.pallas_call(
        partial(qkv_grad_kernel, fsdp),
        grid_spec=pltpu.PrefetchScalarGridSpec(
            num_scalar_prefetch=1,
            grid=(1,),
            in_specs=[fixed((rows, model))] * len(slots) + [fixed(d_qkv_t.shape)],
            out_specs=[fixed(out)] * 2,
            scratch_shapes=[pltpu.VMEM((model, width), jnp.float32)],
        ),
        out_shape=[jax.ShapeDtypeStruct(out, jnp.bfloat16)] * 2,
        cost_estimate=pl.CostEstimate(
            flops=2 * rows * len(slots) * model * width, transcendentals=0, bytes_accessed=8_000_000
        ),
        name="qkv_grads",
    )(which, *slots, d_qkv_t)


def body(
    inputs,
    doc_starts,
    qkv_weight,
    query_bias,
    value_bias,
    out_weight,
    out_bias,
    norm1_gain,
    norm1_bias,
    in_weight,
    in_bias,
    back_weight,
    back_bias,
    norm2_gain,
    norm2_bias,
    cotangent,
):
    bf16, f32 = jnp.bfloat16, jnp.float32
    tokens = inputs[0]
    rows, model = tokens.shape
    starts = doc_starts[0]
    docs = starts.shape[0]
    ctx = lax.axis_size("ctx")
    fsdp = lax.axis_size("fsdp")
    groups = math.gcd(H, ctx)
    parts = ctx // groups
    heads = H // groups
    span = heads * HD
    width = 3 * span
    index = lax.axis_index("ctx")
    g, s = index // parts, index % parts
    f = lax.axis_index("fsdp")
    shard = model // fsdp

    slots = [tokens] + [ctx_shift(tokens, groups, parts, d, 0) for d in range(1, groups)]

    own_cols = pick(qkv_weight.reshape(shard, 3, groups, span), g, 2).reshape(shard, width)
    small = jnp.concatenate(
        [
            query_bias, value_bias, out_bias, norm1_gain, norm1_bias,
            back_bias, norm2_gain, norm2_bias, in_bias,
        ]
    )
    count = small.shape[0]
    extra = -(-count // (width * PAD)) * PAD
    small_block = jnp.pad(small, (0, extra * width - count)).reshape(extra, width)
    first = jnp.concatenate([own_cols, small_block], axis=0)
    first_top = gather_top(first)
    first_top, out_held, in_held, back_held = together(
        first_top, out_weight, in_weight, back_weight
    )
    out_top, in_top, back_top = gather_top(out_held), gather_top(in_held), gather_top(back_held)
    first = gather_rest(first, first_top)
    own_weight = first[:, :shard].reshape(model, width)
    flat = first[:, shard:].reshape(fsdp, extra * width)[:, :count].astype(f32)
    vector = lambda i: flat[:, i * shard : (i + 1) * shard].reshape(model)
    query_shift, value_shift = vector(0), vector(1)
    vectors = jnp.pad(jnp.stack([vector(i) for i in range(2, 8)]), ((0, 2), (0, 0)))
    in_shift = flat[:, 8 * shard :].reshape(1, -1)

    zero = jnp.zeros((span,), f32)
    own_shift = jnp.concatenate(
        [
            lax.dynamic_slice(query_shift, (g * span,), (span,)),
            zero,
            lax.dynamic_slice(value_shift, (g * span,), (span,)),
        ]
    )
    own, others = [], []
    for slot in slots:
        projected = lax.dot_general(
            own_weight, slot, (((0,), (1,)), ((), ())), preferred_element_type=f32
        )
        low = (projected + own_shift[:, None]).astype(bf16).reshape(3, heads, HD, rows)
        own.append(low)
    for e in range(1, parts):
        for low in own:
            others.append(ctx_shift(low[1:], groups, parts, 0, e))
    if parts > 1:
        in_top, others[0], others[1] = together(in_top, others[0], others[1])

    bounds = jnp.concatenate([starts, jnp.full((1,), ctx * rows, jnp.int32)])
    base = ((g - jnp.arange(groups, dtype=jnp.int32) + groups) % groups) * parts + s
    heads_at = base * rows
    tails_at = heads_at + rows - 1
    low_edge = jnp.max(jnp.where(starts[None] <= heads_at[:, None], starts[None], 0), axis=1)
    high_edge = jnp.min(
        jnp.where(bounds[None] > tails_at[:, None], bounds[None], ctx * rows), axis=1
    )
    ranges = jnp.stack([low_edge // rows, (high_edge + rows - 1) // rows], axis=1).reshape(-1)
    meta = jnp.concatenate([jnp.stack([g, s]).astype(jnp.int32), starts, ranges.astype(jnp.int32)])

    out_full = gather_rest(out_weight, out_top).reshape(model, model)
    in_full = gather_rest(in_weight, in_top).reshape(model, -1)
    meta, out_full, in_full = together(meta, out_full, in_full)
    low, wide, log_total = attend(meta, own, others, groups, parts, docs, rows, heads)
    low, qkv_held = together(low, qkv_weight)
    attended_t = jnp.zeros((groups * span, rows), bf16)
    turned = []
    for j in range(groups):
        piece = low[:, :, j * rows : (j + 1) * rows]
        turned.append(ctx_shift(piece, groups, parts, -j, 0) if j else piece)
    for j, piece in enumerate(together(*turned)):
        attended_t = lax.dynamic_update_slice(
            attended_t, piece.reshape(span, rows), (((g + j) % groups) * span, 0)
        )
    back_full = gather_rest(back_weight, back_top).reshape(-1, model)

    (
        result, d_resid1, d_attended_t, hidden_low, act_low, d_ffn_low, d_pre_low, d_branch_low,
        sums, in_sums,
    ) = feed_forward(
        fsdp, tokens, attended_t, cotangent[0], out_full, in_full, back_full, vectors, in_shift
    )
    grads = []
    for j in range(groups):
        part = lax.dynamic_slice(d_attended_t, (((g + j) % groups) * span, 0), (span, rows))
        part = part.reshape(heads, HD, rows)
        grads.append(ctx_shift(part, groups, parts, j, 0) if j else part)

    inner = in_full.shape[1]
    inner_shard = in_bias.shape[0]
    line = jnp.concatenate(
        [sums[:6].reshape(6, fsdp, shard).transpose(1, 0, 2).reshape(fsdp, -1), in_sums.reshape(fsdp, -1)],
        axis=1,
    )
    line_rows = -(inner_shard + shard) % 64 or 64
    line = jnp.pad(line, ((0, 0), (0, line_rows * model - line.shape[1])))
    line = line.reshape(fsdp, line_rows, model)
    mine = bit_at("fsdp", 0)
    which = jnp.stack([1 - mine, mine]).astype(jnp.int32)
    lower_send, upper_send, lower, upper = weight_grads(
        which, act_low, hidden_low, attended_t, line, d_ffn_low, d_pre_low, d_branch_low
    )
    lower = add_low(lower, swap(lower_send, "fsdp", 0))
    upper = add_low(upper, swap(upper_send, "fsdp", 0))
    fsdp_bits, ctx_bits = range(bits_of("fsdp")), range(bits_of("ctx"))
    chunks = inner // (2 * model)

    def pair_step(i, state):
        lower, upper = state
        lower_steps = [("fsdp", b) for b in fsdp_bits[1:]] + [("ctx", 0)]
        upper_steps = [("ctx", 0)] + [("fsdp", b) for b in fsdp_bits[1:]]
        return halve(lower, *lower_steps[i], 1), halve(upper, *upper_steps[i], 2)

    def merge(state):
        lower, upper = state
        return (
            jnp.concatenate(
                [lower[0]] + [upper[0, :, c * model : (c + 1) * model] for c in range(chunks)], axis=0
            ),
        )

    steps = [partial(pair_step, i) for i in range(len(fsdp_bits))]
    last = steps.pop()
    steps.append(lambda state: merge(last(state)))
    for bit in ctx_bits[1:-1]:
        steps.append(lambda state, bit=bit: (halve(state[0], "ctx", bit, 0),))
    state = (lower, upper)

    pieces, received = [], [[] for unused in range(groups)]
    held, theirs = None, None

    def send(piece):
        pieces.append(piece)
        for j in range(groups):
            part = piece[:, :, j * rows : (j + 1) * rows]
            received[j].append(ctx_shift(part, groups, parts, -j, 0) if j else part)

    def settle(dq, dkv, theirs):
        for other in theirs:
            dkv = dkv + other.astype(f32)
        send(jnp.concatenate([dq[None], dkv.astype(bf16)], axis=0))

    for head in range(heads):
        if head and steps:
            state = steps.pop(0)(state)
        meta, *state = together(meta, *state)
        dq, dkv, *rest = attend_back(
            head, meta, own, others, grads, wide, log_total, groups, parts, docs, rows
        )
        if head:
            dq, *theirs = together(dq, *theirs)
            settle(*held, theirs)
        held = (dq, dkv)
        theirs = [ctx_shift(rest[0][e - 1], groups, parts, 0, -e) for e in range(1, parts)]
    settle(*held, theirs)
    qkv_top = gather_top(qkv_held)
    qkv_full = gather_rest(qkv_held, qkv_top).reshape(model, 3 * model)
    for advance in steps:
        state = advance(state)
    merged = exchange(state[0], "ctx", ctx_bits[-1])
    for bit in reversed(ctx_bits[1:-1]):
        merged = double(merged, "ctx", bit, 0)
    other = swap(merged, "ctx", 0)
    lower_rows = (inner_shard + shard + line_rows) // 2
    lower = join(bit_at("ctx", 0), merged[:lower_rows], other[:lower_rows], 0)
    wide_half = lambda m: jnp.concatenate(
        [m[lower_rows + c * shard : lower_rows + (c + 1) * shard] for c in range(chunks)], axis=1
    )
    upper = join(bit_at("ctx", 0), wide_half(merged), wide_half(other), 1)

    d_qkv_t = jnp.stack(pieces, axis=1).reshape(width, groups * rows)
    qkv_send, qkv_sum = qkv_grads(which, slots, d_qkv_t, fsdp)
    qkv_sum = add_low(qkv_sum, swap(qkv_send, "fsdp", 0))
    for bit in fsdp_bits[1:]:
        qkv_sum = halve(qkv_sum, "fsdp", bit, 1)
    qkv_sum = qkv_sum[0]
    wide_sum = qkv_sum.astype(f32)
    for e in range(1, parts):
        wide_sum = wide_sum + ctx_shift(qkv_sum, groups, parts, 0, e).astype(f32)
    qkv_low = wide_sum.astype(bf16)
    flat = [part for parts_of in received for part in parts_of]
    qkv_low, *flat = together(qkv_low, *flat)
    received = [flat[j * heads : (j + 1) * heads] for j in range(groups)]
    by_group = jnp.zeros((groups,) + qkv_low.shape, bf16)
    for j in range(groups):
        piece = ctx_shift(qkv_low, groups, parts, -j, 0) if j else qkv_low
        by_group = lax.dynamic_update_slice(by_group, piece[None], ((g + j) % groups, 0, 0))
    natural = by_group.reshape(groups, shard + PAD, 3, span).transpose(1, 2, 0, 3)
    natural = natural.reshape(shard + PAD, 3 * model).astype(f32)
    grad_qkv_shard = natural[:shard]
    bias_line = natural[shard]
    grad_query_shift = lax.dynamic_slice(bias_line, (f * shard,), (shard,))
    grad_value_shift = lax.dynamic_slice(bias_line, (2 * model + f * shard,), (shard,))

    natural = jnp.zeros((3, groups, heads, HD, rows), bf16)
    for j in range(groups):
        part = jnp.stack(received[j], axis=1)[:, None]
        natural = lax.dynamic_update_slice(natural, part, (0, (g + j) % groups, 0, 0, 0))
    input_grad = d_resid1 + lax.dot_general(
        natural.reshape(3 * model, rows),
        qkv_full,
        (((0,), (1,)), ((), ())),
        preferred_element_type=f32,
    )

    ends = inner_shard + shard
    flat = lower[ends:].reshape(-1).astype(f32)
    offsets = lambda i: flat[i * shard : (i + 1) * shard]
    return (
        result[None],
        input_grad[None],
        grad_qkv_shard,
        grad_query_shift,
        grad_value_shift,
        lower[inner_shard:ends].astype(f32),
        offsets(0),
        offsets(1),
        offsets(2),
        upper.astype(f32),
        flat[6 * shard : 6 * shard + inner_shard],
        lower[:inner_shard].astype(f32),
        offsets(3),
        offsets(4),
        offsets(5),
    )


def solution(mesh):
    rows, one = P("fsdp", None), P("fsdp")
    whole = P("fsdp", "ctx", None)
    return jax.shard_map(
        body,
        mesh=mesh,
        in_specs=(
            whole, rows, rows, one, one, rows, one, one, one, rows, one, rows, one, one, one, whole,
        ),
        out_specs=(
            whole, whole, rows, one, one, rows, one, one, one, rows, one, rows, one, one, one,
        ),
        check_vma=False,
    )
```

```python
from functools import partial
import math

import jax
import jax.numpy as jnp
from jax import lax
from jax.experimental import pallas as pl
from jax.experimental.pallas import tpu as pltpu
from jax.sharding import PartitionSpec as P

H = 12
HD = 64
EPSILON = 1e-05
BIG = 2.0**100
LOG2E = 1.4426950408889634
PAD = 16
KERNEL_FLOPS = 3_000_000_000
KERNEL_BYTES = 20_000_000


def ctx_shift(array, groups, parts, dg, ds):
    pairs = []
    for g in range(groups):
        for s in range(parts):
            pairs.append((g * parts + s, ((g + dg) % groups) * parts + (s + ds) % parts))
    return lax.ppermute(array, "ctx", pairs)


def swap(array, axis, bit):
    size = lax.axis_size(axis)
    return lax.ppermute(array, axis, [(i, i ^ (1 << bit)) for i in range(size)])


def bits_of(axis):
    return lax.axis_size(axis).bit_length() - 1


def bit_at(axis, bit):
    return (lax.axis_index(axis) >> bit) & 1


def pick(array, which, dim):
    return lax.dynamic_index_in_dim(array, which, dim, keepdims=False)


def together(*values):
    return lax.optimization_barrier(values)


def join(mine, own, other, dim):
    return jnp.where(
        mine == 0,
        jnp.concatenate([own, other], axis=dim),
        jnp.concatenate([other, own], axis=dim),
    )


def gather_top(shard):
    return swap(shard, "fsdp", bits_of("fsdp") - 1)


def gather_rest(shard, other):
    top = bits_of("fsdp") - 1
    held = join(bit_at("fsdp", top), shard[None], other[None], 0)
    for bit in reversed(range(top)):
        got = swap(held, "fsdp", bit)
        pair = join(bit_at("fsdp", bit), held[:, None], got[:, None], 1)
        held = pair.reshape((-1,) + shard.shape)
    return held


def halve(held, axis, bit, dim):
    mine = bit_at(axis, bit)
    if axis == "fsdp":
        pairs = held.reshape((held.shape[0] // 2, 2) + held.shape[1:])
        keep, send = pick(pairs, mine, 1), pick(pairs, 1 - mine, 1)
    else:
        half = held.shape[dim] // 2
        keep = lax.dynamic_slice_in_dim(held, mine * half, half, dim)
        send = lax.dynamic_slice_in_dim(held, (1 - mine) * half, half, dim)
    return add_low(keep, swap(send, axis, bit))


def add_low(a, b):
    return (a.astype(jnp.float32) + b.astype(jnp.float32)).astype(jnp.bfloat16)


def exchange(held, axis, bit):
    return add_low(held, swap(held, axis, bit))


def double(held, axis, bit, dim):
    return join(bit_at(axis, bit), held, swap(held, axis, bit), dim)


def doc_row(meta, base, length, docs):
    pos = base + lax.broadcasted_iota(jnp.int32, (1, length), 1)
    doc = jnp.full((1, length), -1, jnp.int32)
    for j in range(docs):
        doc = doc + (pos >= meta[2 + j]).astype(jnp.int32)
    return doc


def dot(a, b):
    return jnp.dot(a, b, preferred_element_type=jnp.float32)


def dot_t(a, b):
    return lax.dot_general(a, b, (((1,), (1,)), ((), ())), preferred_element_type=jnp.float32)


def fill_keys(meta, own, others, groups, parts, docs, rows, store):
    g, s = meta[0], meta[1]
    for j in range(groups):
        for e in range(parts):
            block = lax.rem(g - j + groups, groups) * parts + lax.rem(s - e + parts, parts)
            if e == 0:
                key_t, value_t = own[j][1, 0], own[j][2, 0]
            else:
                ref = others[(e - 1) * groups + j]
                key_t, value_t = ref[0, 0], ref[1, 0]
            doc = doc_row(meta, block * rows, rows, docs)
            hot = (lax.broadcasted_iota(jnp.int32, (HD, rows), 0) == doc).astype(jnp.float32)
            keys = jnp.concatenate([key_t, hot.astype(jnp.bfloat16)], axis=0)
            store(block, keys, key_t, value_t)


def query_full(meta, query_t, j, groups, parts, docs, rows):
    g, s = meta[0], meta[1]
    block = lax.rem(g - j + groups, groups) * parts + s
    doc = doc_row(meta, block * rows, rows, docs)
    shut = jnp.where(lax.broadcasted_iota(jnp.int32, (HD, rows), 0) == doc, 0.0, -BIG)
    return jnp.concatenate([query_t, shut.astype(jnp.bfloat16)], axis=0)


def attend_kernel(groups, parts, docs, rows, meta, *refs):
    own = refs[:groups]
    others = refs[groups : groups * parts]
    low_ref, wide_ref, log_ref, queries_ref, keys_ref, values_ref = refs[groups * parts :]
    coeff = LOG2E * HD**-0.5

    def store(block, keys, key_t, value_t):
        keys_ref[block] = keys.T
        values_ref[block] = value_t

    fill_keys(meta, own, others, groups, parts, docs, rows, store)
    for j in range(groups):
        queries_ref[j] = query_full(meta, own[j][0, 0], j, groups, parts, docs, rows)

    def one_slot(j, carry):
        full = queries_ref[j]

        def step(t, state):
            best, total, accum = state
            scores = dot(keys_ref[t], full)
            new_best = jnp.maximum(best, jnp.max(scores, axis=0, keepdims=True))
            weights = jnp.exp2((scores - new_best) * coeff)
            shrink = jnp.exp2((best - new_best) * coeff)
            total = total * shrink + jnp.sum(weights, axis=0, keepdims=True)
            accum = accum * shrink + dot(values_ref[t], weights.astype(jnp.bfloat16))
            return new_best, total, accum

        best, total, accum = lax.fori_loop(
            meta[2 + docs + 2 * j],
            meta[3 + docs + 2 * j],
            step,
            (
                jnp.full((1, rows), -BIG, jnp.float32),
                jnp.zeros((1, rows), jnp.float32),
                jnp.zeros((HD, rows), jnp.float32),
            ),
        )
        attended = accum / total
        at = pl.ds(pl.multiple_of(j * rows, rows), rows)
        wide_ref[0, :, at] = attended
        low_ref[0, :, at] = attended.astype(jnp.bfloat16)
        log_ref[0, :, at] = best * coeff + jnp.log2(total)
        return carry

    lax.fori_loop(0, groups, one_slot, 0)


def attend_back_kernel(groups, parts, docs, rows, meta, *refs):
    own = refs[:groups]
    others = refs[groups : groups * parts]
    grads = refs[groups * parts : groups * parts + groups]
    rest = refs[groups * parts + groups :]
    wide_ref, log_ref = rest[:2]
    dq_ref, mine_ref = rest[2:4]
    theirs = rest[4] if parts > 1 else None
    queries_ref, grads_ref, keys_ref, keys_t_ref, values_ref, accum_ref = rest[-6:]
    coeff = LOG2E * HD**-0.5

    def store(block, keys, key_t, value_t):
        keys_ref[block] = keys.T
        keys_t_ref[block] = key_t
        values_ref[block] = value_t.T

    fill_keys(meta, own, others, groups, parts, docs, rows, store)
    accum_ref[...] = jnp.zeros_like(accum_ref)
    for j in range(groups):
        queries_ref[j] = query_full(meta, own[j][0, 0], j, groups, parts, docs, rows)
        grads_ref[j] = grads[j][0]

    def one_slot(j, carry):
        at = pl.ds(pl.multiple_of(j * rows, rows), rows)
        full = queries_ref[j]
        grad_t = grads_ref[j]
        delta = jnp.sum(grad_t.astype(jnp.float32) * wide_ref[0, :, at], axis=0, keepdims=True)
        log_total = log_ref[0, :, at]
        blank = jnp.zeros((HD, rows), jnp.bfloat16)
        both = jnp.concatenate(
            [
                jnp.concatenate([full[:HD], blank], axis=1),
                jnp.concatenate([blank, grad_t], axis=1),
            ],
            axis=0,
        )

        def step(t, grad_query):
            scores = dot(keys_ref[t], full)
            probs = jnp.exp2(scores * coeff - log_total)
            d_probs = dot(values_ref[t], grad_t)
            d_scores = (probs * (d_probs - delta)).astype(jnp.bfloat16)
            joined = jnp.concatenate([d_scores, probs.astype(jnp.bfloat16)], axis=1)
            accum_ref[t] += dot_t(joined, both)
            return grad_query + dot(keys_t_ref[t], d_scores)

        grad_query = lax.fori_loop(
            meta[2 + docs + 2 * j],
            meta[3 + docs + 2 * j],
            step,
            jnp.zeros((HD, rows), jnp.float32),
        )
        dq_ref[:, at] = (grad_query * HD**-0.5).astype(jnp.bfloat16)
        return carry

    lax.fori_loop(0, groups, one_slot, 0)
    g, s = meta[0], meta[1]
    for j in range(groups):
        for e in range(parts):
            block = lax.rem(g - j + groups, groups) * parts + lax.rem(s - e + parts, parts)
            terms = accum_ref[block].T
            at = slice(j * rows, (j + 1) * rows)
            d_key = terms[:HD] * HD**-0.5
            d_value = terms[HD:]
            if e == 0:
                mine_ref[0, :, at] = d_key
                mine_ref[1, :, at] = d_value
            else:
                theirs[e - 1, 0, :, at] = d_key.astype(jnp.bfloat16)
                theirs[e - 1, 1, :, at] = d_value.astype(jnp.bfloat16)


def head_block(head, *shape):
    dims = tuple(1 if n is None else n for n in shape)
    where = shape.index(None)

    def at(h, meta):
        chosen = h if head is None else head
        return tuple(chosen if i == where else 0 for i in range(len(dims)))

    return pl.BlockSpec(dims, at)


def attend(meta, own, others, groups, parts, docs, rows, heads):
    tiles = groups * parts
    tokens = groups * rows
    block = partial(head_block, None)
    grid_spec = pltpu.PrefetchScalarGridSpec(
        num_scalar_prefetch=1,
        grid=(heads,),
        in_specs=[block(3, None, HD, rows)] * groups
        + [block(2, None, HD, rows)] * (groups * (parts - 1)),
        out_specs=[block(None, HD, tokens), block(None, HD, tokens), block(None, 1, tokens)],
        scratch_shapes=[
            pltpu.VMEM((groups, 2 * HD, rows), jnp.bfloat16),
            pltpu.VMEM((tiles, rows, 2 * HD), jnp.bfloat16),
            pltpu.VMEM((tiles, HD, rows), jnp.bfloat16),
        ],
    )
    return pl.pallas_call(
        partial(attend_kernel, groups, parts, docs, rows),
        grid_spec=grid_spec,
        out_shape=[
            jax.ShapeDtypeStruct((heads, HD, tokens), jnp.bfloat16),
            jax.ShapeDtypeStruct((heads, HD, tokens), jnp.float32),
            jax.ShapeDtypeStruct((heads, 1, tokens), jnp.float32),
        ],
        cost_estimate=pl.CostEstimate(
            flops=KERNEL_FLOPS * 2 * heads,
            transcendentals=0,
            bytes_accessed=KERNEL_BYTES * heads,
        ),
        name="attend",
    )(meta, *own, *others)


def attend_back(head, meta, own, others, grads, wide, log_total, groups, parts, docs, rows):
    tiles = groups * parts
    tokens = groups * rows
    block = partial(head_block, head)
    plain = lambda *dims: pl.BlockSpec(dims, lambda h, meta: (0,) * len(dims))
    out_specs = [plain(HD, tokens), plain(2, HD, tokens)]
    out_shape = [
        jax.ShapeDtypeStruct((HD, tokens), jnp.bfloat16),
        jax.ShapeDtypeStruct((2, HD, tokens), jnp.float32),
    ]
    if parts > 1:
        out_specs.append(plain(parts - 1, 2, HD, tokens))
        out_shape.append(jax.ShapeDtypeStruct((parts - 1, 2, HD, tokens), jnp.bfloat16))
    grid_spec = pltpu.PrefetchScalarGridSpec(
        num_scalar_prefetch=1,
        grid=(1,),
        in_specs=[block(3, None, HD, rows)] * groups
        + [block(2, None, HD, rows)] * (groups * (parts - 1))
        + [block(None, HD, rows)] * groups
        + [block(None, HD, tokens), block(None, 1, tokens)],
        out_specs=out_specs,
        scratch_shapes=[
            pltpu.VMEM((groups, 2 * HD, rows), jnp.bfloat16),
            pltpu.VMEM((groups, HD, rows), jnp.bfloat16),
            pltpu.VMEM((tiles, rows, 2 * HD), jnp.bfloat16),
            pltpu.VMEM((tiles, HD, rows), jnp.bfloat16),
            pltpu.VMEM((tiles, rows, HD), jnp.bfloat16),
            pltpu.VMEM((tiles, rows, 2 * HD), jnp.float32),
        ],
    )
    return pl.pallas_call(
        partial(attend_back_kernel, groups, parts, docs, rows),
        grid_spec=grid_spec,
        out_shape=out_shape,
        cost_estimate=pl.CostEstimate(
            flops=KERNEL_FLOPS * 5, transcendentals=0, bytes_accessed=KERNEL_BYTES
        ),
        name="attend_back",
    )(meta, *own, *others, *grads, wide, log_total)


ERFC = (
    -1.26551223, 1.00002368, 0.37409196, 0.09678418, -0.18628806,
    0.27886807, -1.13520398, 1.48851587, -0.82215223, 0.17087277,
)


def normal_terms(v):
    z = jnp.abs(v) * (0.5**0.5)
    t = 1.0 / (1.0 + 0.5 * z)
    poly = jnp.full_like(t, ERFC[-1])
    for term in reversed(ERFC[:-1]):
        poly = poly * t + term
    square = z * z
    tail = 0.5 * t * jnp.exp(poly - square)
    below = jnp.where(v < 0, tail, 1.0 - tail)
    return below, jnp.exp(-square) * (2.0 * math.pi) ** -0.5


def normed(resid):
    centred = resid - jnp.mean(resid, axis=-1, keepdims=True)
    spread = jnp.mean(centred * centred, axis=-1, keepdims=True)
    scale = lax.rsqrt(spread + EPSILON)
    return centred * scale, scale


def norm_back(grad, gain, unit, scale):
    e = grad * gain
    inner = jnp.mean(e * unit, axis=-1, keepdims=True)
    return (e - jnp.mean(e, axis=-1, keepdims=True) - unit * inner) * scale


def over_blocks(count, aligned, step, value):
    if aligned:
        return lax.fori_loop(0, count, step, value)
    for i in range(count):
        value = step(i, value)
    return value


def feed_kernel(
    tokens_ref,
    attended_ref,
    cot_ref,
    out_ref,
    in_ref,
    back_ref,
    vec_ref,
    in_bias_ref,
    result_ref,
    d_resid1_ref,
    d_attended_ref,
    hidden_ref,
    act_ref,
    d_ffn_ref,
    d_pre_ref,
    d_branch_ref,
    sums_ref,
    in_sums_ref,
    slope_ref,
):
    f32, bf16 = jnp.float32, jnp.bfloat16
    out_shift, gain_one, shift_one = vec_ref[2:3], vec_ref[3:4], vec_ref[4:5]
    back_shift, gain_two, shift_two = vec_ref[5:6], vec_ref[6:7], vec_ref[7:8]

    @pl.when(pl.program_id(0) == 0)
    def _():
        sums_ref[...] = jnp.zeros_like(sums_ref)
        in_sums_ref[...] = jnp.zeros_like(in_sums_ref)

    total = lambda a: jnp.sum(a, axis=0, keepdims=True)
    branch = dot(attended_ref[...].T, out_ref[...]) + out_shift
    unit1, scale1 = normed(tokens_ref[...].astype(f32) + branch)
    hidden = unit1 * gain_one + shift_one
    hidden_low = hidden.astype(bf16)
    count, unused, shard = hidden_ref.shape
    for i in range(count):
        hidden_ref[i] = hidden_low[:, i * shard : (i + 1) * shard]
    resid2 = hidden + back_shift
    blocks, unused, size = act_ref.shape
    aligned = size % 128 == 0
    columns = lambda i: pl.ds(pl.multiple_of(i * size, size) if aligned else i * size, size)

    def forward(i, resid2):
        cols = columns(i)
        pre = dot(hidden_low, in_ref[:, cols]) + in_bias_ref[:, cols]
        below, density = normal_terms(pre)
        act = (pre * below).astype(bf16)
        act_ref[i] = act
        slope_ref[i] = below + pre * density
        return resid2 + dot(act, back_ref[cols, :])

    resid2 = over_blocks(blocks, aligned, forward, hidden + back_shift)
    unit2, scale2 = normed(resid2)
    result_ref[...] = (unit2 * gain_two + shift_two).astype(bf16)
    cot = cot_ref[...].astype(f32)
    d_resid2 = norm_back(cot, gain_two, unit2, scale2)
    d_ffn = d_resid2.astype(bf16)
    d_ffn_ref[...] = d_ffn

    def backward(i, d_hidden):
        cols = columns(i)
        d_act = dot_t(d_ffn, back_ref[cols, :])
        d_pre = (d_act * slope_ref[i]).astype(bf16)
        d_pre_ref[:, cols] = d_pre
        in_sums_ref[:, cols] += total(d_pre.astype(f32))
        return d_hidden + dot_t(d_pre, in_ref[:, cols])

    d_hidden = over_blocks(blocks, aligned, backward, d_resid2)
    d_resid1 = norm_back(d_hidden, gain_one, unit1, scale1)
    d_resid1_ref[...] = d_resid1
    d_branch = d_resid1.astype(bf16)
    d_branch_ref[...] = d_branch
    d_attended_ref[...] = dot_t(out_ref[...], d_branch).astype(bf16)
    sums_ref[...] += jnp.concatenate(
        [
            total(d_branch.astype(f32)),
            total(d_hidden * unit1),
            total(d_hidden),
            total(d_ffn.astype(f32)),
            total(cot * unit2),
            total(cot),
            jnp.zeros((2, cot.shape[1]), f32),
        ],
        axis=0,
    )


def feed_forward(fsdp, tokens, attended_t, cotangent, out_full, in_full, back_full, vectors, in_shift):
    f32, bf16 = jnp.float32, jnp.bfloat16
    rows, model = tokens.shape
    inner = in_full.shape[1]
    tile = math.gcd(rows, 256)
    by_rows = lambda n: pl.BlockSpec((tile, n), lambda i: (i, 0))
    by_cols = lambda n: pl.BlockSpec((n, tile), lambda i: (0, i))
    blocks = lambda n: pl.BlockSpec((fsdp, tile, n // fsdp), lambda i: (0, i, 0))
    fixed = lambda m, n: pl.BlockSpec((m, n), lambda i: (0, 0))
    shape = jax.ShapeDtypeStruct
    return pl.pallas_call(
        feed_kernel,
        grid=(rows // tile,),
        in_specs=[
            by_rows(model), by_cols(model), by_rows(model), fixed(model, model),
            fixed(model, inner), fixed(inner, model), fixed(8, model), fixed(1, inner),
        ],
        out_specs=[
            by_rows(model), by_rows(model), by_cols(model), blocks(model), blocks(inner),
            by_rows(model), by_rows(inner), by_rows(model), fixed(8, model), fixed(1, inner),
        ],
        out_shape=[
            shape((rows, model), bf16), shape((rows, model), f32), shape((model, rows), bf16),
            shape((fsdp, rows, model // fsdp), bf16), shape((fsdp, rows, inner // fsdp), bf16),
            shape((rows, model), bf16),
            shape((rows, inner), bf16), shape((rows, model), bf16), shape((8, model), f32),
            shape((1, inner), f32),
        ],
        scratch_shapes=[pltpu.VMEM((fsdp, tile, inner // fsdp), f32)],
        cost_estimate=pl.CostEstimate(
            flops=rows * model * (8 * inner + 4 * model), transcendentals=0, bytes_accessed=30_000_000
        ),
        name="feed_forward",
    )(tokens, attended_t, cotangent, out_full, in_full, back_full, vectors, in_shift)


def weight_grad_kernel(which, *refs):
    ins, (d_ffn, d_pre, d_branch), outs = refs[:8], refs[8:11], refs[11:]
    bf16 = jnp.bfloat16
    for side in range(2):
        act, hidden, attended_t, line = ins[4 * side : 4 * side + 4]
        lower, upper = outs[2 * side : 2 * side + 2]
        first, second = act.shape[2], attended_t.shape[0]
        lower[0, :first] = dot(act[0].T, d_ffn[...]).astype(bf16)
        lower[0, first : first + second] = dot(attended_t[...], d_branch[...]).astype(bf16)
        lower[0, first + second :] = line[0].astype(bf16)
        upper[0] = dot(hidden[0].T, d_pre[...]).astype(bf16)


def weight_grads(which, act, hidden, attended_t, line, d_ffn, d_pre, d_branch):
    fsdp, rows, inner_shard = act.shape
    shard = hidden.shape[2]
    model, inner = d_ffn.shape[1], d_pre.shape[1]
    line_rows = line.shape[1]
    tall = inner_shard + shard + line_rows
    half = fsdp // 2
    in_specs = []
    for side in range(2):
        block = lambda i, w, side=side: 2 * i + w[side]
        in_specs += [
            pl.BlockSpec((1, rows, inner_shard), lambda i, w, b=block: (b(i, w), 0, 0)),
            pl.BlockSpec((1, rows, shard), lambda i, w, b=block: (b(i, w), 0, 0)),
            pl.BlockSpec((shard, rows), lambda i, w, b=block: (b(i, w), 0)),
            pl.BlockSpec((1, line_rows, model), lambda i, w, b=block: (b(i, w), 0, 0)),
        ]
    in_specs += [pl.BlockSpec((rows, n), lambda i, w: (0, 0)) for n in (model, inner, model)]
    out = [(tall, model), (shard, inner)] * 2
    return pl.pallas_call(
        weight_grad_kernel,
        grid_spec=pltpu.PrefetchScalarGridSpec(
            num_scalar_prefetch=1,
            grid=(half,),
            in_specs=in_specs,
            out_specs=[pl.BlockSpec((1,) + o, lambda i, w: (i, 0, 0)) for o in out],
        ),
        out_shape=[jax.ShapeDtypeStruct((half,) + o, jnp.bfloat16) for o in out],
        cost_estimate=pl.CostEstimate(
            flops=2 * rows * model * (2 * inner + model), transcendentals=0, bytes_accessed=25_000_000
        ),
        name="weight_grads",
    )(which, act, hidden, attended_t, line, act, hidden, attended_t, line, d_ffn, d_pre, d_branch)


def qkv_grad_kernel(fsdp, which, *refs):
    slots, (d_qkv, send, keep, total) = refs[:-4], refs[-4:]
    rows = slots[0].shape[0]
    shard = send.shape[1] - PAD
    value = None
    for j, slot in enumerate(slots):
        term = dot_t(slot[...].T, d_qkv[:, j * rows : (j + 1) * rows])
        value = term if value is None else value + term
    total[...] = value
    ones = jnp.ones((PAD, d_qkv.shape[1]), jnp.bfloat16)
    sums = dot_t(ones, d_qkv[...]).astype(jnp.bfloat16)
    for side, ref in enumerate((send, keep)):
        for i in range(fsdp // 2):
            at = pl.multiple_of((2 * i + which[side]) * shard, math.gcd(shard, 64))
            ref[i, :shard] = total[pl.ds(at, shard), :].astype(jnp.bfloat16)
            ref[i, shard:] = sums


def qkv_grads(which, slots, d_qkv_t, fsdp):
    rows, model = slots[0].shape
    width = d_qkv_t.shape[0]
    out = (fsdp // 2, model // fsdp + PAD, width)
    fixed = lambda dims: pl.BlockSpec(dims, lambda i, w: (0,) * len(dims))
    return pl.pallas_call(
        partial(qkv_grad_kernel, fsdp),
        grid_spec=pltpu.PrefetchScalarGridSpec(
            num_scalar_prefetch=1,
            grid=(1,),
            in_specs=[fixed((rows, model))] * len(slots) + [fixed(d_qkv_t.shape)],
            out_specs=[fixed(out)] * 2,
            scratch_shapes=[pltpu.VMEM((model, width), jnp.float32)],
        ),
        out_shape=[jax.ShapeDtypeStruct(out, jnp.bfloat16)] * 2,
        cost_estimate=pl.CostEstimate(
            flops=2 * rows * len(slots) * model * width, transcendentals=0, bytes_accessed=8_000_000
        ),
        name="qkv_grads",
    )(which, *slots, d_qkv_t)


def body(
    inputs,
    doc_starts,
    qkv_weight,
    query_bias,
    value_bias,
    out_weight,
    out_bias,
    norm1_gain,
    norm1_bias,
    in_weight,
    in_bias,
    back_weight,
    back_bias,
    norm2_gain,
    norm2_bias,
    cotangent,
):
    bf16, f32 = jnp.bfloat16, jnp.float32
    tokens = inputs[0]
    rows, model = tokens.shape
    starts = doc_starts[0]
    docs = starts.shape[0]
    ctx = lax.axis_size("ctx")
    fsdp = lax.axis_size("fsdp")
    groups = math.gcd(H, ctx)
    parts = ctx // groups
    heads = H // groups
    span = heads * HD
    width = 3 * span
    index = lax.axis_index("ctx")
    g, s = index // parts, index % parts
    f = lax.axis_index("fsdp")
    shard = model // fsdp

    slots = [tokens] + [ctx_shift(tokens, groups, parts, d, 0) for d in range(1, groups)]

    own_cols = pick(qkv_weight.reshape(shard, 3, groups, span), g, 2).reshape(shard, width)
    small = jnp.concatenate(
        [
            query_bias, value_bias, out_bias, norm1_gain, norm1_bias,
            back_bias, norm2_gain, norm2_bias, in_bias,
        ]
    )
    count = small.shape[0]
    extra = -(-count // (width * PAD)) * PAD
    small_block = jnp.pad(small, (0, extra * width - count)).reshape(extra, width)
    first = jnp.concatenate([own_cols, small_block], axis=0)
    first_top = gather_top(first)
    first_top, out_held, in_held, back_held = together(
        first_top, out_weight, in_weight, back_weight
    )
    out_top, in_top, back_top = gather_top(out_held), gather_top(in_held), gather_top(back_held)
    first = gather_rest(first, first_top)
    own_weight = first[:, :shard].reshape(model, width)
    flat = first[:, shard:].reshape(fsdp, extra * width)[:, :count].astype(f32)
    vectors = flat[:, : 8 * shard].reshape(fsdp, 8, shard).transpose(1, 0, 2).reshape(8, model)
    query_shift, value_shift = vectors[0], vectors[1]
    in_shift = flat[:, 8 * shard :].reshape(1, -1)

    zero = jnp.zeros((span,), f32)
    own_shift = jnp.concatenate(
        [
            lax.dynamic_slice(query_shift, (g * span,), (span,)),
            zero,
            lax.dynamic_slice(value_shift, (g * span,), (span,)),
        ]
    )
    own, others = [], []
    for slot in slots:
        projected = lax.dot_general(
            own_weight, slot, (((0,), (1,)), ((), ())), preferred_element_type=f32
        )
        low = (projected + own_shift[:, None]).astype(bf16).reshape(3, heads, HD, rows)
        own.append(low)
    for e in range(1, parts):
        for low in own:
            others.append(ctx_shift(low[1:], groups, parts, 0, e))
    if parts > 1:
        in_top, others[0] = together(in_top, others[0])

    bounds = jnp.concatenate([starts, jnp.full((1,), ctx * rows, jnp.int32)])
    base = ((g - jnp.arange(groups, dtype=jnp.int32) + groups) % groups) * parts + s
    heads_at = base * rows
    tails_at = heads_at + rows - 1
    low_edge = jnp.max(jnp.where(starts[None] <= heads_at[:, None], starts[None], 0), axis=1)
    high_edge = jnp.min(
        jnp.where(bounds[None] > tails_at[:, None], bounds[None], ctx * rows), axis=1
    )
    ranges = jnp.stack([low_edge // rows, (high_edge + rows - 1) // rows], axis=1).reshape(-1)
    meta = jnp.concatenate([jnp.stack([g, s]).astype(jnp.int32), starts, ranges.astype(jnp.int32)])

    out_full = gather_rest(out_weight, out_top).reshape(model, model)
    in_full = gather_rest(in_weight, in_top).reshape(model, -1)
    meta, out_full, in_full = together(meta, out_full, in_full)
    low, wide, log_total = attend(meta, own, others, groups, parts, docs, rows, heads)
    attended_t = jnp.zeros((groups * span, rows), bf16)
    turned = []
    for j in range(groups):
        piece = low[:, :, j * rows : (j + 1) * rows]
        turned.append(ctx_shift(piece, groups, parts, -j, 0) if j else piece)
    for j, piece in enumerate(together(*turned)):
        attended_t = lax.dynamic_update_slice(
            attended_t, piece.reshape(span, rows), (((g + j) % groups) * span, 0)
        )
    back_full = gather_rest(back_weight, back_top).reshape(-1, model)

    (
        result, d_resid1, d_attended_t, hidden_low, act_low, d_ffn_low, d_pre_low, d_branch_low,
        sums, in_sums,
    ) = feed_forward(
        fsdp, tokens, attended_t, cotangent[0], out_full, in_full, back_full, vectors, in_shift
    )
    grads = []
    for j in range(groups):
        part = lax.dynamic_slice(d_attended_t, (((g + j) % groups) * span, 0), (span, rows))
        part = part.reshape(heads, HD, rows)
        grads.append(ctx_shift(part, groups, parts, j, 0) if j else part)

    inner = in_full.shape[1]
    inner_shard = in_bias.shape[0]
    line = jnp.concatenate(
        [sums[:6].reshape(6, fsdp, shard).transpose(1, 0, 2).reshape(fsdp, -1), in_sums.reshape(fsdp, -1)],
        axis=1,
    )
    line_rows = -(inner_shard + shard) % 64 or 64
    line = jnp.pad(line, ((0, 0), (0, line_rows * model - line.shape[1])))
    line = line.reshape(fsdp, line_rows, model)
    mine = bit_at("fsdp", 0)
    which = jnp.stack([1 - mine, mine]).astype(jnp.int32)
    lower_send, upper_send, lower, upper = weight_grads(
        which, act_low, hidden_low, attended_t, line, d_ffn_low, d_pre_low, d_branch_low
    )
    lower = add_low(lower, swap(lower_send, "fsdp", 0))
    upper = add_low(upper, swap(upper_send, "fsdp", 0))
    fsdp_bits, ctx_bits = range(bits_of("fsdp")), range(bits_of("ctx"))
    chunks = inner // (2 * model)

    def pair_step(i, state):
        lower, upper = state
        lower_steps = [("fsdp", b) for b in fsdp_bits[1:]] + [("ctx", 0)]
        upper_steps = [("ctx", 0)] + [("fsdp", b) for b in fsdp_bits[1:]]
        return halve(lower, *lower_steps[i], 1), halve(upper, *upper_steps[i], 2)

    def merge(state):
        lower, upper = state
        return (
            jnp.concatenate(
                [lower[0]] + [upper[0, :, c * model : (c + 1) * model] for c in range(chunks)], axis=0
            ),
        )

    steps = [partial(pair_step, i) for i in range(len(fsdp_bits))]
    last = steps.pop()
    steps.append(lambda state: merge(last(state)))
    for bit in ctx_bits[1:-1]:
        steps.append(lambda state, bit=bit: (halve(state[0], "ctx", bit, 0),))
    state = (lower, upper)

    pieces = []
    held, theirs = None, None

    def settle(dq, dkv, theirs):
        for other in theirs:
            dkv = dkv + other.astype(f32)
        pieces.append(jnp.concatenate([dq[None], dkv.astype(bf16)], axis=0))

    def send(piece):
        parts_of = []
        for j in range(groups):
            part = piece[..., j * rows : (j + 1) * rows]
            parts_of.append(ctx_shift(part, groups, parts, -j, 0) if j else part)
        return parts_of

    for head in range(heads):
        if head and steps:
            state = steps.pop(0)(state)
        meta, *state = together(meta, *state)
        dq, dkv, *rest = attend_back(
            head, meta, own, others, grads, wide, log_total, groups, parts, docs, rows
        )
        if head:
            dq, *theirs = together(dq, *theirs)
            settle(*held, theirs)
        if head == 1:
            early = send(pieces[0])
            dq, qkv_held = together(dq, qkv_weight)
            qkv_top = gather_top(qkv_held)
        elif head == 2:
            if steps:
                state = steps.pop(0)(state)
            count = len(early)
            dq, qkv_top, *landed = together(dq, qkv_top, *early, *state)
            early, state = landed[:count], landed[count:]
        held = (dq, dkv)
        theirs = [ctx_shift(rest[0][e - 1], groups, parts, 0, -e) for e in range(1, parts)]
    settle(*held, theirs)
    for advance in steps:
        state = advance(state)
    merged = exchange(state[0], "ctx", ctx_bits[-1])
    late, merged = together(jnp.stack(pieces[1:], axis=1), merged)
    late = send(late)
    for bit in reversed(ctx_bits[1:-1]):
        merged = double(merged, "ctx", bit, 0)
    other = swap(merged, "ctx", 0)
    d_qkv_t = jnp.stack(pieces, axis=1).reshape(width, groups * rows)
    qkv_send, qkv_sum = qkv_grads(which, slots, d_qkv_t, fsdp)
    qkv_sum = add_low(qkv_sum, swap(qkv_send, "fsdp", 0))
    for bit in fsdp_bits[1:]:
        qkv_sum = halve(qkv_sum, "fsdp", bit, 1)
    qkv_sum = qkv_sum[0]
    wide_sum = qkv_sum.astype(f32)
    for e in range(1, parts):
        wide_sum = wide_sum + ctx_shift(qkv_sum, groups, parts, 0, e).astype(f32)
    qkv_low = wide_sum.astype(bf16)
    qkv_full = gather_rest(qkv_held, qkv_top).reshape(model, 3 * model)
    by_group = jnp.zeros((groups,) + qkv_low.shape, bf16)
    turns = [ctx_shift(qkv_low, groups, parts, -j, 0) if j else qkv_low for j in range(groups)]
    other, *landed = together(other, *turns, *late)
    turns, late = landed[:groups], landed[groups:]
    for j, piece in enumerate(turns):
        by_group = lax.dynamic_update_slice(by_group, piece[None], ((g + j) % groups, 0, 0))
    natural = by_group.reshape(groups, shard + PAD, 3, span).transpose(1, 2, 0, 3)
    natural = natural.reshape(shard + PAD, 3 * model).astype(f32)
    grad_qkv_shard = natural[:shard]
    bias_line = natural[shard]
    grad_query_shift = lax.dynamic_slice(bias_line, (f * shard,), (shard,))
    grad_value_shift = lax.dynamic_slice(bias_line, (2 * model + f * shard,), (shard,))

    natural = jnp.zeros((3, groups, heads, HD, rows), bf16)
    for j in range(groups):
        part = jnp.concatenate([early[j][:, None], late[j]], axis=1)[:, None]
        natural = lax.dynamic_update_slice(natural, part, (0, (g + j) % groups, 0, 0, 0))
    input_grad = d_resid1 + lax.dot_general(
        natural.reshape(3 * model, rows),
        qkv_full,
        (((0,), (1,)), ((), ())),
        preferred_element_type=f32,
    )

    lower_rows = (inner_shard + shard + line_rows) // 2
    lower = join(bit_at("ctx", 0), merged[:lower_rows], other[:lower_rows], 0)
    wide_half = lambda m: jnp.concatenate(
        [m[lower_rows + c * shard : lower_rows + (c + 1) * shard] for c in range(chunks)], axis=1
    )
    upper = join(bit_at("ctx", 0), wide_half(merged), wide_half(other), 1)

    ends = inner_shard + shard
    flat = lower[ends:].reshape(-1).astype(f32)
    offsets = lambda i: flat[i * shard : (i + 1) * shard]
    return (
        result[None],
        input_grad[None],
        grad_qkv_shard,
        grad_query_shift,
        grad_value_shift,
        lower[inner_shard:ends].astype(f32),
        offsets(0),
        offsets(1),
        offsets(2),
        upper.astype(f32),
        flat[6 * shard : 6 * shard + inner_shard],
        lower[:inner_shard].astype(f32),
        offsets(3),
        offsets(4),
        offsets(5),
    )


def solution(mesh):
    rows, one = P("fsdp", None), P("fsdp")
    whole = P("fsdp", "ctx", None)
    return jax.shard_map(
        body,
        mesh=mesh,
        in_specs=(
            whole, rows, rows, one, one, rows, one, one, one, rows, one, rows, one, one, one, whole,
        ),
        out_specs=(
            whole, whole, rows, one, one, rows, one, one, one, rows, one, rows, one, one, one,
        ),
        check_vma=False,
    )
```

```python
from functools import partial
import math

import jax
import jax.numpy as jnp
from jax import lax
from jax.experimental import pallas as pl
from jax.experimental.pallas import tpu as pltpu
from jax.sharding import PartitionSpec as P

H = 12
HD = 64
EPSILON = 1e-05
BIG = 2.0**100
LOG2E = 1.4426950408889634
PAD = 16
KERNEL_FLOPS = 3_000_000_000
KERNEL_BYTES = 20_000_000


def ctx_shift(array, groups, parts, dg, ds):
    pairs = []
    for g in range(groups):
        for s in range(parts):
            pairs.append((g * parts + s, ((g + dg) % groups) * parts + (s + ds) % parts))
    return lax.ppermute(array, "ctx", pairs)


def swap(array, axis, bit):
    size = lax.axis_size(axis)
    return lax.ppermute(array, axis, [(i, i ^ (1 << bit)) for i in range(size)])


def bits_of(axis):
    return lax.axis_size(axis).bit_length() - 1


def bit_at(axis, bit):
    return (lax.axis_index(axis) >> bit) & 1


def pick(array, which, dim):
    return lax.dynamic_index_in_dim(array, which, dim, keepdims=False)


def together(*values):
    return lax.optimization_barrier(values)


def join(mine, own, other, dim):
    return jnp.where(
        mine == 0,
        jnp.concatenate([own, other], axis=dim),
        jnp.concatenate([other, own], axis=dim),
    )


def gather_top(shard):
    return swap(shard, "fsdp", bits_of("fsdp") - 1)


def gather_rest(shard, other):
    top = bits_of("fsdp") - 1
    held = join(bit_at("fsdp", top), shard[None], other[None], 0)
    for bit in reversed(range(top)):
        got = swap(held, "fsdp", bit)
        pair = join(bit_at("fsdp", bit), held[:, None], got[:, None], 1)
        held = pair.reshape((-1,) + shard.shape)
    return held


def halve(held, axis, bit, dim):
    mine = bit_at(axis, bit)
    if axis == "fsdp":
        pairs = held.reshape((held.shape[0] // 2, 2) + held.shape[1:])
        keep, send = pick(pairs, mine, 1), pick(pairs, 1 - mine, 1)
    else:
        half = held.shape[dim] // 2
        keep = lax.dynamic_slice_in_dim(held, mine * half, half, dim)
        send = lax.dynamic_slice_in_dim(held, (1 - mine) * half, half, dim)
    return add_low(keep, swap(send, axis, bit))


def add_low(a, b):
    return (a.astype(jnp.float32) + b.astype(jnp.float32)).astype(jnp.bfloat16)


def double(held, axis, bit, dim):
    return join(bit_at(axis, bit), held, swap(held, axis, bit), dim)


def doc_row(meta, base, length, docs):
    pos = base + lax.broadcasted_iota(jnp.int32, (1, length), 1)
    doc = jnp.full((1, length), -1, jnp.int32)
    for j in range(docs):
        doc = doc + (pos >= meta[2 + j]).astype(jnp.int32)
    return doc


def dot(a, b):
    return jnp.dot(a, b, preferred_element_type=jnp.float32)


def dot_t(a, b):
    return lax.dot_general(a, b, (((1,), (1,)), ((), ())), preferred_element_type=jnp.float32)


def fill_keys(meta, own, others, groups, parts, docs, rows, store):
    g, s = meta[0], meta[1]
    for j in range(groups):
        for e in range(parts):
            block = lax.rem(g - j + groups, groups) * parts + lax.rem(s - e + parts, parts)
            if e == 0:
                key_t, value_t = own[j][1, 0], own[j][2, 0]
            else:
                ref = others[(e - 1) * groups + j]
                key_t, value_t = ref[0, 0], ref[1, 0]
            doc = doc_row(meta, block * rows, rows, docs)
            hot = (lax.broadcasted_iota(jnp.int32, (HD, rows), 0) == doc).astype(jnp.float32)
            keys = jnp.concatenate([key_t, hot.astype(jnp.bfloat16)], axis=0)
            store(block, keys, key_t, value_t)


def query_full(meta, query_t, j, groups, parts, docs, rows):
    g, s = meta[0], meta[1]
    block = lax.rem(g - j + groups, groups) * parts + s
    doc = doc_row(meta, block * rows, rows, docs)
    shut = jnp.where(lax.broadcasted_iota(jnp.int32, (HD, rows), 0) == doc, 0.0, -BIG)
    return jnp.concatenate([query_t, shut.astype(jnp.bfloat16)], axis=0)


def attend_kernel(groups, parts, docs, rows, meta, *refs):
    own = refs[:groups]
    others = refs[groups : groups * parts]
    low_ref, wide_ref, log_ref, queries_ref, keys_ref, values_ref = refs[groups * parts :]
    coeff = LOG2E * HD**-0.5

    def store(block, keys, key_t, value_t):
        keys_ref[block] = keys.T
        values_ref[block] = value_t

    fill_keys(meta, own, others, groups, parts, docs, rows, store)
    for j in range(groups):
        queries_ref[j] = query_full(meta, own[j][0, 0], j, groups, parts, docs, rows)

    def one_slot(j, carry):
        full = queries_ref[j]

        def step(t, state):
            best, total, accum = state
            scores = dot(keys_ref[t], full)
            new_best = jnp.maximum(best, jnp.max(scores, axis=0, keepdims=True))
            weights = jnp.exp2((scores - new_best) * coeff)
            shrink = jnp.exp2((best - new_best) * coeff)
            total = total * shrink + jnp.sum(weights, axis=0, keepdims=True)
            accum = accum * shrink + dot(values_ref[t], weights.astype(jnp.bfloat16))
            return new_best, total, accum

        best, total, accum = lax.fori_loop(
            meta[2 + docs + 2 * j],
            meta[3 + docs + 2 * j],
            step,
            (
                jnp.full((1, rows), -BIG, jnp.float32),
                jnp.zeros((1, rows), jnp.float32),
                jnp.zeros((HD, rows), jnp.float32),
            ),
        )
        attended = accum / total
        at = pl.ds(pl.multiple_of(j * rows, rows), rows)
        wide_ref[0, :, at] = attended
        low_ref[0, :, at] = attended.astype(jnp.bfloat16)
        log_ref[0, :, at] = best * coeff + jnp.log2(total)
        return carry

    lax.fori_loop(0, groups, one_slot, 0)


def attend_back_kernel(groups, parts, docs, rows, meta, *refs):
    own = refs[:groups]
    others = refs[groups : groups * parts]
    grads = refs[groups * parts : groups * parts + groups]
    rest = refs[groups * parts + groups :]
    wide_ref, log_ref = rest[:2]
    dq_ref, mine_ref = rest[2:4]
    theirs = rest[4] if parts > 1 else None
    queries_ref, grads_ref, keys_ref, keys_t_ref, values_ref, accum_ref = rest[-6:]
    coeff = LOG2E * HD**-0.5

    def store(block, keys, key_t, value_t):
        keys_ref[block] = keys.T
        keys_t_ref[block] = key_t
        values_ref[block] = value_t.T

    fill_keys(meta, own, others, groups, parts, docs, rows, store)
    accum_ref[...] = jnp.zeros_like(accum_ref)
    for j in range(groups):
        queries_ref[j] = query_full(meta, own[j][0, 0], j, groups, parts, docs, rows)
        grads_ref[j] = grads[j][0]

    def one_slot(j, carry):
        at = pl.ds(pl.multiple_of(j * rows, rows), rows)
        full = queries_ref[j]
        grad_t = grads_ref[j]
        delta = jnp.sum(grad_t.astype(jnp.float32) * wide_ref[0, :, at], axis=0, keepdims=True)
        log_total = log_ref[0, :, at]
        blank = jnp.zeros((HD, rows), jnp.bfloat16)
        both = jnp.concatenate(
            [
                jnp.concatenate([full[:HD], blank], axis=1),
                jnp.concatenate([blank, grad_t], axis=1),
            ],
            axis=0,
        )

        def step(t, grad_query):
            scores = dot(keys_ref[t], full)
            probs = jnp.exp2(scores * coeff - log_total)
            d_probs = dot(values_ref[t], grad_t)
            d_scores = (probs * (d_probs - delta)).astype(jnp.bfloat16)
            joined = jnp.concatenate([d_scores, probs.astype(jnp.bfloat16)], axis=1)
            accum_ref[t] += dot_t(joined, both)
            return grad_query + dot(keys_t_ref[t], d_scores)

        grad_query = lax.fori_loop(
            meta[2 + docs + 2 * j],
            meta[3 + docs + 2 * j],
            step,
            jnp.zeros((HD, rows), jnp.float32),
        )
        dq_ref[:, at] = (grad_query * HD**-0.5).astype(jnp.bfloat16)
        return carry

    lax.fori_loop(0, groups, one_slot, 0)
    g, s = meta[0], meta[1]
    for j in range(groups):
        for e in range(parts):
            block = lax.rem(g - j + groups, groups) * parts + lax.rem(s - e + parts, parts)
            terms = accum_ref[block].T
            at = slice(j * rows, (j + 1) * rows)
            d_key = terms[:HD] * HD**-0.5
            d_value = terms[HD:]
            if e == 0:
                mine_ref[0, :, at] = d_key
                mine_ref[1, :, at] = d_value
            else:
                theirs[e - 1, 0, :, at] = d_key.astype(jnp.bfloat16)
                theirs[e - 1, 1, :, at] = d_value.astype(jnp.bfloat16)


def head_block(head, *shape):
    dims = tuple(1 if n is None else n for n in shape)
    where = shape.index(None)

    def at(h, meta):
        chosen = h if head is None else head
        return tuple(chosen if i == where else 0 for i in range(len(dims)))

    return pl.BlockSpec(dims, at)


def attend(meta, own, others, groups, parts, docs, rows, heads):
    tiles = groups * parts
    tokens = groups * rows
    block = partial(head_block, None)
    grid_spec = pltpu.PrefetchScalarGridSpec(
        num_scalar_prefetch=1,
        grid=(heads,),
        in_specs=[block(3, None, HD, rows)] * groups
        + [block(2, None, HD, rows)] * (groups * (parts - 1)),
        out_specs=[block(None, HD, tokens), block(None, HD, tokens), block(None, 1, tokens)],
        scratch_shapes=[
            pltpu.VMEM((groups, 2 * HD, rows), jnp.bfloat16),
            pltpu.VMEM((tiles, rows, 2 * HD), jnp.bfloat16),
            pltpu.VMEM((tiles, HD, rows), jnp.bfloat16),
        ],
    )
    return pl.pallas_call(
        partial(attend_kernel, groups, parts, docs, rows),
        grid_spec=grid_spec,
        out_shape=[
            jax.ShapeDtypeStruct((heads, HD, tokens), jnp.bfloat16),
            jax.ShapeDtypeStruct((heads, HD, tokens), jnp.float32),
            jax.ShapeDtypeStruct((heads, 1, tokens), jnp.float32),
        ],
        cost_estimate=pl.CostEstimate(
            flops=KERNEL_FLOPS * 2 * heads,
            transcendentals=0,
            bytes_accessed=KERNEL_BYTES * heads,
        ),
        name="attend",
    )(meta, *own, *others)


def attend_back(head, meta, own, others, grads, wide, log_total, groups, parts, docs, rows):
    tiles = groups * parts
    tokens = groups * rows
    block = partial(head_block, head)
    plain = lambda *dims: pl.BlockSpec(dims, lambda h, meta: (0,) * len(dims))
    out_specs = [plain(HD, tokens), plain(2, HD, tokens)]
    out_shape = [
        jax.ShapeDtypeStruct((HD, tokens), jnp.bfloat16),
        jax.ShapeDtypeStruct((2, HD, tokens), jnp.float32),
    ]
    if parts > 1:
        out_specs.append(plain(parts - 1, 2, HD, tokens))
        out_shape.append(jax.ShapeDtypeStruct((parts - 1, 2, HD, tokens), jnp.bfloat16))
    grid_spec = pltpu.PrefetchScalarGridSpec(
        num_scalar_prefetch=1,
        grid=(1,),
        in_specs=[block(3, None, HD, rows)] * groups
        + [block(2, None, HD, rows)] * (groups * (parts - 1))
        + [block(None, HD, rows)] * groups
        + [block(None, HD, tokens), block(None, 1, tokens)],
        out_specs=out_specs,
        scratch_shapes=[
            pltpu.VMEM((groups, 2 * HD, rows), jnp.bfloat16),
            pltpu.VMEM((groups, HD, rows), jnp.bfloat16),
            pltpu.VMEM((tiles, rows, 2 * HD), jnp.bfloat16),
            pltpu.VMEM((tiles, HD, rows), jnp.bfloat16),
            pltpu.VMEM((tiles, rows, HD), jnp.bfloat16),
            pltpu.VMEM((tiles, rows, 2 * HD), jnp.float32),
        ],
    )
    return pl.pallas_call(
        partial(attend_back_kernel, groups, parts, docs, rows),
        grid_spec=grid_spec,
        out_shape=out_shape,
        cost_estimate=pl.CostEstimate(
            flops=KERNEL_FLOPS * 5, transcendentals=0, bytes_accessed=KERNEL_BYTES
        ),
        name="attend_back",
    )(meta, *own, *others, *grads, wide, log_total)


ERFC = (
    -1.26551223, 1.00002368, 0.37409196, 0.09678418, -0.18628806,
    0.27886807, -1.13520398, 1.48851587, -0.82215223, 0.17087277,
)


def normal_terms(v):
    z = jnp.abs(v) * (0.5**0.5)
    t = 1.0 / (1.0 + 0.5 * z)
    poly = jnp.full_like(t, ERFC[-1])
    for term in reversed(ERFC[:-1]):
        poly = poly * t + term
    square = z * z
    tail = 0.5 * t * jnp.exp(poly - square)
    below = jnp.where(v < 0, tail, 1.0 - tail)
    return below, jnp.exp(-square) * (2.0 * math.pi) ** -0.5


def normed(resid):
    centred = resid - jnp.mean(resid, axis=-1, keepdims=True)
    spread = jnp.mean(centred * centred, axis=-1, keepdims=True)
    scale = lax.rsqrt(spread + EPSILON)
    return centred * scale, scale


def norm_back(grad, gain, unit, scale):
    e = grad * gain
    inner = jnp.mean(e * unit, axis=-1, keepdims=True)
    return (e - jnp.mean(e, axis=-1, keepdims=True) - unit * inner) * scale


def over_blocks(count, aligned, step, value):
    if aligned:
        return lax.fori_loop(0, count, step, value)
    for i in range(count):
        value = step(i, value)
    return value


def feed_kernel(
    tokens_ref,
    attended_ref,
    cot_ref,
    out_ref,
    in_ref,
    back_ref,
    vec_ref,
    in_bias_ref,
    result_ref,
    d_resid1_ref,
    d_attended_ref,
    hidden_ref,
    act_ref,
    d_ffn_ref,
    d_pre_ref,
    d_branch_ref,
    sums_ref,
    in_sums_ref,
    slope_ref,
):
    f32, bf16 = jnp.float32, jnp.bfloat16
    out_shift, gain_one, shift_one = vec_ref[2:3], vec_ref[3:4], vec_ref[4:5]
    back_shift, gain_two, shift_two = vec_ref[5:6], vec_ref[6:7], vec_ref[7:8]

    @pl.when(pl.program_id(0) == 0)
    def _():
        sums_ref[...] = jnp.zeros_like(sums_ref)
        in_sums_ref[...] = jnp.zeros_like(in_sums_ref)

    total = lambda a: jnp.sum(a, axis=0, keepdims=True)
    branch = dot(attended_ref[...].T, out_ref[...]) + out_shift
    unit1, scale1 = normed(tokens_ref[...].astype(f32) + branch)
    hidden = unit1 * gain_one + shift_one
    hidden_low = hidden.astype(bf16)
    count, unused, shard = hidden_ref.shape
    for i in range(count):
        hidden_ref[i] = hidden_low[:, i * shard : (i + 1) * shard]
    resid2 = hidden + back_shift
    blocks, unused, size = act_ref.shape
    aligned = size % 128 == 0
    columns = lambda i: pl.ds(pl.multiple_of(i * size, size) if aligned else i * size, size)

    def forward(i, resid2):
        cols = columns(i)
        pre = dot(hidden_low, in_ref[:, cols]) + in_bias_ref[:, cols]
        below, density = normal_terms(pre)
        act = (pre * below).astype(bf16)
        act_ref[i] = act
        slope_ref[i] = below + pre * density
        return resid2 + dot(act, back_ref[cols, :])

    resid2 = over_blocks(blocks, aligned, forward, hidden + back_shift)
    unit2, scale2 = normed(resid2)
    result_ref[...] = (unit2 * gain_two + shift_two).astype(bf16)
    cot = cot_ref[...].astype(f32)
    d_resid2 = norm_back(cot, gain_two, unit2, scale2)
    d_ffn = d_resid2.astype(bf16)
    d_ffn_ref[...] = d_ffn

    def backward(i, d_hidden):
        cols = columns(i)
        d_act = dot_t(d_ffn, back_ref[cols, :])
        d_pre = (d_act * slope_ref[i]).astype(bf16)
        d_pre_ref[:, cols] = d_pre
        in_sums_ref[:, cols] += total(d_pre.astype(f32))
        return d_hidden + dot_t(d_pre, in_ref[:, cols])

    d_hidden = over_blocks(blocks, aligned, backward, d_resid2)
    d_resid1 = norm_back(d_hidden, gain_one, unit1, scale1)
    d_resid1_ref[...] = d_resid1
    d_branch = d_resid1.astype(bf16)
    d_branch_ref[...] = d_branch
    d_attended_ref[...] = dot_t(out_ref[...], d_branch).astype(bf16)
    sums_ref[...] += jnp.concatenate(
        [
            total(d_branch.astype(f32)),
            total(d_hidden * unit1),
            total(d_hidden),
            total(d_ffn.astype(f32)),
            total(cot * unit2),
            total(cot),
            jnp.zeros((2, cot.shape[1]), f32),
        ],
        axis=0,
    )


def feed_forward(fsdp, tokens, attended_t, cotangent, out_full, in_full, back_full, vectors, in_shift):
    f32, bf16 = jnp.float32, jnp.bfloat16
    rows, model = tokens.shape
    inner = in_full.shape[1]
    tile = math.gcd(rows, 256)
    by_rows = lambda n: pl.BlockSpec((tile, n), lambda i: (i, 0))
    by_cols = lambda n: pl.BlockSpec((n, tile), lambda i: (0, i))
    blocks = lambda n: pl.BlockSpec((fsdp, tile, n // fsdp), lambda i: (0, i, 0))
    fixed = lambda m, n: pl.BlockSpec((m, n), lambda i: (0, 0))
    shape = jax.ShapeDtypeStruct
    return pl.pallas_call(
        feed_kernel,
        grid=(rows // tile,),
        in_specs=[
            by_rows(model), by_cols(model), by_rows(model), fixed(model, model),
            fixed(model, inner), fixed(inner, model), fixed(8, model), fixed(1, inner),
        ],
        out_specs=[
            by_rows(model), by_rows(model), by_cols(model), blocks(model), blocks(inner),
            by_rows(model), by_rows(inner), by_rows(model), fixed(8, model), fixed(1, inner),
        ],
        out_shape=[
            shape((rows, model), bf16), shape((rows, model), f32), shape((model, rows), bf16),
            shape((fsdp, rows, model // fsdp), bf16), shape((fsdp, rows, inner // fsdp), bf16),
            shape((rows, model), bf16),
            shape((rows, inner), bf16), shape((rows, model), bf16), shape((8, model), f32),
            shape((1, inner), f32),
        ],
        scratch_shapes=[pltpu.VMEM((fsdp, tile, inner // fsdp), f32)],
        cost_estimate=pl.CostEstimate(
            flops=rows * model * (8 * inner + 4 * model), transcendentals=0, bytes_accessed=30_000_000
        ),
        name="feed_forward",
    )(tokens, attended_t, cotangent, out_full, in_full, back_full, vectors, in_shift)


def weight_grad_kernel(which, *refs):
    ins, (d_ffn, d_pre, d_branch), outs = refs[:8], refs[8:11], refs[11:]
    bf16 = jnp.bfloat16
    for side in range(2):
        act, hidden, attended_t, line = ins[4 * side : 4 * side + 4]
        lower, upper = outs[2 * side : 2 * side + 2]
        first, second = act.shape[2], attended_t.shape[0]
        lower[0, :first] = dot(act[0].T, d_ffn[...]).astype(bf16)
        lower[0, first : first + second] = dot(attended_t[...], d_branch[...]).astype(bf16)
        lower[0, first + second :] = line[0].astype(bf16)
        upper[0] = dot(hidden[0].T, d_pre[...]).astype(bf16)


def weight_grads(which, act, hidden, attended_t, line, d_ffn, d_pre, d_branch):
    fsdp, rows, inner_shard = act.shape
    shard = hidden.shape[2]
    model, inner = d_ffn.shape[1], d_pre.shape[1]
    line_rows = line.shape[1]
    tall = inner_shard + shard + line_rows
    half = fsdp // 2
    in_specs = []
    for side in range(2):
        block = lambda i, w, side=side: 2 * i + w[side]
        in_specs += [
            pl.BlockSpec((1, rows, inner_shard), lambda i, w, b=block: (b(i, w), 0, 0)),
            pl.BlockSpec((1, rows, shard), lambda i, w, b=block: (b(i, w), 0, 0)),
            pl.BlockSpec((shard, rows), lambda i, w, b=block: (b(i, w), 0)),
            pl.BlockSpec((1, line_rows, model), lambda i, w, b=block: (b(i, w), 0, 0)),
        ]
    in_specs += [pl.BlockSpec((rows, n), lambda i, w: (0, 0)) for n in (model, inner, model)]
    out = [(tall, model), (shard, inner)] * 2
    return pl.pallas_call(
        weight_grad_kernel,
        grid_spec=pltpu.PrefetchScalarGridSpec(
            num_scalar_prefetch=1,
            grid=(half,),
            in_specs=in_specs,
            out_specs=[pl.BlockSpec((1,) + o, lambda i, w: (i, 0, 0)) for o in out],
        ),
        out_shape=[jax.ShapeDtypeStruct((half,) + o, jnp.bfloat16) for o in out],
        cost_estimate=pl.CostEstimate(
            flops=2 * rows * model * (2 * inner + model), transcendentals=0, bytes_accessed=25_000_000
        ),
        name="weight_grads",
    )(which, act, hidden, attended_t, line, act, hidden, attended_t, line, d_ffn, d_pre, d_branch)


def qkv_grad_kernel(fsdp, which, *refs):
    slots, (d_qkv, send, keep, total) = refs[:-4], refs[-4:]
    rows = slots[0].shape[0]
    shard = send.shape[1] - PAD
    value = None
    for j, slot in enumerate(slots):
        term = dot_t(slot[...].T, d_qkv[:, j * rows : (j + 1) * rows])
        value = term if value is None else value + term
    total[...] = value
    ones = jnp.ones((PAD, d_qkv.shape[1]), jnp.bfloat16)
    sums = dot_t(ones, d_qkv[...]).astype(jnp.bfloat16)
    for side, ref in enumerate((send, keep)):
        for i in range(fsdp // 2):
            at = pl.multiple_of((2 * i + which[side]) * shard, math.gcd(shard, 64))
            ref[i, :shard] = total[pl.ds(at, shard), :].astype(jnp.bfloat16)
            ref[i, shard:] = sums


def qkv_grads(which, slots, d_qkv_t, fsdp):
    rows, model = slots[0].shape
    width = d_qkv_t.shape[0]
    out = (fsdp // 2, model // fsdp + PAD, width)
    fixed = lambda dims: pl.BlockSpec(dims, lambda i, w: (0,) * len(dims))
    return pl.pallas_call(
        partial(qkv_grad_kernel, fsdp),
        grid_spec=pltpu.PrefetchScalarGridSpec(
            num_scalar_prefetch=1,
            grid=(1,),
            in_specs=[fixed((rows, model))] * len(slots) + [fixed(d_qkv_t.shape)],
            out_specs=[fixed(out)] * 2,
            scratch_shapes=[pltpu.VMEM((model, width), jnp.float32)],
        ),
        out_shape=[jax.ShapeDtypeStruct(out, jnp.bfloat16)] * 2,
        cost_estimate=pl.CostEstimate(
            flops=2 * rows * len(slots) * model * width, transcendentals=0, bytes_accessed=8_000_000
        ),
        name="qkv_grads",
    )(which, *slots, d_qkv_t)


def body(
    inputs,
    doc_starts,
    qkv_weight,
    query_bias,
    value_bias,
    out_weight,
    out_bias,
    norm1_gain,
    norm1_bias,
    in_weight,
    in_bias,
    back_weight,
    back_bias,
    norm2_gain,
    norm2_bias,
    cotangent,
):
    bf16, f32 = jnp.bfloat16, jnp.float32
    tokens = inputs[0]
    rows, model = tokens.shape
    starts = doc_starts[0]
    docs = starts.shape[0]
    ctx = lax.axis_size("ctx")
    fsdp = lax.axis_size("fsdp")
    groups = math.gcd(H, ctx)
    parts = ctx // groups
    heads = H // groups
    span = heads * HD
    width = 3 * span
    index = lax.axis_index("ctx")
    g, s = index // parts, index % parts
    f = lax.axis_index("fsdp")
    shard = model // fsdp

    slots = [tokens] + [ctx_shift(tokens, groups, parts, d, 0) for d in range(1, groups)]

    own_cols = pick(qkv_weight.reshape(shard, 3, groups, span), g, 2).reshape(shard, width)
    small = jnp.concatenate(
        [
            query_bias, value_bias, out_bias, norm1_gain, norm1_bias,
            back_bias, norm2_gain, norm2_bias, in_bias,
        ]
    )
    count = small.shape[0]
    extra = -(-count // (width * PAD)) * PAD
    small_block = jnp.pad(small, (0, extra * width - count)).reshape(extra, width)
    first = jnp.concatenate([own_cols, small_block], axis=0)
    first_top = gather_top(first)
    first_top, out_held, in_held, back_held = together(
        first_top, out_weight, in_weight, back_weight
    )
    out_top, in_top, back_top = gather_top(out_held), gather_top(in_held), gather_top(back_held)
    first = gather_rest(first, first_top)
    own_weight = first[:, :shard].reshape(model, width)
    flat = first[:, shard:].reshape(fsdp, extra * width)[:, :count].astype(f32)
    vectors = flat[:, : 8 * shard].reshape(fsdp, 8, shard).transpose(1, 0, 2).reshape(8, model)
    query_shift, value_shift = vectors[0], vectors[1]
    in_shift = flat[:, 8 * shard :].reshape(1, -1)

    zero = jnp.zeros((span,), f32)
    own_shift = jnp.concatenate(
        [
            lax.dynamic_slice(query_shift, (g * span,), (span,)),
            zero,
            lax.dynamic_slice(value_shift, (g * span,), (span,)),
        ]
    )
    own, others = [], []
    for slot in slots:
        projected = lax.dot_general(
            own_weight, slot, (((0,), (1,)), ((), ())), preferred_element_type=f32
        )
        low = (projected + own_shift[:, None]).astype(bf16).reshape(3, heads, HD, rows)
        own.append(low)
    for e in range(1, parts):
        for low in own:
            others.append(ctx_shift(low[1:], groups, parts, 0, e))
    if parts > 1:
        in_top, others[0] = together(in_top, others[0])

    bounds = jnp.concatenate([starts, jnp.full((1,), ctx * rows, jnp.int32)])
    base = ((g - jnp.arange(groups, dtype=jnp.int32) + groups) % groups) * parts + s
    heads_at = base * rows
    tails_at = heads_at + rows - 1
    low_edge = jnp.max(jnp.where(starts[None] <= heads_at[:, None], starts[None], 0), axis=1)
    high_edge = jnp.min(
        jnp.where(bounds[None] > tails_at[:, None], bounds[None], ctx * rows), axis=1
    )
    ranges = jnp.stack([low_edge // rows, (high_edge + rows - 1) // rows], axis=1).reshape(-1)
    meta = jnp.concatenate([jnp.stack([g, s]).astype(jnp.int32), starts, ranges.astype(jnp.int32)])

    out_full = gather_rest(out_weight, out_top).reshape(model, model)
    in_full = gather_rest(in_weight, in_top).reshape(model, -1)
    meta, out_full, in_full = together(meta, out_full, in_full)
    low, wide, log_total = attend(meta, own, others, groups, parts, docs, rows, heads)
    attended_t = jnp.zeros((groups * span, rows), bf16)
    turned = []
    for j in range(groups):
        piece = low[:, :, j * rows : (j + 1) * rows]
        turned.append(ctx_shift(piece, groups, parts, -j, 0) if j else piece)
    for j, piece in enumerate(together(*turned)):
        attended_t = lax.dynamic_update_slice(
            attended_t, piece.reshape(span, rows), (((g + j) % groups) * span, 0)
        )
    back_full = gather_rest(back_weight, back_top).reshape(-1, model)

    (
        result, d_resid1, d_attended_t, hidden_low, act_low, d_ffn_low, d_pre_low, d_branch_low,
        sums, in_sums,
    ) = feed_forward(
        fsdp, tokens, attended_t, cotangent[0], out_full, in_full, back_full, vectors, in_shift
    )
    grads = []
    for j in range(groups):
        part = lax.dynamic_slice(d_attended_t, (((g + j) % groups) * span, 0), (span, rows))
        part = part.reshape(heads, HD, rows)
        grads.append(ctx_shift(part, groups, parts, j, 0) if j else part)

    inner = in_full.shape[1]
    inner_shard = in_bias.shape[0]
    line = jnp.concatenate(
        [sums[:6].reshape(6, fsdp, shard).transpose(1, 0, 2).reshape(fsdp, -1), in_sums.reshape(fsdp, -1)],
        axis=1,
    )
    line_rows = -(inner_shard + shard) % 64 or 64
    line = jnp.pad(line, ((0, 0), (0, line_rows * model - line.shape[1])))
    line = line.reshape(fsdp, line_rows, model)
    mine = bit_at("fsdp", 0)
    which = jnp.stack([1 - mine, mine]).astype(jnp.int32)
    lower_send, upper_send, lower, upper = weight_grads(
        which, act_low, hidden_low, attended_t, line, d_ffn_low, d_pre_low, d_branch_low
    )
    lower = add_low(lower, swap(lower_send, "fsdp", 0))
    upper = add_low(upper, swap(upper_send, "fsdp", 0))
    fsdp_bits, ctx_bits = range(bits_of("fsdp")), range(bits_of("ctx"))
    chunks = inner // (2 * model)

    def pair_step(i, state):
        lower, upper = state
        lower_steps = [("fsdp", b) for b in fsdp_bits[1:]] + [("ctx", 0)]
        upper_steps = [("ctx", 0)] + [("fsdp", b) for b in fsdp_bits[1:]]
        return halve(lower, *lower_steps[i], 1), halve(upper, *upper_steps[i], 2)

    def merge(state):
        lower, upper = state
        return (
            jnp.concatenate(
                [lower[0]] + [upper[0, :, c * model : (c + 1) * model] for c in range(chunks)], axis=0
            ),
        )

    steps = [partial(pair_step, i) for i in range(len(fsdp_bits))]
    last = steps.pop()
    steps.append(lambda state: merge(last(state)))
    for bit in ctx_bits[1:-1]:
        steps.append(lambda state, bit=bit: (halve(state[0], "ctx", bit, 0),))
    state = (lower, upper)

    pieces = []
    held, theirs = None, None

    def settle(dq, dkv, theirs):
        for other in theirs:
            dkv = dkv + other.astype(f32)
        pieces.append(jnp.concatenate([dq[None], dkv.astype(bf16)], axis=0))

    def send(piece):
        parts_of = []
        for j in range(groups):
            part = piece[..., j * rows : (j + 1) * rows]
            parts_of.append(ctx_shift(part, groups, parts, -j, 0) if j else part)
        return parts_of

    for head in range(heads):
        meta, *state = together(meta, *state)
        flying = steps.pop(0)(state) if steps else state
        dq, dkv, *rest = attend_back(
            head, meta, own, others, grads, wide, log_total, groups, parts, docs, rows
        )
        if head:
            dq, dkv, *landed = together(dq, dkv, *rest, *flying)
            rest, state = landed[: len(rest)], landed[len(rest) :]
            dq, *theirs = together(dq, *theirs)
            settle(*held, theirs)
        else:
            state = flying
        if head == 1:
            early = send(pieces[0])
            dq, qkv_held = together(dq, qkv_weight)
            qkv_top = gather_top(qkv_held)
        elif head == 2:
            dq, qkv_top, *early = together(dq, qkv_top, *early)
        held = (dq, dkv)
        theirs = [ctx_shift(rest[0][e - 1], groups, parts, 0, -e) for e in range(1, parts)]
    settle(*held, theirs)
    for advance in steps:
        state = advance(state)
    other = swap(state[0], "ctx", ctx_bits[-1])
    other, *pieces = together(other, *pieces)
    merged = add_low(state[0], other)
    late, merged = together(jnp.stack(pieces[1:], axis=1), merged)
    for bit in reversed(ctx_bits[1:-1]):
        merged = double(merged, "ctx", bit, 0)

    d_qkv_t = jnp.stack(pieces, axis=1).reshape(width, groups * rows)
    qkv_send, qkv_sum = qkv_grads(which, slots, d_qkv_t, fsdp)
    qkv_sum = add_low(qkv_sum, swap(qkv_send, "fsdp", 0))
    wide_sum = qkv_sum.astype(f32)
    for e in range(1, parts):
        wide_sum = wide_sum + ctx_shift(qkv_sum, groups, parts, 0, e).astype(f32)
    qkv_sum, merged = together(wide_sum.astype(bf16), merged)
    other = swap(merged, "ctx", 0)
    late = send(late)
    for bit in fsdp_bits[1:]:
        qkv_sum = halve(qkv_sum, "fsdp", bit, 1)
    qkv_low = qkv_sum[0]
    qkv_full = gather_rest(qkv_held, qkv_top).reshape(model, 3 * model)
    by_group = jnp.zeros((groups,) + qkv_low.shape, bf16)
    turns = [ctx_shift(qkv_low, groups, parts, -j, 0) if j else qkv_low for j in range(groups)]
    other, *landed = together(other, *turns, *late)
    turns, late = landed[:groups], landed[groups:]
    for j, piece in enumerate(turns):
        by_group = lax.dynamic_update_slice(by_group, piece[None], ((g + j) % groups, 0, 0))
    natural = by_group.reshape(groups, shard + PAD, 3, span).transpose(1, 2, 0, 3)
    natural = natural.reshape(shard + PAD, 3 * model).astype(f32)
    grad_qkv_shard = natural[:shard]
    bias_line = natural[shard]
    grad_query_shift = lax.dynamic_slice(bias_line, (f * shard,), (shard,))
    grad_value_shift = lax.dynamic_slice(bias_line, (2 * model + f * shard,), (shard,))

    natural = jnp.zeros((3, groups, heads, HD, rows), bf16)
    for j in range(groups):
        part = jnp.concatenate([early[j][:, None], late[j]], axis=1)[:, None]
        natural = lax.dynamic_update_slice(natural, part, (0, (g + j) % groups, 0, 0, 0))
    input_grad = d_resid1 + lax.dot_general(
        natural.reshape(3 * model, rows),
        qkv_full,
        (((0,), (1,)), ((), ())),
        preferred_element_type=f32,
    )

    lower_rows = (inner_shard + shard + line_rows) // 2
    lower = join(bit_at("ctx", 0), merged[:lower_rows], other[:lower_rows], 0)
    wide_half = lambda m: jnp.concatenate(
        [m[lower_rows + c * shard : lower_rows + (c + 1) * shard] for c in range(chunks)], axis=1
    )
    upper = join(bit_at("ctx", 0), wide_half(merged), wide_half(other), 1)

    ends = inner_shard + shard
    flat = lower[ends:].reshape(-1).astype(f32)
    offsets = lambda i: flat[i * shard : (i + 1) * shard]
    return (
        result[None],
        input_grad[None],
        grad_qkv_shard,
        grad_query_shift,
        grad_value_shift,
        lower[inner_shard:ends].astype(f32),
        offsets(0),
        offsets(1),
        offsets(2),
        upper.astype(f32),
        flat[6 * shard : 6 * shard + inner_shard],
        lower[:inner_shard].astype(f32),
        offsets(3),
        offsets(4),
        offsets(5),
    )


def solution(mesh):
    rows, one = P("fsdp", None), P("fsdp")
    whole = P("fsdp", "ctx", None)
    return jax.shard_map(
        body,
        mesh=mesh,
        in_specs=(
            whole, rows, rows, one, one, rows, one, one, one, rows, one, rows, one, one, one, whole,
        ),
        out_specs=(
            whole, whole, rows, one, one, rows, one, one, one, rows, one, rows, one, one, one,
        ),
        check_vma=False,
    )
```

```python
from functools import partial
import math

import jax
import jax.numpy as jnp
from jax import lax
from jax.experimental import pallas as pl
from jax.experimental.pallas import tpu as pltpu
from jax.sharding import PartitionSpec as P

H = 12
HD = 64
EPSILON = 1e-05
BIG = 2.0**100
LOG2E = 1.4426950408889634
PAD = 16
KERNEL_FLOPS = 3_000_000_000
KERNEL_BYTES = 20_000_000


def ctx_swap(array, groups, parts, flip):
    pairs = []
    for g in range(groups):
        for s in range(parts):
            pairs.append((g * parts + s, (g ^ flip) * parts + s))
    return lax.ppermute(array, "ctx", pairs)


def part_shift(array, groups, parts, by):
    pairs = []
    for g in range(groups):
        for s in range(parts):
            pairs.append((g * parts + s, g * parts + (s + by) % parts))
    return lax.ppermute(array, "ctx", pairs)


def gather_groups(array, groups, parts):
    return [array] + [ctx_swap(array, groups, parts, i) for i in range(1, groups)]


def swap(array, axis, bit):
    size = lax.axis_size(axis)
    return lax.ppermute(array, axis, [(i, i ^ (1 << bit)) for i in range(size)])


def bits_of(axis):
    return lax.axis_size(axis).bit_length() - 1


def bit_at(axis, bit):
    return (lax.axis_index(axis) >> bit) & 1


def pick(array, which, dim):
    return lax.dynamic_index_in_dim(array, which, dim, keepdims=False)


def together(*values):
    return lax.optimization_barrier(values)


def join(mine, own, other, dim):
    return jnp.where(
        mine == 0,
        jnp.concatenate([own, other], axis=dim),
        jnp.concatenate([other, own], axis=dim),
    )


def gather_top(shard):
    return swap(shard, "fsdp", bits_of("fsdp") - 1)


def gather_rest(shard, other):
    top = bits_of("fsdp") - 1
    held = join(bit_at("fsdp", top), shard[None], other[None], 0)
    for bit in reversed(range(top)):
        got = swap(held, "fsdp", bit)
        pair = join(bit_at("fsdp", bit), held[:, None], got[:, None], 1)
        held = pair.reshape((-1,) + shard.shape)
    return held


def halve(held, axis, bit, dim):
    mine = bit_at(axis, bit)
    if axis == "fsdp":
        pairs = held.reshape((held.shape[0] // 2, 2) + held.shape[1:])
        keep, send = pick(pairs, mine, 1), pick(pairs, 1 - mine, 1)
    else:
        half = held.shape[dim] // 2
        keep = lax.dynamic_slice_in_dim(held, mine * half, half, dim)
        send = lax.dynamic_slice_in_dim(held, (1 - mine) * half, half, dim)
    return add_low(keep, swap(send, axis, bit))


def add_low(a, b):
    return (a.astype(jnp.float32) + b.astype(jnp.float32)).astype(jnp.bfloat16)


def double(held, axis, bit, dim):
    return join(bit_at(axis, bit), held, swap(held, axis, bit), dim)


def doc_row(meta, base, length, docs):
    pos = base + lax.broadcasted_iota(jnp.int32, (1, length), 1)
    doc = jnp.full((1, length), -1, jnp.int32)
    for j in range(docs):
        doc = doc + (pos >= meta[2 + j]).astype(jnp.int32)
    return doc


def dot(a, b):
    return jnp.dot(a, b, preferred_element_type=jnp.float32)


def dot_t(a, b):
    return lax.dot_general(a, b, (((1,), (1,)), ((), ())), preferred_element_type=jnp.float32)


def fill_keys(meta, own, others, groups, parts, docs, rows, store):
    g, s = meta[0], meta[1]
    for j in range(groups):
        for e in range(parts):
            block = (g ^ j) * parts + lax.rem(s - e + parts, parts)
            if e == 0:
                key_t, value_t = own[j][1, 0], own[j][2, 0]
            else:
                ref = others[(e - 1) * groups + j]
                key_t, value_t = ref[0, 0], ref[1, 0]
            doc = doc_row(meta, block * rows, rows, docs)
            hot = (lax.broadcasted_iota(jnp.int32, (HD, rows), 0) == doc).astype(jnp.float32)
            keys = jnp.concatenate([key_t, hot.astype(jnp.bfloat16)], axis=0)
            store(block, keys, key_t, value_t)


def query_full(meta, query_t, j, groups, parts, docs, rows):
    g, s = meta[0], meta[1]
    block = (g ^ j) * parts + s
    doc = doc_row(meta, block * rows, rows, docs)
    shut = jnp.where(lax.broadcasted_iota(jnp.int32, (HD, rows), 0) == doc, 0.0, -BIG)
    return jnp.concatenate([query_t, shut.astype(jnp.bfloat16)], axis=0)


def attend_kernel(groups, parts, docs, rows, meta, *refs):
    own = refs[:groups]
    others = refs[groups : groups * parts]
    low_ref, wide_ref, log_ref, queries_ref, keys_ref, values_ref = refs[groups * parts :]
    coeff = LOG2E * HD**-0.5

    def store(block, keys, key_t, value_t):
        keys_ref[block] = keys.T
        values_ref[block] = value_t

    fill_keys(meta, own, others, groups, parts, docs, rows, store)
    for j in range(groups):
        queries_ref[j] = query_full(meta, own[j][0, 0], j, groups, parts, docs, rows)

    def one_slot(j, carry):
        full = queries_ref[j]

        def step(t, state):
            best, total, accum = state
            scores = dot(keys_ref[t], full)
            new_best = jnp.maximum(best, jnp.max(scores, axis=0, keepdims=True))
            weights = jnp.exp2((scores - new_best) * coeff)
            shrink = jnp.exp2((best - new_best) * coeff)
            total = total * shrink + jnp.sum(weights, axis=0, keepdims=True)
            accum = accum * shrink + dot(values_ref[t], weights.astype(jnp.bfloat16))
            return new_best, total, accum

        best, total, accum = lax.fori_loop(
            meta[2 + docs + 2 * j],
            meta[3 + docs + 2 * j],
            step,
            (
                jnp.full((1, rows), -BIG, jnp.float32),
                jnp.zeros((1, rows), jnp.float32),
                jnp.zeros((HD, rows), jnp.float32),
            ),
        )
        attended = accum / total
        at = pl.ds(pl.multiple_of(j * rows, rows), rows)
        wide_ref[0, :, at] = attended
        low_ref[0, :, at] = attended.astype(jnp.bfloat16)
        log_ref[0, :, at] = best * coeff + jnp.log2(total)
        return carry

    lax.fori_loop(0, groups, one_slot, 0)


def attend_back_kernel(groups, parts, docs, rows, meta, *refs):
    own = refs[:groups]
    others = refs[groups : groups * parts]
    grads = refs[groups * parts : groups * parts + groups]
    rest = refs[groups * parts + groups :]
    wide_ref, log_ref = rest[:2]
    dq_ref, mine_ref = rest[2:4]
    theirs = rest[4] if parts > 1 else None
    queries_ref, grads_ref, keys_ref, keys_t_ref, values_ref, accum_ref = rest[-6:]
    coeff = LOG2E * HD**-0.5

    def store(block, keys, key_t, value_t):
        keys_ref[block] = keys.T
        keys_t_ref[block] = key_t
        values_ref[block] = value_t.T

    fill_keys(meta, own, others, groups, parts, docs, rows, store)
    accum_ref[...] = jnp.zeros_like(accum_ref)
    for j in range(groups):
        queries_ref[j] = query_full(meta, own[j][0, 0], j, groups, parts, docs, rows)
        grads_ref[j] = grads[j][0]

    def one_slot(j, carry):
        at = pl.ds(pl.multiple_of(j * rows, rows), rows)
        full = queries_ref[j]
        grad_t = grads_ref[j]
        delta = jnp.sum(grad_t.astype(jnp.float32) * wide_ref[0, :, at], axis=0, keepdims=True)
        log_total = log_ref[0, :, at]
        blank = jnp.zeros((HD, rows), jnp.bfloat16)
        both = jnp.concatenate(
            [
                jnp.concatenate([full[:HD], blank], axis=1),
                jnp.concatenate([blank, grad_t], axis=1),
            ],
            axis=0,
        )

        def step(t, grad_query):
            scores = dot(keys_ref[t], full)
            probs = jnp.exp2(scores * coeff - log_total)
            d_probs = dot(values_ref[t], grad_t)
            d_scores = (probs * (d_probs - delta)).astype(jnp.bfloat16)
            joined = jnp.concatenate([d_scores, probs.astype(jnp.bfloat16)], axis=1)
            accum_ref[t] += dot_t(joined, both)
            return grad_query + dot(keys_t_ref[t], d_scores)

        grad_query = lax.fori_loop(
            meta[2 + docs + 2 * j],
            meta[3 + docs + 2 * j],
            step,
            jnp.zeros((HD, rows), jnp.float32),
        )
        dq_ref[:, at] = (grad_query * HD**-0.5).astype(jnp.bfloat16)
        return carry

    lax.fori_loop(0, groups, one_slot, 0)
    g, s = meta[0], meta[1]
    for j in range(groups):
        for e in range(parts):
            block = (g ^ j) * parts + lax.rem(s - e + parts, parts)
            terms = accum_ref[block].T
            at = slice(j * rows, (j + 1) * rows)
            d_key = terms[:HD] * HD**-0.5
            d_value = terms[HD:]
            if e == 0:
                mine_ref[0, :, at] = d_key
                mine_ref[1, :, at] = d_value
            else:
                theirs[e - 1, 0, :, at] = d_key.astype(jnp.bfloat16)
                theirs[e - 1, 1, :, at] = d_value.astype(jnp.bfloat16)


def head_block(head, *shape):
    dims = tuple(1 if n is None else n for n in shape)
    where = shape.index(None)

    def at(h, meta):
        chosen = h if head is None else head
        return tuple(chosen if i == where else 0 for i in range(len(dims)))

    return pl.BlockSpec(dims, at)


def attend(meta, own, others, groups, parts, docs, rows, heads):
    tiles = groups * parts
    tokens = groups * rows
    block = partial(head_block, None)
    grid_spec = pltpu.PrefetchScalarGridSpec(
        num_scalar_prefetch=1,
        grid=(heads,),
        in_specs=[block(3, None, HD, rows)] * groups
        + [block(2, None, HD, rows)] * (groups * (parts - 1)),
        out_specs=[block(None, HD, tokens), block(None, HD, tokens), block(None, 1, tokens)],
        scratch_shapes=[
            pltpu.VMEM((groups, 2 * HD, rows), jnp.bfloat16),
            pltpu.VMEM((tiles, rows, 2 * HD), jnp.bfloat16),
            pltpu.VMEM((tiles, HD, rows), jnp.bfloat16),
        ],
    )
    return pl.pallas_call(
        partial(attend_kernel, groups, parts, docs, rows),
        grid_spec=grid_spec,
        out_shape=[
            jax.ShapeDtypeStruct((heads, HD, tokens), jnp.bfloat16),
            jax.ShapeDtypeStruct((heads, HD, tokens), jnp.float32),
            jax.ShapeDtypeStruct((heads, 1, tokens), jnp.float32),
        ],
        cost_estimate=pl.CostEstimate(
            flops=KERNEL_FLOPS * 2 * heads,
            transcendentals=0,
            bytes_accessed=KERNEL_BYTES * heads,
        ),
        name="attend",
    )(meta, *own, *others)


def attend_back(head, meta, own, others, grads, wide, log_total, groups, parts, docs, rows):
    tiles = groups * parts
    tokens = groups * rows
    block = partial(head_block, head)
    plain = lambda *dims: pl.BlockSpec(dims, lambda h, meta: (0,) * len(dims))
    out_specs = [plain(HD, tokens), plain(2, HD, tokens)]
    out_shape = [
        jax.ShapeDtypeStruct((HD, tokens), jnp.bfloat16),
        jax.ShapeDtypeStruct((2, HD, tokens), jnp.float32),
    ]
    if parts > 1:
        out_specs.append(plain(parts - 1, 2, HD, tokens))
        out_shape.append(jax.ShapeDtypeStruct((parts - 1, 2, HD, tokens), jnp.bfloat16))
    grid_spec = pltpu.PrefetchScalarGridSpec(
        num_scalar_prefetch=1,
        grid=(1,),
        in_specs=[block(3, None, HD, rows)] * groups
        + [block(2, None, HD, rows)] * (groups * (parts - 1))
        + [block(None, HD, rows)] * groups
        + [block(None, HD, tokens), block(None, 1, tokens)],
        out_specs=out_specs,
        scratch_shapes=[
            pltpu.VMEM((groups, 2 * HD, rows), jnp.bfloat16),
            pltpu.VMEM((groups, HD, rows), jnp.bfloat16),
            pltpu.VMEM((tiles, rows, 2 * HD), jnp.bfloat16),
            pltpu.VMEM((tiles, HD, rows), jnp.bfloat16),
            pltpu.VMEM((tiles, rows, HD), jnp.bfloat16),
            pltpu.VMEM((tiles, rows, 2 * HD), jnp.float32),
        ],
    )
    return pl.pallas_call(
        partial(attend_back_kernel, groups, parts, docs, rows),
        grid_spec=grid_spec,
        out_shape=out_shape,
        cost_estimate=pl.CostEstimate(
            flops=KERNEL_FLOPS * 5, transcendentals=0, bytes_accessed=KERNEL_BYTES
        ),
        name="attend_back",
    )(meta, *own, *others, *grads, wide, log_total)


ERFC = (
    -1.26551223, 1.00002368, 0.37409196, 0.09678418, -0.18628806,
    0.27886807, -1.13520398, 1.48851587, -0.82215223, 0.17087277,
)


def normal_terms(v):
    z = jnp.abs(v) * (0.5**0.5)
    t = 1.0 / (1.0 + 0.5 * z)
    poly = jnp.full_like(t, ERFC[-1])
    for term in reversed(ERFC[:-1]):
        poly = poly * t + term
    square = z * z
    tail = 0.5 * t * jnp.exp(poly - square)
    below = jnp.where(v < 0, tail, 1.0 - tail)
    return below, jnp.exp(-square) * (2.0 * math.pi) ** -0.5


def normed(resid):
    centred = resid - jnp.mean(resid, axis=-1, keepdims=True)
    spread = jnp.mean(centred * centred, axis=-1, keepdims=True)
    scale = lax.rsqrt(spread + EPSILON)
    return centred * scale, scale


def norm_back(grad, gain, unit, scale):
    e = grad * gain
    inner = jnp.mean(e * unit, axis=-1, keepdims=True)
    return (e - jnp.mean(e, axis=-1, keepdims=True) - unit * inner) * scale


def over_blocks(count, aligned, step, value):
    if aligned:
        return lax.fori_loop(0, count, step, value)
    for i in range(count):
        value = step(i, value)
    return value


def feed_kernel(
    tokens_ref,
    attended_ref,
    cot_ref,
    out_ref,
    in_ref,
    back_ref,
    vec_ref,
    in_bias_ref,
    result_ref,
    d_resid1_ref,
    d_attended_ref,
    hidden_ref,
    act_ref,
    d_ffn_ref,
    d_pre_ref,
    d_branch_ref,
    sums_ref,
    in_sums_ref,
    slope_ref,
):
    f32, bf16 = jnp.float32, jnp.bfloat16
    out_shift, gain_one, shift_one = vec_ref[2:3], vec_ref[3:4], vec_ref[4:5]
    back_shift, gain_two, shift_two = vec_ref[5:6], vec_ref[6:7], vec_ref[7:8]

    @pl.when(pl.program_id(0) == 0)
    def _():
        sums_ref[...] = jnp.zeros_like(sums_ref)
        in_sums_ref[...] = jnp.zeros_like(in_sums_ref)

    total = lambda a: jnp.sum(a, axis=0, keepdims=True)
    branch = dot(attended_ref[...].T, out_ref[...]) + out_shift
    unit1, scale1 = normed(tokens_ref[...].astype(f32) + branch)
    hidden = unit1 * gain_one + shift_one
    hidden_low = hidden.astype(bf16)
    count, unused, shard = hidden_ref.shape
    for i in range(count):
        hidden_ref[i] = hidden_low[:, i * shard : (i + 1) * shard]
    resid2 = hidden + back_shift
    blocks, unused, size = act_ref.shape
    aligned = size % 128 == 0
    columns = lambda i: pl.ds(pl.multiple_of(i * size, size) if aligned else i * size, size)

    def forward(i, resid2):
        cols = columns(i)
        pre = dot(hidden_low, in_ref[:, cols]) + in_bias_ref[:, cols]
        below, density = normal_terms(pre)
        act = (pre * below).astype(bf16)
        act_ref[i] = act
        slope_ref[i] = below + pre * density
        return resid2 + dot(act, back_ref[cols, :])

    resid2 = over_blocks(blocks, aligned, forward, hidden + back_shift)
    unit2, scale2 = normed(resid2)
    result_ref[...] = (unit2 * gain_two + shift_two).astype(bf16)
    cot = cot_ref[...].astype(f32)
    d_resid2 = norm_back(cot, gain_two, unit2, scale2)
    d_ffn = d_resid2.astype(bf16)
    d_ffn_ref[...] = d_ffn

    def backward(i, d_hidden):
        cols = columns(i)
        d_act = dot_t(d_ffn, back_ref[cols, :])
        d_pre = (d_act * slope_ref[i]).astype(bf16)
        d_pre_ref[:, cols] = d_pre
        in_sums_ref[:, cols] += total(d_pre.astype(f32))
        return d_hidden + dot_t(d_pre, in_ref[:, cols])

    d_hidden = over_blocks(blocks, aligned, backward, d_resid2)
    d_resid1 = norm_back(d_hidden, gain_one, unit1, scale1)
    d_resid1_ref[...] = d_resid1
    d_branch = d_resid1.astype(bf16)
    d_branch_ref[...] = d_branch
    d_attended_ref[...] = dot_t(out_ref[...], d_branch).astype(bf16)
    sums_ref[...] += jnp.concatenate(
        [
            total(d_branch.astype(f32)),
            total(d_hidden * unit1),
            total(d_hidden),
            total(d_ffn.astype(f32)),
            total(cot * unit2),
            total(cot),
            jnp.zeros((2, cot.shape[1]), f32),
        ],
        axis=0,
    )


def feed_forward(fsdp, tokens, attended_t, cotangent, out_full, in_full, back_full, vectors, in_shift):
    f32, bf16 = jnp.float32, jnp.bfloat16
    rows, model = tokens.shape
    inner = in_full.shape[1]
    tile = math.gcd(rows, 256)
    by_rows = lambda n: pl.BlockSpec((tile, n), lambda i: (i, 0))
    by_cols = lambda n: pl.BlockSpec((n, tile), lambda i: (0, i))
    blocks = lambda n: pl.BlockSpec((fsdp, tile, n // fsdp), lambda i: (0, i, 0))
    fixed = lambda m, n: pl.BlockSpec((m, n), lambda i: (0, 0))
    shape = jax.ShapeDtypeStruct
    return pl.pallas_call(
        feed_kernel,
        grid=(rows // tile,),
        in_specs=[
            by_rows(model), by_cols(model), by_rows(model), fixed(model, model),
            fixed(model, inner), fixed(inner, model), fixed(8, model), fixed(1, inner),
        ],
        out_specs=[
            by_rows(model), by_rows(model), by_cols(model), blocks(model), blocks(inner),
            by_rows(model), by_rows(inner), by_rows(model), fixed(8, model), fixed(1, inner),
        ],
        out_shape=[
            shape((rows, model), bf16), shape((rows, model), f32), shape((model, rows), bf16),
            shape((fsdp, rows, model // fsdp), bf16), shape((fsdp, rows, inner // fsdp), bf16),
            shape((rows, model), bf16),
            shape((rows, inner), bf16), shape((rows, model), bf16), shape((8, model), f32),
            shape((1, inner), f32),
        ],
        scratch_shapes=[pltpu.VMEM((fsdp, tile, inner // fsdp), f32)],
        cost_estimate=pl.CostEstimate(
            flops=rows * model * (8 * inner + 4 * model), transcendentals=0, bytes_accessed=30_000_000
        ),
        name="feed_forward",
    )(tokens, attended_t, cotangent, out_full, in_full, back_full, vectors, in_shift)


def weight_grad_kernel(which, *refs):
    ins, (d_ffn, d_pre, d_branch), outs = refs[:8], refs[8:11], refs[11:]
    bf16 = jnp.bfloat16
    for side in range(2):
        act, hidden, attended_t, line = ins[4 * side : 4 * side + 4]
        lower, upper = outs[2 * side : 2 * side + 2]
        first, second = act.shape[2], attended_t.shape[0]
        lower[0, :first] = dot(act[0].T, d_ffn[...]).astype(bf16)
        lower[0, first : first + second] = dot(attended_t[...], d_branch[...]).astype(bf16)
        lower[0, first + second :] = line[0].astype(bf16)
        upper[0] = dot(hidden[0].T, d_pre[...]).astype(bf16)


def weight_grads(which, act, hidden, attended_t, line, d_ffn, d_pre, d_branch):
    fsdp, rows, inner_shard = act.shape
    shard = hidden.shape[2]
    model, inner = d_ffn.shape[1], d_pre.shape[1]
    line_rows = line.shape[1]
    tall = inner_shard + shard + line_rows
    half = fsdp // 2
    in_specs = []
    for side in range(2):
        block = lambda i, w, side=side: 2 * i + w[side]
        in_specs += [
            pl.BlockSpec((1, rows, inner_shard), lambda i, w, b=block: (b(i, w), 0, 0)),
            pl.BlockSpec((1, rows, shard), lambda i, w, b=block: (b(i, w), 0, 0)),
            pl.BlockSpec((shard, rows), lambda i, w, b=block: (b(i, w), 0)),
            pl.BlockSpec((1, line_rows, model), lambda i, w, b=block: (b(i, w), 0, 0)),
        ]
    in_specs += [pl.BlockSpec((rows, n), lambda i, w: (0, 0)) for n in (model, inner, model)]
    out = [(tall, model), (shard, inner)] * 2
    return pl.pallas_call(
        weight_grad_kernel,
        grid_spec=pltpu.PrefetchScalarGridSpec(
            num_scalar_prefetch=1,
            grid=(half,),
            in_specs=in_specs,
            out_specs=[pl.BlockSpec((1,) + o, lambda i, w: (i, 0, 0)) for o in out],
        ),
        out_shape=[jax.ShapeDtypeStruct((half,) + o, jnp.bfloat16) for o in out],
        cost_estimate=pl.CostEstimate(
            flops=2 * rows * model * (2 * inner + model), transcendentals=0, bytes_accessed=25_000_000
        ),
        name="weight_grads",
    )(which, act, hidden, attended_t, line, act, hidden, attended_t, line, d_ffn, d_pre, d_branch)


def qkv_grad_kernel(fsdp, which, *refs):
    slots, (d_qkv, send, keep, total) = refs[:-4], refs[-4:]
    rows = slots[0].shape[0]
    shard = send.shape[1] - PAD
    value = None
    for j, slot in enumerate(slots):
        term = dot_t(slot[...].T, d_qkv[:, j * rows : (j + 1) * rows])
        value = term if value is None else value + term
    total[...] = value
    ones = jnp.ones((PAD, d_qkv.shape[1]), jnp.bfloat16)
    sums = dot_t(ones, d_qkv[...]).astype(jnp.bfloat16)
    for side, ref in enumerate((send, keep)):
        for i in range(fsdp // 2):
            at = pl.multiple_of((2 * i + which[side]) * shard, math.gcd(shard, 64))
            ref[i, :shard] = total[pl.ds(at, shard), :].astype(jnp.bfloat16)
            ref[i, shard:] = sums


def qkv_grads(which, slots, d_qkv_t, fsdp):
    rows, model = slots[0].shape
    width = d_qkv_t.shape[0]
    out = (fsdp // 2, model // fsdp + PAD, width)
    fixed = lambda dims: pl.BlockSpec(dims, lambda i, w: (0,) * len(dims))
    return pl.pallas_call(
        partial(qkv_grad_kernel, fsdp),
        grid_spec=pltpu.PrefetchScalarGridSpec(
            num_scalar_prefetch=1,
            grid=(1,),
            in_specs=[fixed((rows, model))] * len(slots) + [fixed(d_qkv_t.shape)],
            out_specs=[fixed(out)] * 2,
            scratch_shapes=[pltpu.VMEM((model, width), jnp.float32)],
        ),
        out_shape=[jax.ShapeDtypeStruct(out, jnp.bfloat16)] * 2,
        cost_estimate=pl.CostEstimate(
            flops=2 * rows * len(slots) * model * width, transcendentals=0, bytes_accessed=8_000_000
        ),
        name="qkv_grads",
    )(which, *slots, d_qkv_t)


def body(
    inputs,
    doc_starts,
    qkv_weight,
    query_bias,
    value_bias,
    out_weight,
    out_bias,
    norm1_gain,
    norm1_bias,
    in_weight,
    in_bias,
    back_weight,
    back_bias,
    norm2_gain,
    norm2_bias,
    cotangent,
):
    bf16, f32 = jnp.bfloat16, jnp.float32
    tokens = inputs[0]
    rows, model = tokens.shape
    starts = doc_starts[0]
    docs = starts.shape[0]
    ctx = lax.axis_size("ctx")
    fsdp = lax.axis_size("fsdp")
    groups = math.gcd(H, ctx)
    parts = ctx // groups
    heads = H // groups
    span = heads * HD
    width = 3 * span
    index = lax.axis_index("ctx")
    g, s = index // parts, index % parts
    f = lax.axis_index("fsdp")
    shard = model // fsdp

    slots = gather_groups(tokens, groups, parts)

    own_cols = pick(qkv_weight.reshape(shard, 3, groups, span), g, 2).reshape(shard, width)
    small = jnp.concatenate(
        [
            query_bias, value_bias, out_bias, norm1_gain, norm1_bias,
            back_bias, norm2_gain, norm2_bias, in_bias,
        ]
    )
    count = small.shape[0]
    extra = -(-count // (width * PAD)) * PAD
    small_block = jnp.pad(small, (0, extra * width - count)).reshape(extra, width)
    first = jnp.concatenate([own_cols, small_block], axis=0)
    first_top = gather_top(first)
    first_top, out_held, in_held, back_held = together(
        first_top, out_weight, in_weight, back_weight
    )
    out_top, in_top, back_top = gather_top(out_held), gather_top(in_held), gather_top(back_held)
    first = gather_rest(first, first_top)
    own_weight = first[:, :shard].reshape(model, width)
    flat = first[:, shard:].reshape(fsdp, extra * width)[:, :count].astype(f32)
    vectors = flat[:, : 8 * shard].reshape(fsdp, 8, shard).transpose(1, 0, 2).reshape(8, model)
    query_shift, value_shift = vectors[0], vectors[1]
    in_shift = flat[:, 8 * shard :].reshape(1, -1)

    zero = jnp.zeros((span,), f32)
    own_shift = jnp.concatenate(
        [
            lax.dynamic_slice(query_shift, (g * span,), (span,)),
            zero,
            lax.dynamic_slice(value_shift, (g * span,), (span,)),
        ]
    )
    own, others = [], []
    for slot in slots:
        projected = lax.dot_general(
            own_weight, slot, (((0,), (1,)), ((), ())), preferred_element_type=f32
        )
        low = (projected + own_shift[:, None]).astype(bf16).reshape(3, heads, HD, rows)
        own.append(low)
    for e in range(1, parts):
        for low in own:
            others.append(part_shift(low[1:], groups, parts, e))
    if parts > 1:
        in_top, others[0] = together(in_top, others[0])

    bounds = jnp.concatenate([starts, jnp.full((1,), ctx * rows, jnp.int32)])
    base = (g ^ jnp.arange(groups, dtype=jnp.int32)) * parts + s
    heads_at = base * rows
    tails_at = heads_at + rows - 1
    low_edge = jnp.max(jnp.where(starts[None] <= heads_at[:, None], starts[None], 0), axis=1)
    high_edge = jnp.min(
        jnp.where(bounds[None] > tails_at[:, None], bounds[None], ctx * rows), axis=1
    )
    ranges = jnp.stack([low_edge // rows, (high_edge + rows - 1) // rows], axis=1).reshape(-1)
    meta = jnp.concatenate([jnp.stack([g, s]).astype(jnp.int32), starts, ranges.astype(jnp.int32)])

    out_full = gather_rest(out_weight, out_top).reshape(model, model)
    in_full = gather_rest(in_weight, in_top).reshape(model, -1)
    meta, out_full, in_full = together(meta, out_full, in_full)
    low, wide, log_total = attend(meta, own, others, groups, parts, docs, rows, heads)
    attended_t = jnp.zeros((groups * span, rows), bf16)
    turned = []
    for j in range(groups):
        piece = low[:, :, j * rows : (j + 1) * rows]
        turned.append(ctx_swap(piece, groups, parts, j) if j else piece)
    for j, piece in enumerate(together(*turned)):
        attended_t = lax.dynamic_update_slice(
            attended_t, piece.reshape(span, rows), ((g ^ j) * span, 0)
        )
    back_full = gather_rest(back_weight, back_top).reshape(-1, model)

    (
        result, d_resid1, d_attended_t, hidden_low, act_low, d_ffn_low, d_pre_low, d_branch_low,
        sums, in_sums,
    ) = feed_forward(
        fsdp, tokens, attended_t, cotangent[0], out_full, in_full, back_full, vectors, in_shift
    )
    grads = []
    for j in range(groups):
        part = lax.dynamic_slice(d_attended_t, ((g ^ j) * span, 0), (span, rows))
        part = part.reshape(heads, HD, rows)
        grads.append(ctx_swap(part, groups, parts, j) if j else part)

    inner = in_full.shape[1]
    inner_shard = in_bias.shape[0]
    line = jnp.concatenate(
        [sums[:6].reshape(6, fsdp, shard).transpose(1, 0, 2).reshape(fsdp, -1), in_sums.reshape(fsdp, -1)],
        axis=1,
    )
    line_rows = -(inner_shard + shard) % 64 or 64
    line = jnp.pad(line, ((0, 0), (0, line_rows * model - line.shape[1])))
    line = line.reshape(fsdp, line_rows, model)
    mine = bit_at("fsdp", 0)
    which = jnp.stack([1 - mine, mine]).astype(jnp.int32)
    lower_send, upper_send, lower, upper = weight_grads(
        which, act_low, hidden_low, attended_t, line, d_ffn_low, d_pre_low, d_branch_low
    )
    lower = add_low(lower, swap(lower_send, "fsdp", 0))
    upper = add_low(upper, swap(upper_send, "fsdp", 0))
    fsdp_bits, ctx_bits = range(bits_of("fsdp")), range(bits_of("ctx"))
    chunks = inner // (2 * model)

    def pair_step(i, state):
        lower, upper = state
        lower_steps = [("fsdp", b) for b in fsdp_bits[1:]] + [("ctx", 0)]
        upper_steps = [("ctx", 0)] + [("fsdp", b) for b in fsdp_bits[1:]]
        return halve(lower, *lower_steps[i], 1), halve(upper, *upper_steps[i], 2)

    def merge(state):
        lower, upper = state
        return (
            jnp.concatenate(
                [lower[0]] + [upper[0, :, c * model : (c + 1) * model] for c in range(chunks)], axis=0
            ),
        )

    steps = [partial(pair_step, i) for i in range(len(fsdp_bits))]
    last = steps.pop()
    steps.append(lambda state: merge(last(state)))
    for bit in ctx_bits[1:-1]:
        steps.append(lambda state, bit=bit: (halve(state[0], "ctx", bit, 0),))
    state = (lower, upper)

    pieces = []
    held, theirs = None, None

    def settle(dq, dkv, theirs):
        for other in theirs:
            dkv = dkv + other.astype(f32)
        pieces.append(jnp.concatenate([dq[None], dkv.astype(bf16)], axis=0))

    def send(piece):
        parts_of = []
        for j in range(groups):
            part = piece[..., j * rows : (j + 1) * rows]
            parts_of.append(ctx_swap(part, groups, parts, j) if j else part)
        return parts_of

    for head in range(heads):
        meta, *state = together(meta, *state)
        flying = steps.pop(0)(state) if steps else state
        dq, dkv, *rest = attend_back(
            head, meta, own, others, grads, wide, log_total, groups, parts, docs, rows
        )
        if head:
            dq, dkv, *landed = together(dq, dkv, *rest, *flying)
            rest, state = landed[: len(rest)], landed[len(rest) :]
            dq, *theirs = together(dq, *theirs)
            settle(*held, theirs)
        else:
            state = flying
        if head == 1:
            early = send(pieces[0])
            dq, qkv_held = together(dq, qkv_weight)
            qkv_top = gather_top(qkv_held)
        elif head == 2:
            middle = send(pieces[1])
            dq, qkv_top, *early = together(dq, qkv_top, *early)
        held = (dq, dkv)
        theirs = [part_shift(rest[0][e - 1], groups, parts, -e) for e in range(1, parts)]
    settle(*held, theirs)
    for advance in steps:
        state = advance(state)
    other = swap(state[0], "ctx", ctx_bits[-1])
    count = len(middle)
    other, *landed = together(other, *middle, *pieces)
    middle, pieces = landed[:count], landed[count:]
    merged = add_low(state[0], other)
    late, merged = together(pieces[2], merged)
    for bit in reversed(ctx_bits[1:-1]):
        merged = double(merged, "ctx", bit, 0)

    d_qkv_t = jnp.stack(pieces, axis=1).reshape(width, groups * rows)
    qkv_send, qkv_sum = qkv_grads(which, slots, d_qkv_t, fsdp)
    qkv_sum = add_low(qkv_sum, swap(qkv_send, "fsdp", 0))
    wide_sum = qkv_sum.astype(f32)
    for e in range(1, parts):
        wide_sum = wide_sum + part_shift(qkv_sum, groups, parts, e).astype(f32)
    qkv_sum, merged = together(wide_sum.astype(bf16), merged)
    other = swap(merged, "ctx", 0)
    late = send(late)
    for bit in fsdp_bits[1:]:
        qkv_sum = halve(qkv_sum, "fsdp", bit, 1)
    qkv_low = qkv_sum[0]
    qkv_full = gather_rest(qkv_held, qkv_top).reshape(model, 3 * model)
    by_group = jnp.zeros((groups,) + qkv_low.shape, bf16)
    turns = [ctx_swap(qkv_low, groups, parts, j) if j else qkv_low for j in range(groups)]
    other, *late = together(other, *late)
    turns = together(*turns)
    for j, piece in enumerate(turns):
        by_group = lax.dynamic_update_slice(by_group, piece[None], (g ^ j, 0, 0))
    natural = by_group.reshape(groups, shard + PAD, 3, span).transpose(1, 2, 0, 3)
    natural = natural.reshape(shard + PAD, 3 * model).astype(f32)
    grad_qkv_shard = natural[:shard]
    bias_line = natural[shard]
    grad_query_shift = lax.dynamic_slice(bias_line, (f * shard,), (shard,))
    grad_value_shift = lax.dynamic_slice(bias_line, (2 * model + f * shard,), (shard,))

    natural = jnp.zeros((3, groups, heads, HD, rows), bf16)
    for j in range(groups):
        part = jnp.stack([early[j], middle[j], late[j]], axis=1)[:, None]
        natural = lax.dynamic_update_slice(natural, part, (0, g ^ j, 0, 0, 0))
    input_grad = d_resid1 + lax.dot_general(
        natural.reshape(3 * model, rows),
        qkv_full,
        (((0,), (1,)), ((), ())),
        preferred_element_type=f32,
    )

    lower_rows = (inner_shard + shard + line_rows) // 2
    lower = join(bit_at("ctx", 0), merged[:lower_rows], other[:lower_rows], 0)
    wide_half = lambda m: jnp.concatenate(
        [m[lower_rows + c * shard : lower_rows + (c + 1) * shard] for c in range(chunks)], axis=1
    )
    upper = join(bit_at("ctx", 0), wide_half(merged), wide_half(other), 1)

    ends = inner_shard + shard
    flat = lower[ends:].reshape(-1).astype(f32)
    offsets = lambda i: flat[i * shard : (i + 1) * shard]
    return (
        result[None],
        input_grad[None],
        grad_qkv_shard,
        grad_query_shift,
        grad_value_shift,
        lower[inner_shard:ends].astype(f32),
        offsets(0),
        offsets(1),
        offsets(2),
        upper.astype(f32),
        flat[6 * shard : 6 * shard + inner_shard],
        lower[:inner_shard].astype(f32),
        offsets(3),
        offsets(4),
        offsets(5),
    )


def solution(mesh):
    rows, one = P("fsdp", None), P("fsdp")
    whole = P("fsdp", "ctx", None)
    return jax.shard_map(
        body,
        mesh=mesh,
        in_specs=(
            whole, rows, rows, one, one, rows, one, one, one, rows, one, rows, one, one, one, whole,
        ),
        out_specs=(
            whole, whole, rows, one, one, rows, one, one, one, rows, one, rows, one, one, one,
        ),
        check_vma=False,
    )
```

```python
from functools import partial
import math

import jax
import jax.numpy as jnp
from jax import lax
from jax.experimental import pallas as pl
from jax.experimental.pallas import tpu as pltpu
from jax.sharding import PartitionSpec as P

H = 12
HD = 64
EPSILON = 1e-05
BIG = 2.0**100
LOG2E = 1.4426950408889634
PAD = 16
KERNEL_FLOPS = 3_000_000_000
KERNEL_BYTES = 20_000_000


def ctx_swap(array, groups, parts, flip):
    pairs = []
    for g in range(groups):
        for s in range(parts):
            pairs.append((g * parts + s, (g ^ flip) * parts + s))
    return lax.ppermute(array, "ctx", pairs)


def part_shift(array, groups, parts, by):
    pairs = []
    for g in range(groups):
        for s in range(parts):
            pairs.append((g * parts + s, g * parts + (s + by) % parts))
    return lax.ppermute(array, "ctx", pairs)


def gather_groups(array, groups, parts):
    return [array] + [ctx_swap(array, groups, parts, i) for i in range(1, groups)]


def swap(array, axis, bit):
    size = lax.axis_size(axis)
    return lax.ppermute(array, axis, [(i, i ^ (1 << bit)) for i in range(size)])


def bits_of(axis):
    return lax.axis_size(axis).bit_length() - 1


def bit_at(axis, bit):
    return (lax.axis_index(axis) >> bit) & 1


def pick(array, which, dim):
    return lax.dynamic_index_in_dim(array, which, dim, keepdims=False)


def together(*values):
    return lax.optimization_barrier(values)


def join(mine, own, other, dim):
    return jnp.where(
        mine == 0,
        jnp.concatenate([own, other], axis=dim),
        jnp.concatenate([other, own], axis=dim),
    )


def gather_top(shard):
    return swap(shard, "fsdp", bits_of("fsdp") - 1)


def gather_rest(shard, other):
    top = bits_of("fsdp") - 1
    held = join(bit_at("fsdp", top), shard[None], other[None], 0)
    for bit in reversed(range(top)):
        got = swap(held, "fsdp", bit)
        pair = join(bit_at("fsdp", bit), held[:, None], got[:, None], 1)
        held = pair.reshape((-1,) + shard.shape)
    return held


def halve(held, axis, bit, dim):
    mine = bit_at(axis, bit)
    if axis == "fsdp":
        pairs = held.reshape((held.shape[0] // 2, 2) + held.shape[1:])
        keep, send = pick(pairs, mine, 1), pick(pairs, 1 - mine, 1)
    else:
        half = held.shape[dim] // 2
        keep = lax.dynamic_slice_in_dim(held, mine * half, half, dim)
        send = lax.dynamic_slice_in_dim(held, (1 - mine) * half, half, dim)
    return add_low(keep, swap(send, axis, bit))


def add_low(a, b):
    return (a.astype(jnp.float32) + b.astype(jnp.float32)).astype(jnp.bfloat16)


def double(held, axis, bit, dim):
    return join(bit_at(axis, bit), held, swap(held, axis, bit), dim)


def doc_row(meta, base, length, docs):
    pos = base + lax.broadcasted_iota(jnp.int32, (1, length), 1)
    doc = jnp.full((1, length), -1, jnp.int32)
    for j in range(docs):
        doc = doc + (pos >= meta[2 + j]).astype(jnp.int32)
    return doc


def dot(a, b):
    return jnp.dot(a, b, preferred_element_type=jnp.float32)


def dot_t(a, b):
    return lax.dot_general(a, b, (((1,), (1,)), ((), ())), preferred_element_type=jnp.float32)


def fill_keys(meta, own, others, groups, parts, docs, rows, store):
    g, s = meta[0], meta[1]
    for j in range(groups):
        for e in range(parts):
            block = (g ^ j) * parts + lax.rem(s - e + parts, parts)
            if e == 0:
                key_t, value_t = own[j][1, 0], own[j][2, 0]
            else:
                ref = others[(e - 1) * groups + j]
                key_t, value_t = ref[0, 0], ref[1, 0]
            doc = doc_row(meta, block * rows, rows, docs)
            hot = (lax.broadcasted_iota(jnp.int32, (HD, rows), 0) == doc).astype(jnp.float32)
            keys = jnp.concatenate([key_t, hot.astype(jnp.bfloat16)], axis=0)
            store(block, keys, key_t, value_t)


def query_full(meta, query_t, j, groups, parts, docs, rows):
    g, s = meta[0], meta[1]
    block = (g ^ j) * parts + s
    doc = doc_row(meta, block * rows, rows, docs)
    shut = jnp.where(lax.broadcasted_iota(jnp.int32, (HD, rows), 0) == doc, 0.0, -BIG)
    return jnp.concatenate([query_t, shut.astype(jnp.bfloat16)], axis=0)


def attend_kernel(groups, parts, docs, rows, meta, *refs):
    own = refs[:groups]
    others = refs[groups : groups * parts]
    low_ref, wide_ref, log_ref, queries_ref, keys_ref, values_ref = refs[groups * parts :]
    coeff = LOG2E * HD**-0.5

    def store(block, keys, key_t, value_t):
        keys_ref[block] = keys.T
        values_ref[block] = value_t

    fill_keys(meta, own, others, groups, parts, docs, rows, store)
    for j in range(groups):
        queries_ref[j] = query_full(meta, own[j][0, 0], j, groups, parts, docs, rows)

    def one_slot(j, carry):
        full = queries_ref[j]

        def step(t, state):
            best, total, accum = state
            scores = dot(keys_ref[t], full)
            new_best = jnp.maximum(best, jnp.max(scores, axis=0, keepdims=True))
            weights = jnp.exp2((scores - new_best) * coeff)
            shrink = jnp.exp2((best - new_best) * coeff)
            total = total * shrink + jnp.sum(weights, axis=0, keepdims=True)
            accum = accum * shrink + dot(values_ref[t], weights.astype(jnp.bfloat16))
            return new_best, total, accum

        best, total, accum = lax.fori_loop(
            meta[2 + docs + 2 * j],
            meta[3 + docs + 2 * j],
            step,
            (
                jnp.full((1, rows), -BIG, jnp.float32),
                jnp.zeros((1, rows), jnp.float32),
                jnp.zeros((HD, rows), jnp.float32),
            ),
        )
        attended = accum / total
        at = pl.ds(pl.multiple_of(j * rows, rows), rows)
        wide_ref[0, :, at] = attended
        low_ref[0, :, at] = attended.astype(jnp.bfloat16)
        log_ref[0, :, at] = best * coeff + jnp.log2(total)
        return carry

    lax.fori_loop(0, groups, one_slot, 0)


def attend_back_kernel(groups, parts, docs, rows, meta, *refs):
    own = refs[:groups]
    others = refs[groups : groups * parts]
    grads = refs[groups * parts : groups * parts + groups]
    rest = refs[groups * parts + groups :]
    wide_ref, log_ref = rest[:2]
    dq_ref, mine_ref = rest[2:4]
    theirs = rest[4] if parts > 1 else None
    queries_ref, grads_ref, keys_ref, keys_t_ref, values_ref, accum_ref = rest[-6:]
    coeff = LOG2E * HD**-0.5

    def store(block, keys, key_t, value_t):
        keys_ref[block] = keys.T
        keys_t_ref[block] = key_t
        values_ref[block] = value_t.T

    fill_keys(meta, own, others, groups, parts, docs, rows, store)
    accum_ref[...] = jnp.zeros_like(accum_ref)
    for j in range(groups):
        queries_ref[j] = query_full(meta, own[j][0, 0], j, groups, parts, docs, rows)
        grads_ref[j] = grads[j][0]

    def one_slot(j, carry):
        at = pl.ds(pl.multiple_of(j * rows, rows), rows)
        full = queries_ref[j]
        grad_t = grads_ref[j]
        delta = jnp.sum(grad_t.astype(jnp.float32) * wide_ref[0, :, at], axis=0, keepdims=True)
        log_total = log_ref[0, :, at]
        blank = jnp.zeros((HD, rows), jnp.bfloat16)
        both = jnp.concatenate(
            [
                jnp.concatenate([full[:HD], blank], axis=1),
                jnp.concatenate([blank, grad_t], axis=1),
            ],
            axis=0,
        )

        def step(t, grad_query):
            scores = dot(keys_ref[t], full)
            probs = jnp.exp2(scores * coeff - log_total)
            d_probs = dot(values_ref[t], grad_t)
            d_scores = (probs * (d_probs - delta)).astype(jnp.bfloat16)
            joined = jnp.concatenate([d_scores, probs.astype(jnp.bfloat16)], axis=1)
            accum_ref[t] += dot_t(joined, both)
            return grad_query + dot(keys_t_ref[t], d_scores)

        grad_query = lax.fori_loop(
            meta[2 + docs + 2 * j],
            meta[3 + docs + 2 * j],
            step,
            jnp.zeros((HD, rows), jnp.float32),
        )
        dq_ref[:, at] = (grad_query * HD**-0.5).astype(jnp.bfloat16)
        return carry

    lax.fori_loop(0, groups, one_slot, 0)
    g, s = meta[0], meta[1]
    for j in range(groups):
        for e in range(parts):
            block = (g ^ j) * parts + lax.rem(s - e + parts, parts)
            terms = accum_ref[block].T
            at = slice(j * rows, (j + 1) * rows)
            d_key = terms[:HD] * HD**-0.5
            d_value = terms[HD:]
            if e == 0:
                mine_ref[0, :, at] = d_key
                mine_ref[1, :, at] = d_value
            else:
                theirs[e - 1, 0, :, at] = d_key.astype(jnp.bfloat16)
                theirs[e - 1, 1, :, at] = d_value.astype(jnp.bfloat16)


def head_block(head, *shape):
    dims = tuple(1 if n is None else n for n in shape)
    where = shape.index(None)

    def at(h, meta):
        chosen = h if head is None else head
        return tuple(chosen if i == where else 0 for i in range(len(dims)))

    return pl.BlockSpec(dims, at)


def attend(meta, own, others, groups, parts, docs, rows, heads):
    tiles = groups * parts
    tokens = groups * rows
    block = partial(head_block, None)
    grid_spec = pltpu.PrefetchScalarGridSpec(
        num_scalar_prefetch=1,
        grid=(heads,),
        in_specs=[block(3, None, HD, rows)] * groups
        + [block(2, None, HD, rows)] * (groups * (parts - 1)),
        out_specs=[block(None, HD, tokens), block(None, HD, tokens), block(None, 1, tokens)],
        scratch_shapes=[
            pltpu.VMEM((groups, 2 * HD, rows), jnp.bfloat16),
            pltpu.VMEM((tiles, rows, 2 * HD), jnp.bfloat16),
            pltpu.VMEM((tiles, HD, rows), jnp.bfloat16),
        ],
    )
    return pl.pallas_call(
        partial(attend_kernel, groups, parts, docs, rows),
        grid_spec=grid_spec,
        out_shape=[
            jax.ShapeDtypeStruct((heads, HD, tokens), jnp.bfloat16),
            jax.ShapeDtypeStruct((heads, HD, tokens), jnp.float32),
            jax.ShapeDtypeStruct((heads, 1, tokens), jnp.float32),
        ],
        cost_estimate=pl.CostEstimate(
            flops=KERNEL_FLOPS * 2 * heads,
            transcendentals=0,
            bytes_accessed=KERNEL_BYTES * heads,
        ),
        name="attend",
    )(meta, *own, *others)


def attend_back(head, meta, own, others, grads, wide, log_total, groups, parts, docs, rows):
    tiles = groups * parts
    tokens = groups * rows
    block = partial(head_block, head)
    plain = lambda *dims: pl.BlockSpec(dims, lambda h, meta: (0,) * len(dims))
    out_specs = [plain(HD, tokens), plain(2, HD, tokens)]
    out_shape = [
        jax.ShapeDtypeStruct((HD, tokens), jnp.bfloat16),
        jax.ShapeDtypeStruct((2, HD, tokens), jnp.float32),
    ]
    if parts > 1:
        out_specs.append(plain(parts - 1, 2, HD, tokens))
        out_shape.append(jax.ShapeDtypeStruct((parts - 1, 2, HD, tokens), jnp.bfloat16))
    grid_spec = pltpu.PrefetchScalarGridSpec(
        num_scalar_prefetch=1,
        grid=(1,),
        in_specs=[block(3, None, HD, rows)] * groups
        + [block(2, None, HD, rows)] * (groups * (parts - 1))
        + [block(None, HD, rows)] * groups
        + [block(None, HD, tokens), block(None, 1, tokens)],
        out_specs=out_specs,
        scratch_shapes=[
            pltpu.VMEM((groups, 2 * HD, rows), jnp.bfloat16),
            pltpu.VMEM((groups, HD, rows), jnp.bfloat16),
            pltpu.VMEM((tiles, rows, 2 * HD), jnp.bfloat16),
            pltpu.VMEM((tiles, HD, rows), jnp.bfloat16),
            pltpu.VMEM((tiles, rows, HD), jnp.bfloat16),
            pltpu.VMEM((tiles, rows, 2 * HD), jnp.float32),
        ],
    )
    return pl.pallas_call(
        partial(attend_back_kernel, groups, parts, docs, rows),
        grid_spec=grid_spec,
        out_shape=out_shape,
        cost_estimate=pl.CostEstimate(
            flops=KERNEL_FLOPS * 5, transcendentals=0, bytes_accessed=KERNEL_BYTES
        ),
        name="attend_back",
    )(meta, *own, *others, *grads, wide, log_total)


ERFC = (
    -1.26551223, 1.00002368, 0.37409196, 0.09678418, -0.18628806,
    0.27886807, -1.13520398, 1.48851587, -0.82215223, 0.17087277,
)


def normal_terms(v):
    z = jnp.abs(v) * (0.5**0.5)
    t = 1.0 / (1.0 + 0.5 * z)
    poly = jnp.full_like(t, ERFC[-1])
    for term in reversed(ERFC[:-1]):
        poly = poly * t + term
    square = z * z
    tail = 0.5 * t * jnp.exp(poly - square)
    below = jnp.where(v < 0, tail, 1.0 - tail)
    return below, jnp.exp(-square) * (2.0 * math.pi) ** -0.5


def normed(resid):
    centred = resid - jnp.mean(resid, axis=-1, keepdims=True)
    spread = jnp.mean(centred * centred, axis=-1, keepdims=True)
    scale = lax.rsqrt(spread + EPSILON)
    return centred * scale, scale


def norm_back(grad, gain, unit, scale):
    e = grad * gain
    inner = jnp.mean(e * unit, axis=-1, keepdims=True)
    return (e - jnp.mean(e, axis=-1, keepdims=True) - unit * inner) * scale


def over_blocks(count, aligned, step, value):
    if aligned:
        return lax.fori_loop(0, count, step, value)
    for i in range(count):
        value = step(i, value)
    return value


def feed_kernel(
    tokens_ref,
    attended_ref,
    cot_ref,
    out_ref,
    in_ref,
    back_ref,
    vec_ref,
    in_bias_ref,
    result_ref,
    d_resid1_ref,
    d_attended_ref,
    hidden_ref,
    act_ref,
    d_ffn_ref,
    d_pre_ref,
    d_branch_ref,
    sums_ref,
    in_sums_ref,
    slope_ref,
):
    f32, bf16 = jnp.float32, jnp.bfloat16
    out_shift, gain_one, shift_one = vec_ref[2:3], vec_ref[3:4], vec_ref[4:5]
    back_shift, gain_two, shift_two = vec_ref[5:6], vec_ref[6:7], vec_ref[7:8]

    @pl.when(pl.program_id(0) == 0)
    def _():
        sums_ref[...] = jnp.zeros_like(sums_ref)
        in_sums_ref[...] = jnp.zeros_like(in_sums_ref)

    total = lambda a: jnp.sum(a, axis=0, keepdims=True)
    branch = dot(attended_ref[...].T, out_ref[...]) + out_shift
    unit1, scale1 = normed(tokens_ref[...].astype(f32) + branch)
    hidden = unit1 * gain_one + shift_one
    hidden_low = hidden.astype(bf16)
    count, unused, shard = hidden_ref.shape
    for i in range(count):
        hidden_ref[i] = hidden_low[:, i * shard : (i + 1) * shard]
    resid2 = hidden + back_shift
    blocks, unused, size = act_ref.shape
    aligned = size % 128 == 0
    columns = lambda i: pl.ds(pl.multiple_of(i * size, size) if aligned else i * size, size)

    def forward(i, resid2):
        cols = columns(i)
        pre = dot(hidden_low, in_ref[:, cols]) + in_bias_ref[:, cols]
        below, density = normal_terms(pre)
        act = (pre * below).astype(bf16)
        act_ref[i] = act
        slope_ref[i] = below + pre * density
        return resid2 + dot(act, back_ref[cols, :])

    resid2 = over_blocks(blocks, aligned, forward, hidden + back_shift)
    unit2, scale2 = normed(resid2)
    result_ref[...] = (unit2 * gain_two + shift_two).astype(bf16)
    cot = cot_ref[...].astype(f32)
    d_resid2 = norm_back(cot, gain_two, unit2, scale2)
    d_ffn = d_resid2.astype(bf16)
    d_ffn_ref[...] = d_ffn

    def backward(i, d_hidden):
        cols = columns(i)
        d_act = dot_t(d_ffn, back_ref[cols, :])
        d_pre = (d_act * slope_ref[i]).astype(bf16)
        d_pre_ref[:, cols] = d_pre
        in_sums_ref[:, cols] += total(d_pre.astype(f32))
        return d_hidden + dot_t(d_pre, in_ref[:, cols])

    d_hidden = over_blocks(blocks, aligned, backward, d_resid2)
    d_resid1 = norm_back(d_hidden, gain_one, unit1, scale1)
    d_resid1_ref[...] = d_resid1
    d_branch = d_resid1.astype(bf16)
    d_branch_ref[...] = d_branch
    d_attended_ref[...] = dot_t(out_ref[...], d_branch).astype(bf16)
    sums_ref[...] += jnp.concatenate(
        [
            total(d_branch.astype(f32)),
            total(d_hidden * unit1),
            total(d_hidden),
            total(d_ffn.astype(f32)),
            total(cot * unit2),
            total(cot),
            jnp.zeros((2, cot.shape[1]), f32),
        ],
        axis=0,
    )


def feed_forward(fsdp, tokens, attended_t, cotangent, out_full, in_full, back_full, vectors, in_shift):
    f32, bf16 = jnp.float32, jnp.bfloat16
    rows, model = tokens.shape
    inner = in_full.shape[1]
    tile = math.gcd(rows, 256)
    by_rows = lambda n: pl.BlockSpec((tile, n), lambda i: (i, 0))
    by_cols = lambda n: pl.BlockSpec((n, tile), lambda i: (0, i))
    blocks = lambda n: pl.BlockSpec((fsdp, tile, n // fsdp), lambda i: (0, i, 0))
    fixed = lambda m, n: pl.BlockSpec((m, n), lambda i: (0, 0))
    shape = jax.ShapeDtypeStruct
    return pl.pallas_call(
        feed_kernel,
        grid=(rows // tile,),
        in_specs=[
            by_rows(model), by_cols(model), by_rows(model), fixed(model, model),
            fixed(model, inner), fixed(inner, model), fixed(8, model), fixed(1, inner),
        ],
        out_specs=[
            by_rows(model), by_rows(model), by_cols(model), blocks(model), blocks(inner),
            by_rows(model), by_rows(inner), by_rows(model), fixed(8, model), fixed(1, inner),
        ],
        out_shape=[
            shape((rows, model), bf16), shape((rows, model), f32), shape((model, rows), bf16),
            shape((fsdp, rows, model // fsdp), bf16), shape((fsdp, rows, inner // fsdp), bf16),
            shape((rows, model), bf16),
            shape((rows, inner), bf16), shape((rows, model), bf16), shape((8, model), f32),
            shape((1, inner), f32),
        ],
        scratch_shapes=[pltpu.VMEM((fsdp, tile, inner // fsdp), f32)],
        cost_estimate=pl.CostEstimate(
            flops=rows * model * (8 * inner + 4 * model), transcendentals=0, bytes_accessed=30_000_000
        ),
        name="feed_forward",
    )(tokens, attended_t, cotangent, out_full, in_full, back_full, vectors, in_shift)


def weight_grad_kernel(which, *refs):
    ins, (d_ffn, d_pre, d_branch), outs = refs[:8], refs[8:11], refs[11:]
    bf16 = jnp.bfloat16
    for side in range(2):
        act, hidden, attended_t, line = ins[4 * side : 4 * side + 4]
        lower, upper = outs[2 * side : 2 * side + 2]
        first, second = act.shape[2], attended_t.shape[0]
        lower[0, :first] = dot(act[0].T, d_ffn[...]).astype(bf16)
        lower[0, first : first + second] = dot(attended_t[...], d_branch[...]).astype(bf16)
        lower[0, first + second :] = line[0].astype(bf16)
        upper[0] = dot(hidden[0].T, d_pre[...]).astype(bf16)


def weight_grads(which, act, hidden, attended_t, line, d_ffn, d_pre, d_branch):
    fsdp, rows, inner_shard = act.shape
    shard = hidden.shape[2]
    model, inner = d_ffn.shape[1], d_pre.shape[1]
    line_rows = line.shape[1]
    tall = inner_shard + shard + line_rows
    half = fsdp // 2
    in_specs = []
    for side in range(2):
        block = lambda i, w, side=side: 2 * i + w[side]
        in_specs += [
            pl.BlockSpec((1, rows, inner_shard), lambda i, w, b=block: (b(i, w), 0, 0)),
            pl.BlockSpec((1, rows, shard), lambda i, w, b=block: (b(i, w), 0, 0)),
            pl.BlockSpec((shard, rows), lambda i, w, b=block: (b(i, w), 0)),
            pl.BlockSpec((1, line_rows, model), lambda i, w, b=block: (b(i, w), 0, 0)),
        ]
    in_specs += [pl.BlockSpec((rows, n), lambda i, w: (0, 0)) for n in (model, inner, model)]
    out = [(tall, model), (shard, inner)] * 2
    return pl.pallas_call(
        weight_grad_kernel,
        grid_spec=pltpu.PrefetchScalarGridSpec(
            num_scalar_prefetch=1,
            grid=(half,),
            in_specs=in_specs,
            out_specs=[pl.BlockSpec((1,) + o, lambda i, w: (i, 0, 0)) for o in out],
        ),
        out_shape=[jax.ShapeDtypeStruct((half,) + o, jnp.bfloat16) for o in out],
        cost_estimate=pl.CostEstimate(
            flops=2 * rows * model * (2 * inner + model), transcendentals=0, bytes_accessed=25_000_000
        ),
        name="weight_grads",
    )(which, act, hidden, attended_t, line, act, hidden, attended_t, line, d_ffn, d_pre, d_branch)


def qkv_grad_kernel(fsdp, which, *refs):
    slots, (d_qkv, send, keep, total) = refs[:-4], refs[-4:]
    rows = slots[0].shape[0]
    shard = send.shape[1] - PAD
    value = None
    for j, slot in enumerate(slots):
        term = dot_t(slot[...].T, d_qkv[:, j * rows : (j + 1) * rows])
        value = term if value is None else value + term
    total[...] = value
    ones = jnp.ones((PAD, d_qkv.shape[1]), jnp.bfloat16)
    sums = dot_t(ones, d_qkv[...]).astype(jnp.bfloat16)
    for side, ref in enumerate((send, keep)):
        for i in range(fsdp // 2):
            at = pl.multiple_of((2 * i + which[side]) * shard, math.gcd(shard, 64))
            ref[i, :shard] = total[pl.ds(at, shard), :].astype(jnp.bfloat16)
            ref[i, shard:] = sums


def qkv_grads(which, slots, d_qkv_t, fsdp):
    rows, model = slots[0].shape
    width = d_qkv_t.shape[0]
    out = (fsdp // 2, model // fsdp + PAD, width)
    fixed = lambda dims: pl.BlockSpec(dims, lambda i, w: (0,) * len(dims))
    return pl.pallas_call(
        partial(qkv_grad_kernel, fsdp),
        grid_spec=pltpu.PrefetchScalarGridSpec(
            num_scalar_prefetch=1,
            grid=(1,),
            in_specs=[fixed((rows, model))] * len(slots) + [fixed(d_qkv_t.shape)],
            out_specs=[fixed(out)] * 2,
            scratch_shapes=[pltpu.VMEM((model, width), jnp.float32)],
        ),
        out_shape=[jax.ShapeDtypeStruct(out, jnp.bfloat16)] * 2,
        cost_estimate=pl.CostEstimate(
            flops=2 * rows * len(slots) * model * width, transcendentals=0, bytes_accessed=8_000_000
        ),
        name="qkv_grads",
    )(which, *slots, d_qkv_t)


def body(
    inputs,
    doc_starts,
    qkv_weight,
    query_bias,
    value_bias,
    out_weight,
    out_bias,
    norm1_gain,
    norm1_bias,
    in_weight,
    in_bias,
    back_weight,
    back_bias,
    norm2_gain,
    norm2_bias,
    cotangent,
):
    bf16, f32 = jnp.bfloat16, jnp.float32
    tokens = inputs[0]
    rows, model = tokens.shape
    starts = doc_starts[0]
    docs = starts.shape[0]
    ctx = lax.axis_size("ctx")
    fsdp = lax.axis_size("fsdp")
    groups = math.gcd(H, ctx)
    parts = ctx // groups
    heads = H // groups
    span = heads * HD
    width = 3 * span
    index = lax.axis_index("ctx")
    g, s = index // parts, index % parts
    f = lax.axis_index("fsdp")
    shard = model // fsdp

    slots = gather_groups(tokens, groups, parts)

    own_cols = pick(qkv_weight.reshape(shard, 3, groups, span), g, 2).reshape(shard, width)
    small = jnp.concatenate(
        [
            query_bias, value_bias, out_bias, norm1_gain, norm1_bias,
            back_bias, norm2_gain, norm2_bias, in_bias,
        ]
    )
    count = small.shape[0]
    extra = -(-count // (width * PAD)) * PAD
    small_block = jnp.pad(small, (0, extra * width - count)).reshape(extra, width)
    first = jnp.concatenate([own_cols, small_block], axis=0)
    first_top = gather_top(first)
    first_top, out_held, in_held, back_held = together(
        first_top, out_weight, in_weight, back_weight
    )
    out_top, in_top, back_top = gather_top(out_held), gather_top(in_held), gather_top(back_held)
    first = gather_rest(first, first_top)
    own_weight = first[:, :shard].reshape(model, width)
    flat = first[:, shard:].reshape(fsdp, extra * width)[:, :count].astype(f32)
    vectors = flat[:, : 8 * shard].reshape(fsdp, 8, shard).transpose(1, 0, 2).reshape(8, model)
    query_shift, value_shift = vectors[0], vectors[1]
    in_shift = flat[:, 8 * shard :].reshape(1, -1)

    zero = jnp.zeros((span,), f32)
    own_shift = jnp.concatenate(
        [
            lax.dynamic_slice(query_shift, (g * span,), (span,)),
            zero,
            lax.dynamic_slice(value_shift, (g * span,), (span,)),
        ]
    )
    own, others = [], []
    for slot in slots:
        projected = lax.dot_general(
            own_weight, slot, (((0,), (1,)), ((), ())), preferred_element_type=f32
        )
        low = (projected + own_shift[:, None]).astype(bf16).reshape(3, heads, HD, rows)
        own.append(low)
    for e in range(1, parts):
        for low in own:
            others.append(part_shift(low[1:], groups, parts, e))
    if parts > 1:
        in_top, others[0] = together(in_top, others[0])

    bounds = jnp.concatenate([starts, jnp.full((1,), ctx * rows, jnp.int32)])
    base = (g ^ jnp.arange(groups, dtype=jnp.int32)) * parts + s
    heads_at = base * rows
    tails_at = heads_at + rows - 1
    low_edge = jnp.max(jnp.where(starts[None] <= heads_at[:, None], starts[None], 0), axis=1)
    high_edge = jnp.min(
        jnp.where(bounds[None] > tails_at[:, None], bounds[None], ctx * rows), axis=1
    )
    ranges = jnp.stack([low_edge // rows, (high_edge + rows - 1) // rows], axis=1).reshape(-1)
    meta = jnp.concatenate([jnp.stack([g, s]).astype(jnp.int32), starts, ranges.astype(jnp.int32)])

    out_full = gather_rest(out_weight, out_top).reshape(model, model)
    in_full = gather_rest(in_weight, in_top).reshape(model, -1)
    meta, out_full, in_full = together(meta, out_full, in_full)
    low, wide, log_total = attend(meta, own, others, groups, parts, docs, rows, heads)
    attended_t = jnp.zeros((groups * span, rows), bf16)
    turned = []
    for j in range(groups):
        piece = low[:, :, j * rows : (j + 1) * rows]
        turned.append(ctx_swap(piece, groups, parts, j) if j else piece)
    for j, piece in enumerate(together(*turned)):
        attended_t = lax.dynamic_update_slice(
            attended_t, piece.reshape(span, rows), ((g ^ j) * span, 0)
        )
    back_full = gather_rest(back_weight, back_top).reshape(-1, model)

    (
        result, d_resid1, d_attended_t, hidden_low, act_low, d_ffn_low, d_pre_low, d_branch_low,
        sums, in_sums,
    ) = feed_forward(
        fsdp, tokens, attended_t, cotangent[0], out_full, in_full, back_full, vectors, in_shift
    )
    grads = []
    for j in range(groups):
        part = lax.dynamic_slice(d_attended_t, ((g ^ j) * span, 0), (span, rows))
        part = part.reshape(heads, HD, rows)
        grads.append(ctx_swap(part, groups, parts, j) if j else part)

    inner = in_full.shape[1]
    inner_shard = in_bias.shape[0]
    line = jnp.concatenate(
        [sums[:6].reshape(6, fsdp, shard).transpose(1, 0, 2).reshape(fsdp, -1), in_sums.reshape(fsdp, -1)],
        axis=1,
    )
    line_rows = -(inner_shard + shard) % 64 or 64
    line = jnp.pad(line, ((0, 0), (0, line_rows * model - line.shape[1])))
    line = line.reshape(fsdp, line_rows, model)
    mine = bit_at("fsdp", 0)
    which = jnp.stack([1 - mine, mine]).astype(jnp.int32)
    lower_send, upper_send, lower, upper = weight_grads(
        which, act_low, hidden_low, attended_t, line, d_ffn_low, d_pre_low, d_branch_low
    )
    lower = add_low(lower, swap(lower_send, "fsdp", 0))
    upper = add_low(upper, swap(upper_send, "fsdp", 0))
    fsdp_bits, ctx_bits = range(bits_of("fsdp")), range(bits_of("ctx"))
    chunks = inner // (2 * model)

    def pair_step(i, state):
        lower, upper = state
        lower_steps = [("fsdp", b) for b in fsdp_bits[1:]] + [("ctx", 0)]
        upper_steps = [("ctx", 0)] + [("fsdp", b) for b in fsdp_bits[1:]]
        return halve(lower, *lower_steps[i], 1), halve(upper, *upper_steps[i], 2)

    def merge(state):
        lower, upper = state
        return (
            jnp.concatenate(
                [lower[0]] + [upper[0, :, c * model : (c + 1) * model] for c in range(chunks)], axis=0
            ),
        )

    steps = [partial(pair_step, i) for i in range(len(fsdp_bits))]
    last = steps.pop()
    steps.append(lambda state: merge(last(state)))
    for bit in ctx_bits[1:-1]:
        steps.append(lambda state, bit=bit: (halve(state[0], "ctx", bit, 0),))
    state = (lower, upper)

    pieces = []
    held, theirs = None, None

    def settle(dq, dkv, theirs):
        for other in theirs:
            dkv = dkv + other.astype(f32)
        pieces.append(jnp.concatenate([dq[None], dkv.astype(bf16)], axis=0))

    def send(piece):
        parts_of = []
        for j in range(groups):
            part = piece[..., j * rows : (j + 1) * rows]
            parts_of.append(ctx_swap(part, groups, parts, j) if j else part)
        return parts_of

    for head in range(heads):
        meta, *state = together(meta, *state)
        flying = steps.pop(0)(state) if steps else state
        dq, dkv, *rest = attend_back(
            head, meta, own, others, grads, wide, log_total, groups, parts, docs, rows
        )
        if head:
            dq, dkv, *landed = together(dq, dkv, *rest, *flying)
            rest, state = landed[: len(rest)], landed[len(rest) :]
            dq, *theirs = together(dq, *theirs)
            settle(*held, theirs)
        else:
            state = flying
        if head == 1:
            early = send(pieces[0])
            dq, qkv_held = together(dq, qkv_weight)
            qkv_top = gather_top(qkv_held)
        elif head == 2:
            middle = send(pieces[1])
            dq, *early = together(dq, *early)
        held = (dq, dkv)
        theirs = [part_shift(rest[0][e - 1], groups, parts, -e) for e in range(1, parts)]
    settle(*held, theirs)
    for advance in steps:
        state = advance(state)
    other = swap(state[0], "ctx", ctx_bits[-1])
    d_qkv_t = jnp.stack(pieces, axis=1).reshape(width, groups * rows)
    qkv_send, qkv_sum = qkv_grads(which, slots, d_qkv_t, fsdp)
    other, qkv_send, qkv_sum, qkv_top, *middle = together(
        other, qkv_send, qkv_sum, qkv_top, *middle
    )
    qkv_full = gather_rest(qkv_held, qkv_top).reshape(model, 3 * model)
    merged = add_low(state[0], other)
    late, merged = together(pieces[2], merged)
    for bit in reversed(ctx_bits[1:-1]):
        merged = double(merged, "ctx", bit, 0)
    qkv_sum = add_low(qkv_sum, swap(qkv_send, "fsdp", 0))
    wide_sum = qkv_sum.astype(f32)
    for e in range(1, parts):
        wide_sum = wide_sum + part_shift(qkv_sum, groups, parts, e).astype(f32)
    qkv_sum, merged, qkv_full = together(wide_sum.astype(bf16), merged, qkv_full)
    other = swap(merged, "ctx", 0)
    late = send(late)
    for bit in fsdp_bits[1:]:
        qkv_sum = halve(qkv_sum, "fsdp", bit, 1)
    qkv_low = qkv_sum[0]
    by_group = jnp.zeros((groups,) + qkv_low.shape, bf16)
    turns = [ctx_swap(qkv_low, groups, parts, j) if j else qkv_low for j in range(groups)]
    other, *late = together(other, *late)
    turns = together(*turns)
    for j, piece in enumerate(turns):
        by_group = lax.dynamic_update_slice(by_group, piece[None], (g ^ j, 0, 0))
    natural = by_group.reshape(groups, shard + PAD, 3, span).transpose(1, 2, 0, 3)
    natural = natural.reshape(shard + PAD, 3 * model).astype(f32)
    grad_qkv_shard = natural[:shard]
    bias_line = natural[shard]
    grad_query_shift = lax.dynamic_slice(bias_line, (f * shard,), (shard,))
    grad_value_shift = lax.dynamic_slice(bias_line, (2 * model + f * shard,), (shard,))

    natural = jnp.zeros((3, groups, heads, HD, rows), bf16)
    for j in range(groups):
        part = jnp.stack([early[j], middle[j], late[j]], axis=1)[:, None]
        natural = lax.dynamic_update_slice(natural, part, (0, g ^ j, 0, 0, 0))
    input_grad = d_resid1 + lax.dot_general(
        natural.reshape(3 * model, rows),
        qkv_full,
        (((0,), (1,)), ((), ())),
        preferred_element_type=f32,
    )

    lower_rows = (inner_shard + shard + line_rows) // 2
    lower = join(bit_at("ctx", 0), merged[:lower_rows], other[:lower_rows], 0)
    wide_half = lambda m: jnp.concatenate(
        [m[lower_rows + c * shard : lower_rows + (c + 1) * shard] for c in range(chunks)], axis=1
    )
    upper = join(bit_at("ctx", 0), wide_half(merged), wide_half(other), 1)

    ends = inner_shard + shard
    flat = lower[ends:].reshape(-1).astype(f32)
    offsets = lambda i: flat[i * shard : (i + 1) * shard]
    return (
        result[None],
        input_grad[None],
        grad_qkv_shard,
        grad_query_shift,
        grad_value_shift,
        lower[inner_shard:ends].astype(f32),
        offsets(0),
        offsets(1),
        offsets(2),
        upper.astype(f32),
        flat[6 * shard : 6 * shard + inner_shard],
        lower[:inner_shard].astype(f32),
        offsets(3),
        offsets(4),
        offsets(5),
    )


def solution(mesh):
    rows, one = P("fsdp", None), P("fsdp")
    whole = P("fsdp", "ctx", None)
    return jax.shard_map(
        body,
        mesh=mesh,
        in_specs=(
            whole, rows, rows, one, one, rows, one, one, one, rows, one, rows, one, one, one, whole,
        ),
        out_specs=(
            whole, whole, rows, one, one, rows, one, one, one, rows, one, rows, one, one, one,
        ),
        check_vma=False,
    )
```

```python
from functools import partial
import math

import jax
import jax.numpy as jnp
from jax import lax
from jax.experimental import pallas as pl
from jax.experimental.pallas import tpu as pltpu
from jax.sharding import PartitionSpec as P

H = 12
HD = 64
EPSILON = 1e-05
BIG = 2.0**100
LOG2E = 1.4426950408889634
PAD = 16
KERNEL_FLOPS = 3_000_000_000
KERNEL_BYTES = 20_000_000


def ctx_swap(array, groups, parts, flip):
    pairs = []
    for g in range(groups):
        for s in range(parts):
            pairs.append((g * parts + s, (g ^ flip) * parts + s))
    return lax.ppermute(array, "ctx", pairs)


def part_shift(array, groups, parts, by):
    pairs = []
    for g in range(groups):
        for s in range(parts):
            pairs.append((g * parts + s, g * parts + (s + by) % parts))
    return lax.ppermute(array, "ctx", pairs)


def gather_groups(array, groups, parts):
    return [array] + [ctx_swap(array, groups, parts, i) for i in range(1, groups)]


def swap(array, axis, bit):
    size = lax.axis_size(axis)
    return lax.ppermute(array, axis, [(i, i ^ (1 << bit)) for i in range(size)])


def bits_of(axis):
    return lax.axis_size(axis).bit_length() - 1


def bit_at(axis, bit):
    return (lax.axis_index(axis) >> bit) & 1


def pick(array, which, dim):
    return lax.dynamic_index_in_dim(array, which, dim, keepdims=False)


def together(*values):
    return lax.optimization_barrier(values)


def join(mine, own, other, dim):
    return jnp.where(
        mine == 0,
        jnp.concatenate([own, other], axis=dim),
        jnp.concatenate([other, own], axis=dim),
    )


def gather_top(shard):
    return swap(shard, "fsdp", bits_of("fsdp") - 1)


def gather_rest(shard, other):
    top = bits_of("fsdp") - 1
    held = join(bit_at("fsdp", top), shard[None], other[None], 0)
    for bit in reversed(range(top)):
        got = swap(held, "fsdp", bit)
        pair = join(bit_at("fsdp", bit), held[:, None], got[:, None], 1)
        held = pair.reshape((-1,) + shard.shape)
    return held


def halve(held, axis, bit, dim):
    mine = bit_at(axis, bit)
    if axis == "fsdp":
        pairs = held.reshape((held.shape[0] // 2, 2) + held.shape[1:])
        keep, send = pick(pairs, mine, 1), pick(pairs, 1 - mine, 1)
    else:
        half = held.shape[dim] // 2
        keep = lax.dynamic_slice_in_dim(held, mine * half, half, dim)
        send = lax.dynamic_slice_in_dim(held, (1 - mine) * half, half, dim)
    return add_low(keep, swap(send, axis, bit))


def add_low(a, b):
    return (a.astype(jnp.float32) + b.astype(jnp.float32)).astype(jnp.bfloat16)


def double(held, axis, bit, dim):
    return join(bit_at(axis, bit), held, swap(held, axis, bit), dim)


def doc_row(meta, base, length, docs):
    pos = base + lax.broadcasted_iota(jnp.int32, (1, length), 1)
    doc = jnp.full((1, length), -1, jnp.int32)
    for j in range(docs):
        doc = doc + (pos >= meta[2 + j]).astype(jnp.int32)
    return doc


def dot(a, b):
    return jnp.dot(a, b, preferred_element_type=jnp.float32)


def dot_t(a, b):
    return lax.dot_general(a, b, (((1,), (1,)), ((), ())), preferred_element_type=jnp.float32)


def fill_keys(meta, own, others, groups, parts, docs, rows, store):
    g, s = meta[0], meta[1]
    for j in range(groups):
        for e in range(parts):
            block = (g ^ j) * parts + lax.rem(s - e + parts, parts)
            if e == 0:
                key_t, value_t = own[j][1, 0], own[j][2, 0]
            else:
                ref = others[(e - 1) * groups + j]
                key_t, value_t = ref[0, 0], ref[1, 0]
            doc = doc_row(meta, block * rows, rows, docs)
            hot = (lax.broadcasted_iota(jnp.int32, (HD, rows), 0) == doc).astype(jnp.float32)
            keys = jnp.concatenate([key_t, hot.astype(jnp.bfloat16)], axis=0)
            store(block, keys, key_t, value_t)


def query_full(meta, query_t, j, groups, parts, docs, rows):
    g, s = meta[0], meta[1]
    block = (g ^ j) * parts + s
    doc = doc_row(meta, block * rows, rows, docs)
    shut = jnp.where(lax.broadcasted_iota(jnp.int32, (HD, rows), 0) == doc, 0.0, -BIG)
    return jnp.concatenate([query_t, shut.astype(jnp.bfloat16)], axis=0)


def attend_kernel(groups, parts, docs, rows, meta, *refs):
    own = refs[:groups]
    others = refs[groups : groups * parts]
    low_ref, wide_ref, log_ref, queries_ref, keys_ref, values_ref = refs[groups * parts :]
    coeff = LOG2E * HD**-0.5

    def store(block, keys, key_t, value_t):
        keys_ref[block] = keys.T
        values_ref[block] = value_t

    fill_keys(meta, own, others, groups, parts, docs, rows, store)
    for j in range(groups):
        queries_ref[j] = query_full(meta, own[j][0, 0], j, groups, parts, docs, rows)

    def one_slot(j, carry):
        full = queries_ref[j]

        def step(t, state):
            best, total, accum = state
            scores = dot(keys_ref[t], full)
            new_best = jnp.maximum(best, jnp.max(scores, axis=0, keepdims=True))
            weights = jnp.exp2((scores - new_best) * coeff)
            shrink = jnp.exp2((best - new_best) * coeff)
            total = total * shrink + jnp.sum(weights, axis=0, keepdims=True)
            accum = accum * shrink + dot(values_ref[t], weights.astype(jnp.bfloat16))
            return new_best, total, accum

        best, total, accum = lax.fori_loop(
            meta[2 + docs + 2 * j],
            meta[3 + docs + 2 * j],
            step,
            (
                jnp.full((1, rows), -BIG, jnp.float32),
                jnp.zeros((1, rows), jnp.float32),
                jnp.zeros((HD, rows), jnp.float32),
            ),
        )
        attended = accum / total
        at = pl.ds(pl.multiple_of(j * rows, rows), rows)
        wide_ref[0, :, at] = attended
        low_ref[0, :, at] = attended.astype(jnp.bfloat16)
        log_ref[0, :, at] = best * coeff + jnp.log2(total)
        return carry

    lax.fori_loop(0, groups, one_slot, 0)


def attend_back_kernel(groups, parts, docs, rows, meta, *refs):
    own = refs[:groups]
    others = refs[groups : groups * parts]
    grads = refs[groups * parts : groups * parts + groups]
    rest = refs[groups * parts + groups :]
    wide_ref, log_ref = rest[:2]
    dq_ref, mine_ref = rest[2:4]
    theirs = rest[4] if parts > 1 else None
    queries_ref, grads_ref, keys_ref, keys_t_ref, values_ref, accum_ref = rest[-6:]
    coeff = LOG2E * HD**-0.5

    def store(block, keys, key_t, value_t):
        keys_ref[block] = keys.T
        keys_t_ref[block] = key_t
        values_ref[block] = value_t.T

    fill_keys(meta, own, others, groups, parts, docs, rows, store)
    accum_ref[...] = jnp.zeros_like(accum_ref)
    for j in range(groups):
        queries_ref[j] = query_full(meta, own[j][0, 0], j, groups, parts, docs, rows)
        grads_ref[j] = grads[j][0]

    def one_slot(j, carry):
        at = pl.ds(pl.multiple_of(j * rows, rows), rows)
        full = queries_ref[j]
        grad_t = grads_ref[j]
        delta = jnp.sum(grad_t.astype(jnp.float32) * wide_ref[0, :, at], axis=0, keepdims=True)
        log_total = log_ref[0, :, at]
        blank = jnp.zeros((HD, rows), jnp.bfloat16)
        both = jnp.concatenate(
            [
                jnp.concatenate([full[:HD], blank], axis=1),
                jnp.concatenate([blank, grad_t], axis=1),
            ],
            axis=0,
        )

        def step(t, grad_query):
            scores = dot(keys_ref[t], full)
            probs = jnp.exp2(scores * coeff - log_total)
            d_probs = dot(values_ref[t], grad_t)
            d_scores = (probs * (d_probs - delta)).astype(jnp.bfloat16)
            joined = jnp.concatenate([d_scores, probs.astype(jnp.bfloat16)], axis=1)
            accum_ref[t] += dot_t(joined, both)
            return grad_query + dot(keys_t_ref[t], d_scores)

        grad_query = lax.fori_loop(
            meta[2 + docs + 2 * j],
            meta[3 + docs + 2 * j],
            step,
            jnp.zeros((HD, rows), jnp.float32),
        )
        dq_ref[:, at] = (grad_query * HD**-0.5).astype(jnp.bfloat16)
        return carry

    lax.fori_loop(0, groups, one_slot, 0)
    g, s = meta[0], meta[1]

    def finish(j, carry):
        at = pl.ds(pl.multiple_of(j * rows, rows), rows)
        for e in range(parts):
            terms = accum_ref[(g ^ j) * parts + lax.rem(s - e + parts, parts)].T
            d_key = terms[:HD] * HD**-0.5
            d_value = terms[HD:]
            if e == 0:
                mine_ref[0, :, at] = d_key
                mine_ref[1, :, at] = d_value
            else:
                theirs[e - 1, 0, :, at] = d_key.astype(jnp.bfloat16)
                theirs[e - 1, 1, :, at] = d_value.astype(jnp.bfloat16)
        return carry

    lax.fori_loop(0, groups, finish, 0)


def head_block(head, *shape):
    dims = tuple(1 if n is None else n for n in shape)
    where = shape.index(None)

    def at(h, meta):
        chosen = h if head is None else head
        return tuple(chosen if i == where else 0 for i in range(len(dims)))

    return pl.BlockSpec(dims, at)


def attend(meta, own, others, groups, parts, docs, rows, heads):
    tiles = groups * parts
    tokens = groups * rows
    block = partial(head_block, None)
    grid_spec = pltpu.PrefetchScalarGridSpec(
        num_scalar_prefetch=1,
        grid=(heads,),
        in_specs=[block(3, None, HD, rows)] * groups
        + [block(2, None, HD, rows)] * (groups * (parts - 1)),
        out_specs=[block(None, HD, tokens), block(None, HD, tokens), block(None, 1, tokens)],
        scratch_shapes=[
            pltpu.VMEM((groups, 2 * HD, rows), jnp.bfloat16),
            pltpu.VMEM((tiles, rows, 2 * HD), jnp.bfloat16),
            pltpu.VMEM((tiles, HD, rows), jnp.bfloat16),
        ],
    )
    return pl.pallas_call(
        partial(attend_kernel, groups, parts, docs, rows),
        grid_spec=grid_spec,
        out_shape=[
            jax.ShapeDtypeStruct((heads, HD, tokens), jnp.bfloat16),
            jax.ShapeDtypeStruct((heads, HD, tokens), jnp.float32),
            jax.ShapeDtypeStruct((heads, 1, tokens), jnp.float32),
        ],
        cost_estimate=pl.CostEstimate(
            flops=KERNEL_FLOPS * 2 * heads,
            transcendentals=0,
            bytes_accessed=KERNEL_BYTES * heads,
        ),
        name="attend",
    )(meta, *own, *others)


def attend_back(head, meta, own, others, grads, wide, log_total, groups, parts, docs, rows):
    tiles = groups * parts
    tokens = groups * rows
    block = partial(head_block, head)
    plain = lambda *dims: pl.BlockSpec(dims, lambda h, meta: (0,) * len(dims))
    out_specs = [plain(HD, tokens), plain(2, HD, tokens)]
    out_shape = [
        jax.ShapeDtypeStruct((HD, tokens), jnp.bfloat16),
        jax.ShapeDtypeStruct((2, HD, tokens), jnp.float32),
    ]
    if parts > 1:
        out_specs.append(plain(parts - 1, 2, HD, tokens))
        out_shape.append(jax.ShapeDtypeStruct((parts - 1, 2, HD, tokens), jnp.bfloat16))
    grid_spec = pltpu.PrefetchScalarGridSpec(
        num_scalar_prefetch=1,
        grid=(1,),
        in_specs=[block(3, None, HD, rows)] * groups
        + [block(2, None, HD, rows)] * (groups * (parts - 1))
        + [block(None, HD, rows)] * groups
        + [block(None, HD, tokens), block(None, 1, tokens)],
        out_specs=out_specs,
        scratch_shapes=[
            pltpu.VMEM((groups, 2 * HD, rows), jnp.bfloat16),
            pltpu.VMEM((groups, HD, rows), jnp.bfloat16),
            pltpu.VMEM((tiles, rows, 2 * HD), jnp.bfloat16),
            pltpu.VMEM((tiles, HD, rows), jnp.bfloat16),
            pltpu.VMEM((tiles, rows, HD), jnp.bfloat16),
            pltpu.VMEM((tiles, rows, 2 * HD), jnp.float32),
        ],
    )
    return pl.pallas_call(
        partial(attend_back_kernel, groups, parts, docs, rows),
        grid_spec=grid_spec,
        out_shape=out_shape,
        cost_estimate=pl.CostEstimate(
            flops=KERNEL_FLOPS * 5, transcendentals=0, bytes_accessed=KERNEL_BYTES
        ),
        name="attend_back",
    )(meta, *own, *others, *grads, wide, log_total)


ERFC = (
    -1.26551223, 1.00002368, 0.37409196, 0.09678418, -0.18628806,
    0.27886807, -1.13520398, 1.48851587, -0.82215223, 0.17087277,
)


def normal_terms(v):
    z = jnp.abs(v) * (0.5**0.5)
    t = 1.0 / (1.0 + 0.5 * z)
    poly = jnp.full_like(t, ERFC[-1])
    for term in reversed(ERFC[:-1]):
        poly = poly * t + term
    square = z * z
    tail = 0.5 * t * jnp.exp(poly - square)
    below = jnp.where(v < 0, tail, 1.0 - tail)
    return below, jnp.exp(-square) * (2.0 * math.pi) ** -0.5


def normed(resid):
    centred = resid - jnp.mean(resid, axis=-1, keepdims=True)
    spread = jnp.mean(centred * centred, axis=-1, keepdims=True)
    scale = lax.rsqrt(spread + EPSILON)
    return centred * scale, scale


def norm_back(grad, gain, unit, scale):
    e = grad * gain
    inner = jnp.mean(e * unit, axis=-1, keepdims=True)
    return (e - jnp.mean(e, axis=-1, keepdims=True) - unit * inner) * scale


def over_blocks(count, aligned, step, value):
    if aligned:
        return lax.fori_loop(0, count, step, value)
    for i in range(count):
        value = step(i, value)
    return value


def feed_kernel(
    tokens_ref,
    attended_ref,
    cot_ref,
    out_ref,
    in_ref,
    back_ref,
    vec_ref,
    in_bias_ref,
    result_ref,
    d_resid1_ref,
    d_attended_ref,
    hidden_ref,
    act_ref,
    d_ffn_ref,
    d_pre_ref,
    d_branch_ref,
    sums_ref,
    in_sums_ref,
    slope_ref,
):
    f32, bf16 = jnp.float32, jnp.bfloat16
    out_shift, gain_one, shift_one = vec_ref[2:3], vec_ref[3:4], vec_ref[4:5]
    back_shift, gain_two, shift_two = vec_ref[5:6], vec_ref[6:7], vec_ref[7:8]

    @pl.when(pl.program_id(0) == 0)
    def _():
        sums_ref[...] = jnp.zeros_like(sums_ref)
        in_sums_ref[...] = jnp.zeros_like(in_sums_ref)

    total = lambda a: jnp.sum(a, axis=0, keepdims=True)
    width = out_ref.shape[0]
    step = math.gcd(width, 256)
    part = lambda i: pl.ds(pl.multiple_of(i * step, step), step)
    resid1 = lax.fori_loop(
        0,
        width // step,
        lambda i, value: value + dot(attended_ref[part(i), :].T, out_ref[part(i), :]),
        tokens_ref[...].astype(f32) + out_shift,
    )
    unit1, scale1 = normed(resid1)
    hidden = unit1 * gain_one + shift_one
    hidden_low = hidden.astype(bf16)
    count, unused, shard = hidden_ref.shape
    for i in range(count):
        hidden_ref[i] = hidden_low[:, i * shard : (i + 1) * shard]
    resid2 = hidden + back_shift
    blocks, unused, size = act_ref.shape
    pieces = size // 256 if size % 256 == 0 else 1
    piece = size // pieces
    aligned = piece % 128 == 0
    columns = lambda i: pl.ds(pl.multiple_of(i * piece, piece) if aligned else i * piece, piece)

    def forward(i, resid2):
        cols = columns(i)
        pre = dot(hidden_low, in_ref[:, cols]) + in_bias_ref[:, cols]
        below, density = normal_terms(pre)
        act = (pre * below).astype(bf16)
        act_ref[i // pieces, :, columns(i % pieces)] = act
        slope_ref[i] = below + pre * density
        return resid2 + dot(act, back_ref[cols, :])

    resid2 = over_blocks(blocks * pieces, aligned, forward, hidden + back_shift)
    unit2, scale2 = normed(resid2)
    result_ref[...] = (unit2 * gain_two + shift_two).astype(bf16)
    cot = cot_ref[...].astype(f32)
    d_resid2 = norm_back(cot, gain_two, unit2, scale2)
    d_ffn = d_resid2.astype(bf16)
    d_ffn_ref[...] = d_ffn

    def backward(i, d_hidden):
        cols = columns(i)
        d_act = dot_t(d_ffn, back_ref[cols, :])
        d_pre = (d_act * slope_ref[i]).astype(bf16)
        d_pre_ref[:, cols] = d_pre
        in_sums_ref[:, cols] += total(d_pre.astype(f32))
        return d_hidden + dot_t(d_pre, in_ref[:, cols])

    d_hidden = over_blocks(blocks * pieces, aligned, backward, d_resid2)
    d_resid1 = norm_back(d_hidden, gain_one, unit1, scale1)
    d_resid1_ref[...] = d_resid1
    d_branch = d_resid1.astype(bf16)
    d_branch_ref[...] = d_branch

    def attended_step(i, carry):
        d_attended_ref[part(i), :] = dot_t(out_ref[part(i), :], d_branch).astype(bf16)
        return carry

    lax.fori_loop(0, width // step, attended_step, 0)
    sums_ref[...] += jnp.concatenate(
        [
            total(d_branch.astype(f32)),
            total(d_hidden * unit1),
            total(d_hidden),
            total(d_ffn.astype(f32)),
            total(cot * unit2),
            total(cot),
            jnp.zeros((2, cot.shape[1]), f32),
        ],
        axis=0,
    )


def feed_forward(fsdp, tokens, attended_t, cotangent, out_full, in_full, back_full, vectors, in_shift):
    f32, bf16 = jnp.float32, jnp.bfloat16
    rows, model = tokens.shape
    inner = in_full.shape[1]
    tile = math.gcd(rows, 256)
    pieces = inner // fsdp // 256 if (inner // fsdp) % 256 == 0 else 1
    by_rows = lambda n: pl.BlockSpec((tile, n), lambda i: (i, 0))
    by_cols = lambda n: pl.BlockSpec((n, tile), lambda i: (0, i))
    blocks = lambda n: pl.BlockSpec((fsdp, tile, n // fsdp), lambda i: (0, i, 0))
    fixed = lambda m, n: pl.BlockSpec((m, n), lambda i: (0, 0))
    shape = jax.ShapeDtypeStruct
    return pl.pallas_call(
        feed_kernel,
        grid=(rows // tile,),
        in_specs=[
            by_rows(model), by_cols(model), by_rows(model), fixed(model, model),
            fixed(model, inner), fixed(inner, model), fixed(8, model), fixed(1, inner),
        ],
        out_specs=[
            by_rows(model), by_rows(model), by_cols(model), blocks(model), blocks(inner),
            by_rows(model), by_rows(inner), by_rows(model), fixed(8, model), fixed(1, inner),
        ],
        out_shape=[
            shape((rows, model), bf16), shape((rows, model), f32), shape((model, rows), bf16),
            shape((fsdp, rows, model // fsdp), bf16), shape((fsdp, rows, inner // fsdp), bf16),
            shape((rows, model), bf16),
            shape((rows, inner), bf16), shape((rows, model), bf16), shape((8, model), f32),
            shape((1, inner), f32),
        ],
        scratch_shapes=[pltpu.VMEM((fsdp * pieces, tile, inner // (fsdp * pieces)), f32)],
        cost_estimate=pl.CostEstimate(
            flops=rows * model * (8 * inner + 4 * model), transcendentals=0, bytes_accessed=30_000_000
        ),
        name="feed_forward",
    )(tokens, attended_t, cotangent, out_full, in_full, back_full, vectors, in_shift)


def weight_grad_kernel(which, *refs):
    ins, (d_ffn, d_pre, d_branch), outs = refs[:8], refs[8:11], refs[11:]
    bf16 = jnp.bfloat16
    first, second = ins[0].shape[2], ins[2].shape[0]
    size = math.gcd(first, 256)
    wide = math.gcd(d_pre.shape[1], 768)
    at = lambda i, n: pl.ds(i * n if isinstance(i, int) else pl.multiple_of(i * n, n), n)

    def rows_step(i, carry):
        for side in range(2):
            outs[2 * side][0, at(i, size)] = dot(ins[4 * side][0, :, at(i, size)].T, d_ffn[...]).astype(bf16)
        return carry

    over_blocks(first // size, size % 128 == 0, rows_step, 0)
    turned = [ins[4 * side + 1][0].T for side in range(2)]

    def columns_step(i, carry):
        for side in range(2):
            outs[2 * side + 1][0, :, at(i, wide)] = dot(turned[side], d_pre[:, at(i, wide)]).astype(bf16)
        return carry

    over_blocks(d_pre.shape[1] // wide, True, columns_step, 0)
    for side in range(2):
        lower = outs[2 * side]
        lower[0, first : first + second] = dot(ins[4 * side + 2][...], d_branch[...]).astype(bf16)
        lower[0, first + second :] = ins[4 * side + 3][0].astype(bf16)


def weight_grads(which, act, hidden, attended_t, line, d_ffn, d_pre, d_branch):
    fsdp, rows, inner_shard = act.shape
    shard = hidden.shape[2]
    model, inner = d_ffn.shape[1], d_pre.shape[1]
    line_rows = line.shape[1]
    tall = inner_shard + shard + line_rows
    half = fsdp // 2
    in_specs = []
    for side in range(2):
        block = lambda i, w, side=side: 2 * i + w[side]
        in_specs += [
            pl.BlockSpec((1, rows, inner_shard), lambda i, w, b=block: (b(i, w), 0, 0)),
            pl.BlockSpec((1, rows, shard), lambda i, w, b=block: (b(i, w), 0, 0)),
            pl.BlockSpec((shard, rows), lambda i, w, b=block: (b(i, w), 0)),
            pl.BlockSpec((1, line_rows, model), lambda i, w, b=block: (b(i, w), 0, 0)),
        ]
    in_specs += [pl.BlockSpec((rows, n), lambda i, w: (0, 0)) for n in (model, inner, model)]
    out = [(tall, model), (shard, inner)] * 2
    return pl.pallas_call(
        weight_grad_kernel,
        grid_spec=pltpu.PrefetchScalarGridSpec(
            num_scalar_prefetch=1,
            grid=(half,),
            in_specs=in_specs,
            out_specs=[pl.BlockSpec((1,) + o, lambda i, w: (i, 0, 0)) for o in out],
        ),
        out_shape=[jax.ShapeDtypeStruct((half,) + o, jnp.bfloat16) for o in out],
        cost_estimate=pl.CostEstimate(
            flops=2 * rows * model * (2 * inner + model), transcendentals=0, bytes_accessed=25_000_000
        ),
        name="weight_grads",
    )(which, act, hidden, attended_t, line, act, hidden, attended_t, line, d_ffn, d_pre, d_branch)


def qkv_grad_kernel(fsdp, which, *refs):
    slots, (d_qkv, send, keep, total) = refs[:-4], refs[-4:]
    rows = slots[0].shape[0]
    shard = send.shape[1] - PAD
    size = math.gcd(total.shape[0], 256)

    def step(i, carry):
        at = pl.ds(pl.multiple_of(i * size, size), size)
        value = None
        for j, slot in enumerate(slots):
            term = dot_t(slot[:, at].T, d_qkv[:, j * rows : (j + 1) * rows])
            value = term if value is None else value + term
        total[at] = value
        return carry

    lax.fori_loop(0, total.shape[0] // size, step, 0)
    ones = jnp.ones((PAD, d_qkv.shape[1]), jnp.bfloat16)
    sums = dot_t(ones, d_qkv[...]).astype(jnp.bfloat16)
    for side, ref in enumerate((send, keep)):
        for i in range(fsdp // 2):
            at = pl.multiple_of((2 * i + which[side]) * shard, math.gcd(shard, 64))
            ref[i, :shard] = total[pl.ds(at, shard), :].astype(jnp.bfloat16)
            ref[i, shard:] = sums


def qkv_grads(which, slots, d_qkv_t, fsdp):
    rows, model = slots[0].shape
    width = d_qkv_t.shape[0]
    out = (fsdp // 2, model // fsdp + PAD, width)
    fixed = lambda dims: pl.BlockSpec(dims, lambda i, w: (0,) * len(dims))
    return pl.pallas_call(
        partial(qkv_grad_kernel, fsdp),
        grid_spec=pltpu.PrefetchScalarGridSpec(
            num_scalar_prefetch=1,
            grid=(1,),
            in_specs=[fixed((rows, model))] * len(slots) + [fixed(d_qkv_t.shape)],
            out_specs=[fixed(out)] * 2,
            scratch_shapes=[pltpu.VMEM((model, width), jnp.float32)],
        ),
        out_shape=[jax.ShapeDtypeStruct(out, jnp.bfloat16)] * 2,
        cost_estimate=pl.CostEstimate(
            flops=2 * rows * len(slots) * model * width, transcendentals=0, bytes_accessed=8_000_000
        ),
        name="qkv_grads",
    )(which, *slots, d_qkv_t)


def body(
    inputs,
    doc_starts,
    qkv_weight,
    query_bias,
    value_bias,
    out_weight,
    out_bias,
    norm1_gain,
    norm1_bias,
    in_weight,
    in_bias,
    back_weight,
    back_bias,
    norm2_gain,
    norm2_bias,
    cotangent,
):
    bf16, f32 = jnp.bfloat16, jnp.float32
    tokens = inputs[0]
    rows, model = tokens.shape
    starts = doc_starts[0]
    docs = starts.shape[0]
    ctx = lax.axis_size("ctx")
    fsdp = lax.axis_size("fsdp")
    groups = math.gcd(H, ctx)
    parts = ctx // groups
    heads = H // groups
    span = heads * HD
    width = 3 * span
    index = lax.axis_index("ctx")
    g, s = index // parts, index % parts
    f = lax.axis_index("fsdp")
    shard = model // fsdp

    slots = gather_groups(tokens, groups, parts)

    own_cols = jnp.concatenate(
        [lax.dynamic_slice_in_dim(qkv_weight, i * model + g * span, span, 1) for i in range(3)], axis=1
    )
    small = jnp.concatenate(
        [
            query_bias, value_bias, out_bias, norm1_gain, norm1_bias,
            back_bias, norm2_gain, norm2_bias, in_bias,
        ]
    )
    count = small.shape[0]
    extra = -(-count // (width * PAD)) * PAD
    small_block = jnp.pad(small, (0, extra * width - count)).reshape(extra, width)
    first = jnp.concatenate([own_cols, small_block], axis=0)
    first_top = gather_top(first)
    first_top, out_held, in_held, back_held = together(
        first_top, out_weight, in_weight, back_weight
    )
    out_top, in_top, back_top = gather_top(out_held), gather_top(in_held), gather_top(back_held)
    first = gather_rest(first, first_top)
    own_weight = first[:, :shard].reshape(model, width)
    flat = first[:, shard:].reshape(fsdp, extra * width)[:, :count].astype(f32)
    vectors = flat[:, : 8 * shard].reshape(fsdp, 8, shard).transpose(1, 0, 2).reshape(8, model)
    query_shift, value_shift = vectors[0], vectors[1]
    in_shift = flat[:, 8 * shard :].reshape(1, -1)

    zero = jnp.zeros((span,), f32)
    own_shift = jnp.concatenate(
        [
            lax.dynamic_slice(query_shift, (g * span,), (span,)),
            zero,
            lax.dynamic_slice(value_shift, (g * span,), (span,)),
        ]
    )
    own, others = [], []
    for slot in slots:
        projected = lax.dot_general(
            own_weight, slot, (((0,), (1,)), ((), ())), preferred_element_type=f32
        )
        low = (projected + own_shift[:, None]).astype(bf16).reshape(3, heads, HD, rows)
        own.append(low)
    for e in range(1, parts):
        for low in own:
            others.append(part_shift(low[1:], groups, parts, e))
    if parts > 1:
        in_top, others[0] = together(in_top, others[0])

    bounds = jnp.concatenate([starts, jnp.full((1,), ctx * rows, jnp.int32)])
    base = (g ^ jnp.arange(groups, dtype=jnp.int32)) * parts + s
    heads_at = base * rows
    tails_at = heads_at + rows - 1
    low_edge = jnp.max(jnp.where(starts[None] <= heads_at[:, None], starts[None], 0), axis=1)
    high_edge = jnp.min(
        jnp.where(bounds[None] > tails_at[:, None], bounds[None], ctx * rows), axis=1
    )
    ranges = jnp.stack([low_edge // rows, (high_edge + rows - 1) // rows], axis=1).reshape(-1)
    meta = jnp.concatenate([jnp.stack([g, s]).astype(jnp.int32), starts, ranges.astype(jnp.int32)])

    out_full = gather_rest(out_weight, out_top).reshape(model, model)
    in_full = gather_rest(in_weight, in_top).reshape(model, -1)
    meta, out_full, in_full = together(meta, out_full, in_full)
    low, wide, log_total = attend(meta, own, others, groups, parts, docs, rows, heads)
    attended_t = jnp.zeros((groups * span, rows), bf16)
    turned = []
    for j in range(groups):
        piece = low[:, :, j * rows : (j + 1) * rows]
        turned.append(ctx_swap(piece, groups, parts, j) if j else piece)
    for j, piece in enumerate(together(*turned)):
        attended_t = lax.dynamic_update_slice(
            attended_t, piece.reshape(span, rows), ((g ^ j) * span, 0)
        )
    back_full = gather_rest(back_weight, back_top).reshape(-1, model)

    (
        result, d_resid1, d_attended_t, hidden_low, act_low, d_ffn_low, d_pre_low, d_branch_low,
        sums, in_sums,
    ) = feed_forward(
        fsdp, tokens, attended_t, cotangent[0], out_full, in_full, back_full, vectors, in_shift
    )
    grads = []
    for j in range(groups):
        part = lax.dynamic_slice(d_attended_t, ((g ^ j) * span, 0), (span, rows))
        part = part.reshape(heads, HD, rows)
        grads.append(ctx_swap(part, groups, parts, j) if j else part)

    inner = in_full.shape[1]
    inner_shard = in_bias.shape[0]
    line = jnp.concatenate(
        [sums[:6].reshape(6, fsdp, shard).transpose(1, 0, 2).reshape(fsdp, -1), in_sums.reshape(fsdp, -1)],
        axis=1,
    )
    line_rows = -(inner_shard + shard) % 64 or 64
    line = jnp.pad(line, ((0, 0), (0, line_rows * model - line.shape[1])))
    line = line.reshape(fsdp, line_rows, model)
    mine = bit_at("fsdp", 0)
    which = jnp.stack([1 - mine, mine]).astype(jnp.int32)
    lower_send, upper_send, lower, upper = weight_grads(
        which, act_low, hidden_low, attended_t, line, d_ffn_low, d_pre_low, d_branch_low
    )
    lower = add_low(lower, swap(lower_send, "fsdp", 0))
    upper = add_low(upper, swap(upper_send, "fsdp", 0))
    fsdp_bits, ctx_bits = range(bits_of("fsdp")), range(bits_of("ctx"))
    chunks = inner // (2 * model)

    def pair_step(i, state):
        lower, upper = state
        lower_steps = [("fsdp", b) for b in fsdp_bits[1:]] + [("ctx", 0)]
        upper_steps = [("ctx", 0)] + [("fsdp", b) for b in fsdp_bits[1:]]
        return halve(lower, *lower_steps[i], 1), halve(upper, *upper_steps[i], 2)

    def merge(state):
        lower, upper = state
        return (
            jnp.concatenate(
                [lower[0]] + [upper[0, :, c * model : (c + 1) * model] for c in range(chunks)], axis=0
            ),
        )

    steps = [partial(pair_step, i) for i in range(len(fsdp_bits))]
    last = steps.pop()
    steps.append(lambda state: merge(last(state)))
    for bit in ctx_bits[1:-1]:
        steps.append(lambda state, bit=bit: (halve(state[0], "ctx", bit, 0),))
    state = (lower, upper)

    pieces = []
    held, theirs = None, None

    def settle(dq, dkv, theirs):
        for other in theirs:
            dkv = dkv + other.astype(f32)
        pieces.append(jnp.concatenate([dq[None], dkv.astype(bf16)], axis=0))

    def send(piece):
        parts_of = []
        for j in range(groups):
            part = piece[..., j * rows : (j + 1) * rows]
            parts_of.append(ctx_swap(part, groups, parts, j) if j else part)
        return parts_of

    for head in range(heads):
        meta, *state = together(meta, *state)
        flying = steps.pop(0)(state) if steps else state
        dq, dkv, *rest = attend_back(
            head, meta, own, others, grads, wide, log_total, groups, parts, docs, rows
        )
        if head:
            dq, dkv, *landed = together(dq, dkv, *rest, *flying)
            rest, state = landed[: len(rest)], landed[len(rest) :]
            dq, *theirs = together(dq, *theirs)
            settle(*held, theirs)
        else:
            state = flying
        if head == 1:
            early = send(pieces[0])
            dq, qkv_held = together(dq, qkv_weight)
            qkv_top = gather_top(qkv_held)
        elif head == 2:
            middle = send(pieces[1])
            dq, *early = together(dq, *early)
        held = (dq, dkv)
        theirs = [part_shift(rest[0][e - 1], groups, parts, -e) for e in range(1, parts)]
    settle(*held, theirs)
    for advance in steps:
        state = advance(state)
    other = swap(state[0], "ctx", ctx_bits[-1])
    d_qkv_t = jnp.stack(pieces, axis=1).reshape(width, groups * rows)
    qkv_send, qkv_sum = qkv_grads(which, slots, d_qkv_t, fsdp)
    other, qkv_send, qkv_sum, qkv_top, *middle = together(
        other, qkv_send, qkv_sum, qkv_top, *middle
    )
    qkv_full = gather_rest(qkv_held, qkv_top).reshape(model, 3 * model)
    merged = add_low(state[0], other)
    late, merged = together(pieces[2], merged)
    for bit in reversed(ctx_bits[1:-1]):
        merged = double(merged, "ctx", bit, 0)
    qkv_sum = add_low(qkv_sum, swap(qkv_send, "fsdp", 0))
    wide_sum = qkv_sum.astype(f32)
    for e in range(1, parts):
        wide_sum = wide_sum + part_shift(qkv_sum, groups, parts, e).astype(f32)
    qkv_sum, merged, qkv_full = together(wide_sum.astype(bf16), merged, qkv_full)
    other = swap(merged, "ctx", 0)
    late = send(late)
    for bit in fsdp_bits[1:]:
        qkv_sum = halve(qkv_sum, "fsdp", bit, 1)
    qkv_low = qkv_sum[0]
    by_group = jnp.zeros((groups,) + qkv_low.shape, bf16)
    turns = [ctx_swap(qkv_low, groups, parts, j) if j else qkv_low for j in range(groups)]
    other, *late = together(other, *late)
    turns = list(together(*turns))
    for j, piece in enumerate(turns):
        by_group = lax.dynamic_update_slice(by_group, piece[None], (g ^ j, 0, 0))
    natural = jnp.concatenate(
        [by_group[b, :, i * span : (i + 1) * span] for i in range(3) for b in range(groups)], axis=1
    ).astype(f32)
    grad_qkv_shard = natural[:shard]
    bias_line = natural[shard]
    grad_query_shift = lax.dynamic_slice(bias_line, (f * shard,), (shard,))
    grad_value_shift = lax.dynamic_slice(bias_line, (2 * model + f * shard,), (shard,))

    natural = jnp.zeros((3, groups, heads, HD, rows), bf16)
    for j in range(groups):
        part = jnp.stack([early[j], middle[j], late[j]], axis=1)[:, None]
        natural = lax.dynamic_update_slice(natural, part, (0, g ^ j, 0, 0, 0))
    input_grad = d_resid1 + lax.dot_general(
        natural.reshape(3 * model, rows),
        qkv_full,
        (((0,), (1,)), ((), ())),
        preferred_element_type=f32,
    )

    lower_rows = (inner_shard + shard + line_rows) // 2
    lower = join(bit_at("ctx", 0), merged[:lower_rows], other[:lower_rows], 0)
    wide_half = lambda m: jnp.concatenate(
        [m[lower_rows + c * shard : lower_rows + (c + 1) * shard] for c in range(chunks)], axis=1
    )
    upper = join(bit_at("ctx", 0), wide_half(merged), wide_half(other), 1)

    ends = inner_shard + shard
    flat = lower[ends:].reshape(-1).astype(f32)
    offsets = lambda i: flat[i * shard : (i + 1) * shard]
    return (
        result[None],
        input_grad[None],
        grad_qkv_shard,
        grad_query_shift,
        grad_value_shift,
        lower[inner_shard:ends].astype(f32),
        offsets(0),
        offsets(1),
        offsets(2),
        upper.astype(f32),
        flat[6 * shard : 6 * shard + inner_shard],
        lower[:inner_shard].astype(f32),
        offsets(3),
        offsets(4),
        offsets(5),
    )


def solution(mesh):
    rows, one = P("fsdp", None), P("fsdp")
    whole = P("fsdp", "ctx", None)
    return jax.shard_map(
        body,
        mesh=mesh,
        in_specs=(
            whole, rows, rows, one, one, rows, one, one, one, rows, one, rows, one, one, one, whole,
        ),
        out_specs=(
            whole, whole, rows, one, one, rows, one, one, one, rows, one, rows, one, one, one,
        ),
        check_vma=False,
    )
```

```python
from functools import partial
import math

import jax
import jax.numpy as jnp
from jax import lax
from jax.experimental import pallas as pl
from jax.experimental.pallas import tpu as pltpu
from jax.sharding import PartitionSpec as P

H = 12
HD = 64
EPSILON = 1e-05
BIG = 2.0**100
LOG2E = 1.4426950408889634
PAD = 16
KERNEL_FLOPS = 3_000_000_000
KERNEL_BYTES = 20_000_000


def ctx_swap(array, groups, parts, flip):
    pairs = []
    for g in range(groups):
        for s in range(parts):
            pairs.append((g * parts + s, (g ^ flip) * parts + s))
    return lax.ppermute(array, "ctx", pairs)


def part_shift(array, groups, parts, by):
    pairs = []
    for g in range(groups):
        for s in range(parts):
            pairs.append((g * parts + s, g * parts + (s + by) % parts))
    return lax.ppermute(array, "ctx", pairs)


def gather_groups(array, groups, parts):
    return [array] + [ctx_swap(array, groups, parts, i) for i in range(1, groups)]


def swap(array, axis, bit):
    size = lax.axis_size(axis)
    return lax.ppermute(array, axis, [(i, i ^ (1 << bit)) for i in range(size)])


def bits_of(axis):
    return lax.axis_size(axis).bit_length() - 1


def bit_at(axis, bit):
    return (lax.axis_index(axis) >> bit) & 1


def pick(array, which, dim):
    return lax.dynamic_index_in_dim(array, which, dim, keepdims=False)


def together(*values):
    return lax.optimization_barrier(values)


def join(mine, own, other, dim):
    return jnp.where(
        mine == 0,
        jnp.concatenate([own, other], axis=dim),
        jnp.concatenate([other, own], axis=dim),
    )


def gather_top(shard):
    return swap(shard, "fsdp", bits_of("fsdp") - 1)


def gather_rest(shard, other):
    top = bits_of("fsdp") - 1
    held = join(bit_at("fsdp", top), shard[None], other[None], 0)
    for bit in reversed(range(top)):
        got = swap(held, "fsdp", bit)
        pair = join(bit_at("fsdp", bit), held[:, None], got[:, None], 1)
        held = pair.reshape((-1,) + shard.shape)
    return held


def halve(held, axis, bit, dim):
    mine = bit_at(axis, bit)
    if axis == "fsdp":
        pairs = held.reshape((held.shape[0] // 2, 2) + held.shape[1:])
        keep, send = pick(pairs, mine, 1), pick(pairs, 1 - mine, 1)
    else:
        half = held.shape[dim] // 2
        keep = lax.dynamic_slice_in_dim(held, mine * half, half, dim)
        send = lax.dynamic_slice_in_dim(held, (1 - mine) * half, half, dim)
    return add_low(keep, swap(send, axis, bit))


def add_low(a, b):
    return (a.astype(jnp.float32) + b.astype(jnp.float32)).astype(jnp.bfloat16)


def double(held, axis, bit, dim):
    return join(bit_at(axis, bit), held, swap(held, axis, bit), dim)


def doc_row(meta, base, length, docs):
    pos = base + lax.broadcasted_iota(jnp.int32, (1, length), 1)
    doc = jnp.full((1, length), -1, jnp.int32)
    for j in range(docs):
        doc = doc + (pos >= meta[2 + j]).astype(jnp.int32)
    return doc


def dot(a, b):
    return jnp.dot(a, b, preferred_element_type=jnp.float32)


def dot_t(a, b):
    return lax.dot_general(a, b, (((1,), (1,)), ((), ())), preferred_element_type=jnp.float32)


def fill_keys(meta, own, others, groups, parts, docs, rows, store):
    g, s = meta[0], meta[1]
    for j in range(groups):
        for e in range(parts):
            block = (g ^ j) * parts + lax.rem(s - e + parts, parts)
            if e == 0:
                key_t, value_t = own[j][1, 0], own[j][2, 0]
            else:
                ref = others[(e - 1) * groups + j]
                key_t, value_t = ref[0, 0], ref[1, 0]
            doc = doc_row(meta, block * rows, rows, docs)
            hot = (lax.broadcasted_iota(jnp.int32, (HD, rows), 0) == doc).astype(jnp.float32)
            keys = jnp.concatenate([key_t, hot.astype(jnp.bfloat16)], axis=0)
            store(block, keys, key_t, value_t)


def query_full(meta, query_t, j, groups, parts, docs, rows):
    g, s = meta[0], meta[1]
    block = (g ^ j) * parts + s
    doc = doc_row(meta, block * rows, rows, docs)
    shut = jnp.where(lax.broadcasted_iota(jnp.int32, (HD, rows), 0) == doc, 0.0, -BIG)
    return jnp.concatenate([query_t, shut.astype(jnp.bfloat16)], axis=0)


def attend_kernel(groups, parts, docs, rows, meta, *refs):
    own = refs[:groups]
    others = refs[groups : groups * parts]
    low_ref, wide_ref, log_ref, queries_ref, keys_ref, values_ref = refs[groups * parts :]
    coeff = LOG2E * HD**-0.5

    def store(block, keys, key_t, value_t):
        keys_ref[block] = keys.T
        values_ref[block] = value_t

    fill_keys(meta, own, others, groups, parts, docs, rows, store)
    for j in range(groups):
        queries_ref[j] = query_full(meta, own[j][0, 0], j, groups, parts, docs, rows)

    def one_slot(j, carry):
        full = queries_ref[j]

        def step(t, state):
            best, total, accum = state
            scores = dot(keys_ref[t], full)
            new_best = jnp.maximum(best, jnp.max(scores, axis=0, keepdims=True))
            weights = jnp.exp2((scores - new_best) * coeff)
            shrink = jnp.exp2((best - new_best) * coeff)
            total = total * shrink + jnp.sum(weights, axis=0, keepdims=True)
            accum = accum * shrink + dot(values_ref[t], weights.astype(jnp.bfloat16))
            return new_best, total, accum

        best, total, accum = lax.fori_loop(
            meta[2 + docs + 2 * j],
            meta[3 + docs + 2 * j],
            step,
            (
                jnp.full((1, rows), -BIG, jnp.float32),
                jnp.zeros((1, rows), jnp.float32),
                jnp.zeros((HD, rows), jnp.float32),
            ),
        )
        attended = accum / total
        at = pl.ds(pl.multiple_of(j * rows, rows), rows)
        wide_ref[0, :, at] = attended
        low_ref[0, :, at] = attended.astype(jnp.bfloat16)
        log_ref[0, :, at] = best * coeff + jnp.log2(total)
        return carry

    lax.fori_loop(0, groups, one_slot, 0)


def attend_back_kernel(groups, parts, docs, rows, meta, *refs):
    own = refs[:groups]
    others = refs[groups : groups * parts]
    grads = refs[groups * parts : groups * parts + groups]
    rest = refs[groups * parts + groups :]
    wide_ref, log_ref = rest[:2]
    dq_ref, mine_ref = rest[2:4]
    theirs = rest[4] if parts > 1 else None
    queries_ref, grads_ref, keys_ref, keys_t_ref, values_ref, accum_ref = rest[-6:]
    coeff = LOG2E * HD**-0.5

    def store(block, keys, key_t, value_t):
        keys_ref[block] = keys.T
        keys_t_ref[block] = key_t
        values_ref[block] = value_t.T

    fill_keys(meta, own, others, groups, parts, docs, rows, store)
    accum_ref[...] = jnp.zeros_like(accum_ref)
    for j in range(groups):
        queries_ref[j] = query_full(meta, own[j][0, 0], j, groups, parts, docs, rows)
        grads_ref[j] = grads[j][0]

    def one_slot(j, carry):
        at = pl.ds(pl.multiple_of(j * rows, rows), rows)
        full = queries_ref[j]
        grad_t = grads_ref[j]
        delta = jnp.sum(grad_t.astype(jnp.float32) * wide_ref[0, :, at], axis=0, keepdims=True)
        log_total = log_ref[0, :, at]
        blank = jnp.zeros((HD, rows), jnp.bfloat16)
        both = jnp.concatenate(
            [
                jnp.concatenate([full[:HD], blank], axis=1),
                jnp.concatenate([blank, grad_t], axis=1),
            ],
            axis=0,
        )

        def step(t, grad_query):
            scores = dot(keys_ref[t], full)
            probs = jnp.exp2(scores * coeff - log_total)
            d_probs = dot(values_ref[t], grad_t)
            d_scores = (probs * (d_probs - delta)).astype(jnp.bfloat16)
            joined = jnp.concatenate([d_scores, probs.astype(jnp.bfloat16)], axis=1)
            accum_ref[t] += dot_t(joined, both)
            return grad_query + dot(keys_t_ref[t], d_scores)

        grad_query = lax.fori_loop(
            meta[2 + docs + 2 * j],
            meta[3 + docs + 2 * j],
            step,
            jnp.zeros((HD, rows), jnp.float32),
        )
        dq_ref[:, at] = (grad_query * HD**-0.5).astype(jnp.bfloat16)
        return carry

    lax.fori_loop(0, groups, one_slot, 0)
    g, s = meta[0], meta[1]

    def finish(j, carry):
        at = pl.ds(pl.multiple_of(j * rows, rows), rows)
        for e in range(parts):
            terms = accum_ref[(g ^ j) * parts + lax.rem(s - e + parts, parts)].T
            d_key = terms[:HD] * HD**-0.5
            d_value = terms[HD:]
            if e == 0:
                mine_ref[0, :, at] = d_key
                mine_ref[1, :, at] = d_value
            else:
                theirs[e - 1, 0, :, at] = d_key.astype(jnp.bfloat16)
                theirs[e - 1, 1, :, at] = d_value.astype(jnp.bfloat16)
        return carry

    lax.fori_loop(0, groups, finish, 0)


def head_block(head, *shape):
    dims = tuple(1 if n is None else n for n in shape)
    where = shape.index(None)

    def at(h, meta):
        chosen = h if head is None else head
        return tuple(chosen if i == where else 0 for i in range(len(dims)))

    return pl.BlockSpec(dims, at)


def attend(meta, own, others, groups, parts, docs, rows, heads):
    tiles = groups * parts
    tokens = groups * rows
    block = partial(head_block, None)
    grid_spec = pltpu.PrefetchScalarGridSpec(
        num_scalar_prefetch=1,
        grid=(heads,),
        in_specs=[block(3, None, HD, rows)] * groups
        + [block(2, None, HD, rows)] * (groups * (parts - 1)),
        out_specs=[block(None, HD, tokens), block(None, HD, tokens), block(None, 1, tokens)],
        scratch_shapes=[
            pltpu.VMEM((groups, 2 * HD, rows), jnp.bfloat16),
            pltpu.VMEM((tiles, rows, 2 * HD), jnp.bfloat16),
            pltpu.VMEM((tiles, HD, rows), jnp.bfloat16),
        ],
    )
    return pl.pallas_call(
        partial(attend_kernel, groups, parts, docs, rows),
        grid_spec=grid_spec,
        out_shape=[
            jax.ShapeDtypeStruct((heads, HD, tokens), jnp.bfloat16),
            jax.ShapeDtypeStruct((heads, HD, tokens), jnp.float32),
            jax.ShapeDtypeStruct((heads, 1, tokens), jnp.float32),
        ],
        cost_estimate=pl.CostEstimate(
            flops=KERNEL_FLOPS * 2 * heads,
            transcendentals=0,
            bytes_accessed=KERNEL_BYTES * heads,
        ),
        name="attend",
    )(meta, *own, *others)


def attend_back(head, meta, own, others, grads, wide, log_total, groups, parts, docs, rows):
    tiles = groups * parts
    tokens = groups * rows
    block = partial(head_block, head)
    plain = lambda *dims: pl.BlockSpec(dims, lambda h, meta: (0,) * len(dims))
    out_specs = [plain(HD, tokens), plain(2, HD, tokens)]
    out_shape = [
        jax.ShapeDtypeStruct((HD, tokens), jnp.bfloat16),
        jax.ShapeDtypeStruct((2, HD, tokens), jnp.float32),
    ]
    if parts > 1:
        out_specs.append(plain(parts - 1, 2, HD, tokens))
        out_shape.append(jax.ShapeDtypeStruct((parts - 1, 2, HD, tokens), jnp.bfloat16))
    grid_spec = pltpu.PrefetchScalarGridSpec(
        num_scalar_prefetch=1,
        grid=(1,),
        in_specs=[block(3, None, HD, rows)] * groups
        + [block(2, None, HD, rows)] * (groups * (parts - 1))
        + [block(None, HD, rows)] * groups
        + [block(None, HD, tokens), block(None, 1, tokens)],
        out_specs=out_specs,
        scratch_shapes=[
            pltpu.VMEM((groups, 2 * HD, rows), jnp.bfloat16),
            pltpu.VMEM((groups, HD, rows), jnp.bfloat16),
            pltpu.VMEM((tiles, rows, 2 * HD), jnp.bfloat16),
            pltpu.VMEM((tiles, HD, rows), jnp.bfloat16),
            pltpu.VMEM((tiles, rows, HD), jnp.bfloat16),
            pltpu.VMEM((tiles, rows, 2 * HD), jnp.float32),
        ],
    )
    return pl.pallas_call(
        partial(attend_back_kernel, groups, parts, docs, rows),
        grid_spec=grid_spec,
        out_shape=out_shape,
        cost_estimate=pl.CostEstimate(
            flops=KERNEL_FLOPS * 5, transcendentals=0, bytes_accessed=KERNEL_BYTES
        ),
        name="attend_back",
    )(meta, *own, *others, *grads, wide, log_total)


ERFC = (
    -1.26551223, 1.00002368, 0.37409196, 0.09678418, -0.18628806,
    0.27886807, -1.13520398, 1.48851587, -0.82215223, 0.17087277,
)


def normal_terms(v):
    z = jnp.abs(v) * (0.5**0.5)
    t = 1.0 / (1.0 + 0.5 * z)
    poly = jnp.full_like(t, ERFC[-1])
    for term in reversed(ERFC[:-1]):
        poly = poly * t + term
    square = z * z
    tail = 0.5 * t * jnp.exp(poly - square)
    below = jnp.where(v < 0, tail, 1.0 - tail)
    return below, jnp.exp(-square) * (2.0 * math.pi) ** -0.5


def normed(resid):
    centred = resid - jnp.mean(resid, axis=-1, keepdims=True)
    spread = jnp.mean(centred * centred, axis=-1, keepdims=True)
    scale = lax.rsqrt(spread + EPSILON)
    return centred * scale, scale


def norm_back(grad, gain, unit, scale):
    e = grad * gain
    inner = jnp.mean(e * unit, axis=-1, keepdims=True)
    return (e - jnp.mean(e, axis=-1, keepdims=True) - unit * inner) * scale


def over_blocks(count, aligned, step, value):
    if aligned:
        return lax.fori_loop(0, count, step, value, unroll=4)
    for i in range(count):
        value = step(i, value)
    return value


def feed_kernel(
    tokens_ref,
    attended_ref,
    cot_ref,
    out_ref,
    in_ref,
    back_ref,
    vec_ref,
    in_bias_ref,
    result_ref,
    d_resid1_ref,
    d_attended_ref,
    hidden_ref,
    act_ref,
    d_ffn_ref,
    d_pre_ref,
    d_branch_ref,
    sums_ref,
    in_sums_ref,
    slope_ref,
):
    f32, bf16 = jnp.float32, jnp.bfloat16
    out_shift, gain_one, shift_one = vec_ref[2:3], vec_ref[3:4], vec_ref[4:5]
    back_shift, gain_two, shift_two = vec_ref[5:6], vec_ref[6:7], vec_ref[7:8]

    @pl.when(pl.program_id(0) == 0)
    def _():
        sums_ref[...] = jnp.zeros_like(sums_ref)
        in_sums_ref[...] = jnp.zeros_like(in_sums_ref)

    total = lambda a: jnp.sum(a, axis=0, keepdims=True)
    branch = dot(attended_ref[...].T, out_ref[...]) + out_shift
    unit1, scale1 = normed(tokens_ref[...].astype(f32) + branch)
    hidden = unit1 * gain_one + shift_one
    hidden_low = hidden.astype(bf16)
    count, unused, shard = hidden_ref.shape
    for i in range(count):
        hidden_ref[i] = hidden_low[:, i * shard : (i + 1) * shard]
    resid2 = hidden + back_shift
    blocks, unused, size = act_ref.shape
    aligned = size % 128 == 0
    columns = lambda i: pl.ds(pl.multiple_of(i * size, size) if aligned else i * size, size)

    def forward(i, resid2):
        cols = columns(i)
        pre = dot(hidden_low, in_ref[:, cols]) + in_bias_ref[:, cols]
        below, density = normal_terms(pre)
        act = (pre * below).astype(bf16)
        act_ref[i] = act
        slope_ref[i] = below + pre * density
        return resid2 + dot(act, back_ref[cols, :])

    resid2 = over_blocks(blocks, aligned, forward, hidden + back_shift)
    unit2, scale2 = normed(resid2)
    result_ref[...] = (unit2 * gain_two + shift_two).astype(bf16)
    cot = cot_ref[...].astype(f32)
    d_resid2 = norm_back(cot, gain_two, unit2, scale2)
    d_ffn = d_resid2.astype(bf16)
    d_ffn_ref[...] = d_ffn

    def backward(i, d_hidden):
        cols = columns(i)
        d_act = dot_t(d_ffn, back_ref[cols, :])
        d_pre = (d_act * slope_ref[i]).astype(bf16)
        d_pre_ref[:, cols] = d_pre
        in_sums_ref[:, cols] += total(d_pre.astype(f32))
        return d_hidden + dot_t(d_pre, in_ref[:, cols])

    d_hidden = over_blocks(blocks, aligned, backward, d_resid2)
    d_resid1 = norm_back(d_hidden, gain_one, unit1, scale1)
    d_resid1_ref[...] = d_resid1
    d_branch = d_resid1.astype(bf16)
    d_branch_ref[...] = d_branch
    d_attended_ref[...] = dot_t(out_ref[...], d_branch).astype(bf16)
    sums_ref[...] += jnp.concatenate(
        [
            total(d_branch.astype(f32)),
            total(d_hidden * unit1),
            total(d_hidden),
            total(d_ffn.astype(f32)),
            total(cot * unit2),
            total(cot),
            jnp.zeros((2, cot.shape[1]), f32),
        ],
        axis=0,
    )


def feed_forward(fsdp, tokens, attended_t, cotangent, out_full, in_full, back_full, vectors, in_shift):
    f32, bf16 = jnp.float32, jnp.bfloat16
    rows, model = tokens.shape
    inner = in_full.shape[1]
    tile = math.gcd(rows, 256)
    by_rows = lambda n: pl.BlockSpec((tile, n), lambda i: (i, 0))
    by_cols = lambda n: pl.BlockSpec((n, tile), lambda i: (0, i))
    blocks = lambda n: pl.BlockSpec((fsdp, tile, n // fsdp), lambda i: (0, i, 0))
    fixed = lambda m, n: pl.BlockSpec((m, n), lambda i: (0, 0))
    shape = jax.ShapeDtypeStruct
    return pl.pallas_call(
        feed_kernel,
        grid=(rows // tile,),
        in_specs=[
            by_rows(model), by_cols(model), by_rows(model), fixed(model, model),
            fixed(model, inner), fixed(inner, model), fixed(8, model), fixed(1, inner),
        ],
        out_specs=[
            by_rows(model), by_rows(model), by_cols(model), blocks(model), blocks(inner),
            by_rows(model), by_rows(inner), by_rows(model), fixed(8, model), fixed(1, inner),
        ],
        out_shape=[
            shape((rows, model), bf16), shape((rows, model), f32), shape((model, rows), bf16),
            shape((fsdp, rows, model // fsdp), bf16), shape((fsdp, rows, inner // fsdp), bf16),
            shape((rows, model), bf16),
            shape((rows, inner), bf16), shape((rows, model), bf16), shape((8, model), f32),
            shape((1, inner), f32),
        ],
        scratch_shapes=[pltpu.VMEM((fsdp, tile, inner // fsdp), f32)],
        cost_estimate=pl.CostEstimate(
            flops=rows * model * (8 * inner + 4 * model), transcendentals=0, bytes_accessed=30_000_000
        ),
        name="feed_forward",
    )(tokens, attended_t, cotangent, out_full, in_full, back_full, vectors, in_shift)


def weight_grad_kernel(which, *refs):
    ins, (d_ffn, d_pre, d_branch), outs = refs[:8], refs[8:11], refs[11:]
    bf16 = jnp.bfloat16
    for side in range(2):
        act, hidden, attended_t, line = ins[4 * side : 4 * side + 4]
        lower, upper = outs[2 * side : 2 * side + 2]
        first, second = act.shape[2], attended_t.shape[0]
        lower[0, :first] = dot(act[0].T, d_ffn[...]).astype(bf16)
        lower[0, first : first + second] = dot(attended_t[...], d_branch[...]).astype(bf16)
        lower[0, first + second :] = line[0].astype(bf16)
        upper[0] = dot(hidden[0].T, d_pre[...]).astype(bf16)


def weight_grads(which, act, hidden, attended_t, line, d_ffn, d_pre, d_branch):
    fsdp, rows, inner_shard = act.shape
    shard = hidden.shape[2]
    model, inner = d_ffn.shape[1], d_pre.shape[1]
    line_rows = line.shape[1]
    tall = inner_shard + shard + line_rows
    half = fsdp // 2
    in_specs = []
    for side in range(2):
        block = lambda i, w, side=side: 2 * i + w[side]
        in_specs += [
            pl.BlockSpec((1, rows, inner_shard), lambda i, w, b=block: (b(i, w), 0, 0)),
            pl.BlockSpec((1, rows, shard), lambda i, w, b=block: (b(i, w), 0, 0)),
            pl.BlockSpec((shard, rows), lambda i, w, b=block: (b(i, w), 0)),
            pl.BlockSpec((1, line_rows, model), lambda i, w, b=block: (b(i, w), 0, 0)),
        ]
    in_specs += [pl.BlockSpec((rows, n), lambda i, w: (0, 0)) for n in (model, inner, model)]
    out = [(tall, model), (shard, inner)] * 2
    return pl.pallas_call(
        weight_grad_kernel,
        grid_spec=pltpu.PrefetchScalarGridSpec(
            num_scalar_prefetch=1,
            grid=(half,),
            in_specs=in_specs,
            out_specs=[pl.BlockSpec((1,) + o, lambda i, w: (i, 0, 0)) for o in out],
        ),
        out_shape=[jax.ShapeDtypeStruct((half,) + o, jnp.bfloat16) for o in out],
        cost_estimate=pl.CostEstimate(
            flops=2 * rows * model * (2 * inner + model), transcendentals=0, bytes_accessed=25_000_000
        ),
        name="weight_grads",
    )(which, act, hidden, attended_t, line, act, hidden, attended_t, line, d_ffn, d_pre, d_branch)


def qkv_grad_kernel(fsdp, which, *refs):
    slots, (d_qkv, send, keep, total) = refs[:-4], refs[-4:]
    rows = slots[0].shape[0]
    shard = send.shape[1] - PAD
    size = math.gcd(total.shape[0], 256)

    def step(i, carry):
        at = pl.ds(pl.multiple_of(i * size, size), size)
        value = None
        for j, slot in enumerate(slots):
            term = dot_t(slot[:, at].T, d_qkv[:, j * rows : (j + 1) * rows])
            value = term if value is None else value + term
        total[at] = value
        return carry

    lax.fori_loop(0, total.shape[0] // size, step, 0)
    ones = jnp.ones((PAD, d_qkv.shape[1]), jnp.bfloat16)
    sums = dot_t(ones, d_qkv[...]).astype(jnp.bfloat16)
    for side, ref in enumerate((send, keep)):
        for i in range(fsdp // 2):
            at = pl.multiple_of((2 * i + which[side]) * shard, math.gcd(shard, 64))
            ref[i, :shard] = total[pl.ds(at, shard), :].astype(jnp.bfloat16)
            ref[i, shard:] = sums


def qkv_grads(which, slots, d_qkv_t, fsdp):
    rows, model = slots[0].shape
    width = d_qkv_t.shape[0]
    out = (fsdp // 2, model // fsdp + PAD, width)
    fixed = lambda dims: pl.BlockSpec(dims, lambda i, w: (0,) * len(dims))
    return pl.pallas_call(
        partial(qkv_grad_kernel, fsdp),
        grid_spec=pltpu.PrefetchScalarGridSpec(
            num_scalar_prefetch=1,
            grid=(1,),
            in_specs=[fixed((rows, model))] * len(slots) + [fixed(d_qkv_t.shape)],
            out_specs=[fixed(out)] * 2,
            scratch_shapes=[pltpu.VMEM((model, width), jnp.float32)],
        ),
        out_shape=[jax.ShapeDtypeStruct(out, jnp.bfloat16)] * 2,
        cost_estimate=pl.CostEstimate(
            flops=2 * rows * len(slots) * model * width, transcendentals=0, bytes_accessed=8_000_000
        ),
        name="qkv_grads",
    )(which, *slots, d_qkv_t)


def body(
    inputs,
    doc_starts,
    qkv_weight,
    query_bias,
    value_bias,
    out_weight,
    out_bias,
    norm1_gain,
    norm1_bias,
    in_weight,
    in_bias,
    back_weight,
    back_bias,
    norm2_gain,
    norm2_bias,
    cotangent,
):
    bf16, f32 = jnp.bfloat16, jnp.float32
    tokens = inputs[0]
    rows, model = tokens.shape
    starts = doc_starts[0]
    docs = starts.shape[0]
    ctx = lax.axis_size("ctx")
    fsdp = lax.axis_size("fsdp")
    groups = math.gcd(H, ctx)
    parts = ctx // groups
    heads = H // groups
    span = heads * HD
    width = 3 * span
    index = lax.axis_index("ctx")
    g, s = index // parts, index % parts
    f = lax.axis_index("fsdp")
    shard = model // fsdp

    slots = gather_groups(tokens, groups, parts)

    own_cols = jnp.concatenate(
        [lax.dynamic_slice_in_dim(qkv_weight, i * model + g * span, span, 1) for i in range(3)], axis=1
    )
    small = jnp.concatenate(
        [
            query_bias, value_bias, out_bias, norm1_gain, norm1_bias,
            back_bias, norm2_gain, norm2_bias, in_bias,
        ]
    )
    count = small.shape[0]
    extra = -(-count // (width * PAD)) * PAD
    small_block = jnp.pad(small, (0, extra * width - count)).reshape(extra, width)
    first = jnp.concatenate([own_cols, small_block], axis=0)
    first_top = gather_top(first)
    first_top, out_held, in_held, back_held = together(
        first_top, out_weight, in_weight, back_weight
    )
    out_top, in_top, back_top = gather_top(out_held), gather_top(in_held), gather_top(back_held)
    first = gather_rest(first, first_top)
    own_weight = first[:, :shard].reshape(model, width)
    flat = first[:, shard:].reshape(fsdp, extra * width)[:, :count].astype(f32)
    vectors = flat[:, : 8 * shard].reshape(fsdp, 8, shard).transpose(1, 0, 2).reshape(8, model)
    query_shift, value_shift = vectors[0], vectors[1]
    in_shift = flat[:, 8 * shard :].reshape(1, -1)

    zero = jnp.zeros((span,), f32)
    own_shift = jnp.concatenate(
        [
            lax.dynamic_slice(query_shift, (g * span,), (span,)),
            zero,
            lax.dynamic_slice(value_shift, (g * span,), (span,)),
        ]
    )
    own, others = [], []
    for slot in slots:
        projected = lax.dot_general(
            own_weight, slot, (((0,), (1,)), ((), ())), preferred_element_type=f32
        )
        low = (projected + own_shift[:, None]).astype(bf16).reshape(3, heads, HD, rows)
        own.append(low)
    for e in range(1, parts):
        for low in own:
            others.append(part_shift(low[1:], groups, parts, e))
    if parts > 1:
        in_top, others[0] = together(in_top, others[0])

    bounds = jnp.concatenate([starts, jnp.full((1,), ctx * rows, jnp.int32)])
    base = (g ^ jnp.arange(groups, dtype=jnp.int32)) * parts + s
    heads_at = base * rows
    tails_at = heads_at + rows - 1
    low_edge = jnp.max(jnp.where(starts[None] <= heads_at[:, None], starts[None], 0), axis=1)
    high_edge = jnp.min(
        jnp.where(bounds[None] > tails_at[:, None], bounds[None], ctx * rows), axis=1
    )
    ranges = jnp.stack([low_edge // rows, (high_edge + rows - 1) // rows], axis=1).reshape(-1)
    meta = jnp.concatenate([jnp.stack([g, s]).astype(jnp.int32), starts, ranges.astype(jnp.int32)])

    out_full = gather_rest(out_weight, out_top).reshape(model, model)
    in_full = gather_rest(in_weight, in_top).reshape(model, -1)
    meta, out_full, in_full = together(meta, out_full, in_full)
    low, wide, log_total = attend(meta, own, others, groups, parts, docs, rows, heads)
    attended_t = jnp.zeros((groups * span, rows), bf16)
    turned = []
    for j in range(groups):
        piece = low[:, :, j * rows : (j + 1) * rows]
        turned.append(ctx_swap(piece, groups, parts, j) if j else piece)
    for j, piece in enumerate(together(*turned)):
        attended_t = lax.dynamic_update_slice(
            attended_t, piece.reshape(span, rows), ((g ^ j) * span, 0)
        )
    back_full = gather_rest(back_weight, back_top).reshape(-1, model)

    (
        result, d_resid1, d_attended_t, hidden_low, act_low, d_ffn_low, d_pre_low, d_branch_low,
        sums, in_sums,
    ) = feed_forward(
        fsdp, tokens, attended_t, cotangent[0], out_full, in_full, back_full, vectors, in_shift
    )
    grads = []
    for j in range(groups):
        part = lax.dynamic_slice(d_attended_t, ((g ^ j) * span, 0), (span, rows))
        part = part.reshape(heads, HD, rows)
        grads.append(ctx_swap(part, groups, parts, j) if j else part)

    inner = in_full.shape[1]
    inner_shard = in_bias.shape[0]
    line = jnp.concatenate(
        [sums[:6].reshape(6, fsdp, shard).transpose(1, 0, 2).reshape(fsdp, -1), in_sums.reshape(fsdp, -1)],
        axis=1,
    )
    line_rows = -(inner_shard + shard) % 64 or 64
    line = jnp.pad(line, ((0, 0), (0, line_rows * model - line.shape[1])))
    line = line.reshape(fsdp, line_rows, model)
    mine = bit_at("fsdp", 0)
    which = jnp.stack([1 - mine, mine]).astype(jnp.int32)
    lower_send, upper_send, lower, upper = weight_grads(
        which, act_low, hidden_low, attended_t, line, d_ffn_low, d_pre_low, d_branch_low
    )
    lower = add_low(lower, swap(lower_send, "fsdp", 0))
    upper = add_low(upper, swap(upper_send, "fsdp", 0))
    fsdp_bits, ctx_bits = range(bits_of("fsdp")), range(bits_of("ctx"))
    chunks = inner // (2 * model)

    def pair_step(i, state):
        lower, upper = state
        lower_steps = [("fsdp", b) for b in fsdp_bits[1:]] + [("ctx", 0)]
        upper_steps = [("ctx", 0)] + [("fsdp", b) for b in fsdp_bits[1:]]
        return halve(lower, *lower_steps[i], 1), halve(upper, *upper_steps[i], 2)

    def merge(state):
        lower, upper = state
        return (
            jnp.concatenate(
                [lower[0]] + [upper[0, :, c * model : (c + 1) * model] for c in range(chunks)], axis=0
            ),
        )

    steps = [partial(pair_step, i) for i in range(len(fsdp_bits))]
    last = steps.pop()
    steps.append(lambda state: merge(last(state)))
    for bit in ctx_bits[1:-1]:
        steps.append(lambda state, bit=bit: (halve(state[0], "ctx", bit, 0),))
    state = (lower, upper)

    pieces = []
    held, theirs = None, None

    def settle(dq, dkv, theirs):
        for other in theirs:
            dkv = dkv + other.astype(f32)
        pieces.append(jnp.concatenate([dq[None], dkv.astype(bf16)], axis=0))

    def send(piece):
        parts_of = []
        for j in range(groups):
            part = piece[..., j * rows : (j + 1) * rows]
            parts_of.append(ctx_swap(part, groups, parts, j) if j else part)
        return parts_of

    for head in range(heads):
        meta, *state = together(meta, *state)
        flying = steps.pop(0)(state) if steps else state
        dq, dkv, *rest = attend_back(
            head, meta, own, others, grads, wide, log_total, groups, parts, docs, rows
        )
        if head:
            dq, dkv, *landed = together(dq, dkv, *rest, *flying)
            rest, state = landed[: len(rest)], landed[len(rest) :]
            dq, *theirs = together(dq, *theirs)
            settle(*held, theirs)
        else:
            state = flying
        if head == 1:
            early = send(pieces[0])
            dq, qkv_held = together(dq, qkv_weight)
            qkv_top = gather_top(qkv_held)
        elif head == 2:
            middle = send(pieces[1])
            dq, *early = together(dq, *early)
        held = (dq, dkv)
        theirs = [part_shift(rest[0][e - 1], groups, parts, -e) for e in range(1, parts)]
    settle(*held, theirs)
    for advance in steps:
        state = advance(state)
    other = swap(state[0], "ctx", ctx_bits[-1])
    d_qkv_t = jnp.stack(pieces, axis=1).reshape(width, groups * rows)
    qkv_send, qkv_sum = qkv_grads(which, slots, d_qkv_t, fsdp)
    other, qkv_send, qkv_sum, qkv_top, *middle = together(
        other, qkv_send, qkv_sum, qkv_top, *middle
    )
    qkv_full = gather_rest(qkv_held, qkv_top).reshape(model, 3 * model)
    merged = add_low(state[0], other)
    late, merged = together(pieces[2], merged)
    for bit in reversed(ctx_bits[1:-1]):
        merged = double(merged, "ctx", bit, 0)
    qkv_sum = add_low(qkv_sum, swap(qkv_send, "fsdp", 0))
    wide_sum = qkv_sum.astype(f32)
    for e in range(1, parts):
        wide_sum = wide_sum + part_shift(qkv_sum, groups, parts, e).astype(f32)
    qkv_sum, merged, qkv_full = together(wide_sum.astype(bf16), merged, qkv_full)
    other = swap(merged, "ctx", 0)
    late = send(late)
    for bit in fsdp_bits[1:]:
        qkv_sum = halve(qkv_sum, "fsdp", bit, 1)
    qkv_low = qkv_sum[0]
    by_group = jnp.zeros((groups,) + qkv_low.shape, bf16)
    turns = [ctx_swap(qkv_low, groups, parts, j) if j else qkv_low for j in range(groups)]
    lower_rows = (inner_shard + shard + line_rows) // 2
    lower = join(bit_at("ctx", 0), merged[:lower_rows], other[:lower_rows], 0)
    wide_half = lambda m: jnp.concatenate(
        [m[lower_rows + c * shard : lower_rows + (c + 1) * shard] for c in range(chunks)], axis=1
    )
    upper = join(bit_at("ctx", 0), wide_half(merged), wide_half(other), 1)
    lower, upper, *turns = together(lower.astype(f32), upper.astype(f32), *turns)
    for j, piece in enumerate(turns):
        by_group = lax.dynamic_update_slice(by_group, piece[None], (g ^ j, 0, 0))
    natural = jnp.concatenate(
        [by_group[b, :, i * span : (i + 1) * span] for i in range(3) for b in range(groups)], axis=1
    ).astype(f32)
    grad_qkv_shard = natural[:shard]
    bias_line = natural[shard]
    grad_query_shift = lax.dynamic_slice(bias_line, (f * shard,), (shard,))
    grad_value_shift = lax.dynamic_slice(bias_line, (2 * model + f * shard,), (shard,))

    natural = jnp.zeros((3, groups, heads, HD, rows), bf16)
    for j in range(groups):
        part = jnp.stack([early[j], middle[j], late[j]], axis=1)[:, None]
        natural = lax.dynamic_update_slice(natural, part, (0, g ^ j, 0, 0, 0))
    input_grad = d_resid1 + lax.dot_general(
        natural.reshape(3 * model, rows),
        qkv_full,
        (((0,), (1,)), ((), ())),
        preferred_element_type=f32,
    )

    ends = inner_shard + shard
    flat = lower[ends:].reshape(-1).astype(f32)
    offsets = lambda i: flat[i * shard : (i + 1) * shard]
    return (
        result[None],
        input_grad[None],
        grad_qkv_shard,
        grad_query_shift,
        grad_value_shift,
        lower[inner_shard:ends].astype(f32),
        offsets(0),
        offsets(1),
        offsets(2),
        upper.astype(f32),
        flat[6 * shard : 6 * shard + inner_shard],
        lower[:inner_shard].astype(f32),
        offsets(3),
        offsets(4),
        offsets(5),
    )


def solution(mesh):
    rows, one = P("fsdp", None), P("fsdp")
    whole = P("fsdp", "ctx", None)
    return jax.shard_map(
        body,
        mesh=mesh,
        in_specs=(
            whole, rows, rows, one, one, rows, one, one, one, rows, one, rows, one, one, one, whole,
        ),
        out_specs=(
            whole, whole, rows, one, one, rows, one, one, one, rows, one, rows, one, one, one,
        ),
        check_vma=False,
    )
```

```python
from functools import partial
import math

import jax
import jax.numpy as jnp
from jax import lax
from jax.experimental import pallas as pl
from jax.experimental.pallas import tpu as pltpu
from jax.sharding import PartitionSpec as P

H = 12
HD = 64
EPSILON = 1e-05
BIG = 2.0**100
PAD = 16
KERNEL_FLOPS = 3_000_000_000
KERNEL_BYTES = 20_000_000


def ctx_swap(array, groups, parts, flip):
    pairs = []
    for g in range(groups):
        for s in range(parts):
            pairs.append((g * parts + s, (g ^ flip) * parts + s))
    return lax.ppermute(array, "ctx", pairs)


def part_shift(array, groups, parts, by):
    pairs = []
    for g in range(groups):
        for s in range(parts):
            pairs.append((g * parts + s, g * parts + (s + by) % parts))
    return lax.ppermute(array, "ctx", pairs)


def gather_groups(array, groups, parts):
    return [array] + [ctx_swap(array, groups, parts, i) for i in range(1, groups)]


def swap(array, axis, bit):
    size = lax.axis_size(axis)
    return lax.ppermute(array, axis, [(i, i ^ (1 << bit)) for i in range(size)])


def bits_of(axis):
    return lax.axis_size(axis).bit_length() - 1


def bit_at(axis, bit):
    return (lax.axis_index(axis) >> bit) & 1


def pick(array, which, dim):
    return lax.dynamic_index_in_dim(array, which, dim, keepdims=False)


def together(*values):
    return lax.optimization_barrier(values)


def join(mine, own, other, dim):
    return jnp.where(
        mine == 0,
        jnp.concatenate([own, other], axis=dim),
        jnp.concatenate([other, own], axis=dim),
    )


def gather_top(shard):
    return swap(shard, "fsdp", bits_of("fsdp") - 1)


def gather_rest(shard, other):
    top = bits_of("fsdp") - 1
    held = join(bit_at("fsdp", top), shard[None], other[None], 0)
    for bit in reversed(range(top)):
        got = swap(held, "fsdp", bit)
        pair = join(bit_at("fsdp", bit), held[:, None], got[:, None], 1)
        held = pair.reshape((-1,) + shard.shape)
    return held


def halve(held, axis, bit, dim):
    mine = bit_at(axis, bit)
    if axis == "fsdp":
        pairs = held.reshape((held.shape[0] // 2, 2) + held.shape[1:])
        keep, send = pick(pairs, mine, 1), pick(pairs, 1 - mine, 1)
    else:
        half = held.shape[dim] // 2
        keep = lax.dynamic_slice_in_dim(held, mine * half, half, dim)
        send = lax.dynamic_slice_in_dim(held, (1 - mine) * half, half, dim)
    return add_low(keep, swap(send, axis, bit))


def add_low(a, b):
    return (a.astype(jnp.float32) + b.astype(jnp.float32)).astype(jnp.bfloat16)


def double(held, axis, bit, dim):
    return join(bit_at(axis, bit), held, swap(held, axis, bit), dim)


def doc_row(meta, base, length, docs):
    pos = base + lax.broadcasted_iota(jnp.int32, (1, length), 1)
    doc = jnp.full((1, length), -1, jnp.int32)
    for j in range(docs):
        doc = doc + (pos >= meta[2 + j]).astype(jnp.int32)
    return doc


def dot(a, b):
    return jnp.dot(a, b, preferred_element_type=jnp.float32)


def dot_t(a, b):
    return lax.dot_general(a, b, (((1,), (1,)), ((), ())), preferred_element_type=jnp.float32)


def fill_keys(meta, own, others, groups, parts, docs, rows, store):
    g, s = meta[0], meta[1]
    for j in range(groups):
        for e in range(parts):
            block = (g ^ j) * parts + lax.rem(s - e + parts, parts)
            if e == 0:
                key_t, value_t = own[j][1, 0], own[j][2, 0]
            else:
                ref = others[(e - 1) * groups + j]
                key_t, value_t = ref[0, 0], ref[1, 0]
            doc = doc_row(meta, block * rows, rows, docs)
            hot = (lax.broadcasted_iota(jnp.int32, (HD, rows), 0) == doc).astype(jnp.float32)
            keys = jnp.concatenate([key_t, hot.astype(jnp.bfloat16)], axis=0)
            store(block, keys, key_t, value_t)


def query_full(meta, query_t, j, groups, parts, docs, rows):
    g, s = meta[0], meta[1]
    block = (g ^ j) * parts + s
    doc = doc_row(meta, block * rows, rows, docs)
    shut = jnp.where(lax.broadcasted_iota(jnp.int32, (HD, rows), 0) == doc, 0.0, -BIG)
    scaled = query_t.astype(jnp.float32) * HD**-0.5
    return jnp.concatenate([scaled.astype(jnp.bfloat16), shut.astype(jnp.bfloat16)], axis=0)


def attend_kernel(groups, parts, docs, rows, meta, *refs):
    own = refs[:groups]
    others = refs[groups : groups * parts]
    low_ref, wide_ref, log_ref, queries_ref, keys_ref, values_ref = refs[groups * parts :]

    def store(block, keys, key_t, value_t):
        keys_ref[block] = keys.T
        values_ref[block] = value_t

    fill_keys(meta, own, others, groups, parts, docs, rows, store)
    for j in range(groups):
        queries_ref[j] = query_full(meta, own[j][0, 0], j, groups, parts, docs, rows)

    def one_slot(j, carry):
        full = queries_ref[j]

        def step(t, state):
            best, total, accum = state
            scores = dot(keys_ref[t], full)
            new_best = jnp.maximum(best, jnp.max(scores, axis=0, keepdims=True))
            weights = jnp.exp(scores - new_best)
            shrink = jnp.exp(best - new_best)
            total = total * shrink + jnp.sum(weights, axis=0, keepdims=True)
            accum = accum * shrink + dot(values_ref[t], weights.astype(jnp.bfloat16))
            return new_best, total, accum

        best, total, accum = lax.fori_loop(
            meta[2 + docs + 2 * j],
            meta[3 + docs + 2 * j],
            step,
            (
                jnp.full((1, rows), -BIG, jnp.float32),
                jnp.zeros((1, rows), jnp.float32),
                jnp.zeros((HD, rows), jnp.float32),
            ),
        )
        attended = accum / total
        at = pl.ds(pl.multiple_of(j * rows, rows), rows)
        wide_ref[0, :, at] = attended
        low_ref[0, :, at] = attended.astype(jnp.bfloat16)
        log_ref[0, :, at] = best + jnp.log(total)
        return carry

    lax.fori_loop(0, groups, one_slot, 0)


def attend_back_kernel(groups, parts, docs, rows, meta, *refs):
    own = refs[:groups]
    others = refs[groups : groups * parts]
    grads = refs[groups * parts : groups * parts + groups]
    rest = refs[groups * parts + groups :]
    wide_ref, log_ref = rest[:2]
    dq_ref, mine_ref = rest[2:4]
    theirs = rest[4] if parts > 1 else None
    queries_ref, grads_ref, keys_ref, keys_t_ref, values_ref, accum_ref = rest[-6:]

    def store(block, keys, key_t, value_t):
        keys_ref[block] = keys.T
        keys_t_ref[block] = key_t
        values_ref[block] = value_t.T

    fill_keys(meta, own, others, groups, parts, docs, rows, store)
    accum_ref[...] = jnp.zeros_like(accum_ref)
    for j in range(groups):
        queries_ref[j] = query_full(meta, own[j][0, 0], j, groups, parts, docs, rows)
        grads_ref[j] = grads[j][0]

    def one_slot(j, carry):
        at = pl.ds(pl.multiple_of(j * rows, rows), rows)
        full = queries_ref[j]
        grad_t = grads_ref[j]
        delta = jnp.sum(grad_t.astype(jnp.float32) * wide_ref[0, :, at], axis=0, keepdims=True)
        log_total = log_ref[0, :, at]
        blank = jnp.zeros((HD, rows), jnp.bfloat16)
        both = jnp.concatenate(
            [
                jnp.concatenate([full[:HD], blank], axis=1),
                jnp.concatenate([blank, grad_t], axis=1),
            ],
            axis=0,
        )

        def step(t, grad_query):
            scores = dot(keys_ref[t], full)
            probs = jnp.exp(scores - log_total)
            d_probs = dot(values_ref[t], grad_t)
            d_scores = (probs * (d_probs - delta)).astype(jnp.bfloat16)
            joined = jnp.concatenate([d_scores, probs.astype(jnp.bfloat16)], axis=1)
            accum_ref[t] += dot_t(joined, both)
            return grad_query + dot(keys_t_ref[t], d_scores)

        grad_query = lax.fori_loop(
            meta[2 + docs + 2 * j],
            meta[3 + docs + 2 * j],
            step,
            jnp.zeros((HD, rows), jnp.float32),
        )
        dq_ref[:, at] = (grad_query * HD**-0.5).astype(jnp.bfloat16)
        return carry

    lax.fori_loop(0, groups, one_slot, 0)
    g, s = meta[0], meta[1]

    def finish(j, carry):
        at = pl.ds(pl.multiple_of(j * rows, rows), rows)
        for e in range(parts):
            terms = accum_ref[(g ^ j) * parts + lax.rem(s - e + parts, parts)].T
            d_key = terms[:HD]
            d_value = terms[HD:]
            if e == 0:
                mine_ref[0, :, at] = d_key
                mine_ref[1, :, at] = d_value
            else:
                theirs[e - 1, 0, :, at] = d_key.astype(jnp.bfloat16)
                theirs[e - 1, 1, :, at] = d_value.astype(jnp.bfloat16)
        return carry

    lax.fori_loop(0, groups, finish, 0)


def head_block(head, *shape):
    dims = tuple(1 if n is None else n for n in shape)
    where = shape.index(None)

    def at(h, meta):
        chosen = h if head is None else head
        return tuple(chosen if i == where else 0 for i in range(len(dims)))

    return pl.BlockSpec(dims, at)


def attend(meta, own, others, groups, parts, docs, rows, heads):
    tiles = groups * parts
    tokens = groups * rows
    block = partial(head_block, None)
    grid_spec = pltpu.PrefetchScalarGridSpec(
        num_scalar_prefetch=1,
        grid=(heads,),
        in_specs=[block(3, None, HD, rows)] * groups
        + [block(2, None, HD, rows)] * (groups * (parts - 1)),
        out_specs=[block(None, HD, tokens), block(None, HD, tokens), block(None, 1, tokens)],
        scratch_shapes=[
            pltpu.VMEM((groups, 2 * HD, rows), jnp.bfloat16),
            pltpu.VMEM((tiles, rows, 2 * HD), jnp.bfloat16),
            pltpu.VMEM((tiles, HD, rows), jnp.bfloat16),
        ],
    )
    return pl.pallas_call(
        partial(attend_kernel, groups, parts, docs, rows),
        grid_spec=grid_spec,
        out_shape=[
            jax.ShapeDtypeStruct((heads, HD, tokens), jnp.bfloat16),
            jax.ShapeDtypeStruct((heads, HD, tokens), jnp.float32),
            jax.ShapeDtypeStruct((heads, 1, tokens), jnp.float32),
        ],
        cost_estimate=pl.CostEstimate(
            flops=KERNEL_FLOPS * 2 * heads,
            transcendentals=0,
            bytes_accessed=KERNEL_BYTES * heads,
        ),
        name="attend",
    )(meta, *own, *others)


def attend_back(head, meta, own, others, grads, wide, log_total, groups, parts, docs, rows):
    tiles = groups * parts
    tokens = groups * rows
    block = partial(head_block, head)
    plain = lambda *dims: pl.BlockSpec(dims, lambda h, meta: (0,) * len(dims))
    out_specs = [plain(HD, tokens), plain(2, HD, tokens)]
    out_shape = [
        jax.ShapeDtypeStruct((HD, tokens), jnp.bfloat16),
        jax.ShapeDtypeStruct((2, HD, tokens), jnp.float32),
    ]
    if parts > 1:
        out_specs.append(plain(parts - 1, 2, HD, tokens))
        out_shape.append(jax.ShapeDtypeStruct((parts - 1, 2, HD, tokens), jnp.bfloat16))
    grid_spec = pltpu.PrefetchScalarGridSpec(
        num_scalar_prefetch=1,
        grid=(1,),
        in_specs=[block(3, None, HD, rows)] * groups
        + [block(2, None, HD, rows)] * (groups * (parts - 1))
        + [block(None, HD, rows)] * groups
        + [block(None, HD, tokens), block(None, 1, tokens)],
        out_specs=out_specs,
        scratch_shapes=[
            pltpu.VMEM((groups, 2 * HD, rows), jnp.bfloat16),
            pltpu.VMEM((groups, HD, rows), jnp.bfloat16),
            pltpu.VMEM((tiles, rows, 2 * HD), jnp.bfloat16),
            pltpu.VMEM((tiles, HD, rows), jnp.bfloat16),
            pltpu.VMEM((tiles, rows, HD), jnp.bfloat16),
            pltpu.VMEM((tiles, rows, 2 * HD), jnp.float32),
        ],
    )
    return pl.pallas_call(
        partial(attend_back_kernel, groups, parts, docs, rows),
        grid_spec=grid_spec,
        out_shape=out_shape,
        cost_estimate=pl.CostEstimate(
            flops=KERNEL_FLOPS * 5, transcendentals=0, bytes_accessed=KERNEL_BYTES
        ),
        name="attend_back",
    )(meta, *own, *others, *grads, wide, log_total)


ERFC = (
    -1.26551223, 1.00002368, 0.37409196, 0.09678418, -0.18628806,
    0.27886807, -1.13520398, 1.48851587, -0.82215223, 0.17087277,
)


def normal_terms(v):
    z = jnp.abs(v) * (0.5**0.5)
    t = 1.0 / (1.0 + 0.5 * z)
    poly = jnp.full_like(t, ERFC[-1])
    for term in reversed(ERFC[:-1]):
        poly = poly * t + term
    square = z * z
    tail = 0.5 * t * jnp.exp(poly - square)
    below = jnp.where(v < 0, tail, 1.0 - tail)
    return below, jnp.exp(-square) * (2.0 * math.pi) ** -0.5


def normed(resid):
    centred = resid - jnp.mean(resid, axis=-1, keepdims=True)
    spread = jnp.mean(centred * centred, axis=-1, keepdims=True)
    scale = lax.rsqrt(spread + EPSILON)
    return centred * scale, scale


def norm_back(grad, gain, unit, scale):
    e = grad * gain
    inner = jnp.mean(e * unit, axis=-1, keepdims=True)
    return (e - jnp.mean(e, axis=-1, keepdims=True) - unit * inner) * scale


def over_blocks(count, aligned, step, value):
    if aligned:
        return lax.fori_loop(0, count, step, value, unroll=4)
    for i in range(count):
        value = step(i, value)
    return value


def feed_kernel(
    tokens_ref,
    attended_ref,
    cot_ref,
    out_ref,
    in_ref,
    back_ref,
    vec_ref,
    in_bias_ref,
    result_ref,
    d_resid1_ref,
    d_attended_ref,
    hidden_ref,
    act_ref,
    d_ffn_ref,
    d_pre_ref,
    d_branch_ref,
    sums_ref,
    in_sums_ref,
    slope_ref,
):
    f32, bf16 = jnp.float32, jnp.bfloat16
    out_shift, gain_one, shift_one = vec_ref[2:3], vec_ref[3:4], vec_ref[4:5]
    back_shift, gain_two, shift_two = vec_ref[5:6], vec_ref[6:7], vec_ref[7:8]

    @pl.when(pl.program_id(0) == 0)
    def _():
        sums_ref[...] = jnp.zeros_like(sums_ref)
        in_sums_ref[...] = jnp.zeros_like(in_sums_ref)

    total = lambda a: jnp.sum(a, axis=0, keepdims=True)
    branch = dot(attended_ref[...].T, out_ref[...]) + out_shift
    unit1, scale1 = normed(tokens_ref[...].astype(f32) + branch)
    hidden = unit1 * gain_one + shift_one
    hidden_low = hidden.astype(bf16)
    count, unused, shard = hidden_ref.shape
    for i in range(count):
        hidden_ref[i] = hidden_low[:, i * shard : (i + 1) * shard]
    resid2 = hidden + back_shift
    blocks, unused, size = act_ref.shape
    aligned = size % 128 == 0
    columns = lambda i: pl.ds(pl.multiple_of(i * size, size) if aligned else i * size, size)

    def forward(i, resid2):
        cols = columns(i)
        pre = dot(hidden_low, in_ref[:, cols]) + in_bias_ref[:, cols]
        below, density = normal_terms(pre)
        act = (pre * below).astype(bf16)
        act_ref[i] = act
        slope_ref[i] = below + pre * density
        return resid2 + dot(act, back_ref[cols, :])

    resid2 = over_blocks(blocks, aligned, forward, hidden + back_shift)
    unit2, scale2 = normed(resid2)
    result_ref[...] = (unit2 * gain_two + shift_two).astype(bf16)
    cot = cot_ref[...].astype(f32)
    d_resid2 = norm_back(cot, gain_two, unit2, scale2)
    d_ffn = d_resid2.astype(bf16)
    d_ffn_ref[...] = d_ffn

    def backward(i, d_hidden):
        cols = columns(i)
        d_act = dot_t(d_ffn, back_ref[cols, :])
        d_pre = (d_act * slope_ref[i]).astype(bf16)
        d_pre_ref[:, cols] = d_pre
        in_sums_ref[:, cols] += total(d_pre.astype(f32))
        return d_hidden + dot_t(d_pre, in_ref[:, cols])

    d_hidden = over_blocks(blocks, aligned, backward, d_resid2)
    d_resid1 = norm_back(d_hidden, gain_one, unit1, scale1)
    d_resid1_ref[...] = d_resid1
    d_branch = d_resid1.astype(bf16)
    d_branch_ref[...] = d_branch
    d_attended_ref[...] = dot_t(out_ref[...], d_branch).astype(bf16)
    sums_ref[...] += jnp.concatenate(
        [
            total(d_branch.astype(f32)),
            total(d_hidden * unit1),
            total(d_hidden),
            total(d_ffn.astype(f32)),
            total(cot * unit2),
            total(cot),
            jnp.zeros((2, cot.shape[1]), f32),
        ],
        axis=0,
    )


def feed_forward(fsdp, tokens, attended_t, cotangent, out_full, in_full, back_full, vectors, in_shift):
    f32, bf16 = jnp.float32, jnp.bfloat16
    rows, model = tokens.shape
    inner = in_full.shape[1]
    tile = math.gcd(rows, 256)
    by_rows = lambda n: pl.BlockSpec((tile, n), lambda i: (i, 0))
    by_cols = lambda n: pl.BlockSpec((n, tile), lambda i: (0, i))
    blocks = lambda n: pl.BlockSpec((fsdp, tile, n // fsdp), lambda i: (0, i, 0))
    fixed = lambda m, n: pl.BlockSpec((m, n), lambda i: (0, 0))
    shape = jax.ShapeDtypeStruct
    return pl.pallas_call(
        feed_kernel,
        grid=(rows // tile,),
        in_specs=[
            by_rows(model), by_cols(model), by_rows(model), fixed(model, model),
            fixed(model, inner), fixed(inner, model), fixed(8, model), fixed(1, inner),
        ],
        out_specs=[
            by_rows(model), by_rows(model), by_cols(model), blocks(model), blocks(inner),
            by_rows(model), by_rows(inner), by_rows(model), fixed(8, model), fixed(1, inner),
        ],
        out_shape=[
            shape((rows, model), bf16), shape((rows, model), f32), shape((model, rows), bf16),
            shape((fsdp, rows, model // fsdp), bf16), shape((fsdp, rows, inner // fsdp), bf16),
            shape((rows, model), bf16),
            shape((rows, inner), bf16), shape((rows, model), bf16), shape((8, model), f32),
            shape((1, inner), f32),
        ],
        scratch_shapes=[pltpu.VMEM((fsdp, tile, inner // fsdp), f32)],
        cost_estimate=pl.CostEstimate(
            flops=rows * model * (8 * inner + 4 * model), transcendentals=0, bytes_accessed=30_000_000
        ),
        name="feed_forward",
    )(tokens, attended_t, cotangent, out_full, in_full, back_full, vectors, in_shift)


def weight_grad_kernel(which, *refs):
    ins, (d_ffn, d_pre, d_branch), outs = refs[:8], refs[8:11], refs[11:]
    bf16 = jnp.bfloat16
    for side in range(2):
        act, hidden, attended_t, line = ins[4 * side : 4 * side + 4]
        lower, upper = outs[2 * side : 2 * side + 2]
        first, second = act.shape[2], attended_t.shape[0]
        lower[0, :first] = dot(act[0].T, d_ffn[...]).astype(bf16)
        lower[0, first : first + second] = dot(attended_t[...], d_branch[...]).astype(bf16)
        lower[0, first + second :] = line[0].astype(bf16)
        upper[0] = dot(hidden[0].T, d_pre[...]).astype(bf16)


def weight_grads(which, act, hidden, attended_t, line, d_ffn, d_pre, d_branch):
    fsdp, rows, inner_shard = act.shape
    shard = hidden.shape[2]
    model, inner = d_ffn.shape[1], d_pre.shape[1]
    line_rows = line.shape[1]
    tall = inner_shard + shard + line_rows
    half = fsdp // 2
    in_specs = []
    for side in range(2):
        block = lambda i, w, side=side: 2 * i + w[side]
        in_specs += [
            pl.BlockSpec((1, rows, inner_shard), lambda i, w, b=block: (b(i, w), 0, 0)),
            pl.BlockSpec((1, rows, shard), lambda i, w, b=block: (b(i, w), 0, 0)),
            pl.BlockSpec((shard, rows), lambda i, w, b=block: (b(i, w), 0)),
            pl.BlockSpec((1, line_rows, model), lambda i, w, b=block: (b(i, w), 0, 0)),
        ]
    in_specs += [pl.BlockSpec((rows, n), lambda i, w: (0, 0)) for n in (model, inner, model)]
    out = [(tall, model), (shard, inner)] * 2
    return pl.pallas_call(
        weight_grad_kernel,
        grid_spec=pltpu.PrefetchScalarGridSpec(
            num_scalar_prefetch=1,
            grid=(half,),
            in_specs=in_specs,
            out_specs=[pl.BlockSpec((1,) + o, lambda i, w: (i, 0, 0)) for o in out],
        ),
        out_shape=[jax.ShapeDtypeStruct((half,) + o, jnp.bfloat16) for o in out],
        cost_estimate=pl.CostEstimate(
            flops=2 * rows * model * (2 * inner + model), transcendentals=0, bytes_accessed=25_000_000
        ),
        name="weight_grads",
    )(which, act, hidden, attended_t, line, act, hidden, attended_t, line, d_ffn, d_pre, d_branch)


def qkv_grad_kernel(fsdp, which, *refs):
    slots, (d_qkv, send, keep, total) = refs[:-4], refs[-4:]
    rows = slots[0].shape[0]
    shard = send.shape[1] - PAD
    size = math.gcd(total.shape[0], 256)

    def step(i, carry):
        at = pl.ds(pl.multiple_of(i * size, size), size)
        value = None
        for j, slot in enumerate(slots):
            term = dot_t(slot[:, at].T, d_qkv[:, j * rows : (j + 1) * rows])
            value = term if value is None else value + term
        total[at] = value
        return carry

    lax.fori_loop(0, total.shape[0] // size, step, 0)
    ones = jnp.ones((PAD, d_qkv.shape[1]), jnp.bfloat16)
    sums = dot_t(ones, d_qkv[...]).astype(jnp.bfloat16)
    for side, ref in enumerate((send, keep)):
        for i in range(fsdp // 2):
            at = pl.multiple_of((2 * i + which[side]) * shard, math.gcd(shard, 64))
            ref[i, :shard] = total[pl.ds(at, shard), :].astype(jnp.bfloat16)
            ref[i, shard:] = sums


def qkv_grads(which, slots, d_qkv_t, fsdp):
    rows, model = slots[0].shape
    width = d_qkv_t.shape[0]
    out = (fsdp // 2, model // fsdp + PAD, width)
    fixed = lambda dims: pl.BlockSpec(dims, lambda i, w: (0,) * len(dims))
    return pl.pallas_call(
        partial(qkv_grad_kernel, fsdp),
        grid_spec=pltpu.PrefetchScalarGridSpec(
            num_scalar_prefetch=1,
            grid=(1,),
            in_specs=[fixed((rows, model))] * len(slots) + [fixed(d_qkv_t.shape)],
            out_specs=[fixed(out)] * 2,
            scratch_shapes=[pltpu.VMEM((model, width), jnp.float32)],
        ),
        out_shape=[jax.ShapeDtypeStruct(out, jnp.bfloat16)] * 2,
        cost_estimate=pl.CostEstimate(
            flops=2 * rows * len(slots) * model * width, transcendentals=0, bytes_accessed=8_000_000
        ),
        name="qkv_grads",
    )(which, *slots, d_qkv_t)


def body(
    inputs,
    doc_starts,
    qkv_weight,
    query_bias,
    value_bias,
    out_weight,
    out_bias,
    norm1_gain,
    norm1_bias,
    in_weight,
    in_bias,
    back_weight,
    back_bias,
    norm2_gain,
    norm2_bias,
    cotangent,
):
    bf16, f32 = jnp.bfloat16, jnp.float32
    tokens = inputs[0]
    rows, model = tokens.shape
    starts = doc_starts[0]
    docs = starts.shape[0]
    ctx = lax.axis_size("ctx")
    fsdp = lax.axis_size("fsdp")
    groups = math.gcd(H, ctx)
    parts = ctx // groups
    heads = H // groups
    span = heads * HD
    width = 3 * span
    index = lax.axis_index("ctx")
    g, s = index // parts, index % parts
    f = lax.axis_index("fsdp")
    shard = model // fsdp

    slots = gather_groups(tokens, groups, parts)

    own_cols = jnp.concatenate(
        [lax.dynamic_slice_in_dim(qkv_weight, i * model + g * span, span, 1) for i in range(3)], axis=1
    )
    small = jnp.concatenate(
        [
            query_bias, value_bias, out_bias, norm1_gain, norm1_bias,
            back_bias, norm2_gain, norm2_bias, in_bias,
        ]
    )
    count = small.shape[0]
    extra = -(-count // (width * PAD)) * PAD
    small_block = jnp.pad(small, (0, extra * width - count)).reshape(extra, width)
    first = jnp.concatenate([own_cols, small_block], axis=0)
    first_top = gather_top(first)
    first_top, out_held, in_held, back_held = together(
        first_top, out_weight, in_weight, back_weight
    )
    out_top, in_top, back_top = gather_top(out_held), gather_top(in_held), gather_top(back_held)
    first = gather_rest(first, first_top)
    own_weight = first[:, :shard].reshape(model, width)
    flat = first[:, shard:].reshape(fsdp, extra * width)[:, :count].astype(f32)
    vectors = flat[:, : 8 * shard].reshape(fsdp, 8, shard).transpose(1, 0, 2).reshape(8, model)
    query_shift, value_shift = vectors[0], vectors[1]
    in_shift = flat[:, 8 * shard :].reshape(1, -1)

    zero = jnp.zeros((span,), f32)
    own_shift = jnp.concatenate(
        [
            lax.dynamic_slice(query_shift, (g * span,), (span,)),
            zero,
            lax.dynamic_slice(value_shift, (g * span,), (span,)),
        ]
    )
    own, others = [], []
    for slot in slots:
        projected = lax.dot_general(
            own_weight, slot, (((0,), (1,)), ((), ())), preferred_element_type=f32
        )
        low = (projected + own_shift[:, None]).astype(bf16).reshape(3, heads, HD, rows)
        own.append(low)
    for e in range(1, parts):
        for low in own:
            others.append(part_shift(low[1:], groups, parts, e))
    if parts > 1:
        in_top, others[0] = together(in_top, others[0])

    bounds = jnp.concatenate([starts, jnp.full((1,), ctx * rows, jnp.int32)])
    base = (g ^ jnp.arange(groups, dtype=jnp.int32)) * parts + s
    heads_at = base * rows
    tails_at = heads_at + rows - 1
    low_edge = jnp.max(jnp.where(starts[None] <= heads_at[:, None], starts[None], 0), axis=1)
    high_edge = jnp.min(
        jnp.where(bounds[None] > tails_at[:, None], bounds[None], ctx * rows), axis=1
    )
    ranges = jnp.stack([low_edge // rows, (high_edge + rows - 1) // rows], axis=1).reshape(-1)
    meta = jnp.concatenate([jnp.stack([g, s]).astype(jnp.int32), starts, ranges.astype(jnp.int32)])

    out_full = gather_rest(out_weight, out_top).reshape(model, model)
    in_full = gather_rest(in_weight, in_top).reshape(model, -1)
    meta, out_full, in_full = together(meta, out_full, in_full)
    low, wide, log_total = attend(meta, own, others, groups, parts, docs, rows, heads)
    attended_t = jnp.zeros((groups * span, rows), bf16)
    turned = []
    for j in range(groups):
        piece = low[:, :, j * rows : (j + 1) * rows]
        turned.append(ctx_swap(piece, groups, parts, j) if j else piece)
    for j, piece in enumerate(together(*turned)):
        attended_t = lax.dynamic_update_slice(
            attended_t, piece.reshape(span, rows), ((g ^ j) * span, 0)
        )
    back_full = gather_rest(back_weight, back_top).reshape(-1, model)

    (
        result, d_resid1, d_attended_t, hidden_low, act_low, d_ffn_low, d_pre_low, d_branch_low,
        sums, in_sums,
    ) = feed_forward(
        fsdp, tokens, attended_t, cotangent[0], out_full, in_full, back_full, vectors, in_shift
    )
    grads = []
    for j in range(groups):
        part = lax.dynamic_slice(d_attended_t, ((g ^ j) * span, 0), (span, rows))
        part = part.reshape(heads, HD, rows)
        grads.append(ctx_swap(part, groups, parts, j) if j else part)

    inner = in_full.shape[1]
    inner_shard = in_bias.shape[0]
    line = jnp.concatenate(
        [sums[:6].reshape(6, fsdp, shard).transpose(1, 0, 2).reshape(fsdp, -1), in_sums.reshape(fsdp, -1)],
        axis=1,
    )
    line_rows = -(inner_shard + shard) % 64 or 64
    line = jnp.pad(line, ((0, 0), (0, line_rows * model - line.shape[1])))
    line = line.reshape(fsdp, line_rows, model)
    mine = bit_at("fsdp", 0)
    which = jnp.stack([1 - mine, mine]).astype(jnp.int32)
    lower_send, upper_send, lower, upper = weight_grads(
        which, act_low, hidden_low, attended_t, line, d_ffn_low, d_pre_low, d_branch_low
    )
    lower = add_low(lower, swap(lower_send, "fsdp", 0))
    upper = add_low(upper, swap(upper_send, "fsdp", 0))
    fsdp_bits, ctx_bits = range(bits_of("fsdp")), range(bits_of("ctx"))
    chunks = inner // (2 * model)

    def pair_step(i, state):
        lower, upper = state
        lower_steps = [("fsdp", b) for b in fsdp_bits[1:]] + [("ctx", 0)]
        upper_steps = [("ctx", 0)] + [("fsdp", b) for b in fsdp_bits[1:]]
        return halve(lower, *lower_steps[i], 1), halve(upper, *upper_steps[i], 2)

    def merge(state):
        lower, upper = state
        return (
            jnp.concatenate(
                [lower[0]] + [upper[0, :, c * model : (c + 1) * model] for c in range(chunks)], axis=0
            ),
        )

    steps = [partial(pair_step, i) for i in range(len(fsdp_bits))]
    last = steps.pop()
    steps.append(lambda state: merge(last(state)))
    for bit in ctx_bits[1:-1]:
        steps.append(lambda state, bit=bit: (halve(state[0], "ctx", bit, 0),))
    state = (lower, upper)

    pieces = []
    held, theirs = None, None

    def settle(dq, dkv, theirs):
        for other in theirs:
            dkv = dkv + other.astype(f32)
        pieces.append(jnp.concatenate([dq[None], dkv.astype(bf16)], axis=0))

    def send(piece):
        parts_of = []
        for j in range(groups):
            part = piece[..., j * rows : (j + 1) * rows]
            parts_of.append(ctx_swap(part, groups, parts, j) if j else part)
        return parts_of

    for head in range(heads):
        meta, *state = together(meta, *state)
        flying = steps.pop(0)(state) if steps else state
        dq, dkv, *rest = attend_back(
            head, meta, own, others, grads, wide, log_total, groups, parts, docs, rows
        )
        if head:
            dq, dkv, *landed = together(dq, dkv, *rest, *flying)
            rest, state = landed[: len(rest)], landed[len(rest) :]
            dq, *theirs = together(dq, *theirs)
            settle(*held, theirs)
        else:
            state = flying
        if head == 1:
            early = send(pieces[0])
            dq, qkv_held = together(dq, qkv_weight)
            qkv_top = gather_top(qkv_held)
        elif head == 2:
            middle = send(pieces[1])
            dq, *early = together(dq, *early)
        held = (dq, dkv)
        theirs = [part_shift(rest[0][e - 1], groups, parts, -e) for e in range(1, parts)]
    settle(*held, theirs)
    for advance in steps:
        state = advance(state)
    other = swap(state[0], "ctx", ctx_bits[-1])
    d_qkv_t = jnp.stack(pieces, axis=1).reshape(width, groups * rows)
    qkv_send, qkv_sum = qkv_grads(which, slots, d_qkv_t, fsdp)
    other, qkv_send, qkv_sum, qkv_top, *middle = together(
        other, qkv_send, qkv_sum, qkv_top, *middle
    )
    qkv_full = gather_rest(qkv_held, qkv_top).reshape(model, 3 * model)
    merged = add_low(state[0], other)
    late, merged = together(pieces[2], merged)
    for bit in reversed(ctx_bits[1:-1]):
        merged = double(merged, "ctx", bit, 0)
    qkv_sum = add_low(qkv_sum, swap(qkv_send, "fsdp", 0))
    wide_sum = qkv_sum.astype(f32)
    for e in range(1, parts):
        wide_sum = wide_sum + part_shift(qkv_sum, groups, parts, e).astype(f32)
    qkv_sum, merged, qkv_full = together(wide_sum.astype(bf16), merged, qkv_full)
    other = swap(merged, "ctx", 0)
    late = send(late)
    for bit in fsdp_bits[1:]:
        qkv_sum = halve(qkv_sum, "fsdp", bit, 1)
    qkv_low = qkv_sum[0]
    by_group = jnp.zeros((groups,) + qkv_low.shape, bf16)
    turns = [ctx_swap(qkv_low, groups, parts, j) if j else qkv_low for j in range(groups)]
    lower_rows = (inner_shard + shard + line_rows) // 2
    lower = join(bit_at("ctx", 0), merged[:lower_rows], other[:lower_rows], 0)
    wide_half = lambda m: jnp.concatenate(
        [m[lower_rows + c * shard : lower_rows + (c + 1) * shard] for c in range(chunks)], axis=1
    )
    upper = join(bit_at("ctx", 0), wide_half(merged), wide_half(other), 1)
    lower, upper, *turns = together(lower.astype(f32), upper.astype(f32), *turns)
    for j, piece in enumerate(turns):
        by_group = lax.dynamic_update_slice(by_group, piece[None], (g ^ j, 0, 0))
    natural = jnp.concatenate(
        [by_group[b, :, i * span : (i + 1) * span] for i in range(3) for b in range(groups)], axis=1
    ).astype(f32)
    grad_qkv_shard = natural[:shard]
    bias_line = natural[shard]
    grad_query_shift = lax.dynamic_slice(bias_line, (f * shard,), (shard,))
    grad_value_shift = lax.dynamic_slice(bias_line, (2 * model + f * shard,), (shard,))

    natural = jnp.zeros((3, groups, heads, HD, rows), bf16)
    for j in range(groups):
        part = jnp.stack([early[j], middle[j], late[j]], axis=1)[:, None]
        natural = lax.dynamic_update_slice(natural, part, (0, g ^ j, 0, 0, 0))
    input_grad = d_resid1 + lax.dot_general(
        natural.reshape(3 * model, rows),
        qkv_full,
        (((0,), (1,)), ((), ())),
        preferred_element_type=f32,
    )

    ends = inner_shard + shard
    flat = lower[ends:].reshape(-1).astype(f32)
    offsets = lambda i: flat[i * shard : (i + 1) * shard]
    return (
        result[None],
        input_grad[None],
        grad_qkv_shard,
        grad_query_shift,
        grad_value_shift,
        lower[inner_shard:ends].astype(f32),
        offsets(0),
        offsets(1),
        offsets(2),
        upper.astype(f32),
        flat[6 * shard : 6 * shard + inner_shard],
        lower[:inner_shard].astype(f32),
        offsets(3),
        offsets(4),
        offsets(5),
    )


def solution(mesh):
    rows, one = P("fsdp", None), P("fsdp")
    whole = P("fsdp", "ctx", None)
    return jax.shard_map(
        body,
        mesh=mesh,
        in_specs=(
            whole, rows, rows, one, one, rows, one, one, one, rows, one, rows, one, one, one, whole,
        ),
        out_specs=(
            whole, whole, rows, one, one, rows, one, one, one, rows, one, rows, one, one, one,
        ),
        check_vma=False,
    )
```

```python
from functools import partial
import math

import jax
import jax.numpy as jnp
from jax import lax
from jax.experimental import pallas as pl
from jax.experimental.pallas import tpu as pltpu
from jax.sharding import PartitionSpec as P

H = 12
HD = 64
EPSILON = 1e-05
BIG = 2.0**100
PAD = 16
KERNEL_FLOPS = 3_000_000_000
KERNEL_BYTES = 20_000_000


def ctx_swap(array, groups, parts, flip):
    pairs = []
    for g in range(groups):
        for s in range(parts):
            pairs.append((g * parts + s, (g ^ flip) * parts + s))
    return lax.ppermute(array, "ctx", pairs)


def part_shift(array, groups, parts, by):
    pairs = []
    for g in range(groups):
        for s in range(parts):
            pairs.append((g * parts + s, g * parts + (s + by) % parts))
    return lax.ppermute(array, "ctx", pairs)


def gather_groups(array, groups, parts):
    return [array] + [ctx_swap(array, groups, parts, i) for i in range(1, groups)]


def swap(array, axis, bit):
    size = lax.axis_size(axis)
    return lax.ppermute(array, axis, [(i, i ^ (1 << bit)) for i in range(size)])


def bits_of(axis):
    return lax.axis_size(axis).bit_length() - 1


def bit_at(axis, bit):
    return (lax.axis_index(axis) >> bit) & 1


def pick(array, which, dim):
    return lax.dynamic_index_in_dim(array, which, dim, keepdims=False)


def together(*values):
    return lax.optimization_barrier(values)


def join(mine, own, other, dim):
    return jnp.where(
        mine == 0,
        jnp.concatenate([own, other], axis=dim),
        jnp.concatenate([other, own], axis=dim),
    )


def gather_top(shard):
    return swap(shard, "fsdp", bits_of("fsdp") - 1)


def gather_rest(shard, other):
    top = bits_of("fsdp") - 1
    held = join(bit_at("fsdp", top), shard[None], other[None], 0)
    for bit in reversed(range(top)):
        got = swap(held, "fsdp", bit)
        pair = join(bit_at("fsdp", bit), held[:, None], got[:, None], 1)
        held = pair.reshape((-1,) + shard.shape)
    return held


def halve(held, axis, bit, dim):
    mine = bit_at(axis, bit)
    if axis == "fsdp":
        pairs = held.reshape((held.shape[0] // 2, 2) + held.shape[1:])
        keep, send = pick(pairs, mine, 1), pick(pairs, 1 - mine, 1)
    else:
        half = held.shape[dim] // 2
        keep = lax.dynamic_slice_in_dim(held, mine * half, half, dim)
        send = lax.dynamic_slice_in_dim(held, (1 - mine) * half, half, dim)
    return add_low(keep, swap(send, axis, bit))


def add_low(a, b):
    return (a.astype(jnp.float32) + b.astype(jnp.float32)).astype(jnp.bfloat16)


def double(held, axis, bit, dim):
    return join(bit_at(axis, bit), held, swap(held, axis, bit), dim)


def doc_row(meta, base, length, docs):
    pos = base + lax.broadcasted_iota(jnp.int32, (1, length), 1)
    doc = jnp.full((1, length), -1, jnp.int32)
    for j in range(docs):
        doc = doc + (pos >= meta[2 + j]).astype(jnp.int32)
    return doc


def dot(a, b):
    return jnp.dot(a, b, preferred_element_type=jnp.float32)


def dot_t(a, b):
    return lax.dot_general(a, b, (((1,), (1,)), ((), ())), preferred_element_type=jnp.float32)


def fill_keys(meta, own, others, groups, parts, docs, rows, store):
    g, s = meta[0], meta[1]
    for j in range(groups):
        for e in range(parts):
            block = (g ^ j) * parts + lax.rem(s - e + parts, parts)
            if e == 0:
                key_t, value_t = own[j][1, 0], own[j][2, 0]
            else:
                ref = others[(e - 1) * groups + j]
                key_t, value_t = ref[0, 0], ref[1, 0]
            doc = doc_row(meta, block * rows, rows, docs)
            hot = (lax.broadcasted_iota(jnp.int32, (HD, rows), 0) == doc).astype(jnp.float32)
            keys = jnp.concatenate([key_t, hot.astype(jnp.bfloat16)], axis=0)
            store(block, keys, key_t, value_t)


def query_full(meta, query_t, j, groups, parts, docs, rows):
    g, s = meta[0], meta[1]
    block = (g ^ j) * parts + s
    doc = doc_row(meta, block * rows, rows, docs)
    shut = jnp.where(lax.broadcasted_iota(jnp.int32, (HD, rows), 0) == doc, 0.0, -BIG)
    scaled = query_t.astype(jnp.float32) * HD**-0.5
    return jnp.concatenate([scaled.astype(jnp.bfloat16), shut.astype(jnp.bfloat16)], axis=0)


def attend_kernel(groups, parts, docs, rows, meta, *refs):
    own = refs[:groups]
    others = refs[groups : groups * parts]
    low_ref, wide_ref, log_ref, queries_ref, keys_ref, values_ref = refs[groups * parts :]

    def store(block, keys, key_t, value_t):
        keys_ref[block] = keys.T
        values_ref[block] = value_t

    fill_keys(meta, own, others, groups, parts, docs, rows, store)
    for j in range(groups):
        queries_ref[j] = query_full(meta, own[j][0, 0], j, groups, parts, docs, rows)

    def one_slot(j, carry):
        full = queries_ref[j]

        def step(t, state):
            best, total, accum = state
            scores = dot(keys_ref[t], full)
            new_best = jnp.maximum(best, jnp.max(scores, axis=0, keepdims=True))
            weights = jnp.exp(scores - new_best)
            shrink = jnp.exp(best - new_best)
            total = total * shrink + jnp.sum(weights, axis=0, keepdims=True)
            accum = accum * shrink + dot(values_ref[t], weights.astype(jnp.bfloat16))
            return new_best, total, accum

        best, total, accum = lax.fori_loop(
            meta[2 + docs + 2 * j],
            meta[3 + docs + 2 * j],
            step,
            (
                jnp.full((1, rows), -BIG, jnp.float32),
                jnp.zeros((1, rows), jnp.float32),
                jnp.zeros((HD, rows), jnp.float32),
            ),
        )
        attended = accum / total
        at = pl.ds(pl.multiple_of(j * rows, rows), rows)
        wide_ref[0, :, at] = attended
        low_ref[0, :, at] = attended.astype(jnp.bfloat16)
        log_ref[0, :, at] = best + jnp.log(total)
        return carry

    lax.fori_loop(0, groups, one_slot, 0)


def attend_back_kernel(groups, parts, docs, rows, meta, *refs):
    own = refs[:groups]
    others = refs[groups : groups * parts]
    grads = refs[groups * parts : groups * parts + groups]
    rest = refs[groups * parts + groups :]
    wide_ref, log_ref = rest[:2]
    dq_ref, mine_ref = rest[2:4]
    theirs = rest[4] if parts > 1 else None
    queries_ref, grads_ref, keys_ref, keys_t_ref, values_ref, accum_ref = rest[-6:]

    def store(block, keys, key_t, value_t):
        keys_ref[block] = keys.T
        keys_t_ref[block] = key_t
        values_ref[block] = value_t.T

    fill_keys(meta, own, others, groups, parts, docs, rows, store)
    accum_ref[...] = jnp.zeros_like(accum_ref)
    for j in range(groups):
        queries_ref[j] = query_full(meta, own[j][0, 0], j, groups, parts, docs, rows)
        grads_ref[j] = grads[j][0]

    def one_slot(j, carry):
        at = pl.ds(pl.multiple_of(j * rows, rows), rows)
        full = queries_ref[j]
        grad_t = grads_ref[j]
        delta = jnp.sum(grad_t.astype(jnp.float32) * wide_ref[0, :, at], axis=0, keepdims=True)
        log_total = log_ref[0, :, at]
        blank = jnp.zeros((HD, rows), jnp.bfloat16)
        both = jnp.concatenate(
            [
                jnp.concatenate([full[:HD], blank], axis=1),
                jnp.concatenate([blank, grad_t], axis=1),
            ],
            axis=0,
        )

        def step(t, grad_query):
            scores = dot(keys_ref[t], full)
            probs = jnp.exp(scores - log_total)
            d_probs = dot(values_ref[t], grad_t)
            d_scores = (probs * (d_probs - delta)).astype(jnp.bfloat16)
            joined = jnp.concatenate([d_scores, probs.astype(jnp.bfloat16)], axis=1)
            accum_ref[t] += dot_t(joined, both)
            return grad_query + dot(keys_t_ref[t], d_scores)

        grad_query = lax.fori_loop(
            meta[2 + docs + 2 * j],
            meta[3 + docs + 2 * j],
            step,
            jnp.zeros((HD, rows), jnp.float32),
        )
        dq_ref[:, at] = (grad_query * HD**-0.5).astype(jnp.bfloat16)
        return carry

    lax.fori_loop(0, groups, one_slot, 0)
    g, s = meta[0], meta[1]

    def finish(j, carry):
        at = pl.ds(pl.multiple_of(j * rows, rows), rows)
        for e in range(parts):
            terms = accum_ref[(g ^ j) * parts + lax.rem(s - e + parts, parts)].T
            d_key = terms[:HD]
            d_value = terms[HD:]
            if e == 0:
                mine_ref[0, :, at] = d_key
                mine_ref[1, :, at] = d_value
            else:
                theirs[e - 1, 0, :, at] = d_key.astype(jnp.bfloat16)
                theirs[e - 1, 1, :, at] = d_value.astype(jnp.bfloat16)
        return carry

    lax.fori_loop(0, groups, finish, 0)


def head_block(head, *shape):
    dims = tuple(1 if n is None else n for n in shape)
    where = shape.index(None)

    def at(h, meta):
        chosen = h if head is None else head
        return tuple(chosen if i == where else 0 for i in range(len(dims)))

    return pl.BlockSpec(dims, at)


def attend(meta, own, others, groups, parts, docs, rows, heads):
    tiles = groups * parts
    tokens = groups * rows
    block = partial(head_block, None)
    grid_spec = pltpu.PrefetchScalarGridSpec(
        num_scalar_prefetch=1,
        grid=(heads,),
        in_specs=[block(3, None, HD, rows)] * groups
        + [block(2, None, HD, rows)] * (groups * (parts - 1)),
        out_specs=[block(None, HD, tokens), block(None, HD, tokens), block(None, 1, tokens)],
        scratch_shapes=[
            pltpu.VMEM((groups, 2 * HD, rows), jnp.bfloat16),
            pltpu.VMEM((tiles, rows, 2 * HD), jnp.bfloat16),
            pltpu.VMEM((tiles, HD, rows), jnp.bfloat16),
        ],
    )
    return pl.pallas_call(
        partial(attend_kernel, groups, parts, docs, rows),
        grid_spec=grid_spec,
        out_shape=[
            jax.ShapeDtypeStruct((heads, HD, tokens), jnp.bfloat16),
            jax.ShapeDtypeStruct((heads, HD, tokens), jnp.float32),
            jax.ShapeDtypeStruct((heads, 1, tokens), jnp.float32),
        ],
        cost_estimate=pl.CostEstimate(
            flops=KERNEL_FLOPS * 2 * heads,
            transcendentals=0,
            bytes_accessed=KERNEL_BYTES * heads,
        ),
        name="attend",
    )(meta, *own, *others)


def attend_back(head, meta, own, others, grads, wide, log_total, groups, parts, docs, rows):
    tiles = groups * parts
    tokens = groups * rows
    block = partial(head_block, head)
    plain = lambda *dims: pl.BlockSpec(dims, lambda h, meta: (0,) * len(dims))
    out_specs = [plain(HD, tokens), plain(2, HD, tokens)]
    out_shape = [
        jax.ShapeDtypeStruct((HD, tokens), jnp.bfloat16),
        jax.ShapeDtypeStruct((2, HD, tokens), jnp.float32),
    ]
    if parts > 1:
        out_specs.append(plain(parts - 1, 2, HD, tokens))
        out_shape.append(jax.ShapeDtypeStruct((parts - 1, 2, HD, tokens), jnp.bfloat16))
    grid_spec = pltpu.PrefetchScalarGridSpec(
        num_scalar_prefetch=1,
        grid=(1,),
        in_specs=[block(3, None, HD, rows)] * groups
        + [block(2, None, HD, rows)] * (groups * (parts - 1))
        + [block(None, HD, rows)] * groups
        + [block(None, HD, tokens), block(None, 1, tokens)],
        out_specs=out_specs,
        scratch_shapes=[
            pltpu.VMEM((groups, 2 * HD, rows), jnp.bfloat16),
            pltpu.VMEM((groups, HD, rows), jnp.bfloat16),
            pltpu.VMEM((tiles, rows, 2 * HD), jnp.bfloat16),
            pltpu.VMEM((tiles, HD, rows), jnp.bfloat16),
            pltpu.VMEM((tiles, rows, HD), jnp.bfloat16),
            pltpu.VMEM((tiles, rows, 2 * HD), jnp.float32),
        ],
    )
    return pl.pallas_call(
        partial(attend_back_kernel, groups, parts, docs, rows),
        grid_spec=grid_spec,
        out_shape=out_shape,
        cost_estimate=pl.CostEstimate(
            flops=KERNEL_FLOPS * 5, transcendentals=0, bytes_accessed=KERNEL_BYTES
        ),
        name="attend_back",
    )(meta, *own, *others, *grads, wide, log_total)


ERFC = (
    -1.26551223, 1.00002368, 0.37409196, 0.09678418, -0.18628806,
    0.27886807, -1.13520398, 1.48851587, -0.82215223, 0.17087277,
)


def normal_terms(v):
    z = jnp.abs(v) * (0.5**0.5)
    t = 1.0 / (1.0 + 0.5 * z)
    poly = jnp.full_like(t, ERFC[-1])
    for term in reversed(ERFC[:-1]):
        poly = poly * t + term
    square = z * z
    tail = 0.5 * t * jnp.exp(poly - square)
    below = jnp.where(v < 0, tail, 1.0 - tail)
    return below, jnp.exp(-square) * (2.0 * math.pi) ** -0.5


def normed(resid):
    centred = resid - jnp.mean(resid, axis=-1, keepdims=True)
    spread = jnp.mean(centred * centred, axis=-1, keepdims=True)
    scale = lax.rsqrt(spread + EPSILON)
    return centred * scale, scale


def norm_back(grad, gain, unit, scale):
    e = grad * gain
    inner = jnp.mean(e * unit, axis=-1, keepdims=True)
    return (e - jnp.mean(e, axis=-1, keepdims=True) - unit * inner) * scale


def over_blocks(count, aligned, step, value):
    if aligned:
        return lax.fori_loop(0, count, step, value, unroll=4)
    for i in range(count):
        value = step(i, value)
    return value


def feed_kernel(
    tokens_ref,
    attended_ref,
    cot_ref,
    out_ref,
    in_ref,
    back_ref,
    vec_ref,
    in_bias_ref,
    result_ref,
    d_resid1_ref,
    d_attended_ref,
    hidden_ref,
    act_ref,
    d_ffn_ref,
    d_pre_ref,
    d_branch_ref,
    sums_ref,
    in_sums_ref,
    slope_ref,
):
    f32, bf16 = jnp.float32, jnp.bfloat16
    out_shift, gain_one, shift_one = vec_ref[2:3], vec_ref[3:4], vec_ref[4:5]
    back_shift, gain_two, shift_two = vec_ref[5:6], vec_ref[6:7], vec_ref[7:8]

    @pl.when(pl.program_id(0) == 0)
    def _():
        sums_ref[...] = jnp.zeros_like(sums_ref)
        in_sums_ref[...] = jnp.zeros_like(in_sums_ref)

    total = lambda a: jnp.sum(a, axis=0, keepdims=True)
    branch = dot(attended_ref[...].T, out_ref[...]) + out_shift
    unit1, scale1 = normed(tokens_ref[...].astype(f32) + branch)
    hidden = unit1 * gain_one + shift_one
    hidden_low = hidden.astype(bf16)
    count, unused, shard = hidden_ref.shape
    for i in range(count):
        hidden_ref[i] = hidden_low[:, i * shard : (i + 1) * shard]
    resid2 = hidden + back_shift
    blocks, unused, size = act_ref.shape
    aligned = size % 128 == 0
    columns = lambda i: pl.ds(pl.multiple_of(i * size, size) if aligned else i * size, size)

    def forward(i, resid2):
        cols = columns(i)
        pre = dot(hidden_low, in_ref[:, cols]) + in_bias_ref[:, cols]
        below, density = normal_terms(pre)
        act = (pre * below).astype(bf16)
        act_ref[i] = act
        slope_ref[i] = below + pre * density
        return resid2 + dot(act, back_ref[cols, :])

    resid2 = over_blocks(blocks, aligned, forward, hidden + back_shift)
    unit2, scale2 = normed(resid2)
    result_ref[...] = (unit2 * gain_two + shift_two).astype(bf16)
    cot = cot_ref[...].astype(f32)
    d_resid2 = norm_back(cot, gain_two, unit2, scale2)
    d_ffn = d_resid2.astype(bf16)
    d_ffn_ref[...] = d_ffn

    def backward(i, d_hidden):
        cols = columns(i)
        d_act = dot_t(d_ffn, back_ref[cols, :])
        d_pre = (d_act * slope_ref[i]).astype(bf16)
        d_pre_ref[:, cols] = d_pre
        in_sums_ref[:, cols] += total(d_pre.astype(f32))
        return d_hidden + dot_t(d_pre, in_ref[:, cols])

    d_hidden = over_blocks(blocks, aligned, backward, d_resid2)
    d_resid1 = norm_back(d_hidden, gain_one, unit1, scale1)
    d_resid1_ref[...] = d_resid1
    d_branch = d_resid1.astype(bf16)
    d_branch_ref[...] = d_branch
    d_attended_ref[...] = dot_t(out_ref[...], d_branch).astype(bf16)
    sums_ref[...] += jnp.concatenate(
        [
            total(d_branch.astype(f32)),
            total(d_hidden * unit1),
            total(d_hidden),
            total(d_ffn.astype(f32)),
            total(cot * unit2),
            total(cot),
            jnp.zeros((2, cot.shape[1]), f32),
        ],
        axis=0,
    )


def feed_forward(fsdp, tokens, attended_t, cotangent, out_full, in_full, back_full, vectors, in_shift):
    f32, bf16 = jnp.float32, jnp.bfloat16
    rows, model = tokens.shape
    inner = in_full.shape[1]
    tile = math.gcd(rows, 256)
    by_rows = lambda n: pl.BlockSpec((tile, n), lambda i: (i, 0))
    by_cols = lambda n: pl.BlockSpec((n, tile), lambda i: (0, i))
    blocks = lambda n: pl.BlockSpec((fsdp, tile, n // fsdp), lambda i: (0, i, 0))
    fixed = lambda m, n: pl.BlockSpec((m, n), lambda i: (0, 0))
    shape = jax.ShapeDtypeStruct
    return pl.pallas_call(
        feed_kernel,
        grid=(rows // tile,),
        in_specs=[
            by_rows(model), by_cols(model), by_rows(model), fixed(model, model),
            fixed(model, inner), fixed(inner, model), fixed(8, model), fixed(1, inner),
        ],
        out_specs=[
            by_rows(model), by_rows(model), by_cols(model), blocks(model), blocks(inner),
            by_rows(model), by_rows(inner), by_rows(model), fixed(8, model), fixed(1, inner),
        ],
        out_shape=[
            shape((rows, model), bf16), shape((rows, model), f32), shape((model, rows), bf16),
            shape((fsdp, rows, model // fsdp), bf16), shape((fsdp, rows, inner // fsdp), bf16),
            shape((rows, model), bf16),
            shape((rows, inner), bf16), shape((rows, model), bf16), shape((8, model), f32),
            shape((1, inner), f32),
        ],
        scratch_shapes=[pltpu.VMEM((fsdp, tile, inner // fsdp), f32)],
        cost_estimate=pl.CostEstimate(
            flops=rows * model * (8 * inner + 4 * model), transcendentals=0, bytes_accessed=30_000_000
        ),
        name="feed_forward",
    )(tokens, attended_t, cotangent, out_full, in_full, back_full, vectors, in_shift)


def weight_grad_kernel(which, *refs):
    ins, (d_ffn, d_pre, d_branch), outs = refs[:8], refs[8:11], refs[11:]
    bf16 = jnp.bfloat16
    for side in range(2):
        act, hidden, attended_t, line = ins[4 * side : 4 * side + 4]
        lower, upper = outs[2 * side : 2 * side + 2]
        first, second = act.shape[2], attended_t.shape[0]
        lower[0, :first] = dot(act[0].T, d_ffn[...]).astype(bf16)
        lower[0, first : first + second] = dot(attended_t[...], d_branch[...]).astype(bf16)
        lower[0, first + second :] = line[0].astype(bf16)
        upper[0] = dot(hidden[0].T, d_pre[...]).astype(bf16)


def weight_grads(which, act, hidden, attended_t, line, d_ffn, d_pre, d_branch):
    fsdp, rows, inner_shard = act.shape
    shard = hidden.shape[2]
    model, inner = d_ffn.shape[1], d_pre.shape[1]
    line_rows = line.shape[1]
    tall = inner_shard + shard + line_rows
    half = fsdp // 2
    in_specs = []
    for side in range(2):
        block = lambda i, w, side=side: 2 * i + w[side]
        in_specs += [
            pl.BlockSpec((1, rows, inner_shard), lambda i, w, b=block: (b(i, w), 0, 0)),
            pl.BlockSpec((1, rows, shard), lambda i, w, b=block: (b(i, w), 0, 0)),
            pl.BlockSpec((shard, rows), lambda i, w, b=block: (b(i, w), 0)),
            pl.BlockSpec((1, line_rows, model), lambda i, w, b=block: (b(i, w), 0, 0)),
        ]
    in_specs += [pl.BlockSpec((rows, n), lambda i, w: (0, 0)) for n in (model, inner, model)]
    out = [(tall, model), (shard, inner)] * 2
    return pl.pallas_call(
        weight_grad_kernel,
        grid_spec=pltpu.PrefetchScalarGridSpec(
            num_scalar_prefetch=1,
            grid=(half,),
            in_specs=in_specs,
            out_specs=[pl.BlockSpec((1,) + o, lambda i, w: (i, 0, 0)) for o in out],
        ),
        out_shape=[jax.ShapeDtypeStruct((half,) + o, jnp.bfloat16) for o in out],
        cost_estimate=pl.CostEstimate(
            flops=2 * rows * model * (2 * inner + model), transcendentals=0, bytes_accessed=25_000_000
        ),
        name="weight_grads",
    )(which, act, hidden, attended_t, line, act, hidden, attended_t, line, d_ffn, d_pre, d_branch)


def qkv_grad_kernel(fsdp, which, *refs):
    slots, (d_qkv, send, keep, total) = refs[:-4], refs[-4:]
    rows = slots[0].shape[0]
    shard = send.shape[1] - PAD
    size = math.gcd(total.shape[0], 256)

    def step(i, carry):
        at = pl.ds(pl.multiple_of(i * size, size), size)
        value = None
        for j, slot in enumerate(slots):
            term = dot_t(slot[:, at].T, d_qkv[:, j * rows : (j + 1) * rows])
            value = term if value is None else value + term
        total[at] = value
        return carry

    lax.fori_loop(0, total.shape[0] // size, step, 0)
    ones = jnp.ones((PAD, d_qkv.shape[1]), jnp.bfloat16)
    sums = dot_t(ones, d_qkv[...]).astype(jnp.bfloat16)
    for side, ref in enumerate((send, keep)):
        for i in range(fsdp // 2):
            at = pl.multiple_of((2 * i + which[side]) * shard, math.gcd(shard, 64))
            ref[i, :shard] = total[pl.ds(at, shard), :].astype(jnp.bfloat16)
            ref[i, shard:] = sums


def qkv_grads(which, slots, d_qkv_t, fsdp):
    rows, model = slots[0].shape
    width = d_qkv_t.shape[0]
    out = (fsdp // 2, model // fsdp + PAD, width)
    fixed = lambda dims: pl.BlockSpec(dims, lambda i, w: (0,) * len(dims))
    return pl.pallas_call(
        partial(qkv_grad_kernel, fsdp),
        grid_spec=pltpu.PrefetchScalarGridSpec(
            num_scalar_prefetch=1,
            grid=(1,),
            in_specs=[fixed((rows, model))] * len(slots) + [fixed(d_qkv_t.shape)],
            out_specs=[fixed(out)] * 2,
            scratch_shapes=[pltpu.VMEM((model, width), jnp.float32)],
        ),
        out_shape=[jax.ShapeDtypeStruct(out, jnp.bfloat16)] * 2,
        cost_estimate=pl.CostEstimate(
            flops=2 * rows * len(slots) * model * width, transcendentals=0, bytes_accessed=8_000_000
        ),
        name="qkv_grads",
    )(which, *slots, d_qkv_t)


def body(
    inputs,
    doc_starts,
    qkv_weight,
    query_bias,
    value_bias,
    out_weight,
    out_bias,
    norm1_gain,
    norm1_bias,
    in_weight,
    in_bias,
    back_weight,
    back_bias,
    norm2_gain,
    norm2_bias,
    cotangent,
):
    bf16, f32 = jnp.bfloat16, jnp.float32
    tokens = inputs[0]
    rows, model = tokens.shape
    starts = doc_starts[0]
    docs = starts.shape[0]
    ctx = lax.axis_size("ctx")
    fsdp = lax.axis_size("fsdp")
    groups = math.gcd(H, ctx)
    parts = ctx // groups
    heads = H // groups
    span = heads * HD
    width = 3 * span
    index = lax.axis_index("ctx")
    g, s = index // parts, index % parts
    f = lax.axis_index("fsdp")
    shard = model // fsdp

    slots = gather_groups(tokens, groups, parts)

    own_cols = jnp.concatenate(
        [lax.dynamic_slice_in_dim(qkv_weight, i * model + g * span, span, 1) for i in range(3)], axis=1
    )
    small = jnp.concatenate(
        [
            query_bias, value_bias, out_bias, norm1_gain, norm1_bias,
            back_bias, norm2_gain, norm2_bias, in_bias,
        ]
    )
    count = small.shape[0]
    extra = -(-count // (width * PAD)) * PAD
    small_block = jnp.pad(small, (0, extra * width - count)).reshape(extra, width)
    first = jnp.concatenate([own_cols, small_block], axis=0)
    first_top = gather_top(first)
    first_top, out_held, in_held, back_held = together(
        first_top, out_weight, in_weight, back_weight
    )
    out_top, in_top, back_top = gather_top(out_held), gather_top(in_held), gather_top(back_held)
    first = gather_rest(first, first_top)
    own_weight = first[:, :shard].reshape(model, width)
    flat = first[:, shard:].reshape(fsdp, extra * width)[:, :count].astype(f32)
    vectors = flat[:, : 8 * shard].reshape(fsdp, 8, shard).transpose(1, 0, 2).reshape(8, model)
    query_shift, value_shift = vectors[0], vectors[1]
    in_shift = flat[:, 8 * shard :].reshape(1, -1)

    zero = jnp.zeros((span,), f32)
    own_shift = jnp.concatenate(
        [
            lax.dynamic_slice(query_shift, (g * span,), (span,)),
            zero,
            lax.dynamic_slice(value_shift, (g * span,), (span,)),
        ]
    )
    own, others = [], []
    for slot in slots:
        projected = lax.dot_general(
            own_weight, slot, (((0,), (1,)), ((), ())), preferred_element_type=f32
        )
        low = (projected + own_shift[:, None]).astype(bf16).reshape(3, heads, HD, rows)
        own.append(low)
    for e in range(1, parts):
        for low in own:
            others.append(part_shift(low[1:], groups, parts, e))
    if parts > 1:
        in_top, others[0] = together(in_top, others[0])

    bounds = jnp.concatenate([starts, jnp.full((1,), ctx * rows, jnp.int32)])
    base = (g ^ jnp.arange(groups, dtype=jnp.int32)) * parts + s
    heads_at = base * rows
    tails_at = heads_at + rows - 1
    low_edge = jnp.max(jnp.where(starts[None] <= heads_at[:, None], starts[None], 0), axis=1)
    high_edge = jnp.min(
        jnp.where(bounds[None] > tails_at[:, None], bounds[None], ctx * rows), axis=1
    )
    ranges = jnp.stack([low_edge // rows, (high_edge + rows - 1) // rows], axis=1).reshape(-1)
    meta = jnp.concatenate([jnp.stack([g, s]).astype(jnp.int32), starts, ranges.astype(jnp.int32)])

    out_full = gather_rest(out_weight, out_top).reshape(model, model)
    in_full = gather_rest(in_weight, in_top).reshape(model, -1)
    meta, out_full, in_full = together(meta, out_full, in_full)
    low, wide, log_total = attend(meta, own, others, groups, parts, docs, rows, heads)
    attended_t = jnp.zeros((groups * span, rows), bf16)
    turned = []
    for j in range(groups):
        piece = low[:, :, j * rows : (j + 1) * rows]
        turned.append(ctx_swap(piece, groups, parts, j) if j else piece)
    for j, piece in enumerate(together(*turned)):
        attended_t = lax.dynamic_update_slice(
            attended_t, piece.reshape(span, rows), ((g ^ j) * span, 0)
        )
    back_full = gather_rest(back_weight, back_top).reshape(-1, model)

    (
        result, d_resid1, d_attended_t, hidden_low, act_low, d_ffn_low, d_pre_low, d_branch_low,
        sums, in_sums,
    ) = feed_forward(
        fsdp, tokens, attended_t, cotangent[0], out_full, in_full, back_full, vectors, in_shift
    )
    grads = []
    for j in range(groups):
        part = lax.dynamic_slice(d_attended_t, ((g ^ j) * span, 0), (span, rows))
        part = part.reshape(heads, HD, rows)
        grads.append(ctx_swap(part, groups, parts, j) if j else part)

    inner = in_full.shape[1]
    inner_shard = in_bias.shape[0]
    line = jnp.concatenate(
        [sums[:6].reshape(6, fsdp, shard).transpose(1, 0, 2).reshape(fsdp, -1), in_sums.reshape(fsdp, -1)],
        axis=1,
    )
    line_rows = -(inner_shard + shard) % 32 or 32
    line = jnp.pad(line, ((0, 0), (0, line_rows * model - line.shape[1])))
    line = line.reshape(fsdp, line_rows, model)
    mine = bit_at("fsdp", 0)
    which = jnp.stack([1 - mine, mine]).astype(jnp.int32)
    lower_send, upper_send, lower, upper = weight_grads(
        which, act_low, hidden_low, attended_t, line, d_ffn_low, d_pre_low, d_branch_low
    )
    lower = add_low(lower, swap(lower_send, "fsdp", 0))
    upper = add_low(upper, swap(upper_send, "fsdp", 0))
    fsdp_bits, ctx_bits = range(bits_of("fsdp")), range(bits_of("ctx"))
    chunks = inner // (2 * model)

    def pair_step(i, state):
        lower, upper = state
        lower_steps = [("fsdp", b) for b in fsdp_bits[1:]] + [("ctx", 0)]
        upper_steps = [("ctx", 0)] + [("fsdp", b) for b in fsdp_bits[1:]]
        return halve(lower, *lower_steps[i], 1), halve(upper, *upper_steps[i], 2)

    def merge(state):
        lower, upper = state
        return (
            jnp.concatenate(
                [lower[0]] + [upper[0, :, c * model : (c + 1) * model] for c in range(chunks)], axis=0
            ),
        )

    steps = [partial(pair_step, i) for i in range(len(fsdp_bits))]
    last = steps.pop()
    steps.append(lambda state: merge(last(state)))
    for bit in ctx_bits[1:-1]:
        steps.append(lambda state, bit=bit: (halve(state[0], "ctx", bit, 0),))
    state = (lower, upper)

    pieces = []
    held, theirs = None, None

    def settle(dq, dkv, theirs):
        for other in theirs:
            dkv = dkv + other.astype(f32)
        pieces.append(jnp.concatenate([dq[None], dkv.astype(bf16)], axis=0))

    def send(piece):
        parts_of = []
        for j in range(groups):
            part = piece[..., j * rows : (j + 1) * rows]
            parts_of.append(ctx_swap(part, groups, parts, j) if j else part)
        return parts_of

    for head in range(heads):
        meta, *state = together(meta, *state)
        flying = steps.pop(0)(state) if steps else state
        dq, dkv, *rest = attend_back(
            head, meta, own, others, grads, wide, log_total, groups, parts, docs, rows
        )
        if head:
            dq, dkv, *landed = together(dq, dkv, *rest, *flying)
            rest, state = landed[: len(rest)], landed[len(rest) :]
            dq, *theirs = together(dq, *theirs)
            settle(*held, theirs)
        else:
            state = flying
        if head == 1:
            early = send(pieces[0])
            dq, qkv_held = together(dq, qkv_weight)
            qkv_top = gather_top(qkv_held)
        elif head == 2:
            middle = send(pieces[1])
            dq, *early = together(dq, *early)
        held = (dq, dkv)
        theirs = [part_shift(rest[0][e - 1], groups, parts, -e) for e in range(1, parts)]
    settle(*held, theirs)
    for advance in steps:
        state = advance(state)
    other = swap(state[0], "ctx", ctx_bits[-1])
    d_qkv_t = jnp.stack(pieces, axis=1).reshape(width, groups * rows)
    qkv_send, qkv_sum = qkv_grads(which, slots, d_qkv_t, fsdp)
    other, qkv_send, qkv_sum, qkv_top, *middle = together(
        other, qkv_send, qkv_sum, qkv_top, *middle
    )
    qkv_full = gather_rest(qkv_held, qkv_top).reshape(model, 3 * model)
    merged = add_low(state[0], other)
    late, merged = together(pieces[2], merged)
    for bit in reversed(ctx_bits[1:-1]):
        merged = double(merged, "ctx", bit, 0)
    qkv_sum = add_low(qkv_sum, swap(qkv_send, "fsdp", 0))
    wide_sum = qkv_sum.astype(f32)
    for e in range(1, parts):
        wide_sum = wide_sum + part_shift(qkv_sum, groups, parts, e).astype(f32)
    qkv_sum, merged, qkv_full = together(wide_sum.astype(bf16), merged, qkv_full)
    other = swap(merged, "ctx", 0)
    late = send(late)
    for bit in fsdp_bits[1:]:
        qkv_sum = halve(qkv_sum, "fsdp", bit, 1)
    qkv_low = qkv_sum[0]
    by_group = jnp.zeros((groups,) + qkv_low.shape, bf16)
    turns = [ctx_swap(qkv_low, groups, parts, j) if j else qkv_low for j in range(groups)]
    lower_rows = (inner_shard + shard + line_rows) // 2
    lower = join(bit_at("ctx", 0), merged[:lower_rows], other[:lower_rows], 0)
    wide_half = lambda m: jnp.concatenate(
        [m[lower_rows + c * shard : lower_rows + (c + 1) * shard] for c in range(chunks)], axis=1
    )
    upper = join(bit_at("ctx", 0), wide_half(merged), wide_half(other), 1)
    lower, upper, *turns = together(lower.astype(f32), upper.astype(f32), *turns)
    for j, piece in enumerate(turns):
        by_group = lax.dynamic_update_slice(by_group, piece[None], (g ^ j, 0, 0))
    natural = jnp.concatenate(
        [by_group[b, :, i * span : (i + 1) * span] for i in range(3) for b in range(groups)], axis=1
    ).astype(f32)
    grad_qkv_shard = natural[:shard]
    bias_line = natural[shard]
    grad_query_shift = lax.dynamic_slice(bias_line, (f * shard,), (shard,))
    grad_value_shift = lax.dynamic_slice(bias_line, (2 * model + f * shard,), (shard,))

    natural = jnp.zeros((3, groups, heads, HD, rows), bf16)
    for j in range(groups):
        part = jnp.stack([early[j], middle[j], late[j]], axis=1)[:, None]
        natural = lax.dynamic_update_slice(natural, part, (0, g ^ j, 0, 0, 0))
    input_grad = d_resid1 + lax.dot_general(
        natural.reshape(3 * model, rows),
        qkv_full,
        (((0,), (1,)), ((), ())),
        preferred_element_type=f32,
    )

    ends = inner_shard + shard
    flat = lower[ends:].reshape(-1).astype(f32)
    offsets = lambda i: flat[i * shard : (i + 1) * shard]
    return (
        result[None],
        input_grad[None],
        grad_qkv_shard,
        grad_query_shift,
        grad_value_shift,
        lower[inner_shard:ends].astype(f32),
        offsets(0),
        offsets(1),
        offsets(2),
        upper.astype(f32),
        flat[6 * shard : 6 * shard + inner_shard],
        lower[:inner_shard].astype(f32),
        offsets(3),
        offsets(4),
        offsets(5),
    )


def solution(mesh):
    rows, one = P("fsdp", None), P("fsdp")
    whole = P("fsdp", "ctx", None)
    return jax.shard_map(
        body,
        mesh=mesh,
        in_specs=(
            whole, rows, rows, one, one, rows, one, one, one, rows, one, rows, one, one, one, whole,
        ),
        out_specs=(
            whole, whole, rows, one, one, rows, one, one, one, rows, one, rows, one, one, one,
        ),
        check_vma=False,
    )
```
